32 devices in a mesh: fsdp: 2 (over core), ctx: 4 (over y, x), tp: 4 (over z).
Axes of the slice: x: 2, y: 2, z: 4, core: 2. Of those that a mesh axis runs over, the one named last changes fastest.
Arguments:
- tokens: bfloat16 [4096, 2048], P(('fsdp', 'ctx')), may hold values from -6 to 6
- attn_gain: bfloat16 [2048], P(('fsdp', 'ctx')), may hold values from 0.099609375 to 1.8984375
- w_query: bfloat16 [2048, 2048], P(('fsdp', 'ctx'), 'tp'), may hold values from -0.125 to 0.125
- w_key: bfloat16 [2048, 256], P(('fsdp', 'ctx'), 'tp'), may hold values from -0.125 to 0.125
- w_value: bfloat16 [2048, 256], P(('fsdp', 'ctx'), 'tp'), may hold values from -0.125 to 0.125
- w_out: bfloat16 [2048, 2048], P('tp', ('fsdp', 'ctx')), may hold values from -1 to 1
- mlp_gain: bfloat16 [2048], P(('fsdp', 'ctx')), may hold values from 0.099609375 to 1.8984375
- w_gate: bfloat16 [2048, 5632], P(('fsdp', 'ctx'), 'tp'), may hold values from -0.125 to 0.125
- w_up: bfloat16 [2048, 5632], P(('fsdp', 'ctx'), 'tp'), may hold values from -0.125 to 0.125
- w_down: bfloat16 [5632, 2048], P('tp', ('fsdp', 'ctx')), may hold values from -0.15625 to 0.15625
- cotangent: bfloat16 [4096, 2048], P(('fsdp', 'ctx')), may hold values from -6 to 6
- positions: int32 [4096], P(('fsdp', 'ctx')), may hold values from 0 to 1023, as said below
- segments: int32 [4096], P(('fsdp', 'ctx')), may hold values from 0 to 4095, as said below
Outputs:
- output: bfloat16 [4096, 2048], P(('fsdp', 'ctx'))
- input_grad: bfloat16 [4096, 2048], P(('fsdp', 'ctx'))
- attn_gain_grad: float32 [2048], P(('fsdp', 'ctx'))
- w_query_grad: float32 [2048, 2048], P(('fsdp', 'ctx'), 'tp')
- w_key_grad: float32 [2048, 256], P(('fsdp', 'ctx'), 'tp')
- w_value_grad: float32 [2048, 256], P(('fsdp', 'ctx'), 'tp')
- w_out_grad: float32 [2048, 2048], P('tp', ('fsdp', 'ctx'))
- mlp_gain_grad: float32 [2048], P(('fsdp', 'ctx'))
- w_gate_grad: float32 [2048, 5632], P(('fsdp', 'ctx'), 'tp')
- w_up_grad: float32 [2048, 5632], P(('fsdp', 'ctx'), 'tp')
- w_down_grad: float32 [5632, 2048], P('tp', ('fsdp', 'ctx'))
The draws below stay inside these ranges and needn't reach their ends.
Inputs may be any that keep to these rules, and one draw needn't show every extreme that they name: Every sequence is cut into 8 stretches of 128 consecutive positions, laid in increasing order inside a stretch; its stretches lie on one index of fsdp, two on each index of ctx, in an order drawn from the seed; each device holds 4 stretches, those of one sequence side by side. `segments`: A document is a run of consecutive positions of one sequence with one number, 200 to 2000 long except the last of a sequence, which may be shorter; documents of different sequences have different numbers.
All inputs are finite; a program needn't handle non-finite values.
Results may differ from the reference program's by a relative error of at most 0.025.
Values may be sent and summed in bfloat16 or wider, within the bound.
A program may use at most 192 MiB of HBM per device.

```python
import jax
import jax.numpy as jnp
from jax import lax

D = 2048
H = 32
KVH = 4
HD = 64
FF = 5632
STRETCH = 128
SEQ_GRP = 2
DOC_MIN = 200
DOC_MAX = 2000
LENGTH = 1024
SEQS = 4
TOKENS = 4096
N_FSDP = 2
N_CTX = 4


def stretch_layout(key):
    seq_keys = jax.random.split(jax.random.fold_in(key, 7), SEQS)
    orders = jax.vmap(lambda one_key: jax.random.permutation(one_key, 2 * N_CTX))(seq_keys)
    orders = orders.reshape(N_FSDP, SEQ_GRP, N_CTX, 2).astype(jnp.int32)
    offsets = jnp.arange(STRETCH, dtype=jnp.int32)
    placed = orders[..., None] * STRETCH + offsets
    placed = jnp.transpose(placed, (0, 2, 1, 3, 4))
    return placed.reshape(-1).astype(jnp.int32)


def sequence_numbers():
    fsdp_part = jnp.arange(N_FSDP, dtype=jnp.int32)[:, None, None, None, None] * SEQ_GRP
    group_part = jnp.arange(SEQ_GRP, dtype=jnp.int32)[None, None, :, None, None]
    numbers = jnp.broadcast_to(fsdp_part + group_part, (N_FSDP, N_CTX, SEQ_GRP, 2, STRETCH))
    return numbers.reshape(-1)


def draw_positions(key, part):
    return stretch_layout(key)


def draw_segments(key, part):
    token_pos = stretch_layout(key)
    doc_count = LENGTH // DOC_MIN + 1
    doc_lengths = jax.random.randint(jax.random.fold_in(key, 11), (SEQS, doc_count), DOC_MIN, DOC_MAX + 1).astype(jnp.int32)
    doc_starts = jnp.cumsum(doc_lengths, axis=1) - doc_lengths
    last_starts = jnp.max(jnp.where(doc_starts <= LENGTH - 1, doc_starts, 0), axis=1).astype(jnp.int32)
    seq_ids = sequence_numbers()
    row_starts = doc_starts[seq_ids]
    begins = jnp.max(jnp.where(row_starts <= token_pos[:, None], row_starts, 0), axis=1).astype(jnp.int32)
    labels = jnp.where(begins == last_starts[seq_ids], LENGTH - 1, begins).astype(jnp.int32)
    return (seq_ids * LENGTH + labels).astype(jnp.int32)


def spiked(values, rng, source, target, parts, factor):
    owner, partner = [(jnp.arange(values.shape[position]) // (values.shape[position] // parts)).reshape([-1 if axis == position else 1 for axis in range(values.ndim)]) for position in (source, target)]
    chosen = jax.random.permutation(rng, parts)[partner]
    strong = (owner == chosen) | (owner == (partner + parts // 2) % parts)
    return jnp.where(strong, factor * values, values)


def block_levels(own_key, extent, shards, smallest, top_value):
    level, own = 1.0, jax.random.fold_in(own_key, 6)
    for dim, parts in shards:
        steps = jnp.exp(jax.random.uniform(jax.random.fold_in(own, dim), (parts,), jnp.float32, smallest / len(shards), top_value / len(shards)))
        level = level * jnp.repeat(steps, extent[dim] // parts).reshape([-1 if axis == dim else 1 for axis in range(len(extent))])
    return level


def scatter_about(stream_key, shape, width, reach, cuts=(), kind=jnp.bfloat16):
    drawn = jax.random.normal(stream_key, shape, jnp.float32) * width
    if len(cuts) > 0:
        drawn = block_levels(stream_key, shape, cuts, -0.22, 0.18) * drawn
    return jnp.clip(drawn, min=-reach, max=reach).astype(kind)


def bell_draw_with(own_key, dims, scale, bound, shards, heavy, kind=jnp.bfloat16):
    values = scale * jax.random.normal(own_key, dims, jnp.float32)
    if shards:
        values = values * block_levels(own_key, dims, shards, -0.22, 0.18)
    return jnp.clip(spiked(values, jax.random.fold_in(own_key, 3), *heavy), -bound, bound).astype(kind)


def setup_inputs(seed: int = 0) -> dict:
    streams_of = jax.random.split(jax.random.key(seed), 14)
    return {
        "tokens": scatter_about(streams_of[0], (TOKENS, D), 1.0, 6.0, ((0, 8),)),
        "attn_gain": jnp.clip(1.0 + 0.18 * jax.random.normal(streams_of[1], (D,), jnp.float32), 0.099609375, 1.8984375).astype(jnp.bfloat16),
        "w_query": scatter_about(streams_of[2], (D, H * HD), D ** -0.5, 0.125, ((0, 8), (1, 4))),
        "w_key": scatter_about(streams_of[3], (D, KVH * HD), D ** -0.5, 0.125, ((0, 8), (1, 4))),
        "w_value": scatter_about(streams_of[4], (D, KVH * HD), D ** -0.5, 0.125, ((0, 8), (1, 4))),
        "w_out": scatter_about(streams_of[5], (H * HD, D), (H * HD // 64) ** -0.5, 1.0, ((0, 4), (1, 8))),
        "mlp_gain": jnp.clip(1.0 + 0.18 * jax.random.normal(streams_of[6], (D,), jnp.float32), 0.099609375, 1.8984375).astype(jnp.bfloat16),
        "w_gate": scatter_about(streams_of[7], (D, FF), D ** -0.5, 0.125, ((0, 8), (1, 4))),
        "w_up": scatter_about(streams_of[8], (D, FF), D ** -0.5, 0.125, ((0, 8), (1, 4))),
        "w_down": scatter_about(streams_of[9], (FF, D), (FF // 4) ** -0.5, 0.15625, ((0, 4), (1, 8))),
        "cotangent": bell_draw_with(streams_of[10], (TOKENS, D), 1.0, 6.0, ((0, 8),), (0, 1, 8, 2.0)),
        "positions": draw_positions(jax.random.fold_in(streams_of[13], 71), 0),
        "segments": draw_segments(jax.random.fold_in(streams_of[13], 71), 0),
    }


EPSILON = 1e-05
THETA_BASE = 10000.0
MASKED_SCORE = -1e+30
HIGHEST = lax.Precision.HIGHEST

@jax.custom_vjp
def low(v):
    return lax.optimization_barrier(v.astype(jnp.bfloat16)).astype(jnp.float32)

@jax.custom_vjp
def low_back(v):
    return v

def low_keep(v):
    return (low(v), None)

def low_pass(kept, grad):
    return (grad,)

def back_keep(v):
    return (v, None)

def back_low(kept, grad):
    return (low(grad),)
low.defvjp(low_keep, low_pass)
low_back.defvjp(back_keep, back_low)

def rope_tables(token_pos, half_size):
    frequency = THETA_BASE ** (-jnp.arange(half_size, dtype=jnp.float32) / half_size)
    angles = token_pos.astype(jnp.float32)[:, None] * frequency[None, :]
    return (jnp.cos(angles), jnp.sin(angles))

def rotate(head_rows, cosine, sine):
    half_size = head_rows.shape[-1] // 2
    first_half = head_rows[..., :half_size]
    second_half = head_rows[..., half_size:]
    cos_rows = cosine[:, None, :]
    sin_rows = sine[:, None, :]
    return jnp.concatenate([first_half * cos_rows - second_half * sin_rows, second_half * cos_rows + first_half * sin_rows], axis=-1)

def rms_norm(rows_in, gain_vec):
    return rows_in * lax.rsqrt(lax.optimization_barrier(jnp.mean(rows_in * rows_in, axis=-1, keepdims=True)) + EPSILON) * gain_vec

def project(left_side, right_side):
    return jnp.dot(left_side, right_side, precision=HIGHEST, preferred_element_type=jnp.float32)

def to_sequences(tensor):
    trailing = tensor.shape[1:]
    shaped = tensor.reshape((N_FSDP, N_CTX, SEQ_GRP, 2 * STRETCH) + trailing)
    return jnp.swapaxes(shaped, 1, 2).reshape((SEQS, LENGTH) + trailing)

def from_sequences(tensor):
    trailing = tensor.shape[2:]
    shaped = tensor.reshape((N_FSDP, SEQ_GRP, N_CTX, 2 * STRETCH) + trailing)
    return jnp.swapaxes(shaped, 1, 2).reshape((TOKENS,) + trailing)

def sequence_attention(inputs):
    queries, keys_all, values_all, key_pos, key_seg = inputs
    query_span = min(512, LENGTH)
    groups = H // KVH

    def query_block(pieces):
        query_rows, query_pos, query_seg = pieces
        grouped = query_rows.reshape(query_span, KVH, groups, HD)
        scores = jnp.einsum('qkgd,pkd->kgqp', grouped, keys_all, precision=HIGHEST) * HD ** (-0.5)
        scores = low_back(scores)
        visible = (query_seg[:, None] == key_seg[None, :]) & (key_pos[None, :] <= query_pos[:, None])
        masked = jnp.where(visible, scores, MASKED_SCORE)
        shifted = jnp.exp(masked - lax.optimization_barrier(jnp.max(masked, axis=-1, keepdims=True)))
        attn_probs = low(shifted / lax.optimization_barrier(jnp.sum(shifted, axis=-1, keepdims=True)))
        mixed_heads = jnp.einsum('kgqp,pkd->qkgd', attn_probs, values_all, precision=HIGHEST)
        return mixed_heads.reshape(query_span, H * HD)
    count_blocks = LENGTH // query_span
    blocks = lax.map(jax.checkpoint(query_block), (queries.reshape(count_blocks, query_span, H, HD), key_pos.reshape(count_blocks, query_span), key_seg.reshape(count_blocks, query_span)))
    return blocks.reshape(LENGTH, H * HD)

def reference(tokens, attn_gain, w_query, w_key, w_value, w_out, mlp_gain, w_gate, w_up, w_down, cotangent, positions, segments):
    cosine, sine = rope_tables(positions, HD // 2)
    seq_pos = to_sequences(positions)
    seq_seg = to_sequences(segments)

    def forward(token_rows, gain_one, query_w, key_w, value_w, out_w, gain_two, gate_w, up_w, down_w):
        normed_one = low(rms_norm(token_rows, gain_one))
        query_lin = low_back(project(normed_one, query_w))
        key_lin = low_back(project(normed_one, key_w))
        value_lin = low(low_back(project(normed_one, value_w)))
        query_rot = low(rotate(query_lin.reshape(TOKENS, H, HD), cosine, sine))
        key_rot = low(rotate(key_lin.reshape(TOKENS, KVH, HD), cosine, sine))
        attended = lax.map(sequence_attention, (to_sequences(query_rot), to_sequences(key_rot), to_sequences(value_lin.reshape(TOKENS, KVH, HD)), seq_pos, seq_seg))
        attended = low_back(low(from_sequences(attended)))
        middle = token_rows + low_back(project(attended, out_w))
        normed_two = low(rms_norm(middle, gain_two))
        gate_lin = low_back(project(normed_two, gate_w))
        up_lin = low_back(project(normed_two, up_w))
        hidden = low(jax.nn.silu(gate_lin) * up_lin)
        return middle + low_back(project(hidden, down_w))
    floats = tuple((item.astype(jnp.float32) for item in (tokens, attn_gain, w_query, w_key, w_value, w_out, mlp_gain, w_gate, w_up, w_down)))
    result, pullback = jax.vjp(forward, *floats)
    grads = pullback(cotangent.astype(jnp.float32))
    return (result.astype(jnp.bfloat16), grads[0].astype(jnp.bfloat16), grads[1], grads[2], grads[3], grads[4], grads[5], grads[6], grads[7], grads[8], grads[9])
```

```python
import jax
import jax.numpy as jnp
from jax import lax
from jax.experimental import pallas as pl
from jax.experimental.pallas import tpu as pltpu
from jax.sharding import PartitionSpec as P

H = 32
KVH = 4
HD = 64


EPSILON = 1e-05
THETA_BASE = 10000.0
MASKED_SCORE = -1e30


def shifted(value, axis, steps):
    count = lax.axis_size(axis)
    pairs = [(source, (source + steps) % count) for source in range(count)]
    return lax.ppermute(value, axis, pairs)


def rope_tables(token_pos, half_size):
    frequency = THETA_BASE ** (-jnp.arange(half_size, dtype=jnp.float32) / half_size)
    angles = token_pos.astype(jnp.float32)[:, None] * frequency[None, :]
    return (jnp.cos(angles), jnp.sin(angles))


def rotate(head_rows, cosine, sine):
    half_size = head_rows.shape[-1] // 2
    first_half = head_rows[..., :half_size]
    second_half = head_rows[..., half_size:]
    cos_rows = cosine[:, None, :]
    sin_rows = sine[:, None, :]
    return jnp.concatenate(
        [
            first_half * cos_rows - second_half * sin_rows,
            second_half * cos_rows + first_half * sin_rows,
        ],
        axis=-1,
    )


def rotate_back(head_rows, cosine, sine):
    half_size = head_rows.shape[-1] // 2
    first_half = head_rows[..., :half_size]
    second_half = head_rows[..., half_size:]
    cos_rows = cosine[:, None, :]
    sin_rows = sine[:, None, :]
    return jnp.concatenate(
        [
            first_half * cos_rows + second_half * sin_rows,
            second_half * cos_rows - first_half * sin_rows,
        ],
        axis=-1,
    )


def project(left_side, right_side):
    return jnp.dot(left_side, right_side, preferred_element_type=jnp.float32)


def project_back(left_side, right_side):
    return lax.dot_general(
        left_side, right_side, (((1,), (1,)), ((), ())), preferred_element_type=jnp.float32
    )


def weight_grad(left_side, right_side):
    return lax.dot_general(
        left_side, right_side, (((0,), (0,)), ((), ())), preferred_element_type=jnp.float32
    )


def rms_norm(rows_in, gain_vec):
    inv_rms = lax.rsqrt(jnp.mean(rows_in * rows_in, axis=-1, keepdims=True) + EPSILON)
    unit_rows = rows_in * inv_rms
    return (unit_rows * gain_vec, unit_rows, inv_rms)


def rms_norm_back(gradient, gain_vec, unit_rows, inv_rms):
    gain_grad = jnp.sum(gradient * unit_rows, axis=0)
    scaled_grad = gradient * gain_vec
    return (
        inv_rms
        * (scaled_grad - unit_rows * jnp.mean(scaled_grad * unit_rows, axis=-1, keepdims=True)),
        gain_grad,
    )


def pair_mask(query_pos, query_seg, key_pos, key_seg):
    return (query_seg[:, None] == key_seg[None, :]) & (key_pos[None, :] <= query_pos[:, None])


def split_block(kv_block, kv_heads):
    key_rows = kv_block[:, : kv_heads * HD].reshape(-1, kv_heads, HD)
    value_rows = kv_block[:, kv_heads * HD :].reshape(-1, kv_heads, HD)
    return (key_rows, value_rows)


def attend_block(state_in, queries, kv_block, visible):
    row_top, row_total, output_sum = state_in
    key_rows, value_rows = split_block(kv_block, queries.shape[1])
    scores = jnp.einsum(
        "qkgd,pkd->kgqp", queries, key_rows, preferred_element_type=jnp.float32
    ) * HD ** (-0.5)
    scores = jnp.where(visible, scores, MASKED_SCORE)
    new_top = jnp.maximum(row_top, jnp.max(scores, axis=-1))
    weights = jnp.where(visible, jnp.exp(scores - new_top[..., None]), 0.0)
    decay_factor = jnp.exp(row_top - new_top)
    row_total = row_total * decay_factor + jnp.sum(weights, axis=-1)
    mixed_heads = jnp.einsum(
        "kgqp,pkd->qkgd",
        weights.astype(jnp.bfloat16),
        value_rows,
        preferred_element_type=jnp.float32,
    )
    output_sum = output_sum * jnp.transpose(decay_factor, (2, 0, 1))[..., None] + mixed_heads
    return (new_top, row_total, output_sum)


def block_grads(queries, out_grad, kv_block, visible, log_total, delta_rows):
    key_rows, value_rows = split_block(kv_block, queries.shape[1])
    scale_factor = HD ** (-0.5)
    scores = (
        jnp.einsum("qkgd,pkd->kgqp", queries, key_rows, preferred_element_type=jnp.float32)
        * scale_factor
    )
    probs_full = jnp.where(
        visible, jnp.exp(jnp.where(visible, scores, MASKED_SCORE) - log_total[..., None]), 0.0
    )
    value_grad = jnp.einsum(
        "kgqp,qkgd->pkd",
        probs_full.astype(jnp.bfloat16),
        out_grad,
        preferred_element_type=jnp.float32,
    )
    prob_grad = jnp.einsum(
        "qkgd,pkd->kgqp", out_grad, value_rows, preferred_element_type=jnp.float32
    )
    score_grad = (probs_full * (prob_grad - delta_rows[..., None])).astype(jnp.bfloat16)
    query_grad = (
        jnp.einsum("kgqp,pkd->qkgd", score_grad, key_rows, preferred_element_type=jnp.float32)
        * scale_factor
    )
    key_grad = (
        jnp.einsum("kgqp,qkgd->pkd", score_grad, queries, preferred_element_type=jnp.float32)
        * scale_factor
    )
    block_rows = kv_block.shape[0]
    return (
        query_grad,
        jnp.concatenate(
            [key_grad.reshape(block_rows, -1), value_grad.reshape(block_rows, -1)], axis=-1
        ),
    )


def shards(
    tokens,
    attn_gain,
    w_query,
    w_key,
    w_value,
    w_out,
    mlp_gain,
    w_gate,
    w_up,
    w_down,
    cotangent,
    positions,
    segments,
):
    token_rows = tokens.shape[0]
    gain_one, query_w, key_w, value_w, out_w = (
        lax.all_gather(attn_gain, ("fsdp", "ctx"), axis=0, tiled=True),
        lax.all_gather(w_query, ("fsdp", "ctx"), axis=0, tiled=True),
        lax.all_gather(w_key, ("fsdp", "ctx"), axis=0, tiled=True),
        lax.all_gather(w_value, ("fsdp", "ctx"), axis=0, tiled=True),
        lax.all_gather(w_out, ("fsdp", "ctx"), axis=1, tiled=True),
    )
    gain_two, gate_w, up_w, down_w = (
        lax.all_gather(mlp_gain, ("fsdp", "ctx"), axis=0, tiled=True),
        lax.all_gather(w_gate, ("fsdp", "ctx"), axis=0, tiled=True),
        lax.all_gather(w_up, ("fsdp", "ctx"), axis=0, tiled=True),
        lax.all_gather(w_down, ("fsdp", "ctx"), axis=1, tiled=True),
    )
    head_count = query_w.shape[1] // HD
    kv_heads = key_w.shape[1] // HD
    groups = H // KVH
    cosine, sine = rope_tables(positions, HD // 2)
    token_float = tokens.astype(jnp.float32)
    gain_one_float = gain_one.astype(jnp.float32)
    normed_one, unit_one, inv_one = rms_norm(token_float, gain_one_float)
    normed_low = normed_one.astype(jnp.bfloat16)
    query_lin = project(normed_low, query_w)
    key_lin = project(normed_low, key_w)
    value_low = project(normed_low, value_w).astype(jnp.bfloat16)
    query_rot = rotate(query_lin.reshape(token_rows, head_count, HD), cosine, sine).astype(
        jnp.bfloat16
    )
    key_rot = rotate(key_lin.reshape(token_rows, kv_heads, HD), cosine, sine).astype(jnp.bfloat16)
    queries = query_rot.reshape(token_rows, kv_heads, groups, HD)
    kv_local = jnp.concatenate([key_rot.reshape(token_rows, kv_heads * HD), value_low], axis=-1)
    key_positions, key_segments = (
        lax.all_gather(positions, "ctx", axis=0, tiled=True),
        lax.all_gather(segments, "ctx", axis=0, tiled=True),
    )
    my_index = lax.axis_index("ctx")
    cycle_size = lax.axis_size("ctx")

    def block_marks(source):
        start_row = source * token_rows
        return pair_mask(
            positions,
            segments,
            lax.dynamic_slice_in_dim(key_positions, start_row, token_rows),
            lax.dynamic_slice_in_dim(key_segments, start_row, token_rows),
        )

    start_state = (
        jnp.full((kv_heads, groups, token_rows), MASKED_SCORE, jnp.float32),
        jnp.zeros((kv_heads, groups, token_rows), jnp.float32),
        jnp.zeros((token_rows, kv_heads, groups, HD), jnp.float32),
    )

    def forward_block(state_in, kv_block, source):
        visible = block_marks(source)
        return attend_block(state_in, queries, kv_block, visible)

    def cycle_step(state_in, step_index):
        attn_state, kv_block = state_in
        attn_state = forward_block(attn_state, kv_block, (my_index - step_index) % cycle_size)
        passed = shifted(kv_block, "ctx", 1)
        return ((attn_state, passed), kv_block)

    (attn_state, last_block), kept_blocks = lax.scan(
        cycle_step, (start_state, kv_local), jnp.arange(cycle_size - 1)
    )
    attn_state = forward_block(attn_state, last_block, (my_index + 1) % cycle_size)
    kv_blocks = jnp.concatenate([kept_blocks, last_block[None]], axis=0)
    sources = (my_index - jnp.arange(cycle_size)) % cycle_size
    row_top, row_total, output_sum = attn_state
    attended = output_sum / jnp.transpose(row_total, (2, 0, 1))[..., None]
    log_total = row_top + jnp.log(row_total)
    attended_low = attended.reshape(token_rows, head_count * HD).astype(jnp.bfloat16)
    middle = token_float + lax.psum(project(attended_low, out_w).astype(jnp.bfloat16), "tp").astype(
        jnp.float32
    )
    gain_two_float = gain_two.astype(jnp.float32)
    normed_two, unit_two, inv_two = rms_norm(middle, gain_two_float)
    normed_two_low = normed_two.astype(jnp.bfloat16)
    gate_lin = project(normed_two_low, gate_w)
    up_lin = project(normed_two_low, up_w)
    hidden_low = (jax.nn.silu(gate_lin) * up_lin).astype(jnp.bfloat16)
    result = middle + lax.psum(project(hidden_low, down_w).astype(jnp.bfloat16), "tp").astype(
        jnp.float32
    )
    output = result.astype(jnp.bfloat16)
    hidden_grad = project_back(cotangent, down_w)
    down_w_grad = weight_grad(hidden_low, cotangent)
    sigmoid_gate = jax.nn.sigmoid(gate_lin)
    gate_grad_low = (
        hidden_grad * up_lin * sigmoid_gate * (1.0 + gate_lin * (1.0 - sigmoid_gate))
    ).astype(jnp.bfloat16)
    up_grad_low = (hidden_grad * gate_lin * sigmoid_gate).astype(jnp.bfloat16)
    normed_two_grad = lax.psum(
        (project_back(gate_grad_low, gate_w) + project_back(up_grad_low, up_w)).astype(
            jnp.bfloat16
        ),
        "tp",
    ).astype(jnp.float32)
    gate_w_grad = weight_grad(normed_two_low, gate_grad_low)
    up_w_grad = weight_grad(normed_two_low, up_grad_low)
    norm_back_two, gain_two_grad = rms_norm_back(normed_two_grad, gain_two_float, unit_two, inv_two)
    middle_grad = cotangent.astype(jnp.float32) + norm_back_two
    middle_low = middle_grad.astype(jnp.bfloat16)
    attended_grad_low = project_back(middle_low, out_w).astype(jnp.bfloat16)
    out_w_grad = weight_grad(attended_low, middle_low)
    out_grad = attended_grad_low.reshape(token_rows, kv_heads, groups, HD)
    delta_rows = jnp.transpose(jnp.sum(out_grad.astype(jnp.float32) * attended, axis=-1), (1, 2, 0))

    def backward_block(kv_block, source):
        visible = block_marks(source)
        return block_grads(queries, out_grad, kv_block, visible, log_total, delta_rows)

    query_start = jnp.zeros((token_rows, kv_heads, groups, HD), jnp.float32)

    def back_step(state_in, pieces):
        query_acc, kv_acc = state_in
        query_term, kv_term = backward_block(pieces[0], pieces[1])
        passed = shifted((kv_acc + kv_term).astype(jnp.bfloat16), "ctx", 1).astype(jnp.float32)
        return ((query_acc + query_term, passed), None)

    (query_grad, kv_grad), unused = lax.scan(
        back_step, (query_start, jnp.zeros(kv_local.shape, jnp.float32)), (kv_blocks, sources)
    )
    query_grad_low = (
        rotate_back(query_grad.reshape(token_rows, head_count, HD), cosine, sine)
        .reshape(token_rows, head_count * HD)
        .astype(jnp.bfloat16)
    )
    key_grad_low = (
        rotate_back(kv_grad[:, : kv_heads * HD].reshape(token_rows, kv_heads, HD), cosine, sine)
        .reshape(token_rows, kv_heads * HD)
        .astype(jnp.bfloat16)
    )
    value_grad_low = kv_grad[:, kv_heads * HD :].astype(jnp.bfloat16)
    normed_one_grad = lax.psum(
        (
            project_back(query_grad_low, query_w)
            + project_back(key_grad_low, key_w)
            + project_back(value_grad_low, value_w)
        ).astype(jnp.bfloat16),
        "tp",
    ).astype(jnp.float32)
    query_w_grad = weight_grad(normed_low, query_grad_low)
    key_w_grad = weight_grad(normed_low, key_grad_low)
    value_w_grad = weight_grad(normed_low, value_grad_low)
    norm_back_one, gain_one_grad = rms_norm_back(normed_one_grad, gain_one_float, unit_one, inv_one)
    input_grad = (middle_grad + norm_back_one).astype(jnp.bfloat16)
    summed = (
        lax.psum_scatter(
            gain_one_grad.astype(jnp.bfloat16), ("fsdp", "ctx"), scatter_dimension=0, tiled=True
        ).astype(jnp.float32),
        lax.psum_scatter(
            query_w_grad.astype(jnp.bfloat16), ("fsdp", "ctx"), scatter_dimension=0, tiled=True
        ).astype(jnp.float32),
        lax.psum_scatter(
            key_w_grad.astype(jnp.bfloat16), ("fsdp", "ctx"), scatter_dimension=0, tiled=True
        ).astype(jnp.float32),
        lax.psum_scatter(
            value_w_grad.astype(jnp.bfloat16), ("fsdp", "ctx"), scatter_dimension=0, tiled=True
        ).astype(jnp.float32),
        lax.psum_scatter(
            out_w_grad.astype(jnp.bfloat16), ("fsdp", "ctx"), scatter_dimension=1, tiled=True
        ).astype(jnp.float32),
        lax.psum_scatter(
            gain_two_grad.astype(jnp.bfloat16), ("fsdp", "ctx"), scatter_dimension=0, tiled=True
        ).astype(jnp.float32),
        lax.psum_scatter(
            gate_w_grad.astype(jnp.bfloat16), ("fsdp", "ctx"), scatter_dimension=0, tiled=True
        ).astype(jnp.float32),
        lax.psum_scatter(
            up_w_grad.astype(jnp.bfloat16), ("fsdp", "ctx"), scatter_dimension=0, tiled=True
        ).astype(jnp.float32),
        lax.psum_scatter(
            down_w_grad.astype(jnp.bfloat16), ("fsdp", "ctx"), scatter_dimension=1, tiled=True
        ).astype(jnp.float32),
    )
    return (output, input_grad) + tuple(summed)


MESH = pl.DeviceIdType.MESH
BF = jnp.bfloat16
F32 = jnp.float32


def dotg(left_side, right_side, left_dim, right_dim):
    return lax.dot_general(
        left_side,
        right_side,
        (((left_dim,), (right_dim,)), ((), ())),
        preferred_element_type=F32,
    )


def remote(src, dst, send_sem, recv_sem, device):
    return pltpu.make_async_remote_copy(
        src_ref=src,
        dst_ref=dst,
        send_sem=send_sem,
        recv_sem=recv_sem,
        device_id=device,
        device_id_type=MESH,
    )


class Place:
    def __init__(self):
        self.f = lax.axis_index("fsdp")
        self.c = lax.axis_index("ctx")
        self.z = lax.axis_index("tp")
        self.cx = self.c + 1 - 2 * lax.rem(self.c, 2)
        self.cy = lax.rem(self.c + 2, 4)
        self.cd = 3 - self.c
        self.of = 1 - self.f
        self.own = self.f * 4 + self.c
        self.sx = self.f * 4 + self.cx
        self.sy = self.f * 4 + self.cy
        self.sd = self.f * 4 + self.cd

    def at(self, f=None, c=None, z=None):
        return (
            self.f if f is None else f,
            self.c if c is None else c,
            self.z if z is None else z,
        )


def greet(devices):
    barrier = pltpu.get_barrier_semaphore()
    for device in devices:
        pl.semaphore_signal(barrier, inc=1, device_id=device, device_id_type=MESH)
    pl.semaphore_wait(barrier, len(devices))


def group_devices(me):
    return [
        me.at(c=me.cx),
        me.at(c=me.cy),
        me.at(c=me.cd),
        me.at(f=me.of),
        me.at(f=me.of, c=me.cx),
        me.at(f=me.of, c=me.cy),
        me.at(f=me.of, c=me.cd),
    ]


def column_devices(me):
    return [me.at(z=lax.rem(me.z + step, 4)) for step in (1, 2, 3)]


class Gather:
    def __init__(self, me, index, own, full, send, recv, local_sem):
        self.me, self.own_ref, self.full = me, own, full
        rows = full.shape[1]
        self.half_a = pl.ds(0, rows // 2)
        self.half_b = pl.ds(rows // 2, rows // 2)

        def copy(slot, src, dst, device):
            return remote(src, dst, send.at[index, slot], recv.at[index, slot], device)

        slot_own, slot_x, slot_y = full.at[me.own], full.at[me.sx], full.at[me.sy]
        to_x, to_y, to_core = me.at(c=me.cx), me.at(c=me.cy), me.at(f=me.of)
        diag_a = full.at[me.sd, self.half_a]
        diag_b = full.at[me.sd, self.half_b]
        self.own_x = copy(0, own, slot_own, to_x)
        self.own_y = copy(1, own, slot_own, to_y)
        self.own_core = copy(2, own, slot_own, to_core)
        self.pass_x = copy(3, full.at[me.sy, self.half_a], full.at[me.sy, self.half_a], to_x)
        self.pass_y = copy(4, full.at[me.sx, self.half_b], full.at[me.sx, self.half_b], to_y)
        self.core_x = copy(5, slot_x, slot_x, to_core)
        self.core_y = copy(6, slot_y, slot_y, to_core)
        self.core_a = copy(7, diag_a, diag_a, to_core)
        self.core_b = copy(8, diag_b, diag_b, to_core)
        other = me.of * 4
        into = lambda slot, ref, device: copy(slot, ref, ref, device)
        self.in_x = into(0, slot_x, to_x)
        self.in_y = into(1, slot_y, to_y)
        self.in_a = into(3, diag_a, to_x)
        self.in_b = into(4, diag_b, to_y)
        self.in_core = [
            into(2, full.at[other + me.c], to_core),
            into(5, full.at[other + me.cx], to_core),
            into(6, full.at[other + me.cy], to_core),
            into(7, full.at[other + me.cd, self.half_a], to_core),
            into(8, full.at[other + me.cd, self.half_b], to_core),
        ]
        self.keep = pltpu.make_async_copy(own, slot_own, local_sem.at[index])

    def begin(self):
        self.own_x.start()
        self.own_y.start()
        self.own_core.start()
        self.keep.start()

    def forward(self):
        self.in_y.wait_recv()
        self.pass_x.start()
        self.core_y.start()
        self.in_x.wait_recv()
        self.pass_y.start()
        self.core_x.start()

    def diagonal(self):
        self.in_a.wait_recv()
        self.core_a.start()
        self.in_b.wait_recv()
        self.core_b.start()

    def arrive(self):
        self.keep.wait()
        for piece in self.in_core:
            piece.wait_recv()

    def settle(self):
        for piece in (
            self.own_x,
            self.own_y,
            self.own_core,
            self.pass_x,
            self.pass_y,
            self.core_x,
            self.core_y,
            self.core_a,
            self.core_b,
        ):
            piece.wait_send()


class LineSum:
    def __init__(self, me, part, outer_in, inner_in, send, recv):
        self.me, self.part = me, part
        self.outer_in, self.inner_in = outer_in, inner_in
        self.send, self.recv = send, recv
        z = me.z
        self.is_mid = (z == 1) | (z == 2)
        self.is_end = (z == 0) | (z == 3)
        self.mid_of_end = 1 + z // 3
        self.outer_of_mid = 3 * (z - 1)

    def end_copies(self):
        me, part = self.me, self.part
        mid = self.mid_of_end
        to_mid = me.at(z=mid)
        owners = (3 - me.z, 3 - mid, mid)
        return [
            remote(
                part.at[owner],
                self.outer_in.at[slot],
                self.send.at[slot],
                self.recv.at[slot],
                to_mid,
            )
            for slot, owner in enumerate(owners)
        ]

    def mid_copies(self):
        me, part = self.me, self.part
        far_mid, outer = 3 - me.z, self.outer_of_mid
        far = 3 - outer
        to_mid, to_outer = me.at(z=far_mid), me.at(z=outer)
        return [
            remote(part.at[far], self.inner_in.at[0], self.send.at[0], self.recv.at[3], to_mid),
            remote(part.at[far_mid], self.inner_in.at[1], self.send.at[1], self.recv.at[4], to_mid),
            remote(part.at[outer], self.inner_in.at[0], self.send.at[2], self.recv.at[3], to_outer),
        ]

    def wait_in(self, slot, buffer):
        remote(buffer, buffer, self.send.at[0], self.recv.at[slot], self.me.at(z=3 - self.me.z)).wait_recv()

    def add(self, owner, buffer):
        self.part[owner] = (self.part[owner].astype(F32) + buffer[...].astype(F32)).astype(BF)

    def begin(self):
        @pl.when(self.is_end)
        def _():
            for piece in self.end_copies():
                piece.start()

    def step_one(self):
        @pl.when(self.is_mid)
        def _():
            far = 3 - self.outer_of_mid
            self.wait_in(0, self.outer_in.at[0])
            self.add(far, self.outer_in.at[0])
            self.mid_copies()[0].start()

    def step_two(self):
        @pl.when(self.is_mid)
        def _():
            copies = self.mid_copies()
            self.wait_in(1, self.outer_in.at[1])
            self.add(3 - self.me.z, self.outer_in.at[1])
            copies[1].start()
            self.wait_in(3, self.inner_in.at[0])
            self.add(self.outer_of_mid, self.inner_in.at[0])
            copies[2].start()

    def finish(self, total):
        me = self.me

        @pl.when(self.is_mid)
        def _():
            self.wait_in(2, self.outer_in.at[2])
            self.wait_in(4, self.inner_in.at[1])
            total[...] = (
                self.part[me.z].astype(F32)
                + self.outer_in[2].astype(F32)
                + self.inner_in[1].astype(F32)
            )
            for piece in self.mid_copies():
                piece.wait_send()

        @pl.when(self.is_end)
        def _():
            self.wait_in(3, self.inner_in.at[0])
            total[...] = self.part[me.z].astype(F32) + self.inner_in[0].astype(F32)
            for piece in self.end_copies():
                piece.wait_send()


class LineGather:
    def __init__(self, me, blocks, send, recv):
        self.me, self.blocks, self.send, self.recv = me, blocks, send, recv
        z = me.z
        self.is_mid = (z == 1) | (z == 2)
        self.is_end = (z == 0) | (z == 3)
        self.mid_of_end = 1 + z // 3
        self.outer_of_mid = 3 * (z - 1)

    def copy(self, owner, slot, z):
        ref = self.blocks.at[owner]
        return remote(ref, ref, self.send.at[slot], self.recv.at[owner], self.me.at(z=z))

    def wait_in(self, owner):
        ref = self.blocks.at[owner]
        remote(ref, ref, self.send.at[0], self.recv.at[owner], self.me.at(z=3 - self.me.z)).wait_recv()

    def begin(self):
        me = self.me

        @pl.when(self.is_end)
        def _():
            self.copy(me.z, 0, self.mid_of_end).start()

        @pl.when(self.is_mid)
        def _():
            self.copy(me.z, 0, self.outer_of_mid).start()
            self.copy(me.z, 1, 3 - me.z).start()

    def step_one(self):
        me = self.me

        @pl.when(self.is_mid)
        def _():
            self.wait_in(self.outer_of_mid)
            self.copy(self.outer_of_mid, 2, 3 - me.z).start()
            self.wait_in(3 - me.z)
            self.copy(3 - me.z, 3, self.outer_of_mid).start()

    def step_two(self):
        @pl.when(self.is_mid)
        def _():
            far = 3 - self.outer_of_mid
            self.wait_in(far)
            self.copy(far, 4, self.outer_of_mid).start()

    def finish(self):
        me = self.me

        @pl.when(self.is_mid)
        def _():
            self.copy(me.z, 0, self.outer_of_mid).wait_send()
            self.copy(me.z, 1, 3 - me.z).wait_send()
            self.copy(self.outer_of_mid, 2, 3 - me.z).wait_send()
            self.copy(3 - me.z, 3, self.outer_of_mid).wait_send()
            self.copy(3 - self.outer_of_mid, 4, self.outer_of_mid).wait_send()

        @pl.when(self.is_end)
        def _():
            mid = self.mid_of_end
            self.wait_in(mid)
            self.wait_in(3 - mid)
            self.wait_in(3 - me.z)
            self.copy(me.z, 0, mid).wait_send()


def row_of(gains_ref, which):
    return jnp.concatenate([gains_ref[shard, which : which + 1, :] for shard in range(8)], axis=-1)


def swap_halves(rows):
    lane = lax.broadcasted_iota(jnp.int32, rows.shape, 1)
    return jnp.where(
        lax.rem(lane, HD) < HD // 2, pltpu.roll(rows, 96, 1), pltpu.roll(rows, 32, 1)
    )


def forward_kernel(
    tok,
    w_qkv,
    w_out,
    w_gate,
    w_up,
    w_down,
    gains,
    marks,
    rope_q,
    rope_k,
    f_qkv,
    f_out,
    f_gate,
    f_up,
    f_down,
    f_gains,
    n_one,
    q_heads,
    kv_out,
    bias,
    lse,
    att_low,
    middle,
    n_two,
    s_qkv,
    s_out,
    s_gains,
    s_marks,
    s_kv,
    s_keys,
    s_vals,
    s_qlin,
    s_part,
    s_outer,
    s_inner,
    s_total,
    s_blocks,
    g_send,
    g_recv,
    g_local,
    small_send,
    small_recv,
    kv_send,
    kv_recv,
    sum_send,
    sum_recv,
    all_send,
    all_recv,
    out_sem,
):
    me = Place()
    group = group_devices(me)
    greet(group + column_devices(me))

    qkv = Gather(me, 0, w_qkv, s_qkv, g_send, g_recv, g_local)
    out = Gather(me, 1, w_out, s_out, g_send, g_recv, g_local)
    gate = Gather(me, 2, w_gate, f_gate, g_send, g_recv, g_local)
    up = Gather(me, 3, w_up, f_up, g_send, g_recv, g_local)
    down = Gather(me, 4, w_down, f_down, g_send, g_recv, g_local)

    small = []
    for slot, device in enumerate(group):
        small.append(
            remote(gains, s_gains.at[me.own], small_send.at[slot], small_recv.at[slot], device)
        )
    for slot, device in enumerate(group[:3]):
        small.append(
            remote(
                marks, s_marks.at[me.c], small_send.at[7 + slot], small_recv.at[7 + slot], device
            )
        )
    for piece in small:
        piece.start()
    qkv.begin()
    s_gains[me.own] = gains[...]
    s_marks[me.c] = marks[...]
    sources = [me.sx, me.sy, me.sd, me.of * 4 + me.c, me.of * 4 + me.cx, me.of * 4 + me.cy, me.of * 4 + me.cd]
    for slot, source in enumerate(sources):
        remote(
            gains, s_gains.at[source], small_send.at[slot], small_recv.at[slot], group[slot]
        ).wait_recv()
    for slot, source in enumerate((me.cx, me.cy, me.cd)):
        remote(
            marks, s_marks.at[source], small_send.at[7 + slot], small_recv.at[7 + slot], group[slot]
        ).wait_recv()
    f_gains[...] = s_gains[...]

    gain_one = row_of(s_gains, 0)

    def norm_rows(step, carry):
        rows = pl.ds(pl.multiple_of(step * 64, 64), 64)
        values = tok[rows, :].astype(F32)
        inv = lax.rsqrt(jnp.mean(values * values, axis=-1, keepdims=True) + EPSILON)
        n_one[rows, :] = (values * inv * gain_one).astype(BF)
        return carry

    lax.fori_loop(0, tok.shape[0] // 64, norm_rows, 0)

    qkv.forward()
    out.begin()
    qkv.diagonal()

    def make_bias(group_index):
        own_rows = marks[:, group_index * 256 : (group_index + 1) * 256].astype(F32)
        for source in range(4):
            key_rows = s_marks[source, :, group_index * 256 : (group_index + 1) * 256].astype(F32)
            key_pos = jnp.transpose(jnp.broadcast_to(key_rows[0:1, :], (128, 256)))
            key_seg = jnp.transpose(jnp.broadcast_to(key_rows[1:2, :], (128, 256)))
            for part in range(2):
                lanes = slice(part * 128, (part + 1) * 128)
                seen = (key_seg == own_rows[1:2, lanes]) & (key_pos <= own_rows[0:1, lanes])
                bias[group_index, source * 256 : (source + 1) * 256, lanes] = jnp.where(
                    seen, 0.0, MASKED_SCORE
                )

    make_bias(0)
    make_bias(1)
    qkv.arrive()

    for first in (0, 256, 512):
        lanes = slice(first, min(first + 256, 640))
        total = None
        for shard in range(8):
            term = dotg(
                n_one[:, shard * 256 : (shard + 1) * 256], s_qkv[shard, :, lanes], 1, 0
            )
            total = term if total is None else total + term
        s_qlin[:, lanes] = total

    key_pair = s_qlin[:, 512:640]
    rot_pair = key_pair * rope_k[:, :128] + swap_halves(key_pair) * rope_k[:, 128:]
    s_kv[me.c] = rot_pair.astype(BF)
    kv_copies = [
        remote(s_kv.at[me.c], s_kv.at[me.c], kv_send.at[slot], kv_recv.at[slot], device)
        for slot, device in enumerate(group[:3])
    ]
    for piece in kv_copies:
        piece.start()
    out.forward()
    for piece in (gate, up, down):
        piece.begin()

    lane = lax.broadcasted_iota(jnp.int32, (256, 128), 1)
    for pair in range(4):
        rows = s_qlin[:, pair * 128 : (pair + 1) * 128]
        rot = (rows * rope_q[:, :128] + swap_halves(rows) * rope_q[:, 128:]).astype(BF)
        rot = rot * jnp.bfloat16(HD ** (-0.5))
        for group_index in range(2):
            own = rot[group_index * 256 : (group_index + 1) * 256, :]
            zero = jnp.zeros_like(own)
            q_heads[group_index * 8 + 2 * pair] = jnp.where(lane < HD, own, zero)
            q_heads[group_index * 8 + 2 * pair + 1] = jnp.where(lane >= HD, own, zero)

    for slot, source in enumerate((me.cx, me.cy, me.cd)):
        remote(
            s_kv.at[source], s_kv.at[source], kv_send.at[slot], kv_recv.at[slot], group[slot]
        ).wait_recv()
    lane_kv = lax.broadcasted_iota(jnp.int32, (256, 128), 1)
    for group_index in range(2):
        for source in range(4):
            pairs = s_kv[source, group_index * 256 : (group_index + 1) * 256, :].astype(F32)
            rows = slice(source * 256, (source + 1) * 256)
            s_keys[group_index, rows, :] = jnp.where(
                lane_kv < HD, pairs, pltpu.roll(pairs, HD, 1)
            ).astype(BF)
            s_vals[group_index, :, rows] = jnp.transpose(pairs)[HD:, :].astype(BF)
    kv_out[...] = s_kv[...]

    def attend(step, carry):
        group_index = step // 4
        pair = step - group_index * 4
        halves = []
        for odd in range(2):
            head = step * 2 + odd
            scores = dotg(s_keys[group_index], q_heads[head], 1, 1) + bias[group_index]
            top = jnp.max(scores, axis=0, keepdims=True)
            weights = jnp.exp(scores - top)
            total = jnp.sum(weights, axis=0, keepdims=True)
            mixed = dotg(s_vals[group_index], weights.astype(BF), 1, 0)
            halves.append(mixed / total)
            lse[head] = top + jnp.log(total)
        rows = jnp.transpose(jnp.concatenate(halves, axis=0))
        att_low[
            pl.ds(pl.multiple_of(group_index * 256, 256), 256),
            pl.ds(pl.multiple_of(pair * 128, 128), 128),
        ] = rows.astype(BF)
        return carry

    lax.fori_loop(0, 8, attend, 0)

    out.diagonal()
    out.arrive()
    for shard in range(8):
        lanes = slice(shard * 256, (shard + 1) * 256)
        s_part[:, :, lanes] = (
            dotg(att_low[...], s_out[shard], 1, 0).astype(BF).reshape(4, 128, 256)
        )
    summed = LineSum(me, s_part, s_outer, s_inner, sum_send, sum_recv)
    summed.begin()
    gate.forward()
    keep = [
        pltpu.make_async_copy(s_qkv, f_qkv, out_sem.at[0]),
        pltpu.make_async_copy(s_out, f_out, out_sem.at[1]),
    ]
    for piece in keep:
        piece.start()
    summed.step_one()
    up.forward()
    summed.step_two()
    summed.finish(s_total)

    own_rows = pl.ds(pl.multiple_of(me.z * 128, 128), 128)
    mid_rows = tok[own_rows, :].astype(F32) + s_total[...]
    middle[...] = mid_rows
    inv_two = lax.rsqrt(jnp.mean(mid_rows * mid_rows, axis=-1, keepdims=True) + EPSILON)
    s_blocks[me.z] = (mid_rows * inv_two * row_of(s_gains, 1)).astype(BF)
    spread = LineGather(me, s_blocks, all_send, all_recv)
    spread.begin()
    down.forward()
    gate.diagonal()
    spread.step_one()
    up.diagonal()
    spread.step_two()
    down.diagonal()
    gate.arrive()
    up.arrive()
    down.arrive()
    spread.finish()
    last = pltpu.make_async_copy(s_blocks, n_two, out_sem.at[2])
    last.start()
    for piece in small:
        piece.wait_send()
    for piece in kv_copies:
        piece.wait_send()
    for piece in (qkv, out, gate, up, down):
        piece.settle()
    for piece in keep:
        piece.wait()
    last.wait()


def run_forward(tokens, w_qkv, w_out, w_gate, w_up, w_down, gains, marks, rope_q, rope_k):
    shape = jax.ShapeDtypeStruct
    width = tokens.shape[1]
    hidden = w_gate.shape[1]
    in_vmem = pl.BlockSpec(memory_space=pltpu.VMEM)
    anywhere = pl.BlockSpec(memory_space=pl.ANY)
    dma = pltpu.SemaphoreType.DMA
    return pl.pallas_call(
        forward_kernel,
        name="forward_part",
        out_shape=(
            shape((8, 256, 640), BF),
            shape((8, 512, 256), BF),
            shape((8, 256, hidden), BF),
            shape((8, 256, hidden), BF),
            shape((8, hidden, 256), BF),
            shape((8, 8, 256), F32),
            shape((512, width), BF),
            shape((16, 256, 128), BF),
            shape((4, 512, 128), BF),
            shape((2, 1024, 256), F32),
            shape((16, 1, 256), F32),
            shape((512, 512), BF),
            shape((128, width), F32),
            shape((4, 128, width), BF),
        ),
        in_specs=[in_vmem] * 10,
        out_specs=(anywhere,) * 5 + (in_vmem,) * 8 + (anywhere,),
        scratch_shapes=[
            pltpu.VMEM((8, 256, 640), BF),
            pltpu.VMEM((8, 512, 256), BF),
            pltpu.VMEM((8, 8, 256), F32),
            pltpu.VMEM((4, 8, 512), jnp.int32),
            pltpu.VMEM((4, 512, 128), BF),
            pltpu.VMEM((2, 1024, 128), BF),
            pltpu.VMEM((2, HD, 1024), BF),
            pltpu.VMEM((512, 640), F32),
            pltpu.VMEM((4, 128, width), BF),
            pltpu.VMEM((3, 128, width), BF),
            pltpu.VMEM((2, 128, width), BF),
            pltpu.VMEM((128, width), F32),
            pltpu.VMEM((4, 128, width), BF),
            dma((5, 9)),
            dma((5, 9)),
            dma((5,)),
            dma((10,)),
            dma((10,)),
            dma((3,)),
            dma((3,)),
            dma((3,)),
            dma((5,)),
            dma((5,)),
            dma((4,)),
            dma((3,)),
        ],
        compiler_params=pltpu.CompilerParams(
            collective_id=0, has_side_effects=True, vmem_limit_bytes=60000000
        ),
    )(tokens, w_qkv, w_out, w_gate, w_up, w_down, gains, marks, rope_q, rope_k)


def prepared(tokens, attn_gain, w_query, w_key, w_value, mlp_gain, positions, segments):
    cosine, sine = rope_tables(positions, HD // 2)
    one, zero = jnp.ones_like(cosine), jnp.zeros_like(sine)
    rope_q = jnp.concatenate([cosine] * 4 + [-sine, sine, -sine, sine], axis=-1)
    rope_k = jnp.concatenate([cosine, cosine, one, one, -sine, sine, zero, zero], axis=-1)
    w_qkv = jnp.concatenate([w_query, w_key, w_value], axis=1)
    gains = jnp.pad(jnp.stack([attn_gain, mlp_gain]).astype(F32), ((0, 6), (0, 0)))
    marks = jnp.pad(jnp.stack([positions, segments]), ((0, 6), (0, 0)))
    return w_qkv, gains, marks, rope_q, rope_k


def fast_shards(
    tokens,
    attn_gain,
    w_query,
    w_key,
    w_value,
    w_out,
    mlp_gain,
    w_gate,
    w_up,
    w_down,
    cotangent,
    positions,
    segments,
):
    token_rows = tokens.shape[0]
    w_qkv, gains, marks, rope_q, rope_k = prepared(
        tokens, attn_gain, w_query, w_key, w_value, mlp_gain, positions, segments
    )
    (
        f_qkv, f_out, f_gate, f_up, f_down, f_gains, n_one, q_heads, kv_all, bias, lse, att_low,
        middle_own, n_two,
    ) = run_forward(tokens, w_qkv, w_out, w_gate, w_up, w_down, gains, marks, rope_q, rope_k)
    head_count, kv_heads, groups = 8, 1, 8
    cosine, sine = rope_tables(positions, HD // 2)
    query_w = f_qkv.reshape(2048, 640)[:, :512]
    key_w = f_qkv.reshape(2048, 640)[:, 512:576]
    value_w = f_qkv.reshape(2048, 640)[:, 576:]
    out_w = jnp.transpose(f_out, (1, 0, 2)).reshape(512, 2048)
    down_w = jnp.transpose(f_down, (1, 0, 2)).reshape(-1, 2048)
    gate_w, up_w = f_gate.reshape(2048, -1), f_up.reshape(2048, -1)
    gain_one_float = f_gains[:, 0, :].reshape(-1)
    gain_two_float = f_gains[:, 1, :].reshape(-1)
    token_float = tokens.astype(jnp.float32)
    normed_low = n_one
    inv_one = lax.rsqrt(jnp.mean(token_float * token_float, axis=-1, keepdims=True) + EPSILON)
    unit_one = token_float * inv_one
    attended_low = att_low
    middle = lax.all_gather(middle_own, "tp", axis=0, tiled=True)
    inv_two = lax.rsqrt(jnp.mean(middle * middle, axis=-1, keepdims=True) + EPSILON)
    unit_two = middle * inv_two
    normed_two_low = n_two.reshape(512, 2048)
    my_index = lax.axis_index("ctx")
    cycle_size = lax.axis_size("ctx")
    paired = q_heads.reshape(2, 4, 2, 256, 128)
    paired = paired[:, :, 0] + paired[:, :, 1]
    queries = (jnp.transpose(paired, (0, 2, 1, 3)).reshape(512, 1, 8, 64) * 8).astype(jnp.bfloat16)
    key_positions, key_segments = (
        lax.all_gather(positions, "ctx", axis=0, tiled=True),
        lax.all_gather(segments, "ctx", axis=0, tiled=True),
    )
    log_total = jnp.transpose(lse.reshape(2, 8, 256), (1, 0, 2)).reshape(1, 8, 512)
    attended = att_low.astype(jnp.float32).reshape(512, 1, 8, 64)

    def block_marks(source):
        start_row = source * token_rows
        return pair_mask(
            positions,
            segments,
            lax.dynamic_slice_in_dim(key_positions, start_row, token_rows),
            lax.dynamic_slice_in_dim(key_segments, start_row, token_rows),
        )
    sources = (my_index - jnp.arange(cycle_size)) % cycle_size
    kv_blocks = kv_all[sources]
    kv_local = kv_all[0]
    gate_lin = project(normed_two_low, gate_w)
    up_lin = project(normed_two_low, up_w)
    hidden_low = (jax.nn.silu(gate_lin) * up_lin).astype(jnp.bfloat16)
    result = middle + lax.psum(project(hidden_low, down_w).astype(jnp.bfloat16), "tp").astype(
        jnp.float32
    )
    output = result.astype(jnp.bfloat16)
    hidden_grad = project_back(cotangent, down_w)
    down_w_grad = weight_grad(hidden_low, cotangent)
    sigmoid_gate = jax.nn.sigmoid(gate_lin)
    gate_grad_low = (
        hidden_grad * up_lin * sigmoid_gate * (1.0 + gate_lin * (1.0 - sigmoid_gate))
    ).astype(jnp.bfloat16)
    up_grad_low = (hidden_grad * gate_lin * sigmoid_gate).astype(jnp.bfloat16)
    normed_two_grad = lax.psum(
        (project_back(gate_grad_low, gate_w) + project_back(up_grad_low, up_w)).astype(
            jnp.bfloat16
        ),
        "tp",
    ).astype(jnp.float32)
    gate_w_grad = weight_grad(normed_two_low, gate_grad_low)
    up_w_grad = weight_grad(normed_two_low, up_grad_low)
    norm_back_two, gain_two_grad = rms_norm_back(normed_two_grad, gain_two_float, unit_two, inv_two)
    middle_grad = cotangent.astype(jnp.float32) + norm_back_two
    middle_low = middle_grad.astype(jnp.bfloat16)
    attended_grad_low = project_back(middle_low, out_w).astype(jnp.bfloat16)
    out_w_grad = weight_grad(attended_low, middle_low)
    out_grad = attended_grad_low.reshape(token_rows, kv_heads, groups, HD)
    delta_rows = jnp.transpose(jnp.sum(out_grad.astype(jnp.float32) * attended, axis=-1), (1, 2, 0))

    def backward_block(kv_block, source):
        visible = block_marks(source)
        return block_grads(queries, out_grad, kv_block, visible, log_total, delta_rows)

    query_start = jnp.zeros((token_rows, kv_heads, groups, HD), jnp.float32)

    def back_step(state_in, pieces):
        query_acc, kv_acc = state_in
        query_term, kv_term = backward_block(pieces[0], pieces[1])
        passed = shifted((kv_acc + kv_term).astype(jnp.bfloat16), "ctx", 1).astype(jnp.float32)
        return ((query_acc + query_term, passed), None)

    (query_grad, kv_grad), unused = lax.scan(
        back_step, (query_start, jnp.zeros(kv_local.shape, jnp.float32)), (kv_blocks, sources)
    )
    query_grad_low = (
        rotate_back(query_grad.reshape(token_rows, head_count, HD), cosine, sine)
        .reshape(token_rows, head_count * HD)
        .astype(jnp.bfloat16)
    )
    key_grad_low = (
        rotate_back(kv_grad[:, : kv_heads * HD].reshape(token_rows, kv_heads, HD), cosine, sine)
        .reshape(token_rows, kv_heads * HD)
        .astype(jnp.bfloat16)
    )
    value_grad_low = kv_grad[:, kv_heads * HD :].astype(jnp.bfloat16)
    normed_one_grad = lax.psum(
        (
            project_back(query_grad_low, query_w)
            + project_back(key_grad_low, key_w)
            + project_back(value_grad_low, value_w)
        ).astype(jnp.bfloat16),
        "tp",
    ).astype(jnp.float32)
    query_w_grad = weight_grad(normed_low, query_grad_low)
    key_w_grad = weight_grad(normed_low, key_grad_low)
    value_w_grad = weight_grad(normed_low, value_grad_low)
    norm_back_one, gain_one_grad = rms_norm_back(normed_one_grad, gain_one_float, unit_one, inv_one)
    input_grad = (middle_grad + norm_back_one).astype(jnp.bfloat16)
    summed = (
        lax.psum_scatter(
            gain_one_grad.astype(jnp.bfloat16), ("fsdp", "ctx"), scatter_dimension=0, tiled=True
        ).astype(jnp.float32),
        lax.psum_scatter(
            query_w_grad.astype(jnp.bfloat16), ("fsdp", "ctx"), scatter_dimension=0, tiled=True
        ).astype(jnp.float32),
        lax.psum_scatter(
            key_w_grad.astype(jnp.bfloat16), ("fsdp", "ctx"), scatter_dimension=0, tiled=True
        ).astype(jnp.float32),
        lax.psum_scatter(
            value_w_grad.astype(jnp.bfloat16), ("fsdp", "ctx"), scatter_dimension=0, tiled=True
        ).astype(jnp.float32),
        lax.psum_scatter(
            out_w_grad.astype(jnp.bfloat16), ("fsdp", "ctx"), scatter_dimension=1, tiled=True
        ).astype(jnp.float32),
        lax.psum_scatter(
            gain_two_grad.astype(jnp.bfloat16), ("fsdp", "ctx"), scatter_dimension=0, tiled=True
        ).astype(jnp.float32),
        lax.psum_scatter(
            gate_w_grad.astype(jnp.bfloat16), ("fsdp", "ctx"), scatter_dimension=0, tiled=True
        ).astype(jnp.float32),
        lax.psum_scatter(
            up_w_grad.astype(jnp.bfloat16), ("fsdp", "ctx"), scatter_dimension=0, tiled=True
        ).astype(jnp.float32),
        lax.psum_scatter(
            down_w_grad.astype(jnp.bfloat16), ("fsdp", "ctx"), scatter_dimension=1, tiled=True
        ).astype(jnp.float32),
    )
    return (output, input_grad) + tuple(summed)


def solution(mesh):
    in_specs = (
        P(("fsdp", "ctx"), None),
        P(("fsdp", "ctx")),
        P(("fsdp", "ctx"), "tp"),
        P(("fsdp", "ctx"), "tp"),
        P(("fsdp", "ctx"), "tp"),
        P("tp", ("fsdp", "ctx")),
        P(("fsdp", "ctx")),
        P(("fsdp", "ctx"), "tp"),
        P(("fsdp", "ctx"), "tp"),
        P("tp", ("fsdp", "ctx")),
        P(("fsdp", "ctx"), None),
        P(("fsdp", "ctx")),
        P(("fsdp", "ctx")),
    )
    out_specs = (
        P(("fsdp", "ctx"), None),
        P(("fsdp", "ctx"), None),
        P(("fsdp", "ctx")),
        P(("fsdp", "ctx"), "tp"),
        P(("fsdp", "ctx"), "tp"),
        P(("fsdp", "ctx"), "tp"),
        P("tp", ("fsdp", "ctx")),
        P(("fsdp", "ctx")),
        P(("fsdp", "ctx"), "tp"),
        P(("fsdp", "ctx"), "tp"),
        P("tp", ("fsdp", "ctx")),
    )
    small = (mesh.shape["fsdp"], mesh.shape["ctx"], mesh.shape["tp"]) == (2, 4, 4)
    return jax.shard_map(fast_shards if small else shards, mesh=mesh, in_specs=in_specs, out_specs=out_specs, check_vma=False)
```

```python
import jax
import jax.numpy as jnp
from jax import lax
from jax.experimental import pallas as pl
from jax.experimental.pallas import tpu as pltpu
from jax.sharding import PartitionSpec as P

H = 32
KVH = 4
HD = 64


EPSILON = 1e-05
THETA_BASE = 10000.0
MASKED_SCORE = -1e30


def shifted(value, axis, steps):
    count = lax.axis_size(axis)
    pairs = [(source, (source + steps) % count) for source in range(count)]
    return lax.ppermute(value, axis, pairs)


def rope_tables(token_pos, half_size):
    frequency = THETA_BASE ** (-jnp.arange(half_size, dtype=jnp.float32) / half_size)
    angles = token_pos.astype(jnp.float32)[:, None] * frequency[None, :]
    return (jnp.cos(angles), jnp.sin(angles))


def rotate(head_rows, cosine, sine):
    half_size = head_rows.shape[-1] // 2
    first_half = head_rows[..., :half_size]
    second_half = head_rows[..., half_size:]
    cos_rows = cosine[:, None, :]
    sin_rows = sine[:, None, :]
    return jnp.concatenate(
        [
            first_half * cos_rows - second_half * sin_rows,
            second_half * cos_rows + first_half * sin_rows,
        ],
        axis=-1,
    )


def rotate_back(head_rows, cosine, sine):
    half_size = head_rows.shape[-1] // 2
    first_half = head_rows[..., :half_size]
    second_half = head_rows[..., half_size:]
    cos_rows = cosine[:, None, :]
    sin_rows = sine[:, None, :]
    return jnp.concatenate(
        [
            first_half * cos_rows + second_half * sin_rows,
            second_half * cos_rows - first_half * sin_rows,
        ],
        axis=-1,
    )


def project(left_side, right_side):
    return jnp.dot(left_side, right_side, preferred_element_type=jnp.float32)


def project_back(left_side, right_side):
    return lax.dot_general(
        left_side, right_side, (((1,), (1,)), ((), ())), preferred_element_type=jnp.float32
    )


def weight_grad(left_side, right_side):
    return lax.dot_general(
        left_side, right_side, (((0,), (0,)), ((), ())), preferred_element_type=jnp.float32
    )


def rms_norm(rows_in, gain_vec):
    inv_rms = lax.rsqrt(jnp.mean(rows_in * rows_in, axis=-1, keepdims=True) + EPSILON)
    unit_rows = rows_in * inv_rms
    return (unit_rows * gain_vec, unit_rows, inv_rms)


def rms_norm_back(gradient, gain_vec, unit_rows, inv_rms):
    gain_grad = jnp.sum(gradient * unit_rows, axis=0)
    scaled_grad = gradient * gain_vec
    return (
        inv_rms
        * (scaled_grad - unit_rows * jnp.mean(scaled_grad * unit_rows, axis=-1, keepdims=True)),
        gain_grad,
    )


def pair_mask(query_pos, query_seg, key_pos, key_seg):
    return (query_seg[:, None] == key_seg[None, :]) & (key_pos[None, :] <= query_pos[:, None])


def split_block(kv_block, kv_heads):
    key_rows = kv_block[:, : kv_heads * HD].reshape(-1, kv_heads, HD)
    value_rows = kv_block[:, kv_heads * HD :].reshape(-1, kv_heads, HD)
    return (key_rows, value_rows)


def attend_block(state_in, queries, kv_block, visible):
    row_top, row_total, output_sum = state_in
    key_rows, value_rows = split_block(kv_block, queries.shape[1])
    scores = jnp.einsum(
        "qkgd,pkd->kgqp", queries, key_rows, preferred_element_type=jnp.float32
    ) * HD ** (-0.5)
    scores = jnp.where(visible, scores, MASKED_SCORE)
    new_top = jnp.maximum(row_top, jnp.max(scores, axis=-1))
    weights = jnp.where(visible, jnp.exp(scores - new_top[..., None]), 0.0)
    decay_factor = jnp.exp(row_top - new_top)
    row_total = row_total * decay_factor + jnp.sum(weights, axis=-1)
    mixed_heads = jnp.einsum(
        "kgqp,pkd->qkgd",
        weights.astype(jnp.bfloat16),
        value_rows,
        preferred_element_type=jnp.float32,
    )
    output_sum = output_sum * jnp.transpose(decay_factor, (2, 0, 1))[..., None] + mixed_heads
    return (new_top, row_total, output_sum)


def block_grads(queries, out_grad, kv_block, visible, log_total, delta_rows):
    key_rows, value_rows = split_block(kv_block, queries.shape[1])
    scale_factor = HD ** (-0.5)
    scores = (
        jnp.einsum("qkgd,pkd->kgqp", queries, key_rows, preferred_element_type=jnp.float32)
        * scale_factor
    )
    probs_full = jnp.where(
        visible, jnp.exp(jnp.where(visible, scores, MASKED_SCORE) - log_total[..., None]), 0.0
    )
    value_grad = jnp.einsum(
        "kgqp,qkgd->pkd",
        probs_full.astype(jnp.bfloat16),
        out_grad,
        preferred_element_type=jnp.float32,
    )
    prob_grad = jnp.einsum(
        "qkgd,pkd->kgqp", out_grad, value_rows, preferred_element_type=jnp.float32
    )
    score_grad = (probs_full * (prob_grad - delta_rows[..., None])).astype(jnp.bfloat16)
    query_grad = (
        jnp.einsum("kgqp,pkd->qkgd", score_grad, key_rows, preferred_element_type=jnp.float32)
        * scale_factor
    )
    key_grad = (
        jnp.einsum("kgqp,qkgd->pkd", score_grad, queries, preferred_element_type=jnp.float32)
        * scale_factor
    )
    block_rows = kv_block.shape[0]
    return (
        query_grad,
        jnp.concatenate(
            [key_grad.reshape(block_rows, -1), value_grad.reshape(block_rows, -1)], axis=-1
        ),
    )


def shards(
    tokens,
    attn_gain,
    w_query,
    w_key,
    w_value,
    w_out,
    mlp_gain,
    w_gate,
    w_up,
    w_down,
    cotangent,
    positions,
    segments,
):
    token_rows = tokens.shape[0]
    gain_one, query_w, key_w, value_w, out_w = (
        lax.all_gather(attn_gain, ("fsdp", "ctx"), axis=0, tiled=True),
        lax.all_gather(w_query, ("fsdp", "ctx"), axis=0, tiled=True),
        lax.all_gather(w_key, ("fsdp", "ctx"), axis=0, tiled=True),
        lax.all_gather(w_value, ("fsdp", "ctx"), axis=0, tiled=True),
        lax.all_gather(w_out, ("fsdp", "ctx"), axis=1, tiled=True),
    )
    gain_two, gate_w, up_w, down_w = (
        lax.all_gather(mlp_gain, ("fsdp", "ctx"), axis=0, tiled=True),
        lax.all_gather(w_gate, ("fsdp", "ctx"), axis=0, tiled=True),
        lax.all_gather(w_up, ("fsdp", "ctx"), axis=0, tiled=True),
        lax.all_gather(w_down, ("fsdp", "ctx"), axis=1, tiled=True),
    )
    head_count = query_w.shape[1] // HD
    kv_heads = key_w.shape[1] // HD
    groups = H // KVH
    cosine, sine = rope_tables(positions, HD // 2)
    token_float = tokens.astype(jnp.float32)
    gain_one_float = gain_one.astype(jnp.float32)
    normed_one, unit_one, inv_one = rms_norm(token_float, gain_one_float)
    normed_low = normed_one.astype(jnp.bfloat16)
    query_lin = project(normed_low, query_w)
    key_lin = project(normed_low, key_w)
    value_low = project(normed_low, value_w).astype(jnp.bfloat16)
    query_rot = rotate(query_lin.reshape(token_rows, head_count, HD), cosine, sine).astype(
        jnp.bfloat16
    )
    key_rot = rotate(key_lin.reshape(token_rows, kv_heads, HD), cosine, sine).astype(jnp.bfloat16)
    queries = query_rot.reshape(token_rows, kv_heads, groups, HD)
    kv_local = jnp.concatenate([key_rot.reshape(token_rows, kv_heads * HD), value_low], axis=-1)
    key_positions, key_segments = (
        lax.all_gather(positions, "ctx", axis=0, tiled=True),
        lax.all_gather(segments, "ctx", axis=0, tiled=True),
    )
    my_index = lax.axis_index("ctx")
    cycle_size = lax.axis_size("ctx")

    def block_marks(source):
        start_row = source * token_rows
        return pair_mask(
            positions,
            segments,
            lax.dynamic_slice_in_dim(key_positions, start_row, token_rows),
            lax.dynamic_slice_in_dim(key_segments, start_row, token_rows),
        )

    start_state = (
        jnp.full((kv_heads, groups, token_rows), MASKED_SCORE, jnp.float32),
        jnp.zeros((kv_heads, groups, token_rows), jnp.float32),
        jnp.zeros((token_rows, kv_heads, groups, HD), jnp.float32),
    )

    def forward_block(state_in, kv_block, source):
        visible = block_marks(source)
        return attend_block(state_in, queries, kv_block, visible)

    def cycle_step(state_in, step_index):
        attn_state, kv_block = state_in
        attn_state = forward_block(attn_state, kv_block, (my_index - step_index) % cycle_size)
        passed = shifted(kv_block, "ctx", 1)
        return ((attn_state, passed), kv_block)

    (attn_state, last_block), kept_blocks = lax.scan(
        cycle_step, (start_state, kv_local), jnp.arange(cycle_size - 1)
    )
    attn_state = forward_block(attn_state, last_block, (my_index + 1) % cycle_size)
    kv_blocks = jnp.concatenate([kept_blocks, last_block[None]], axis=0)
    sources = (my_index - jnp.arange(cycle_size)) % cycle_size
    row_top, row_total, output_sum = attn_state
    attended = output_sum / jnp.transpose(row_total, (2, 0, 1))[..., None]
    log_total = row_top + jnp.log(row_total)
    attended_low = attended.reshape(token_rows, head_count * HD).astype(jnp.bfloat16)
    middle = token_float + lax.psum(project(attended_low, out_w).astype(jnp.bfloat16), "tp").astype(
        jnp.float32
    )
    gain_two_float = gain_two.astype(jnp.float32)
    normed_two, unit_two, inv_two = rms_norm(middle, gain_two_float)
    normed_two_low = normed_two.astype(jnp.bfloat16)
    gate_lin = project(normed_two_low, gate_w)
    up_lin = project(normed_two_low, up_w)
    hidden_low = (jax.nn.silu(gate_lin) * up_lin).astype(jnp.bfloat16)
    result = middle + lax.psum(project(hidden_low, down_w).astype(jnp.bfloat16), "tp").astype(
        jnp.float32
    )
    output = result.astype(jnp.bfloat16)
    hidden_grad = project_back(cotangent, down_w)
    down_w_grad = weight_grad(hidden_low, cotangent)
    sigmoid_gate = jax.nn.sigmoid(gate_lin)
    gate_grad_low = (
        hidden_grad * up_lin * sigmoid_gate * (1.0 + gate_lin * (1.0 - sigmoid_gate))
    ).astype(jnp.bfloat16)
    up_grad_low = (hidden_grad * gate_lin * sigmoid_gate).astype(jnp.bfloat16)
    normed_two_grad = lax.psum(
        (project_back(gate_grad_low, gate_w) + project_back(up_grad_low, up_w)).astype(
            jnp.bfloat16
        ),
        "tp",
    ).astype(jnp.float32)
    gate_w_grad = weight_grad(normed_two_low, gate_grad_low)
    up_w_grad = weight_grad(normed_two_low, up_grad_low)
    norm_back_two, gain_two_grad = rms_norm_back(normed_two_grad, gain_two_float, unit_two, inv_two)
    middle_grad = cotangent.astype(jnp.float32) + norm_back_two
    middle_low = middle_grad.astype(jnp.bfloat16)
    attended_grad_low = project_back(middle_low, out_w).astype(jnp.bfloat16)
    out_w_grad = weight_grad(attended_low, middle_low)
    out_grad = attended_grad_low.reshape(token_rows, kv_heads, groups, HD)
    delta_rows = jnp.transpose(jnp.sum(out_grad.astype(jnp.float32) * attended, axis=-1), (1, 2, 0))

    def backward_block(kv_block, source):
        visible = block_marks(source)
        return block_grads(queries, out_grad, kv_block, visible, log_total, delta_rows)

    query_start = jnp.zeros((token_rows, kv_heads, groups, HD), jnp.float32)

    def back_step(state_in, pieces):
        query_acc, kv_acc = state_in
        query_term, kv_term = backward_block(pieces[0], pieces[1])
        passed = shifted((kv_acc + kv_term).astype(jnp.bfloat16), "ctx", 1).astype(jnp.float32)
        return ((query_acc + query_term, passed), None)

    (query_grad, kv_grad), unused = lax.scan(
        back_step, (query_start, jnp.zeros(kv_local.shape, jnp.float32)), (kv_blocks, sources)
    )
    query_grad_low = (
        rotate_back(query_grad.reshape(token_rows, head_count, HD), cosine, sine)
        .reshape(token_rows, head_count * HD)
        .astype(jnp.bfloat16)
    )
    key_grad_low = (
        rotate_back(kv_grad[:, : kv_heads * HD].reshape(token_rows, kv_heads, HD), cosine, sine)
        .reshape(token_rows, kv_heads * HD)
        .astype(jnp.bfloat16)
    )
    value_grad_low = kv_grad[:, kv_heads * HD :].astype(jnp.bfloat16)
    normed_one_grad = lax.psum(
        (
            project_back(query_grad_low, query_w)
            + project_back(key_grad_low, key_w)
            + project_back(value_grad_low, value_w)
        ).astype(jnp.bfloat16),
        "tp",
    ).astype(jnp.float32)
    query_w_grad = weight_grad(normed_low, query_grad_low)
    key_w_grad = weight_grad(normed_low, key_grad_low)
    value_w_grad = weight_grad(normed_low, value_grad_low)
    norm_back_one, gain_one_grad = rms_norm_back(normed_one_grad, gain_one_float, unit_one, inv_one)
    input_grad = (middle_grad + norm_back_one).astype(jnp.bfloat16)
    summed = (
        lax.psum_scatter(
            gain_one_grad.astype(jnp.bfloat16), ("fsdp", "ctx"), scatter_dimension=0, tiled=True
        ).astype(jnp.float32),
        lax.psum_scatter(
            query_w_grad.astype(jnp.bfloat16), ("fsdp", "ctx"), scatter_dimension=0, tiled=True
        ).astype(jnp.float32),
        lax.psum_scatter(
            key_w_grad.astype(jnp.bfloat16), ("fsdp", "ctx"), scatter_dimension=0, tiled=True
        ).astype(jnp.float32),
        lax.psum_scatter(
            value_w_grad.astype(jnp.bfloat16), ("fsdp", "ctx"), scatter_dimension=0, tiled=True
        ).astype(jnp.float32),
        lax.psum_scatter(
            out_w_grad.astype(jnp.bfloat16), ("fsdp", "ctx"), scatter_dimension=1, tiled=True
        ).astype(jnp.float32),
        lax.psum_scatter(
            gain_two_grad.astype(jnp.bfloat16), ("fsdp", "ctx"), scatter_dimension=0, tiled=True
        ).astype(jnp.float32),
        lax.psum_scatter(
            gate_w_grad.astype(jnp.bfloat16), ("fsdp", "ctx"), scatter_dimension=0, tiled=True
        ).astype(jnp.float32),
        lax.psum_scatter(
            up_w_grad.astype(jnp.bfloat16), ("fsdp", "ctx"), scatter_dimension=0, tiled=True
        ).astype(jnp.float32),
        lax.psum_scatter(
            down_w_grad.astype(jnp.bfloat16), ("fsdp", "ctx"), scatter_dimension=1, tiled=True
        ).astype(jnp.float32),
    )
    return (output, input_grad) + tuple(summed)


MESH = pl.DeviceIdType.MESH
BF = jnp.bfloat16
F32 = jnp.float32


def dotg(left_side, right_side, left_dim, right_dim):
    return lax.dot_general(
        left_side,
        right_side,
        (((left_dim,), (right_dim,)), ((), ())),
        preferred_element_type=F32,
    )


def remote(src, dst, send_sem, recv_sem, device):
    return pltpu.make_async_remote_copy(
        src_ref=src,
        dst_ref=dst,
        send_sem=send_sem,
        recv_sem=recv_sem,
        device_id=device,
        device_id_type=MESH,
    )


class Place:
    def __init__(self):
        self.f = lax.axis_index("fsdp")
        self.c = lax.axis_index("ctx")
        self.z = lax.axis_index("tp")
        self.cx = self.c + 1 - 2 * lax.rem(self.c, 2)
        self.cy = lax.rem(self.c + 2, 4)
        self.cd = 3 - self.c
        self.of = 1 - self.f
        self.own = self.f * 4 + self.c
        self.sx = self.f * 4 + self.cx
        self.sy = self.f * 4 + self.cy
        self.sd = self.f * 4 + self.cd

    def at(self, f=None, c=None, z=None):
        return (
            self.f if f is None else f,
            self.c if c is None else c,
            self.z if z is None else z,
        )


def greet(devices):
    barrier = pltpu.get_barrier_semaphore()
    for device in devices:
        pl.semaphore_signal(barrier, inc=1, device_id=device, device_id_type=MESH)
    pl.semaphore_wait(barrier, len(devices))


def group_devices(me):
    return [
        me.at(c=me.cx),
        me.at(c=me.cy),
        me.at(c=me.cd),
        me.at(f=me.of),
        me.at(f=me.of, c=me.cx),
        me.at(f=me.of, c=me.cy),
        me.at(f=me.of, c=me.cd),
    ]


def column_devices(me):
    return [me.at(z=lax.rem(me.z + step, 4)) for step in (1, 2, 3)]


class Gather:
    def __init__(self, me, index, own, full, send, recv, local_sem):
        self.me, self.own_ref, self.full = me, own, full
        rows = full.shape[1]
        self.half_a = pl.ds(0, rows // 2)
        self.half_b = pl.ds(rows // 2, rows // 2)

        def copy(slot, src, dst, device):
            return remote(src, dst, send.at[index, slot], recv.at[index, slot], device)

        slot_own, slot_x, slot_y = full.at[me.own], full.at[me.sx], full.at[me.sy]
        to_x, to_y, to_core = me.at(c=me.cx), me.at(c=me.cy), me.at(f=me.of)
        diag_a = full.at[me.sd, self.half_a]
        diag_b = full.at[me.sd, self.half_b]
        self.own_x = copy(0, own, slot_own, to_x)
        self.own_y = copy(1, own, slot_own, to_y)
        self.own_core = copy(2, own, slot_own, to_core)
        self.pass_x = copy(3, full.at[me.sy, self.half_a], full.at[me.sy, self.half_a], to_x)
        self.pass_y = copy(4, full.at[me.sx, self.half_b], full.at[me.sx, self.half_b], to_y)
        self.core_x = copy(5, slot_x, slot_x, to_core)
        self.core_y = copy(6, slot_y, slot_y, to_core)
        self.core_a = copy(7, diag_a, diag_a, to_core)
        self.core_b = copy(8, diag_b, diag_b, to_core)
        other = me.of * 4
        into = lambda slot, ref, device: copy(slot, ref, ref, device)
        self.in_x = into(0, slot_x, to_x)
        self.in_y = into(1, slot_y, to_y)
        self.in_a = into(3, diag_a, to_x)
        self.in_b = into(4, diag_b, to_y)
        self.in_core = [
            into(2, full.at[other + me.c], to_core),
            into(5, full.at[other + me.cx], to_core),
            into(6, full.at[other + me.cy], to_core),
            into(7, full.at[other + me.cd, self.half_a], to_core),
            into(8, full.at[other + me.cd, self.half_b], to_core),
        ]
        self.keep = pltpu.make_async_copy(own, slot_own, local_sem.at[index])

    def begin(self):
        self.own_x.start()
        self.own_y.start()
        self.own_core.start()
        self.keep.start()

    def forward(self):
        self.in_y.wait_recv()
        self.pass_x.start()
        self.core_y.start()
        self.in_x.wait_recv()
        self.pass_y.start()
        self.core_x.start()

    def diagonal(self):
        self.in_a.wait_recv()
        self.core_a.start()
        self.in_b.wait_recv()
        self.core_b.start()

    def arrive(self):
        self.keep.wait()
        for piece in self.in_core:
            piece.wait_recv()

    def settle(self):
        for piece in (
            self.own_x,
            self.own_y,
            self.own_core,
            self.pass_x,
            self.pass_y,
            self.core_x,
            self.core_y,
            self.core_a,
            self.core_b,
        ):
            piece.wait_send()


class LineSum:
    def __init__(self, me, part, outer_in, inner_in, send, recv):
        self.me, self.part = me, part
        self.outer_in, self.inner_in = outer_in, inner_in
        self.send, self.recv = send, recv
        z = me.z
        self.is_mid = (z == 1) | (z == 2)
        self.is_end = (z == 0) | (z == 3)
        self.mid_of_end = 1 + z // 3
        self.outer_of_mid = 3 * (z - 1)

    def end_copies(self):
        me, part = self.me, self.part
        mid = self.mid_of_end
        to_mid = me.at(z=mid)
        owners = (3 - me.z, 3 - mid, mid)
        return [
            remote(
                part.at[owner],
                self.outer_in.at[slot],
                self.send.at[slot],
                self.recv.at[slot],
                to_mid,
            )
            for slot, owner in enumerate(owners)
        ]

    def mid_copies(self):
        me, part = self.me, self.part
        far_mid, outer = 3 - me.z, self.outer_of_mid
        far = 3 - outer
        to_mid, to_outer = me.at(z=far_mid), me.at(z=outer)
        return [
            remote(part.at[far], self.inner_in.at[0], self.send.at[0], self.recv.at[3], to_mid),
            remote(part.at[far_mid], self.inner_in.at[1], self.send.at[1], self.recv.at[4], to_mid),
            remote(part.at[outer], self.inner_in.at[0], self.send.at[2], self.recv.at[3], to_outer),
        ]

    def wait_in(self, slot, buffer):
        remote(buffer, buffer, self.send.at[0], self.recv.at[slot], self.me.at(z=3 - self.me.z)).wait_recv()

    def add(self, owner, buffer):
        self.part[owner] = (self.part[owner].astype(F32) + buffer[...].astype(F32)).astype(BF)

    def begin(self):
        @pl.when(self.is_end)
        def _():
            for piece in self.end_copies():
                piece.start()

    def step_one(self):
        @pl.when(self.is_mid)
        def _():
            far = 3 - self.outer_of_mid
            self.wait_in(0, self.outer_in.at[0])
            self.add(far, self.outer_in.at[0])
            self.mid_copies()[0].start()

    def step_two(self):
        @pl.when(self.is_mid)
        def _():
            copies = self.mid_copies()
            self.wait_in(1, self.outer_in.at[1])
            self.add(3 - self.me.z, self.outer_in.at[1])
            copies[1].start()
            self.wait_in(3, self.inner_in.at[0])
            self.add(self.outer_of_mid, self.inner_in.at[0])
            copies[2].start()

    def finish(self, total):
        me = self.me

        @pl.when(self.is_mid)
        def _():
            self.wait_in(2, self.outer_in.at[2])
            self.wait_in(4, self.inner_in.at[1])
            total[...] = (
                self.part[me.z].astype(F32)
                + self.outer_in[2].astype(F32)
                + self.inner_in[1].astype(F32)
            )
            for piece in self.mid_copies():
                piece.wait_send()

        @pl.when(self.is_end)
        def _():
            self.wait_in(3, self.inner_in.at[0])
            total[...] = self.part[me.z].astype(F32) + self.inner_in[0].astype(F32)
            for piece in self.end_copies():
                piece.wait_send()


class LineGather:
    def __init__(self, me, blocks, send, recv):
        self.me, self.blocks, self.send, self.recv = me, blocks, send, recv
        z = me.z
        self.is_mid = (z == 1) | (z == 2)
        self.is_end = (z == 0) | (z == 3)
        self.mid_of_end = 1 + z // 3
        self.outer_of_mid = 3 * (z - 1)

    def copy(self, owner, slot, z):
        ref = self.blocks.at[owner]
        return remote(ref, ref, self.send.at[slot], self.recv.at[owner], self.me.at(z=z))

    def wait_in(self, owner):
        ref = self.blocks.at[owner]
        remote(ref, ref, self.send.at[0], self.recv.at[owner], self.me.at(z=3 - self.me.z)).wait_recv()

    def begin(self):
        me = self.me

        @pl.when(self.is_end)
        def _():
            self.copy(me.z, 0, self.mid_of_end).start()

        @pl.when(self.is_mid)
        def _():
            self.copy(me.z, 0, self.outer_of_mid).start()
            self.copy(me.z, 1, 3 - me.z).start()

    def step_one(self):
        me = self.me

        @pl.when(self.is_mid)
        def _():
            self.wait_in(self.outer_of_mid)
            self.copy(self.outer_of_mid, 2, 3 - me.z).start()
            self.wait_in(3 - me.z)
            self.copy(3 - me.z, 3, self.outer_of_mid).start()

    def step_two(self):
        @pl.when(self.is_mid)
        def _():
            far = 3 - self.outer_of_mid
            self.wait_in(far)
            self.copy(far, 4, self.outer_of_mid).start()

    def finish(self):
        me = self.me

        @pl.when(self.is_mid)
        def _():
            self.copy(me.z, 0, self.outer_of_mid).wait_send()
            self.copy(me.z, 1, 3 - me.z).wait_send()
            self.copy(self.outer_of_mid, 2, 3 - me.z).wait_send()
            self.copy(3 - me.z, 3, self.outer_of_mid).wait_send()
            self.copy(3 - self.outer_of_mid, 4, self.outer_of_mid).wait_send()

        @pl.when(self.is_end)
        def _():
            mid = self.mid_of_end
            self.wait_in(mid)
            self.wait_in(3 - mid)
            self.wait_in(3 - me.z)
            self.copy(me.z, 0, mid).wait_send()


def row_of(gains_ref, which):
    return jnp.concatenate([gains_ref[shard, which : which + 1, :] for shard in range(8)], axis=-1)


def swap_halves(rows):
    lane = lax.broadcasted_iota(jnp.int32, rows.shape, 1)
    return jnp.where(
        lax.rem(lane, HD) < HD // 2, pltpu.roll(rows, 96, 1), pltpu.roll(rows, 32, 1)
    )


def forward_kernel(
    tok,
    w_qkv,
    w_out,
    w_gate,
    w_up,
    w_down,
    gains,
    marks,
    rope_q,
    rope_k,
    f_qkv,
    f_out,
    f_gate,
    f_up,
    f_down,
    f_gains,
    n_one,
    q_heads,
    kv_out,
    bias,
    lse,
    att_low,
    middle,
    n_two,
    s_qkv,
    s_out,
    s_gains,
    s_marks,
    s_kv,
    s_keys,
    s_vals,
    s_qlin,
    s_part,
    s_outer,
    s_inner,
    s_total,
    s_blocks,
    g_send,
    g_recv,
    g_local,
    small_send,
    small_recv,
    kv_send,
    kv_recv,
    sum_send,
    sum_recv,
    all_send,
    all_recv,
    out_sem,
):
    me = Place()
    group = group_devices(me)
    greet(group + column_devices(me))

    qkv = Gather(me, 0, w_qkv, s_qkv, g_send, g_recv, g_local)
    out = Gather(me, 1, w_out, s_out, g_send, g_recv, g_local)
    gate = Gather(me, 2, w_gate, f_gate, g_send, g_recv, g_local)
    up = Gather(me, 3, w_up, f_up, g_send, g_recv, g_local)
    down = Gather(me, 4, w_down, f_down, g_send, g_recv, g_local)

    small = []
    for slot, device in enumerate(group):
        small.append(
            remote(gains, s_gains.at[me.own], small_send.at[slot], small_recv.at[slot], device)
        )
    for slot, device in enumerate(group[:3]):
        small.append(
            remote(
                marks, s_marks.at[me.c], small_send.at[7 + slot], small_recv.at[7 + slot], device
            )
        )
    for piece in small:
        piece.start()
    qkv.begin()
    s_gains[me.own] = gains[...]
    s_marks[me.c] = marks[...]
    sources = [me.sx, me.sy, me.sd, me.of * 4 + me.c, me.of * 4 + me.cx, me.of * 4 + me.cy, me.of * 4 + me.cd]
    for slot, source in enumerate(sources):
        remote(
            gains, s_gains.at[source], small_send.at[slot], small_recv.at[slot], group[slot]
        ).wait_recv()
    for slot, source in enumerate((me.cx, me.cy, me.cd)):
        remote(
            marks, s_marks.at[source], small_send.at[7 + slot], small_recv.at[7 + slot], group[slot]
        ).wait_recv()
    f_gains[...] = s_gains[...]

    gain_one = row_of(s_gains, 0)

    def norm_rows(step, carry):
        rows = pl.ds(pl.multiple_of(step * 64, 64), 64)
        values = tok[rows, :].astype(F32)
        inv = lax.rsqrt(jnp.mean(values * values, axis=-1, keepdims=True) + EPSILON)
        n_one[rows, :] = (values * inv * gain_one).astype(BF)
        return carry

    lax.fori_loop(0, tok.shape[0] // 64, norm_rows, 0)

    qkv.forward()
    out.begin()
    qkv.diagonal()

    def make_bias(group_index):
        own_rows = marks[:, group_index * 256 : (group_index + 1) * 256].astype(F32)
        for source in range(4):
            key_rows = s_marks[source, :, group_index * 256 : (group_index + 1) * 256].astype(F32)
            key_pos = jnp.transpose(jnp.broadcast_to(key_rows[0:1, :], (128, 256)))
            key_seg = jnp.transpose(jnp.broadcast_to(key_rows[1:2, :], (128, 256)))
            for part in range(2):
                lanes = slice(part * 128, (part + 1) * 128)
                seen = (key_seg == own_rows[1:2, lanes]) & (key_pos <= own_rows[0:1, lanes])
                bias[group_index, source * 256 : (source + 1) * 256, lanes] = jnp.where(
                    seen, 0.0, MASKED_SCORE
                ).astype(BF)

    make_bias(0)
    make_bias(1)
    qkv.arrive()

    for first in (0, 256, 512):
        lanes = slice(first, min(first + 256, 640))
        total = None
        for shard in range(8):
            term = dotg(
                n_one[:, shard * 256 : (shard + 1) * 256], s_qkv[shard, :, lanes], 1, 0
            )
            total = term if total is None else total + term
        s_qlin[:, lanes] = total

    key_pair = s_qlin[:, 512:640]
    rot_pair = key_pair * rope_k[:, :128] + swap_halves(key_pair) * rope_k[:, 128:]
    s_kv[me.c] = rot_pair.astype(BF)
    kv_copies = [
        remote(s_kv.at[me.c], s_kv.at[me.c], kv_send.at[slot], kv_recv.at[slot], device)
        for slot, device in enumerate(group[:3])
    ]
    for piece in kv_copies:
        piece.start()
    out.forward()
    for piece in (gate, up, down):
        piece.begin()

    lane = lax.broadcasted_iota(jnp.int32, (256, 128), 1)
    for pair in range(4):
        rows = s_qlin[:, pair * 128 : (pair + 1) * 128]
        rot = (rows * rope_q[:, :128] + swap_halves(rows) * rope_q[:, 128:]).astype(BF)
        rot = rot * jnp.bfloat16(HD ** (-0.5))
        for group_index in range(2):
            own = rot[group_index * 256 : (group_index + 1) * 256, :]
            zero = jnp.zeros_like(own)
            q_heads[group_index * 8 + 2 * pair] = jnp.where(lane < HD, own, zero)
            q_heads[group_index * 8 + 2 * pair + 1] = jnp.where(lane >= HD, own, zero)

    for slot, source in enumerate((me.cx, me.cy, me.cd)):
        remote(
            s_kv.at[source], s_kv.at[source], kv_send.at[slot], kv_recv.at[slot], group[slot]
        ).wait_recv()
    lane_kv = lax.broadcasted_iota(jnp.int32, (256, 128), 1)
    for group_index in range(2):
        for source in range(4):
            pairs = s_kv[source, group_index * 256 : (group_index + 1) * 256, :].astype(F32)
            rows = slice(source * 256, (source + 1) * 256)
            s_keys[group_index, rows, :] = jnp.where(
                lane_kv < HD, pairs, pltpu.roll(pairs, HD, 1)
            ).astype(BF)
            s_vals[group_index, :, rows] = jnp.transpose(pairs)[HD:, :].astype(BF)
    kv_out[...] = s_kv[...]

    def attend(step, carry):
        group_index = step // 4
        pair = step - group_index * 4
        halves = []
        for odd in range(2):
            head = step * 2 + odd
            scores = dotg(s_keys[group_index], q_heads[head], 1, 1) + bias[group_index].astype(F32)
            top = jnp.max(scores, axis=0, keepdims=True)
            weights = jnp.exp(scores - top)
            total = jnp.sum(weights, axis=0, keepdims=True)
            mixed = dotg(s_vals[group_index], weights.astype(BF), 1, 0)
            halves.append(mixed / total)
            lse[head] = top + jnp.log(total)
        rows = jnp.transpose(jnp.concatenate(halves, axis=0))
        att_low[
            pl.ds(pl.multiple_of(group_index * 256, 256), 256),
            pl.ds(pl.multiple_of(pair * 128, 128), 128),
        ] = rows.astype(BF)
        return carry

    def project_out(group_index):
        rows = att_low[group_index * 256 : (group_index + 1) * 256, :]
        for shard in range(8):
            lanes = slice(shard * 256, (shard + 1) * 256)
            s_part[group_index, :, :, lanes] = (
                dotg(rows, s_out[shard], 1, 0).astype(BF).reshape(4, 64, 256)
            )

    def second_norm(group_index):
        own_rows = pl.ds(pl.multiple_of(group_index * 256 + me.z * 64, 64), 64)
        mid_rows = tok[own_rows, :].astype(F32) + s_total[group_index]
        middle[group_index] = mid_rows
        inv_two = lax.rsqrt(jnp.mean(mid_rows * mid_rows, axis=-1, keepdims=True) + EPSILON)
        s_blocks[group_index, me.z] = (mid_rows * inv_two * row_of(s_gains, 1)).astype(BF)

    sums = [
        LineSum(me, s_part.at[g], s_outer.at[g], s_inner.at[g], sum_send.at[g], sum_recv.at[g])
        for g in range(2)
    ]
    spreads = [LineGather(me, s_blocks.at[g], all_send.at[g], all_recv.at[g]) for g in range(2)]

    lax.fori_loop(0, 4, attend, 0)
    out.diagonal()
    out.arrive()
    project_out(0)
    sums[0].begin()
    gate.forward()
    keep = [
        pltpu.make_async_copy(s_qkv, f_qkv, out_sem.at[0]),
        pltpu.make_async_copy(s_out, f_out, out_sem.at[1]),
    ]
    for piece in keep:
        piece.start()
    lax.fori_loop(4, 6, attend, 0)
    sums[0].step_one()
    lax.fori_loop(6, 8, attend, 0)
    sums[0].step_two()
    project_out(1)
    sums[1].begin()
    sums[0].finish(s_total.at[0])
    second_norm(0)
    spreads[0].begin()
    sums[1].step_one()
    up.forward()
    spreads[0].step_one()
    sums[1].step_two()
    spreads[0].step_two()
    sums[1].finish(s_total.at[1])
    second_norm(1)
    spreads[1].begin()
    down.forward()
    gate.diagonal()
    spreads[1].step_one()
    up.diagonal()
    spreads[1].step_two()
    down.diagonal()
    spreads[0].finish()
    gate.arrive()
    up.arrive()
    down.arrive()
    spreads[1].finish()
    last = pltpu.make_async_copy(s_blocks, n_two, out_sem.at[2])
    last.start()
    for piece in small:
        piece.wait_send()
    for piece in kv_copies:
        piece.wait_send()
    for piece in (qkv, out, gate, up, down):
        piece.settle()
    for piece in keep:
        piece.wait()
    last.wait()


def run_forward(tokens, w_qkv, w_out, w_gate, w_up, w_down, gains, marks, rope_q, rope_k):
    shape = jax.ShapeDtypeStruct
    width = tokens.shape[1]
    hidden = w_gate.shape[1]
    in_vmem = pl.BlockSpec(memory_space=pltpu.VMEM)
    anywhere = pl.BlockSpec(memory_space=pl.ANY)
    dma = pltpu.SemaphoreType.DMA
    return pl.pallas_call(
        forward_kernel,
        name="forward_part",
        out_shape=(
            shape((8, 256, 640), BF),
            shape((8, 512, 256), BF),
            shape((8, 256, hidden), BF),
            shape((8, 256, hidden), BF),
            shape((8, hidden, 256), BF),
            shape((8, 8, 256), F32),
            shape((512, width), BF),
            shape((16, 256, 128), BF),
            shape((4, 512, 128), BF),
            shape((2, 1024, 256), BF),
            shape((16, 1, 256), F32),
            shape((512, 512), BF),
            shape((2, 64, width), F32),
            shape((2, 4, 64, width), BF),
        ),
        in_specs=[in_vmem] * 10,
        out_specs=(anywhere,) * 5 + (in_vmem,) * 8 + (anywhere,),
        scratch_shapes=[
            pltpu.VMEM((8, 256, 640), BF),
            pltpu.VMEM((8, 512, 256), BF),
            pltpu.VMEM((8, 8, 256), F32),
            pltpu.VMEM((4, 8, 512), jnp.int32),
            pltpu.VMEM((4, 512, 128), BF),
            pltpu.VMEM((2, 1024, 128), BF),
            pltpu.VMEM((2, HD, 1024), BF),
            pltpu.VMEM((512, 640), F32),
            pltpu.VMEM((2, 4, 64, width), BF),
            pltpu.VMEM((2, 3, 64, width), BF),
            pltpu.VMEM((2, 2, 64, width), BF),
            pltpu.VMEM((2, 64, width), F32),
            pltpu.VMEM((2, 4, 64, width), BF),
            dma((5, 9)),
            dma((5, 9)),
            dma((5,)),
            dma((10,)),
            dma((10,)),
            dma((3,)),
            dma((3,)),
            dma((2, 3)),
            dma((2, 5)),
            dma((2, 5)),
            dma((2, 4)),
            dma((3,)),
        ],
        compiler_params=pltpu.CompilerParams(
            collective_id=0, has_side_effects=True, vmem_limit_bytes=60000000
        ),
    )(tokens, w_qkv, w_out, w_gate, w_up, w_down, gains, marks, rope_q, rope_k)


def prepared(tokens, attn_gain, w_query, w_key, w_value, mlp_gain, positions, segments):
    cosine, sine = rope_tables(positions, HD // 2)
    one, zero = jnp.ones_like(cosine), jnp.zeros_like(sine)
    rope_q = jnp.concatenate([cosine] * 4 + [-sine, sine, -sine, sine], axis=-1)
    rope_k = jnp.concatenate([cosine, cosine, one, one, -sine, sine, zero, zero], axis=-1)
    w_qkv = jnp.concatenate([w_query, w_key, w_value], axis=1)
    gains = jnp.pad(jnp.stack([attn_gain, mlp_gain]).astype(F32), ((0, 6), (0, 0)))
    marks = jnp.pad(jnp.stack([positions, segments]), ((0, 6), (0, 0)))
    return w_qkv, gains, marks, rope_q, rope_k
class Scatter:
    def __init__(self, me, index, last, width, x_of, y_of, chips, refs):
        self.me, self.index, self.last, self.width = me, index, last, width
        self.x_of, self.y_of, self.chips = x_of, y_of, chips
        self.stage, self.core_in, self.diag_in, self.near_in = refs[:4]
        self.send, self.recv, self.credit = refs[4:]
        self.columns = (me.c, me.cx, me.cy, me.cd)
        self.to_x, self.to_y, self.to_core = me.at(c=me.cx), me.at(c=me.cy), me.at(f=me.of)
        self.sent = []

    def copy(self, slot, src, dst, device):
        return remote(
            src, dst, self.send.at[self.index, slot], self.recv.at[self.index, slot], device
        )

    def lanes(self, ref):
        return ref.at[:, pl.ds(0, self.width)]

    def core_copy(self, role, slot):
        return self.copy(
            role,
            self.lanes(self.stage.at[slot]),
            self.lanes(self.core_in.at[role]),
            self.to_core,
        )

    def chunk(self, shard):
        return dotg(self.x_of(shard), self.y_of(), 0, 0)

    def partner(self):
        me = self.me
        pending = [None, None]
        for step, role in enumerate((3, 1, 2, 0)):
            slot = step % 2
            value = self.chunk(me.of * 4 + self.columns[role]).astype(BF)
            if pending[slot] is not None:
                pending[slot].wait_send()
            self.lanes(self.stage.at[slot])[...] = value
            if self.index > 0:
                pl.semaphore_wait(self.credit.at[role], 1)
            pending[slot] = self.core_copy(role, slot)
            pending[slot].start()
        for piece in pending:
            piece.wait_send()

    def near(self, role, half, slot):
        rows = pl.ds(half * 128, 128)
        side = role - 1
        device = self.to_x if role == 1 else self.to_y
        return self.copy(
            slot, self.chips(role).at[rows, :], self.near_in.at[side, rows, :], device
        )

    def diag(self, half):
        device = self.to_x if half == 0 else self.to_y
        return self.copy(
            4 + half,
            self.chips(3).at[pl.ds(half * 128, 128), :],
            self.lanes(self.diag_in.at[half]),
            device,
        )

    def own(self):
        me = self.me
        for role in (3, 1, 2, 0):
            value = self.chunk(me.f * 4 + self.columns[role])
            self.core_copy(role, 0).wait_recv()
            chip = self.chips(role)
            chip[...] = (value + self.lanes(self.core_in.at[role])[...].astype(F32)).astype(BF)
            if not self.last:
                pl.semaphore_signal(
                    self.credit.at[role], inc=1, device_id=self.to_core, device_id_type=MESH
                )
            if role == 3:
                self.diag(0).start()
                self.diag(1).start()
            if role == 1:
                self.near(1, 0, 6).start()
            if role == 2:
                self.near(2, 1, 7).start()

    def relay(self):
        first, second = pl.ds(0, 128), pl.ds(128, 128)
        self.diag(0).wait_recv()
        rows = self.chips(2).at[first, :]
        rows[...] = (
            rows[...].astype(F32) + self.lanes(self.diag_in.at[0])[...].astype(F32)
        ).astype(BF)
        self.near(2, 0, 8).start()
        self.diag(1).wait_recv()
        rows = self.chips(1).at[second, :]
        rows[...] = (
            rows[...].astype(F32) + self.lanes(self.diag_in.at[1])[...].astype(F32)
        ).astype(BF)
        self.near(1, 1, 9).start()

    def collect(self, buffer, sem):
        for role, half, slot in ((1, 0, 6), (2, 1, 7), (2, 0, 8), (1, 1, 9)):
            self.near(role, half, slot).wait_recv()
        for side in range(2):
            pltpu.make_async_copy(
                self.near_in.at[side], self.lanes(buffer.at[side]), sem.at[side]
            ).start()

    def collected(self, buffer, sem):
        for side in range(2):
            pltpu.make_async_copy(
                self.near_in.at[side], self.lanes(buffer.at[side]), sem.at[side]
            ).wait()

    def settle(self):
        for half in range(2):
            self.diag(half).wait_send()
        for role, half, slot in ((1, 0, 6), (2, 1, 7), (2, 0, 8), (1, 1, 9)):
            self.near(role, half, slot).wait_send()


def norm_back(gradient, rows_in, gain):
    inv = lax.rsqrt(jnp.mean(rows_in * rows_in, axis=-1, keepdims=True) + EPSILON)
    unit = rows_in * inv
    scaled = gradient * gain
    back = inv * (scaled - unit * jnp.mean(scaled * unit, axis=-1, keepdims=True))
    return back, jnp.sum(gradient * unit, axis=0, keepdims=True)


def backward_kernel(
    cot_h,
    tok_h,
    h_qkv,
    h_out,
    h_gate,
    h_up,
    h_down,
    gains,
    n_one_h,
    q_heads_h,
    kv_h,
    bias_h,
    lse,
    att_h,
    middle_h,
    n_two_h,
    rope_h,
    o_result,
    o_input,
    o_gains,
    o_query,
    o_kv,
    o_out,
    o_gate,
    o_up,
    o_down,
    near_down,
    near_gate,
    near_up,
    near_out,
    near_qkv,
    w_gate,
    w_up,
    w_down,
    w_out,
    w_qkv,
    cot,
    n_two,
    hid,
    gate_g,
    up_g,
    core_in,
    diag_in,
    chip_out,
    chip_qkv,
    sum_stage,
    turn_stage,
    part,
    outer_in,
    inner_in,
    outer_two,
    inner_two,
    mlow,
    total,
    own_out,
    mid,
    mid_g,
    tok_own,
    q_heads,
    bias,
    kv,
    att,
    rope,
    do_heads,
    keys,
    vals,
    keys_t,
    key_acc,
    val_acc,
    kv_send_buf,
    kv_in,
    d_qkv,
    vec,
    vec_in,
    vec_out,
    vec_near,
    tile_sem,
    load_sem,
    sum_send,
    sum_recv,
    all_send,
    all_recv,
    rs_send,
    rs_recv,
    credit,
    kv_send,
    kv_recv,
    vec_send,
    vec_recv,
    fin_sem,
    put_sem,
    own_sem,
):
    me = Place()
    group = group_devices(me)
    hidden = hid.shape[1]
    full_tiles = hidden // 256
    tiles = [(n * 256, min(256, hidden - n * 256)) for n in range((hidden + 255) // 256)]

    def load(src, dst, slot):
        return pltpu.make_async_copy(src, dst, load_sem.at[slot])

    rows_of = [pl.ds(g * 256, 256) for g in range(2)]
    loads = {}
    for g in range(2):
        loads["two", g] = load(n_two_h.at[g], n_two.at[g], g)
        loads["cot", g] = load(cot_h.at[rows_of[g], :], cot.at[rows_of[g], :], 2 + g)
        own = pl.ds(pl.multiple_of(g * 256 + me.z * 64, 64), 64)
        loads["tok", g] = load(tok_h.at[own, :], tok_own.at[g], 4 + g)
    for slot, (name, src, dst) in enumerate(
        (
            ("out", h_out, w_out),
            ("qkv", h_qkv, w_qkv),
            ("heads", q_heads_h, q_heads),
            ("bias", bias_h, bias),
            ("kv", kv_h, kv),
            ("att", att_h, att),
            ("mid", middle_h, mid),
            ("rope", rope_h, rope),
        )
    ):
        loads[name] = load(src, dst, 6 + slot)

    def tile_loads(first, width, slot):
        lanes = pl.ds(first, width)
        return [
            pltpu.make_async_copy(h_gate.at[:, :, lanes], w_gate.at[:, :, lanes], tile_sem.at[0, slot]),
            pltpu.make_async_copy(h_up.at[:, :, lanes], w_up.at[:, :, lanes], tile_sem.at[1, slot]),
            pltpu.make_async_copy(h_down.at[:, lanes, :], w_down.at[:, lanes, :], tile_sem.at[2, slot]),
        ]

    loads["two", 0].start()
    loads["cot", 0].start()
    for slot, (first, width) in enumerate(tiles):
        for piece in tile_loads(first, width, slot):
            piece.start()
    for name in (("two", 1), ("cot", 1), "mid", "out", ("tok", 0), ("tok", 1)):
        loads[name].start()
    for name in ("heads", "bias", "kv", "att", "rope", "qkv"):
        loads[name].start()

    greet(group + column_devices(me))

    gain_one, gain_two = row_of(gains, 0), row_of(gains, 1)

    def feed_tile(g, first, width):
        rows = rows_of[g]
        lanes = pl.ds(first, width)
        normed = n_two[g].reshape(256, 2048)
        gate = dotg(normed, w_gate[:, :, lanes].reshape(2048, width), 1, 0)
        up = dotg(normed, w_up[:, :, lanes].reshape(2048, width), 1, 0)
        hidden_grad = None
        for shard in range(8):
            term = dotg(
                cot[rows, shard * 256 : (shard + 1) * 256], w_down[shard, lanes, :], 1, 1
            )
            hidden_grad = term if hidden_grad is None else hidden_grad + term
        sig = jax.nn.sigmoid(gate)
        silu = gate * sig
        hid[rows, lanes] = (silu * up).astype(BF)
        up_g[rows, lanes] = (hidden_grad * silu).astype(BF)
        gate_g[rows, lanes] = (
            hidden_grad * up * sig * (1.0 + gate * (1.0 - sig))
        ).astype(BF)

    def feed(g, start, stop):
        def body(n, carry):
            if g == 0:
                for kind in range(3):
                    tile_loads(0, 256, n)[kind].wait()
            feed_tile(g, pl.multiple_of(n * 256, 256), 256)
            return carry

        lax.fori_loop(start, min(stop, full_tiles), body, 0)
        if stop > full_tiles and len(tiles) > full_tiles:
            first, width = tiles[-1]
            if g == 0:
                for piece in tile_loads(first, width, full_tiles):
                    piece.wait()
            feed_tile(g, first, width)

    def feed_back(g):
        def body(shard, carry):
            term = dotg(gate_g[rows_of[g], :], w_gate[shard], 1, 1) + dotg(
                up_g[rows_of[g], :], w_up[shard], 1, 1
            )
            part[g, :, :, pl.ds(pl.multiple_of(shard * 256, 256), 256)] = term.astype(BF).reshape(
                4, 64, 256
            )
            return carry

        lax.fori_loop(0, 8, body, 0)

    part_two = n_two

    def feed_out(g):
        def body(shard, carry):
            term = dotg(hid[rows_of[g], :], w_down[shard], 1, 0)
            part_two[g, :, :, pl.ds(pl.multiple_of(shard * 256, 256), 256)] = term.astype(
                BF
            ).reshape(4, 64, 256)
            return carry

        lax.fori_loop(0, 8, body, 0)

    def line_sum(slot, part_ref, outer, inner):
        return LineSum(me, part_ref, outer, inner, sum_send.at[slot], sum_recv.at[slot])

    sum_two = [line_sum(g, part.at[g], outer_in.at[g], inner_in.at[g]) for g in range(2)]
    sum_one = [line_sum(2 + g, part.at[g], outer_in.at[g], inner_in.at[g]) for g in range(2)]

    sum_out = [
        line_sum(4 + g, part_two.at[g], outer_two.at[g], inner_two.at[g]) for g in range(2)
    ]
    spread_mid = [LineGather(me, mlow.at[g], all_send.at[g], all_recv.at[g]) for g in range(2)]
    spread_in = [LineGather(me, o_input.at[g], all_send.at[2 + g], all_recv.at[2 + g]) for g in range(2)]
    spread_out = [LineGather(me, o_result.at[g], all_send.at[4 + g], all_recv.at[4 + g]) for g in range(2)]

    def middle_back(g):
        sum_two[g].finish(total)
        own = pl.ds(pl.multiple_of(g * 256 + me.z * 64, 64), 64)
        back, gain_grad = norm_back(total[...], mid[g], gain_two)
        if g == 0:
            vec[1:2, :] = gain_grad
        else:
            vec[1:2, :] += gain_grad
        grad = cot[own, :].astype(F32) + back
        mid_g[g] = grad
        mlow[g, me.z] = grad.astype(BF)
        spread_mid[g].begin()

    def put_own(g, ref, slot):
        copy = pltpu.make_async_copy(own_out.at[slot], ref.at[g, me.z], own_sem.at[slot])
        copy.start()
        copy.wait()

    def input_back(g):
        sum_one[g].finish(total)
        back, gain_grad = norm_back(total[...], tok_own[g].astype(F32), gain_one)
        if g == 0:
            vec[0:1, :] = gain_grad
        else:
            vec[0:1, :] += gain_grad
        own_out[0] = (mid_g[g] + back).astype(BF)
        put_own(g, o_input, 0)
        spread_in[g].begin()

    def result_rows(g):
        sum_out[g].finish(total)
        own_out[1] = (mid[g] + total[...]).astype(BF)
        put_own(g, o_result, 1)
        spread_out[g].begin()

    wide = lambda ref: (lambda shard: ref[:, pl.ds(pl.multiple_of(shard * 256, 256), 256)])

    def blocks_of(ref):
        return lambda shard: ref[
            :, :, :, pl.ds(pl.multiple_of(shard * 256, 256), 256)
        ].reshape(512, 256)

    spare = w_down
    one_rows = pl.ds(0, 512)

    def one_loads():
        return [
            pltpu.make_async_copy(
                n_one_h.at[:, pl.ds(shard * 256, 256)],
                spare.at[shard, one_rows, :],
                tile_sem.at[0, shard % 6] if shard < 6 else tile_sem.at[1, shard % 6],
            )
            for shard in range(8)
        ]

    stage = w_up.at[pl.ds(4, 2)]
    landing = w_up.at[pl.ds(6, 2)]

    def scatter(index, width, x_of, y_of, chips, near):
        refs = (stage, core_in, diag_in.at[index], near, rs_send, rs_recv, credit)
        return Scatter(me, index, index == 4, width, x_of, y_of, chips, refs)

    rs_down = scatter(
        0, hidden, wide(cot), lambda: hid[...], lambda role: w_gate.at[4 + role], near_down
    )
    rs_gate = scatter(
        1, hidden, blocks_of(n_two), lambda: gate_g[...], lambda role: w_gate.at[role], near_gate
    )
    rs_up = scatter(
        2, hidden, blocks_of(n_two), lambda: up_g[...], lambda role: w_up.at[role], near_up
    )
    rs_out = scatter(3, 512, blocks_of(mlow), lambda: att[...], lambda role: chip_out.at[role], near_out)
    rs_qkv = scatter(
        4,
        640,
        lambda shard: spare[shard, one_rows, :],
        lambda: d_qkv[...],
        lambda role: chip_qkv.at[role],
        near_qkv,
    )

    def finish_rows(job, outs):
        job.collected(landing, fin_sem)
        width = job.width
        pending = [None, None]
        for step in range(4):
            slot = step % 2
            rows = slice(step * 64, (step + 1) * 64)
            if pending[slot] is not None:
                for piece in pending[slot]:
                    piece.wait()
            sum_stage[slot, :, :width] = (
                job.chips(0)[rows, :].astype(F32)
                + landing[0, rows, :width].astype(F32)
                + landing[1, rows, :width].astype(F32)
            )
            pending[slot] = [
                pltpu.make_async_copy(
                    sum_stage.at[slot, :, pl.ds(first, size)],
                    ref.at[pl.ds(step * 64, 64), :],
                    put_sem.at[slot, number],
                )
                for number, (ref, first, size) in enumerate(outs)
            ]
            for piece in pending[slot]:
                piece.start()
        for slot in range(2):
            for piece in pending[slot]:
                piece.wait()

    def finish_turned(job, ref):
        job.collected(landing, fin_sem)
        pending = [None, None]
        for step in range(job.width // 128):
            slot = step % 2
            lanes = slice(step * 128, (step + 1) * 128)
            if pending[slot] is not None:
                pending[slot].wait()
            turn_stage[slot] = jnp.transpose(
                job.chips(0)[:, lanes].astype(F32)
                + landing[0, :, lanes].astype(F32)
                + landing[1, :, lanes].astype(F32)
            )
            pending[slot] = pltpu.make_async_copy(
                turn_stage.at[slot], ref.at[pl.ds(step * 128, 128), :], put_sem.at[slot, 0]
            )
            pending[slot].start()
        for piece in pending:
            piece.wait()

    lane_pair = lax.broadcasted_iota(jnp.int32, (256, 128), 1)

    def out_back(g):
        grad = None
        for shard in range(8):
            lanes = slice(shard * 256, (shard + 1) * 256)
            term = dotg(mlow[g, :, :, lanes].reshape(256, 256), w_out[shard], 1, 1)
            grad = term if grad is None else grad + term
        grad = grad.astype(BF)
        for pair in range(4):
            own = grad[:, pair * 128 : (pair + 1) * 128]
            zero = jnp.zeros_like(own)
            do_heads[2 * pair] = jnp.where(lane_pair < HD, own, zero)
            do_heads[2 * pair + 1] = jnp.where(lane_pair >= HD, own, zero)
        for source in range(4):
            pairs = kv[source, rows_of[g], :].astype(F32)
            turned = pltpu.roll(pairs, HD, 1)
            rows = slice(source * 256, (source + 1) * 256)
            keys[rows, :] = jnp.where(lane_pair < HD, pairs, turned).astype(BF)
            vals[rows, :] = jnp.where(lane_pair < HD, turned, pairs).astype(BF)
            keys_t[:, rows] = jnp.transpose(pairs)[:HD, :].astype(BF)
        key_acc[...] = jnp.zeros_like(key_acc)
        val_acc[...] = jnp.zeros_like(val_acc)

    def attend_back(g, start, stop):
        def body(pair, carry):
            halves = []
            for odd in range(2):
                head = 2 * pair + odd
                query, grad = q_heads[g * 8 + head], do_heads[head]
                scores = dotg(keys[...], query, 1, 1) + bias[g].astype(F32)
                probs = jnp.exp(scores - lse[g * 8 + head])
                prob_grad = dotg(vals[...], grad, 1, 1)
                delta = jnp.sum(probs * prob_grad, axis=0, keepdims=True)
                score_grad = (probs * (prob_grad - delta)).astype(BF)
                val_acc[...] += dotg(probs.astype(BF), grad, 1, 0)
                key_acc[...] += dotg(score_grad, query, 1, 0)
                halves.append(dotg(keys_t[...], score_grad, 1, 0))
            rows = jnp.transpose(jnp.concatenate(halves, axis=0)) * (HD ** (-0.5))
            rows = rows * rope[rows_of[g], :128] - swap_halves(rows) * rope[rows_of[g], 128:]
            d_qkv[rows_of[g], pl.ds(pl.multiple_of(pair * 128, 128), 128)] = rows.astype(BF)
            return carry

        lax.fori_loop(start, stop, body, 0)

    def kv_copies(g):
        return [
            remote(
                kv_send_buf.at[g, column],
                kv_in.at[g, slot],
                kv_send.at[g, slot],
                kv_recv.at[g, slot],
                group[slot],
            )
            for slot, column in enumerate((me.cx, me.cy, me.cd))
        ]

    def kv_begin(g):
        for block in range(4):
            rows = slice(block * 256, (block + 1) * 256)
            key_rows, val_rows = key_acc[rows, :], val_acc[rows, :]
            joined = jnp.where(
                lane_pair < HD,
                key_rows + pltpu.roll(key_rows, HD, 1),
                val_rows + pltpu.roll(val_rows, HD, 1),
            )
            kv_send_buf[g, block] = joined.astype(BF)
        for piece in kv_copies(g):
            piece.start()

    def kv_finish(g):
        rows = kv_send_buf[g, me.c].astype(F32)
        for slot, piece in enumerate(kv_copies(g)):
            piece.wait_recv()
            rows = rows + kv_in[g, slot].astype(F32)
        cos_rows = jnp.where(lane_pair < HD, rope[rows_of[g], :128], 1.0)
        sin_rows = jnp.where(lane_pair < HD, rope[rows_of[g], 128:], 0.0)
        rows = rows * cos_rows - swap_halves(rows) * sin_rows
        d_qkv[rows_of[g], 512:640] = rows.astype(BF)

    def project_back_rows(g):
        def body(shard, carry):
            term = dotg(d_qkv[rows_of[g], :], w_qkv[shard], 1, 1)
            part[g, :, :, pl.ds(pl.multiple_of(shard * 256, 256), 256)] = term.astype(BF).reshape(
                4, 64, 256
            )
            return carry

        lax.fori_loop(0, 8, body, 0)

    line = column_devices(me)

    def vec_line():
        return [
            remote(vec_out, vec_in.at[slot], vec_send.at[slot], vec_recv.at[slot], device)
            for slot, device in enumerate(line)
        ]

    targets = [me.sx, me.sy, me.sd, me.of * 4 + me.c, me.of * 4 + me.cx, me.of * 4 + me.cy, me.of * 4 + me.cd]

    def vec_group():
        return [
            remote(
                vec_in.at[3, target],
                vec_near.at[slot],
                vec_send.at[3 + slot],
                vec_recv.at[3 + slot],
                device,
            )
            for slot, (target, device) in enumerate(zip(targets, group))
        ]

    def vec_begin():
        for shard in range(8):
            for which in range(2):
                for half in range(2):
                    first = shard * 256 + half * 128
                    vec_out[shard, 2 * which + half : 2 * which + half + 1, :] = vec[
                        which : which + 1, first : first + 128
                    ]
            vec_out[shard, 4:8, :] = jnp.zeros((4, 128), F32)
        for piece in vec_line():
            piece.start()

    def vec_middle():
        for piece in vec_line():
            piece.wait_recv()
        vec_in[3] = vec_out[...] + vec_in[0] + vec_in[1] + vec_in[2]
        for piece in vec_group():
            piece.start()

    def vec_finish():
        rows = vec_in[3, me.own]
        for slot, piece in enumerate(vec_group()):
            piece.wait_recv()
            rows = rows + vec_near[slot]
        o_gains[...] = rows

    loads["two", 0].wait()
    loads["cot", 0].wait()
    feed(0, 0, full_tiles + 1)
    feed_back(0)
    sum_two[0].begin()
    loads["two", 1].wait()
    loads["cot", 1].wait()
    feed(1, 0, 3)
    sum_two[0].step_one()
    feed(1, 3, full_tiles + 1)
    sum_two[0].step_two()
    feed_back(1)
    sum_two[1].begin()
    rs_down.partner()
    rs_down.own()
    loads["mid"].wait()
    middle_back(0)
    sum_two[1].step_one()
    spread_mid[0].step_one()
    rs_gate.partner()
    rs_gate.own()
    sum_two[1].step_two()
    spread_mid[0].step_two()
    rs_up.partner()
    rs_up.own()
    rs_down.relay()
    middle_back(1)
    feed_out(0)
    sum_out[0].begin()
    for name in ("out", "heads", "bias", "kv", "att", "rope", "qkv", ("tok", 0), ("tok", 1)):
        loads[name].wait()
    spread_mid[0].finish()
    out_back(0)
    rs_gate.relay()
    spread_mid[1].step_one()
    attend_back(0, 0, 2)
    spread_mid[1].step_two()
    attend_back(0, 2, 4)
    kv_begin(0)
    rs_up.relay()
    feed_out(1)
    for piece in one_loads():
        piece.start()
    sum_out[0].step_one()
    spread_mid[1].finish()
    out_back(1)
    rs_out.partner()
    rs_out.own()
    kv_finish(0)
    project_back_rows(0)
    sum_one[0].begin()
    attend_back(1, 0, 2)
    sum_one[0].step_one()
    sum_out[0].step_two()
    attend_back(1, 2, 4)
    kv_begin(1)
    sum_one[0].step_two()
    result_rows(0)
    rs_out.relay()
    kv_finish(1)
    project_back_rows(1)
    sum_one[1].begin()
    input_back(0)
    for piece in one_loads():
        piece.wait()
    rs_qkv.partner()
    rs_qkv.own()
    sum_out[1].begin()
    sum_one[1].step_one()
    spread_in[0].step_one()
    spread_out[0].step_one()
    rs_down.collect(landing, fin_sem)
    finish_turned(rs_down, o_down)
    rs_gate.collect(landing, fin_sem)
    sum_one[1].step_two()
    spread_in[0].step_two()
    spread_out[0].step_two()
    sum_out[1].step_one()
    rs_qkv.relay()
    finish_rows(rs_gate, [(o_gate, 0, hidden)])
    input_back(1)
    vec_begin()
    rs_up.collect(landing, fin_sem)
    sum_out[1].step_two()
    spread_in[1].step_one()
    finish_rows(rs_up, [(o_up, 0, hidden)])
    vec_middle()
    result_rows(1)
    spread_in[1].step_two()
    rs_out.collect(landing, fin_sem)
    finish_turned(rs_out, o_out)
    rs_qkv.collect(landing, fin_sem)
    spread_out[1].step_one()
    finish_rows(rs_qkv, [(o_query, 0, 512), (o_kv, 512, 128)])
    vec_finish()
    spread_out[1].step_two()
    for spread in spread_in + spread_out:
        spread.finish()
    for job in (rs_down, rs_gate, rs_up, rs_out, rs_qkv):
        job.settle()
    for g in range(2):
        for piece in kv_copies(g):
            piece.wait_send()
    for piece in vec_line() + vec_group():
        piece.wait_send()


def run_backward(
    cotangent, tokens, f_qkv, f_out, f_gate, f_up, f_down, f_gains, n_one, q_heads, kv_all, bias,
    lse, att_low, middle, n_two, rope_q,
):
    shape = jax.ShapeDtypeStruct
    width = tokens.shape[1]
    hidden = f_gate.shape[2]
    vmem = pl.BlockSpec(memory_space=pltpu.VMEM)
    anywhere = pl.BlockSpec(memory_space=pl.ANY)
    dma = pltpu.SemaphoreType.DMA
    buffer = pltpu.VMEM
    return pl.pallas_call(
        backward_kernel,
        name="backward_part",
        out_shape=(
            shape((2, 4, 64, width), BF),
            shape((2, 4, 64, width), BF),
            shape((8, 128), F32),
            shape((256, 512), F32),
            shape((256, 128), F32),
            shape((512, 256), F32),
            shape((256, hidden), F32),
            shape((256, hidden), F32),
            shape((hidden, 256), F32),
            shape((2, 256, hidden), BF),
            shape((2, 256, hidden), BF),
            shape((2, 256, hidden), BF),
            shape((2, 256, 512), BF),
            shape((2, 256, 640), BF),
        ),
        in_specs=[anywhere] * 7 + [vmem] + [anywhere] * 4 + [vmem] + [anywhere] * 4,
        out_specs=(anywhere,) * 2 + (vmem,) + (anywhere,) * 11,
        scratch_shapes=[
            buffer((8, 256, hidden), BF),
            buffer((8, 256, hidden), BF),
            buffer((8, hidden, 256), BF),
            buffer((8, 512, 256), BF),
            buffer((8, 256, 640), BF),
            buffer((512, width), BF),
            buffer((2, 4, 64, width), BF),
            buffer((512, hidden), BF),
            buffer((512, hidden), BF),
            buffer((512, hidden), BF),
            buffer((4, 256, hidden), BF),
            buffer((5, 2, 128, hidden), BF),
            buffer((4, 256, 512), BF),
            buffer((4, 256, 640), BF),
            buffer((2, 64, hidden), F32),
            buffer((2, 128, 256), F32),
            buffer((2, 4, 64, width), BF),
            buffer((2, 3, 64, width), BF),
            buffer((2, 2, 64, width), BF),
            buffer((2, 3, 64, width), BF),
            buffer((2, 2, 64, width), BF),
            buffer((2, 4, 64, width), BF),
            buffer((64, width), F32),
            buffer((2, 64, width), BF),
            buffer((2, 64, width), F32),
            buffer((2, 64, width), F32),
            buffer((2, 64, width), BF),
            buffer((16, 256, 128), BF),
            buffer((2, 1024, 256), BF),
            buffer((4, 512, 128), BF),
            buffer((512, 512), BF),
            buffer((512, 256), F32),
            buffer((8, 256, 128), BF),
            buffer((1024, 128), BF),
            buffer((1024, 128), BF),
            buffer((HD, 1024), BF),
            buffer((1024, 128), F32),
            buffer((1024, 128), F32),
            buffer((2, 4, 256, 128), BF),
            buffer((2, 3, 256, 128), BF),
            buffer((512, 640), BF),
            buffer((2, width), F32),
            buffer((4, 8, 8, 128), F32),
            buffer((8, 8, 128), F32),
            buffer((7, 8, 128), F32),
            dma((3, 6)),
            dma((14,)),
            dma((6, 3)),
            dma((6, 5)),
            dma((6, 5)),
            dma((6, 4)),
            dma((5, 10)),
            dma((5, 10)),
            pltpu.SemaphoreType.REGULAR((4,)),
            dma((2, 3)),
            dma((2, 3)),
            dma((10,)),
            dma((10,)),
            dma((2,)),
            dma((2, 2)),
            dma((2,)),
        ],
        compiler_params=pltpu.CompilerParams(
            collective_id=1, has_side_effects=True, vmem_limit_bytes=67043328
        ),
    )(
        cotangent, tokens, f_qkv, f_out, f_gate, f_up, f_down, f_gains, n_one, q_heads, kv_all,
        bias, lse, att_low, middle, n_two, rope_q,
    )


def fast_shards(
    tokens,
    attn_gain,
    w_query,
    w_key,
    w_value,
    w_out,
    mlp_gain,
    w_gate,
    w_up,
    w_down,
    cotangent,
    positions,
    segments,
):
    w_qkv, gains, marks, rope_q, rope_k = prepared(
        tokens, attn_gain, w_query, w_key, w_value, mlp_gain, positions, segments
    )
    (
        f_qkv, f_out, f_gate, f_up, f_down, f_gains, n_one, q_heads, kv_all, bias, lse, att_low,
        middle, n_two,
    ) = run_forward(tokens, w_qkv, w_out, w_gate, w_up, w_down, gains, marks, rope_q, rope_k)
    (result, input_grad, gain_grads, query_g, kv_g, out_g, gate_g, up_g, down_g, *_) = run_backward(
        cotangent, tokens, f_qkv, f_out, f_gate, f_up, f_down, f_gains, n_one, q_heads, kv_all, bias,
        lse, att_low, middle, n_two, rope_q,
    )
    return (
        result.reshape(tokens.shape),
        input_grad.reshape(tokens.shape),
        gain_grads[0:2].reshape(-1),
        query_g,
        kv_g[:, :HD],
        kv_g[:, HD:],
        out_g,
        gain_grads[2:4].reshape(-1),
        gate_g,
        up_g,
        down_g,
    )


def solution(mesh):
    in_specs = (
        P(("fsdp", "ctx"), None),
        P(("fsdp", "ctx")),
        P(("fsdp", "ctx"), "tp"),
        P(("fsdp", "ctx"), "tp"),
        P(("fsdp", "ctx"), "tp"),
        P("tp", ("fsdp", "ctx")),
        P(("fsdp", "ctx")),
        P(("fsdp", "ctx"), "tp"),
        P(("fsdp", "ctx"), "tp"),
        P("tp", ("fsdp", "ctx")),
        P(("fsdp", "ctx"), None),
        P(("fsdp", "ctx")),
        P(("fsdp", "ctx")),
    )
    out_specs = (
        P(("fsdp", "ctx"), None),
        P(("fsdp", "ctx"), None),
        P(("fsdp", "ctx")),
        P(("fsdp", "ctx"), "tp"),
        P(("fsdp", "ctx"), "tp"),
        P(("fsdp", "ctx"), "tp"),
        P("tp", ("fsdp", "ctx")),
        P(("fsdp", "ctx")),
        P(("fsdp", "ctx"), "tp"),
        P(("fsdp", "ctx"), "tp"),
        P("tp", ("fsdp", "ctx")),
    )
    small = (mesh.shape["fsdp"], mesh.shape["ctx"], mesh.shape["tp"]) == (2, 4, 4)
    return jax.shard_map(fast_shards if small else shards, mesh=mesh, in_specs=in_specs, out_specs=out_specs, check_vma=False)
```

```python
import jax
import jax.numpy as jnp
from jax import lax
from jax.experimental import pallas as pl
from jax.experimental.pallas import tpu as pltpu
from jax.sharding import PartitionSpec as P

H = 32
KVH = 4
HD = 64


EPSILON = 1e-05
THETA_BASE = 10000.0
MASKED_SCORE = -1e30


def shifted(value, axis, steps):
    count = lax.axis_size(axis)
    pairs = [(source, (source + steps) % count) for source in range(count)]
    return lax.ppermute(value, axis, pairs)


def rope_tables(token_pos, half_size):
    frequency = THETA_BASE ** (-jnp.arange(half_size, dtype=jnp.float32) / half_size)
    angles = token_pos.astype(jnp.float32)[:, None] * frequency[None, :]
    return (jnp.cos(angles), jnp.sin(angles))


def rotate(head_rows, cosine, sine):
    half_size = head_rows.shape[-1] // 2
    first_half = head_rows[..., :half_size]
    second_half = head_rows[..., half_size:]
    cos_rows = cosine[:, None, :]
    sin_rows = sine[:, None, :]
    return jnp.concatenate(
        [
            first_half * cos_rows - second_half * sin_rows,
            second_half * cos_rows + first_half * sin_rows,
        ],
        axis=-1,
    )


def rotate_back(head_rows, cosine, sine):
    half_size = head_rows.shape[-1] // 2
    first_half = head_rows[..., :half_size]
    second_half = head_rows[..., half_size:]
    cos_rows = cosine[:, None, :]
    sin_rows = sine[:, None, :]
    return jnp.concatenate(
        [
            first_half * cos_rows + second_half * sin_rows,
            second_half * cos_rows - first_half * sin_rows,
        ],
        axis=-1,
    )


def project(left_side, right_side):
    return jnp.dot(left_side, right_side, preferred_element_type=jnp.float32)


def project_back(left_side, right_side):
    return lax.dot_general(
        left_side, right_side, (((1,), (1,)), ((), ())), preferred_element_type=jnp.float32
    )


def weight_grad(left_side, right_side):
    return lax.dot_general(
        left_side, right_side, (((0,), (0,)), ((), ())), preferred_element_type=jnp.float32
    )


def rms_norm(rows_in, gain_vec):
    inv_rms = lax.rsqrt(jnp.mean(rows_in * rows_in, axis=-1, keepdims=True) + EPSILON)
    unit_rows = rows_in * inv_rms
    return (unit_rows * gain_vec, unit_rows, inv_rms)


def rms_norm_back(gradient, gain_vec, unit_rows, inv_rms):
    gain_grad = jnp.sum(gradient * unit_rows, axis=0)
    scaled_grad = gradient * gain_vec
    return (
        inv_rms
        * (scaled_grad - unit_rows * jnp.mean(scaled_grad * unit_rows, axis=-1, keepdims=True)),
        gain_grad,
    )


def pair_mask(query_pos, query_seg, key_pos, key_seg):
    return (query_seg[:, None] == key_seg[None, :]) & (key_pos[None, :] <= query_pos[:, None])


def split_block(kv_block, kv_heads):
    key_rows = kv_block[:, : kv_heads * HD].reshape(-1, kv_heads, HD)
    value_rows = kv_block[:, kv_heads * HD :].reshape(-1, kv_heads, HD)
    return (key_rows, value_rows)


def attend_block(state_in, queries, kv_block, visible):
    row_top, row_total, output_sum = state_in
    key_rows, value_rows = split_block(kv_block, queries.shape[1])
    scores = jnp.einsum(
        "qkgd,pkd->kgqp", queries, key_rows, preferred_element_type=jnp.float32
    ) * HD ** (-0.5)
    scores = jnp.where(visible, scores, MASKED_SCORE)
    new_top = jnp.maximum(row_top, jnp.max(scores, axis=-1))
    weights = jnp.where(visible, jnp.exp(scores - new_top[..., None]), 0.0)
    decay_factor = jnp.exp(row_top - new_top)
    row_total = row_total * decay_factor + jnp.sum(weights, axis=-1)
    mixed_heads = jnp.einsum(
        "kgqp,pkd->qkgd",
        weights.astype(jnp.bfloat16),
        value_rows,
        preferred_element_type=jnp.float32,
    )
    output_sum = output_sum * jnp.transpose(decay_factor, (2, 0, 1))[..., None] + mixed_heads
    return (new_top, row_total, output_sum)


def block_grads(queries, out_grad, kv_block, visible, log_total, delta_rows):
    key_rows, value_rows = split_block(kv_block, queries.shape[1])
    scale_factor = HD ** (-0.5)
    scores = (
        jnp.einsum("qkgd,pkd->kgqp", queries, key_rows, preferred_element_type=jnp.float32)
        * scale_factor
    )
    probs_full = jnp.where(
        visible, jnp.exp(jnp.where(visible, scores, MASKED_SCORE) - log_total[..., None]), 0.0
    )
    value_grad = jnp.einsum(
        "kgqp,qkgd->pkd",
        probs_full.astype(jnp.bfloat16),
        out_grad,
        preferred_element_type=jnp.float32,
    )
    prob_grad = jnp.einsum(
        "qkgd,pkd->kgqp", out_grad, value_rows, preferred_element_type=jnp.float32
    )
    score_grad = (probs_full * (prob_grad - delta_rows[..., None])).astype(jnp.bfloat16)
    query_grad = (
        jnp.einsum("kgqp,pkd->qkgd", score_grad, key_rows, preferred_element_type=jnp.float32)
        * scale_factor
    )
    key_grad = (
        jnp.einsum("kgqp,qkgd->pkd", score_grad, queries, preferred_element_type=jnp.float32)
        * scale_factor
    )
    block_rows = kv_block.shape[0]
    return (
        query_grad,
        jnp.concatenate(
            [key_grad.reshape(block_rows, -1), value_grad.reshape(block_rows, -1)], axis=-1
        ),
    )


def shards(
    tokens,
    attn_gain,
    w_query,
    w_key,
    w_value,
    w_out,
    mlp_gain,
    w_gate,
    w_up,
    w_down,
    cotangent,
    positions,
    segments,
):
    token_rows = tokens.shape[0]
    gain_one, query_w, key_w, value_w, out_w = (
        lax.all_gather(attn_gain, ("fsdp", "ctx"), axis=0, tiled=True),
        lax.all_gather(w_query, ("fsdp", "ctx"), axis=0, tiled=True),
        lax.all_gather(w_key, ("fsdp", "ctx"), axis=0, tiled=True),
        lax.all_gather(w_value, ("fsdp", "ctx"), axis=0, tiled=True),
        lax.all_gather(w_out, ("fsdp", "ctx"), axis=1, tiled=True),
    )
    gain_two, gate_w, up_w, down_w = (
        lax.all_gather(mlp_gain, ("fsdp", "ctx"), axis=0, tiled=True),
        lax.all_gather(w_gate, ("fsdp", "ctx"), axis=0, tiled=True),
        lax.all_gather(w_up, ("fsdp", "ctx"), axis=0, tiled=True),
        lax.all_gather(w_down, ("fsdp", "ctx"), axis=1, tiled=True),
    )
    head_count = query_w.shape[1] // HD
    kv_heads = key_w.shape[1] // HD
    groups = H // KVH
    cosine, sine = rope_tables(positions, HD // 2)
    token_float = tokens.astype(jnp.float32)
    gain_one_float = gain_one.astype(jnp.float32)
    normed_one, unit_one, inv_one = rms_norm(token_float, gain_one_float)
    normed_low = normed_one.astype(jnp.bfloat16)
    query_lin = project(normed_low, query_w)
    key_lin = project(normed_low, key_w)
    value_low = project(normed_low, value_w).astype(jnp.bfloat16)
    query_rot = rotate(query_lin.reshape(token_rows, head_count, HD), cosine, sine).astype(
        jnp.bfloat16
    )
    key_rot = rotate(key_lin.reshape(token_rows, kv_heads, HD), cosine, sine).astype(jnp.bfloat16)
    queries = query_rot.reshape(token_rows, kv_heads, groups, HD)
    kv_local = jnp.concatenate([key_rot.reshape(token_rows, kv_heads * HD), value_low], axis=-1)
    key_positions, key_segments = (
        lax.all_gather(positions, "ctx", axis=0, tiled=True),
        lax.all_gather(segments, "ctx", axis=0, tiled=True),
    )
    my_index = lax.axis_index("ctx")
    cycle_size = lax.axis_size("ctx")

    def block_marks(source):
        start_row = source * token_rows
        return pair_mask(
            positions,
            segments,
            lax.dynamic_slice_in_dim(key_positions, start_row, token_rows),
            lax.dynamic_slice_in_dim(key_segments, start_row, token_rows),
        )

    start_state = (
        jnp.full((kv_heads, groups, token_rows), MASKED_SCORE, jnp.float32),
        jnp.zeros((kv_heads, groups, token_rows), jnp.float32),
        jnp.zeros((token_rows, kv_heads, groups, HD), jnp.float32),
    )

    def forward_block(state_in, kv_block, source):
        visible = block_marks(source)
        return attend_block(state_in, queries, kv_block, visible)

    def cycle_step(state_in, step_index):
        attn_state, kv_block = state_in
        attn_state = forward_block(attn_state, kv_block, (my_index - step_index) % cycle_size)
        passed = shifted(kv_block, "ctx", 1)
        return ((attn_state, passed), kv_block)

    (attn_state, last_block), kept_blocks = lax.scan(
        cycle_step, (start_state, kv_local), jnp.arange(cycle_size - 1)
    )
    attn_state = forward_block(attn_state, last_block, (my_index + 1) % cycle_size)
    kv_blocks = jnp.concatenate([kept_blocks, last_block[None]], axis=0)
    sources = (my_index - jnp.arange(cycle_size)) % cycle_size
    row_top, row_total, output_sum = attn_state
    attended = output_sum / jnp.transpose(row_total, (2, 0, 1))[..., None]
    log_total = row_top + jnp.log(row_total)
    attended_low = attended.reshape(token_rows, head_count * HD).astype(jnp.bfloat16)
    middle = token_float + lax.psum(project(attended_low, out_w).astype(jnp.bfloat16), "tp").astype(
        jnp.float32
    )
    gain_two_float = gain_two.astype(jnp.float32)
    normed_two, unit_two, inv_two = rms_norm(middle, gain_two_float)
    normed_two_low = normed_two.astype(jnp.bfloat16)
    gate_lin = project(normed_two_low, gate_w)
    up_lin = project(normed_two_low, up_w)
    hidden_low = (jax.nn.silu(gate_lin) * up_lin).astype(jnp.bfloat16)
    result = middle + lax.psum(project(hidden_low, down_w).astype(jnp.bfloat16), "tp").astype(
        jnp.float32
    )
    output = result.astype(jnp.bfloat16)
    hidden_grad = project_back(cotangent, down_w)
    down_w_grad = weight_grad(hidden_low, cotangent)
    sigmoid_gate = jax.nn.sigmoid(gate_lin)
    gate_grad_low = (
        hidden_grad * up_lin * sigmoid_gate * (1.0 + gate_lin * (1.0 - sigmoid_gate))
    ).astype(jnp.bfloat16)
    up_grad_low = (hidden_grad * gate_lin * sigmoid_gate).astype(jnp.bfloat16)
    normed_two_grad = lax.psum(
        (project_back(gate_grad_low, gate_w) + project_back(up_grad_low, up_w)).astype(
            jnp.bfloat16
        ),
        "tp",
    ).astype(jnp.float32)
    gate_w_grad = weight_grad(normed_two_low, gate_grad_low)
    up_w_grad = weight_grad(normed_two_low, up_grad_low)
    norm_back_two, gain_two_grad = rms_norm_back(normed_two_grad, gain_two_float, unit_two, inv_two)
    middle_grad = cotangent.astype(jnp.float32) + norm_back_two
    middle_low = middle_grad.astype(jnp.bfloat16)
    attended_grad_low = project_back(middle_low, out_w).astype(jnp.bfloat16)
    out_w_grad = weight_grad(attended_low, middle_low)
    out_grad = attended_grad_low.reshape(token_rows, kv_heads, groups, HD)
    delta_rows = jnp.transpose(jnp.sum(out_grad.astype(jnp.float32) * attended, axis=-1), (1, 2, 0))

    def backward_block(kv_block, source):
        visible = block_marks(source)
        return block_grads(queries, out_grad, kv_block, visible, log_total, delta_rows)

    query_start = jnp.zeros((token_rows, kv_heads, groups, HD), jnp.float32)

    def back_step(state_in, pieces):
        query_acc, kv_acc = state_in
        query_term, kv_term = backward_block(pieces[0], pieces[1])
        passed = shifted((kv_acc + kv_term).astype(jnp.bfloat16), "ctx", 1).astype(jnp.float32)
        return ((query_acc + query_term, passed), None)

    (query_grad, kv_grad), unused = lax.scan(
        back_step, (query_start, jnp.zeros(kv_local.shape, jnp.float32)), (kv_blocks, sources)
    )
    query_grad_low = (
        rotate_back(query_grad.reshape(token_rows, head_count, HD), cosine, sine)
        .reshape(token_rows, head_count * HD)
        .astype(jnp.bfloat16)
    )
    key_grad_low = (
        rotate_back(kv_grad[:, : kv_heads * HD].reshape(token_rows, kv_heads, HD), cosine, sine)
        .reshape(token_rows, kv_heads * HD)
        .astype(jnp.bfloat16)
    )
    value_grad_low = kv_grad[:, kv_heads * HD :].astype(jnp.bfloat16)
    normed_one_grad = lax.psum(
        (
            project_back(query_grad_low, query_w)
            + project_back(key_grad_low, key_w)
            + project_back(value_grad_low, value_w)
        ).astype(jnp.bfloat16),
        "tp",
    ).astype(jnp.float32)
    query_w_grad = weight_grad(normed_low, query_grad_low)
    key_w_grad = weight_grad(normed_low, key_grad_low)
    value_w_grad = weight_grad(normed_low, value_grad_low)
    norm_back_one, gain_one_grad = rms_norm_back(normed_one_grad, gain_one_float, unit_one, inv_one)
    input_grad = (middle_grad + norm_back_one).astype(jnp.bfloat16)
    summed = (
        lax.psum_scatter(
            gain_one_grad.astype(jnp.bfloat16), ("fsdp", "ctx"), scatter_dimension=0, tiled=True
        ).astype(jnp.float32),
        lax.psum_scatter(
            query_w_grad.astype(jnp.bfloat16), ("fsdp", "ctx"), scatter_dimension=0, tiled=True
        ).astype(jnp.float32),
        lax.psum_scatter(
            key_w_grad.astype(jnp.bfloat16), ("fsdp", "ctx"), scatter_dimension=0, tiled=True
        ).astype(jnp.float32),
        lax.psum_scatter(
            value_w_grad.astype(jnp.bfloat16), ("fsdp", "ctx"), scatter_dimension=0, tiled=True
        ).astype(jnp.float32),
        lax.psum_scatter(
            out_w_grad.astype(jnp.bfloat16), ("fsdp", "ctx"), scatter_dimension=1, tiled=True
        ).astype(jnp.float32),
        lax.psum_scatter(
            gain_two_grad.astype(jnp.bfloat16), ("fsdp", "ctx"), scatter_dimension=0, tiled=True
        ).astype(jnp.float32),
        lax.psum_scatter(
            gate_w_grad.astype(jnp.bfloat16), ("fsdp", "ctx"), scatter_dimension=0, tiled=True
        ).astype(jnp.float32),
        lax.psum_scatter(
            up_w_grad.astype(jnp.bfloat16), ("fsdp", "ctx"), scatter_dimension=0, tiled=True
        ).astype(jnp.float32),
        lax.psum_scatter(
            down_w_grad.astype(jnp.bfloat16), ("fsdp", "ctx"), scatter_dimension=1, tiled=True
        ).astype(jnp.float32),
    )
    return (output, input_grad) + tuple(summed)


MESH = pl.DeviceIdType.MESH
BF = jnp.bfloat16
F32 = jnp.float32


def dotg(left_side, right_side, left_dim, right_dim):
    return lax.dot_general(
        left_side,
        right_side,
        (((left_dim,), (right_dim,)), ((), ())),
        preferred_element_type=F32,
    )


def remote(src, dst, send_sem, recv_sem, device):
    return pltpu.make_async_remote_copy(
        src_ref=src,
        dst_ref=dst,
        send_sem=send_sem,
        recv_sem=recv_sem,
        device_id=device,
        device_id_type=MESH,
    )


class Place:
    def __init__(self):
        self.f = lax.axis_index("fsdp")
        self.c = lax.axis_index("ctx")
        self.z = lax.axis_index("tp")
        self.cx = self.c + 1 - 2 * lax.rem(self.c, 2)
        self.cy = lax.rem(self.c + 2, 4)
        self.cd = 3 - self.c
        self.of = 1 - self.f
        self.own = self.f * 4 + self.c
        self.sx = self.f * 4 + self.cx
        self.sy = self.f * 4 + self.cy
        self.sd = self.f * 4 + self.cd

    def at(self, f=None, c=None, z=None):
        return (
            self.f if f is None else f,
            self.c if c is None else c,
            self.z if z is None else z,
        )


def greet(devices):
    barrier = pltpu.get_barrier_semaphore()
    for device in devices:
        pl.semaphore_signal(barrier, inc=1, device_id=device, device_id_type=MESH)
    pl.semaphore_wait(barrier, len(devices))


def group_devices(me):
    return [
        me.at(c=me.cx),
        me.at(c=me.cy),
        me.at(c=me.cd),
        me.at(f=me.of),
        me.at(f=me.of, c=me.cx),
        me.at(f=me.of, c=me.cy),
        me.at(f=me.of, c=me.cd),
    ]


def column_devices(me):
    return [me.at(z=lax.rem(me.z + step, 4)) for step in (1, 2, 3)]


class Gather:
    def __init__(self, me, index, own, full, send, recv, local_sem):
        self.me, self.own_ref, self.full = me, own, full
        rows = full.shape[1]
        self.half_a = pl.ds(0, rows // 2)
        self.half_b = pl.ds(rows // 2, rows // 2)

        def copy(slot, src, dst, device):
            return remote(src, dst, send.at[index, slot], recv.at[index, slot], device)

        slot_own, slot_x, slot_y = full.at[me.own], full.at[me.sx], full.at[me.sy]
        to_x, to_y, to_core = me.at(c=me.cx), me.at(c=me.cy), me.at(f=me.of)
        diag_a = full.at[me.sd, self.half_a]
        diag_b = full.at[me.sd, self.half_b]
        self.own_x = copy(0, own, slot_own, to_x)
        self.own_y = copy(1, own, slot_own, to_y)
        self.own_core = copy(2, own, slot_own, to_core)
        self.pass_x = copy(3, full.at[me.sy, self.half_a], full.at[me.sy, self.half_a], to_x)
        self.pass_y = copy(4, full.at[me.sx, self.half_b], full.at[me.sx, self.half_b], to_y)
        self.core_x = copy(5, slot_x, slot_x, to_core)
        self.core_y = copy(6, slot_y, slot_y, to_core)
        self.core_a = copy(7, diag_a, diag_a, to_core)
        self.core_b = copy(8, diag_b, diag_b, to_core)
        other = me.of * 4
        into = lambda slot, ref, device: copy(slot, ref, ref, device)
        self.in_x = into(0, slot_x, to_x)
        self.in_y = into(1, slot_y, to_y)
        self.in_a = into(3, diag_a, to_x)
        self.in_b = into(4, diag_b, to_y)
        self.in_core = [
            into(2, full.at[other + me.c], to_core),
            into(5, full.at[other + me.cx], to_core),
            into(6, full.at[other + me.cy], to_core),
            into(7, full.at[other + me.cd, self.half_a], to_core),
            into(8, full.at[other + me.cd, self.half_b], to_core),
        ]
        self.keep = pltpu.make_async_copy(own, slot_own, local_sem.at[index])

    def begin(self):
        self.own_x.start()
        self.own_y.start()
        self.own_core.start()
        self.keep.start()

    def forward(self):
        self.in_y.wait_recv()
        self.pass_x.start()
        self.core_y.start()
        self.in_x.wait_recv()
        self.pass_y.start()
        self.core_x.start()

    def diagonal(self):
        self.in_a.wait_recv()
        self.core_a.start()
        self.in_b.wait_recv()
        self.core_b.start()

    def arrive(self):
        self.keep.wait()
        for piece in self.in_core:
            piece.wait_recv()

    def settle(self):
        for piece in (
            self.own_x,
            self.own_y,
            self.own_core,
            self.pass_x,
            self.pass_y,
            self.core_x,
            self.core_y,
            self.core_a,
            self.core_b,
        ):
            piece.wait_send()


class LineSum:
    def __init__(self, me, part, outer_in, inner_in, send, recv):
        self.me, self.part = me, part
        self.outer_in, self.inner_in = outer_in, inner_in
        self.send, self.recv = send, recv
        z = me.z
        self.is_mid = (z == 1) | (z == 2)
        self.is_end = (z == 0) | (z == 3)
        self.mid_of_end = 1 + z // 3
        self.outer_of_mid = 3 * (z - 1)

    def end_copies(self):
        me, part = self.me, self.part
        mid = self.mid_of_end
        to_mid = me.at(z=mid)
        owners = (3 - me.z, 3 - mid, mid)
        return [
            remote(
                part.at[owner],
                self.outer_in.at[slot],
                self.send.at[slot],
                self.recv.at[slot],
                to_mid,
            )
            for slot, owner in enumerate(owners)
        ]

    def mid_copies(self):
        me, part = self.me, self.part
        far_mid, outer = 3 - me.z, self.outer_of_mid
        far = 3 - outer
        to_mid, to_outer = me.at(z=far_mid), me.at(z=outer)
        return [
            remote(part.at[far], self.inner_in.at[0], self.send.at[0], self.recv.at[3], to_mid),
            remote(part.at[far_mid], self.inner_in.at[1], self.send.at[1], self.recv.at[4], to_mid),
            remote(part.at[outer], self.inner_in.at[0], self.send.at[2], self.recv.at[3], to_outer),
        ]

    def wait_in(self, slot, buffer):
        remote(buffer, buffer, self.send.at[0], self.recv.at[slot], self.me.at(z=3 - self.me.z)).wait_recv()

    def add(self, owner, buffer):
        self.part[owner] = (self.part[owner].astype(F32) + buffer[...].astype(F32)).astype(BF)

    def begin(self):
        @pl.when(self.is_end)
        def _():
            for piece in self.end_copies():
                piece.start()

    def step_one(self):
        @pl.when(self.is_mid)
        def _():
            far = 3 - self.outer_of_mid
            self.wait_in(0, self.outer_in.at[0])
            self.add(far, self.outer_in.at[0])
            self.mid_copies()[0].start()

    def step_two(self):
        @pl.when(self.is_mid)
        def _():
            copies = self.mid_copies()
            self.wait_in(1, self.outer_in.at[1])
            self.add(3 - self.me.z, self.outer_in.at[1])
            copies[1].start()
            self.wait_in(3, self.inner_in.at[0])
            self.add(self.outer_of_mid, self.inner_in.at[0])
            copies[2].start()

    def finish(self, total):
        me = self.me

        @pl.when(self.is_mid)
        def _():
            self.wait_in(2, self.outer_in.at[2])
            self.wait_in(4, self.inner_in.at[1])
            total[...] = (
                self.part[me.z].astype(F32)
                + self.outer_in[2].astype(F32)
                + self.inner_in[1].astype(F32)
            )
            for piece in self.mid_copies():
                piece.wait_send()

        @pl.when(self.is_end)
        def _():
            self.wait_in(3, self.inner_in.at[0])
            total[...] = self.part[me.z].astype(F32) + self.inner_in[0].astype(F32)
            for piece in self.end_copies():
                piece.wait_send()


class LineGather:
    def __init__(self, me, blocks, send, recv):
        self.me, self.blocks, self.send, self.recv = me, blocks, send, recv
        z = me.z
        self.is_mid = (z == 1) | (z == 2)
        self.is_end = (z == 0) | (z == 3)
        self.mid_of_end = 1 + z // 3
        self.outer_of_mid = 3 * (z - 1)

    def copy(self, owner, slot, z):
        ref = self.blocks.at[owner]
        return remote(ref, ref, self.send.at[slot], self.recv.at[owner], self.me.at(z=z))

    def wait_in(self, owner):
        ref = self.blocks.at[owner]
        remote(ref, ref, self.send.at[0], self.recv.at[owner], self.me.at(z=3 - self.me.z)).wait_recv()

    def begin(self):
        me = self.me

        @pl.when(self.is_end)
        def _():
            self.copy(me.z, 0, self.mid_of_end).start()

        @pl.when(self.is_mid)
        def _():
            self.copy(me.z, 0, self.outer_of_mid).start()
            self.copy(me.z, 1, 3 - me.z).start()

    def step_one(self):
        me = self.me

        @pl.when(self.is_mid)
        def _():
            self.wait_in(self.outer_of_mid)
            self.copy(self.outer_of_mid, 2, 3 - me.z).start()
            self.wait_in(3 - me.z)
            self.copy(3 - me.z, 3, self.outer_of_mid).start()

    def step_two(self):
        @pl.when(self.is_mid)
        def _():
            far = 3 - self.outer_of_mid
            self.wait_in(far)
            self.copy(far, 4, self.outer_of_mid).start()

    def finish(self):
        me = self.me

        @pl.when(self.is_mid)
        def _():
            self.copy(me.z, 0, self.outer_of_mid).wait_send()
            self.copy(me.z, 1, 3 - me.z).wait_send()
            self.copy(self.outer_of_mid, 2, 3 - me.z).wait_send()
            self.copy(3 - me.z, 3, self.outer_of_mid).wait_send()
            self.copy(3 - self.outer_of_mid, 4, self.outer_of_mid).wait_send()

        @pl.when(self.is_end)
        def _():
            mid = self.mid_of_end
            self.wait_in(mid)
            self.wait_in(3 - mid)
            self.wait_in(3 - me.z)
            self.copy(me.z, 0, mid).wait_send()


def row_of(gains_ref, which):
    return jnp.concatenate([gains_ref[shard, which : which + 1, :] for shard in range(8)], axis=-1)


def swap_halves(rows):
    lane = lax.broadcasted_iota(jnp.int32, rows.shape, 1)
    return jnp.where(
        lax.rem(lane, HD) < HD // 2, pltpu.roll(rows, 96, 1), pltpu.roll(rows, 32, 1)
    )


class Scatter:
    def __init__(self, me, index, last, width, x_of, y_of, chips, refs):
        self.me, self.index, self.last, self.width = me, index, last, width
        self.x_of, self.y_of, self.chips = x_of, y_of, chips
        self.stage, self.core_in, self.diag_in, self.near_in = refs[:4]
        self.send, self.recv, self.credit = refs[4:]
        self.columns = (me.c, me.cx, me.cy, me.cd)
        self.to_x, self.to_y, self.to_core = me.at(c=me.cx), me.at(c=me.cy), me.at(f=me.of)
        self.sent = []

    def copy(self, slot, src, dst, device):
        return remote(
            src, dst, self.send.at[self.index, slot], self.recv.at[self.index, slot], device
        )

    def lanes(self, ref):
        return ref.at[:, pl.ds(0, self.width)]

    def core_copy(self, role, slot):
        return self.copy(
            role,
            self.lanes(self.stage.at[slot]),
            self.lanes(self.core_in.at[role]),
            self.to_core,
        )

    def chunk(self, shard):
        return dotg(self.x_of(shard), self.y_of(), 0, 0)

    def partner(self):
        me = self.me
        pending = [None, None]
        for step, role in enumerate((3, 1, 2, 0)):
            slot = step % 2
            value = self.chunk(me.of * 4 + self.columns[role]).astype(BF)
            if pending[slot] is not None:
                pending[slot].wait_send()
            self.lanes(self.stage.at[slot])[...] = value
            if self.index > 0:
                pl.semaphore_wait(self.credit.at[role], 1)
            pending[slot] = self.core_copy(role, slot)
            pending[slot].start()
        for piece in pending:
            piece.wait_send()

    def near(self, role, half, slot):
        rows = pl.ds(half * 128, 128)
        side = role - 1
        device = self.to_x if role == 1 else self.to_y
        return self.copy(
            slot, self.chips(role).at[rows, :], self.near_in.at[side, rows, :], device
        )

    def diag(self, half):
        device = self.to_x if half == 0 else self.to_y
        return self.copy(
            4 + half,
            self.chips(3).at[pl.ds(half * 128, 128), :],
            self.lanes(self.diag_in.at[half]),
            device,
        )

    def own(self):
        me = self.me
        for role in (3, 1, 2, 0):
            value = self.chunk(me.f * 4 + self.columns[role])
            self.core_copy(role, 0).wait_recv()
            chip = self.chips(role)
            chip[...] = (value + self.lanes(self.core_in.at[role])[...].astype(F32)).astype(BF)
            if not self.last:
                pl.semaphore_signal(
                    self.credit.at[role], inc=1, device_id=self.to_core, device_id_type=MESH
                )

    def push_diag(self):
        self.diag(0).start()
        self.diag(1).start()

    def push_near(self):
        self.near(1, 0, 6).start()
        self.near(2, 1, 7).start()

    def relay(self):
        first, second = pl.ds(0, 128), pl.ds(128, 128)
        self.diag(0).wait_recv()
        rows = self.chips(2).at[first, :]
        rows[...] = (
            rows[...].astype(F32) + self.lanes(self.diag_in.at[0])[...].astype(F32)
        ).astype(BF)
        self.near(2, 0, 8).start()
        self.diag(1).wait_recv()
        rows = self.chips(1).at[second, :]
        rows[...] = (
            rows[...].astype(F32) + self.lanes(self.diag_in.at[1])[...].astype(F32)
        ).astype(BF)
        self.near(1, 1, 9).start()

    def collect(self, buffer, sem):
        for role, half, slot in ((1, 0, 6), (2, 1, 7), (2, 0, 8), (1, 1, 9)):
            self.near(role, half, slot).wait_recv()
        for side in range(2):
            pltpu.make_async_copy(
                self.near_in.at[side], self.lanes(buffer.at[side]), sem.at[side]
            ).start()

    def collected(self, buffer, sem):
        for side in range(2):
            pltpu.make_async_copy(
                self.near_in.at[side], self.lanes(buffer.at[side]), sem.at[side]
            ).wait()

    def settle(self):
        for half in range(2):
            self.diag(half).wait_send()
        for role, half, slot in ((1, 0, 6), (2, 1, 7), (2, 0, 8), (1, 1, 9)):
            self.near(role, half, slot).wait_send()


def norm_back(gradient, rows_in, gain):
    inv = lax.rsqrt(jnp.mean(rows_in * rows_in, axis=-1, keepdims=True) + EPSILON)
    unit = rows_in * inv
    scaled = gradient * gain
    back = inv * (scaled - unit * jnp.mean(scaled * unit, axis=-1, keepdims=True))
    return back, jnp.sum(gradient * unit, axis=0, keepdims=True)


def layer_kernel(
    tok_h,
    gain_one_in,
    w_query_in,
    w_key_in,
    w_value_in,
    out_h,
    gain_two_in,
    gate_h,
    up_h,
    down_h,
    cot_h,
    pos_in,
    seg_in,
    freq,
    o_result,
    o_input,
    o_gains,
    o_query,
    o_kv,
    o_out,
    o_gate,
    o_up,
    o_down,
    near_down,
    near_gate,
    near_up,
    near_out,
    near_qkv,
    n_one_h,
    own_qkv,
    own_gains,
    own_marks,
    gains,
    marks,
    tok,
    w_gate,
    w_up,
    w_down,
    w_out,
    w_qkv,
    cot,
    n_two,
    hid,
    gate_g,
    up_g,
    core_in,
    diag_in,
    diag_low,
    chip_out,
    chip_qkv,
    sum_stage,
    turn_stage,
    part,
    outer_in,
    inner_in,
    outer_two,
    inner_two,
    mlow,
    total,
    own_out,
    mid,
    mid_g,
    q_heads,
    bias,
    lse,
    kv,
    att,
    rope,
    do_heads,
    keys,
    vals_t,
    vals,
    keys_t,
    key_acc,
    val_acc,
    kv_send_buf,
    kv_in,
    d_qkv,
    vec,
    vec_in,
    vec_out,
    vec_near,
    g_send,
    g_recv,
    g_local,
    small_send,
    small_recv,
    first_send,
    first_recv,
    load_sem,
    sum_send,
    sum_recv,
    all_send,
    all_recv,
    rs_send,
    rs_recv,
    credit,
    kv_send,
    kv_recv,
    vec_send,
    vec_recv,
    fin_sem,
    put_sem,
    own_sem,
):
    me = Place()
    group = group_devices(me)
    hidden = hid.shape[1]
    full_tiles = hidden // 256
    tiles = [(n * 256, min(256, hidden - n * 256)) for n in range((hidden + 255) // 256)]

    rows_of = [pl.ds(g * 256, 256) for g in range(2)]
    load_tok = pltpu.make_async_copy(tok_h, tok, load_sem.at[0])
    load_cot = pltpu.make_async_copy(cot_h, cot, load_sem.at[1])
    save_one = pltpu.make_async_copy(mlow, n_one_h, load_sem.at[2])
    load_one = pltpu.make_async_copy(n_one_h, mlow, load_sem.at[3])
    load_tok.start()
    load_cot.start()

    own_qkv[:, 0:512] = w_query_in[...]
    own_qkv[:, 512:640] = jnp.concatenate([w_key_in[...], w_value_in[...]], axis=1)
    own_gains[0:1, :] = gain_one_in[...].astype(F32)
    own_gains[1:2, :] = gain_two_in[...].astype(F32)
    own_gains[2:8, :] = jnp.zeros((6, 256), F32)
    own_marks[0:1, :] = pos_in[...]
    own_marks[1:2, :] = seg_in[...]
    own_marks[2:8, :] = jnp.zeros((6, 512), jnp.int32)
    greet(group + column_devices(me))

    qkv = Gather(me, 0, own_qkv, w_qkv, g_send, g_recv, g_local)
    out = Gather(me, 1, out_h, w_out, g_send, g_recv, g_local)
    gate = Gather(me, 2, gate_h, w_gate, g_send, g_recv, g_local)
    up = Gather(me, 3, up_h, w_up, g_send, g_recv, g_local)
    down = Gather(me, 4, down_h, w_down, g_send, g_recv, g_local)

    sources = [me.sx, me.sy, me.sd, me.of * 4 + me.c, me.of * 4 + me.cx, me.of * 4 + me.cy, me.of * 4 + me.cd]

    def small_copies(gain_slots, mark_slots):
        return [
            remote(own_gains, gains.at[spot], small_send.at[slot], small_recv.at[slot], group[slot])
            for slot, spot in enumerate(gain_slots)
        ] + [
            remote(
                own_marks, marks.at[spot], small_send.at[7 + slot], small_recv.at[7 + slot], group[slot]
            )
            for slot, spot in enumerate(mark_slots)
        ]

    small = small_copies([me.own] * 7, [me.c] * 3)

    def small_begin():
        for piece in small:
            piece.start()
        gains[me.own] = own_gains[...]
        marks[me.c] = own_marks[...]

    def small_finish():
        for piece in small_copies(sources, (me.cx, me.cy, me.cd)):
            piece.wait_recv()

    def first_norm():
        load_tok.wait()
        gain_one = row_of(gains, 0)

        def body(step, carry):
            values = tok[pl.ds(pl.multiple_of(step * 64, 64), 64), :].astype(F32)
            inv = lax.rsqrt(jnp.mean(values * values, axis=-1, keepdims=True) + EPSILON)
            mlow[step // 4, lax.rem(step, 4)] = (values * inv * gain_one).astype(BF)
            return carry

        lax.fori_loop(0, 8, body, 0)
        save_one.start()

    def make_rope():
        lane = lax.broadcasted_iota(jnp.int32, (128, 128), 1)
        low_half = lax.rem(lane, HD) < HD // 2
        for step in range(4):
            rows = slice(step * 128, (step + 1) * 128)
            places = own_marks[0:1, rows].astype(F32)
            angles = jnp.transpose(jnp.broadcast_to(places, (128, 128))) * freq[...]
            sine = jnp.sin(angles)
            rope[rows, :128] = jnp.cos(angles)
            rope[rows, 128:] = jnp.where(low_half, -sine, sine)

    def make_bias(g):
        own_rows = own_marks[:, g * 256 : (g + 1) * 256].astype(F32)
        for source in range(4):
            key_rows = marks[source, :, g * 256 : (g + 1) * 256].astype(F32)
            key_pos = jnp.transpose(jnp.broadcast_to(key_rows[0:1, :], (128, 256)))
            key_seg = jnp.transpose(jnp.broadcast_to(key_rows[1:2, :], (128, 256)))
            for side in range(2):
                lanes = slice(side * 128, (side + 1) * 128)
                seen = (key_seg == own_rows[1:2, lanes]) & (key_pos <= own_rows[0:1, lanes])
                bias[g, source * 256 : (source + 1) * 256, lanes] = jnp.where(
                    seen, 0.0, MASKED_SCORE
                ).astype(BF)

    lane_pair = lax.broadcasted_iota(jnp.int32, (256, 128), 1)

    def project_in(first, width):
        total_rows = None
        for shard in range(8):
            term = dotg(
                mlow[:, :, :, shard * 256 : (shard + 1) * 256].reshape(512, 256),
                w_qkv[shard, :, first : first + width],
                1,
                0,
            )
            total_rows = term if total_rows is None else total_rows + term
        return total_rows

    def first_copies(places):
        return [
            remote(kv.at[place], kv.at[place], first_send.at[slot], first_recv.at[slot], group[slot])
            for slot, place in enumerate(places)
        ]

    def project_kv():
        rows = project_in(512, 128)
        is_key = lax.broadcasted_iota(jnp.int32, (512, 128), 1) < HD
        cos_rows = jnp.where(is_key, rope[:, :128], 1.0)
        sin_rows = jnp.where(is_key, rope[:, 128:], 0.0)
        kv[me.c] = (rows * cos_rows + swap_halves(rows) * sin_rows).astype(BF)
        for piece in first_copies([me.c] * 3):
            piece.start()

    def project_q(half):
        rows_all = project_in(half * 256, 256)
        for inner in range(2):
            pair = half * 2 + inner
            rows = rows_all[:, inner * 128 : (inner + 1) * 128]
            rot = (rows * rope[:, :128] + swap_halves(rows) * rope[:, 128:]).astype(BF)
            rot = rot * jnp.bfloat16(HD ** (-0.5))
            for g in range(2):
                own = rot[g * 256 : (g + 1) * 256, :]
                zero = jnp.zeros_like(own)
                q_heads[g * 8 + 2 * pair] = jnp.where(lane_pair < HD, own, zero)
                q_heads[g * 8 + 2 * pair + 1] = jnp.where(lane_pair >= HD, own, zero)

    def kv_arrive():
        for piece in first_copies((me.cx, me.cy, me.cd)):
            piece.wait_recv()
        for g in range(2):
            for source in range(4):
                pairs = kv[source, g * 256 : (g + 1) * 256, :].astype(F32)
                rows = slice(source * 256, (source + 1) * 256)
                keys[g, rows, :] = jnp.where(
                    lane_pair < HD, pairs, pltpu.roll(pairs, HD, 1)
                ).astype(BF)
                vals_t[g, :, rows] = jnp.transpose(pairs)[HD:, :].astype(BF)

    def attend(g, start, stop):
        def body(pair, carry):
            halves = []
            for odd in range(2):
                head = g * 8 + pair * 2 + odd
                scores = dotg(keys[g], q_heads[head], 1, 1) + bias[g].astype(F32)
                top = jnp.max(scores, axis=0, keepdims=True)
                weights = jnp.exp(scores - top)
                norm = jnp.sum(weights, axis=0, keepdims=True)
                mixed = dotg(vals_t[g], weights.astype(BF), 1, 0)
                halves.append(mixed / norm)
                lse[head] = top + jnp.log(norm)
            rows = jnp.transpose(jnp.concatenate(halves, axis=0))
            att[rows_of[g], pl.ds(pl.multiple_of(pair * 128, 128), 128)] = rows.astype(BF)
            return carry

        lax.fori_loop(start, stop, body, 0)

    def project_out(g):
        def body(shard, carry):
            part[g, :, :, pl.ds(pl.multiple_of(shard * 256, 256), 256)] = (
                dotg(att[rows_of[g], :], w_out[shard], 1, 0).astype(BF).reshape(4, 64, 256)
            )
            return carry

        lax.fori_loop(0, 8, body, 0)

    def second_norm(g):
        sum_att[g].finish(total)
        own = pl.ds(pl.multiple_of(g * 256 + me.z * 64, 64), 64)
        mid_rows = tok[own, :].astype(F32) + total[...]
        mid[g] = mid_rows
        inv = lax.rsqrt(jnp.mean(mid_rows * mid_rows, axis=-1, keepdims=True) + EPSILON)
        n_two[g, me.z] = (mid_rows * inv * row_of(gains, 1)).astype(BF)
        spread_two[g].begin()

    def feed_tile(g, first, width):
        rows = rows_of[g]
        lanes = pl.ds(first, width)
        normed = n_two[g].reshape(256, 2048)
        gate = dotg(normed, w_gate[:, :, lanes].reshape(2048, width), 1, 0)
        up = dotg(normed, w_up[:, :, lanes].reshape(2048, width), 1, 0)
        hidden_grad = None
        for shard in range(8):
            term = dotg(
                cot[rows, shard * 256 : (shard + 1) * 256], w_down[shard, lanes, :], 1, 1
            )
            hidden_grad = term if hidden_grad is None else hidden_grad + term
        sig = jax.nn.sigmoid(gate)
        silu = gate * sig
        hid[rows, lanes] = (silu * up).astype(BF)
        up_g[rows, lanes] = (hidden_grad * silu).astype(BF)
        gate_g[rows, lanes] = (
            hidden_grad * up * sig * (1.0 + gate * (1.0 - sig))
        ).astype(BF)

    def feed(g, start, stop):
        def body(n, carry):
            feed_tile(g, pl.multiple_of(n * 256, 256), 256)
            return carry

        lax.fori_loop(start, min(stop, full_tiles), body, 0)
        if stop > full_tiles and len(tiles) > full_tiles:
            first, width = tiles[-1]
            feed_tile(g, first, width)

    def feed_back(g):
        def body(shard, carry):
            term = dotg(gate_g[rows_of[g], :], w_gate[shard], 1, 1) + dotg(
                up_g[rows_of[g], :], w_up[shard], 1, 1
            )
            part[g, :, :, pl.ds(pl.multiple_of(shard * 256, 256), 256)] = term.astype(BF).reshape(
                4, 64, 256
            )
            return carry

        lax.fori_loop(0, 8, body, 0)

    part_two = n_two

    def feed_out(g):
        def body(shard, carry):
            term = dotg(hid[rows_of[g], :], w_down[shard], 1, 0)
            part_two[g, :, :, pl.ds(pl.multiple_of(shard * 256, 256), 256)] = term.astype(
                BF
            ).reshape(4, 64, 256)
            return carry

        lax.fori_loop(0, 8, body, 0)

    def line_sum(slot, part_ref, outer, inner):
        return LineSum(me, part_ref, outer, inner, sum_send.at[slot], sum_recv.at[slot])

    sum_two = [line_sum(g, part.at[g], outer_in.at[g], inner_in.at[g]) for g in range(2)]
    sum_one = [line_sum(2 + g, part.at[g], outer_in.at[g], inner_in.at[g]) for g in range(2)]

    sum_out = [
        line_sum(4 + g, part_two.at[g], outer_two.at[g], inner_two.at[g]) for g in range(2)
    ]
    sum_att = [line_sum(6 + g, part.at[g], outer_in.at[g], inner_in.at[g]) for g in range(2)]
    spread_two = [LineGather(me, n_two.at[g], all_send.at[6 + g], all_recv.at[6 + g]) for g in range(2)]
    spread_mid = [LineGather(me, mlow.at[g], all_send.at[g], all_recv.at[g]) for g in range(2)]
    spread_in = [LineGather(me, o_input.at[g], all_send.at[2 + g], all_recv.at[2 + g]) for g in range(2)]
    spread_out = [LineGather(me, o_result.at[g], all_send.at[4 + g], all_recv.at[4 + g]) for g in range(2)]

    def middle_back(g):
        sum_two[g].finish(total)
        own = pl.ds(pl.multiple_of(g * 256 + me.z * 64, 64), 64)
        back, gain_grad = norm_back(total[...], mid[g], row_of(gains, 1))
        if g == 0:
            vec[1:2, :] = gain_grad
        else:
            vec[1:2, :] += gain_grad
        grad = cot[own, :].astype(F32) + back
        mid_g[g] = grad
        mlow[g, me.z] = grad.astype(BF)
        spread_mid[g].begin()

    def put_own(g, ref, slot):
        copy = pltpu.make_async_copy(own_out, ref.at[g, me.z], own_sem.at[slot])
        copy.start()
        copy.wait()

    def input_back(g):
        sum_one[g].finish(total)
        own = pl.ds(pl.multiple_of(g * 256 + me.z * 64, 64), 64)
        back, gain_grad = norm_back(total[...], tok[own, :].astype(F32), row_of(gains, 0))
        if g == 0:
            vec[0:1, :] = gain_grad
        else:
            vec[0:1, :] += gain_grad
        own_out[...] = (mid_g[g] + back).astype(BF)
        put_own(g, o_input, 0)
        spread_in[g].begin()

    def result_rows(g):
        sum_out[g].finish(total)
        own_out[...] = (mid[g] + total[...]).astype(BF)
        put_own(g, o_result, 1)
        spread_out[g].begin()

    wide = lambda ref: (lambda shard: ref[:, pl.ds(pl.multiple_of(shard * 256, 256), 256)])

    def blocks_of(ref):
        return lambda shard: ref[
            :, :, :, pl.ds(pl.multiple_of(shard * 256, 256), 256)
        ].reshape(512, 256)

    stage = w_up.at[pl.ds(4, 2)]
    landing = w_up.at[pl.ds(6, 2)]

    def scatter(index, width, x_of, y_of, chips, near):
        landed = diag_in.at[index] if index < 3 else diag_low.at[index - 3]
        refs = (stage, core_in, landed, near, rs_send, rs_recv, credit)
        return Scatter(me, index, index == 4, width, x_of, y_of, chips, refs)

    rs_down = scatter(
        0, hidden, wide(cot), lambda: hid[...], lambda role: w_gate.at[4 + role], near_down
    )
    rs_gate = scatter(
        1, hidden, blocks_of(n_two), lambda: gate_g[...], lambda role: w_gate.at[role], near_gate
    )
    rs_up = scatter(
        2, hidden, blocks_of(n_two), lambda: up_g[...], lambda role: w_up.at[role], near_up
    )
    rs_out = scatter(3, 512, blocks_of(mlow), lambda: att[...], lambda role: chip_out.at[role], near_out)
    rs_qkv = scatter(
        4,
        640,
        blocks_of(mlow),
        lambda: d_qkv[...],
        lambda role: chip_qkv.at[role],
        near_qkv,
    )

    def finish_rows(job, outs):
        job.collected(landing, fin_sem)
        width = job.width
        pending = [None, None]
        for step in range(4):
            slot = step % 2
            rows = slice(step * 64, (step + 1) * 64)
            if pending[slot] is not None:
                for piece in pending[slot]:
                    piece.wait()
            sum_stage[slot, :, :width] = (
                job.chips(0)[rows, :].astype(F32)
                + landing[0, rows, :width].astype(F32)
                + landing[1, rows, :width].astype(F32)
            )
            pending[slot] = [
                pltpu.make_async_copy(
                    sum_stage.at[slot, :, pl.ds(first, size)],
                    ref.at[pl.ds(step * 64, 64), :],
                    put_sem.at[slot, number],
                )
                for number, (ref, first, size) in enumerate(outs)
            ]
            for piece in pending[slot]:
                piece.start()
        for slot in range(2):
            for piece in pending[slot]:
                piece.wait()

    def finish_turned(job, ref):
        job.collected(landing, fin_sem)
        pending = [None, None]
        for step in range(job.width // 128):
            slot = step % 2
            lanes = slice(step * 128, (step + 1) * 128)
            if pending[slot] is not None:
                pending[slot].wait()
            turn_stage[slot] = jnp.transpose(
                job.chips(0)[:, lanes].astype(F32)
                + landing[0, :, lanes].astype(F32)
                + landing[1, :, lanes].astype(F32)
            )
            pending[slot] = pltpu.make_async_copy(
                turn_stage.at[slot], ref.at[pl.ds(step * 128, 128), :], put_sem.at[slot, 0]
            )
            pending[slot].start()
        for piece in pending:
            piece.wait()

    def out_back(g):
        grad = None
        for shard in range(8):
            lanes = slice(shard * 256, (shard + 1) * 256)
            term = dotg(mlow[g, :, :, lanes].reshape(256, 256), w_out[shard], 1, 1)
            grad = term if grad is None else grad + term
        grad = grad.astype(BF)
        for pair in range(4):
            own = grad[:, pair * 128 : (pair + 1) * 128]
            zero = jnp.zeros_like(own)
            do_heads[2 * pair] = jnp.where(lane_pair < HD, own, zero)
            do_heads[2 * pair + 1] = jnp.where(lane_pair >= HD, own, zero)
        for source in range(4):
            pairs = kv[source, rows_of[g], :].astype(F32)
            turned = pltpu.roll(pairs, HD, 1)
            rows = slice(source * 256, (source + 1) * 256)
            vals[rows, :] = jnp.where(lane_pair < HD, turned, pairs).astype(BF)
            keys_t[:, rows] = jnp.transpose(pairs)[:HD, :].astype(BF)
        key_acc[...] = jnp.zeros_like(key_acc)
        val_acc[...] = jnp.zeros_like(val_acc)

    def attend_back(g, start, stop):
        def body(pair, carry):
            halves = []
            for odd in range(2):
                head = 2 * pair + odd
                query, grad = q_heads[g * 8 + head], do_heads[head]
                scores = dotg(keys[g], query, 1, 1) + bias[g].astype(F32)
                probs = jnp.exp(scores - lse[g * 8 + head])
                prob_grad = dotg(vals[...], grad, 1, 1)
                delta = jnp.sum(probs * prob_grad, axis=0, keepdims=True)
                score_grad = (probs * (prob_grad - delta)).astype(BF)
                val_acc[...] += dotg(probs.astype(BF), grad, 1, 0)
                key_acc[...] += dotg(score_grad, query, 1, 0)
                halves.append(dotg(keys_t[...], score_grad, 1, 0))
            rows = jnp.transpose(jnp.concatenate(halves, axis=0)) * (HD ** (-0.5))
            rows = rows * rope[rows_of[g], :128] - swap_halves(rows) * rope[rows_of[g], 128:]
            d_qkv[rows_of[g], pl.ds(pl.multiple_of(pair * 128, 128), 128)] = rows.astype(BF)
            return carry

        lax.fori_loop(start, stop, body, 0)

    def kv_copies(g):
        return [
            remote(
                kv_send_buf.at[g, column],
                kv_in.at[g, slot],
                kv_send.at[g, slot],
                kv_recv.at[g, slot],
                group[slot],
            )
            for slot, column in enumerate((me.cx, me.cy, me.cd))
        ]

    def kv_begin(g):
        for block in range(4):
            rows = slice(block * 256, (block + 1) * 256)
            key_rows, val_rows = key_acc[rows, :], val_acc[rows, :]
            joined = jnp.where(
                lane_pair < HD,
                key_rows + pltpu.roll(key_rows, HD, 1),
                val_rows + pltpu.roll(val_rows, HD, 1),
            )
            kv_send_buf[g, block] = joined.astype(BF)
        for piece in kv_copies(g):
            piece.start()

    def kv_finish(g):
        rows = kv_send_buf[g, me.c].astype(F32)
        for slot, piece in enumerate(kv_copies(g)):
            piece.wait_recv()
            rows = rows + kv_in[g, slot].astype(F32)
        cos_rows = jnp.where(lane_pair < HD, rope[rows_of[g], :128], 1.0)
        sin_rows = jnp.where(lane_pair < HD, rope[rows_of[g], 128:], 0.0)
        rows = rows * cos_rows - swap_halves(rows) * sin_rows
        d_qkv[rows_of[g], 512:640] = rows.astype(BF)

    def project_back_rows(g):
        def body(shard, carry):
            term = dotg(d_qkv[rows_of[g], :], w_qkv[shard], 1, 1)
            part[g, :, :, pl.ds(pl.multiple_of(shard * 256, 256), 256)] = term.astype(BF).reshape(
                4, 64, 256
            )
            return carry

        lax.fori_loop(0, 8, body, 0)

    line = column_devices(me)

    def vec_line():
        return [
            remote(vec_out, vec_in.at[slot], vec_send.at[slot], vec_recv.at[slot], device)
            for slot, device in enumerate(line)
        ]

    targets = [me.sx, me.sy, me.sd, me.of * 4 + me.c, me.of * 4 + me.cx, me.of * 4 + me.cy, me.of * 4 + me.cd]

    def vec_group():
        return [
            remote(
                vec_in.at[3, target],
                vec_near.at[slot],
                vec_send.at[3 + slot],
                vec_recv.at[3 + slot],
                device,
            )
            for slot, (target, device) in enumerate(zip(targets, group))
        ]

    def vec_begin():
        for shard in range(8):
            for which in range(2):
                for half in range(2):
                    first = shard * 256 + half * 128
                    vec_out[shard, 2 * which + half : 2 * which + half + 1, :] = vec[
                        which : which + 1, first : first + 128
                    ]
            vec_out[shard, 4:8, :] = jnp.zeros((4, 128), F32)
        for piece in vec_line():
            piece.start()

    def vec_middle():
        for piece in vec_line():
            piece.wait_recv()
        vec_in[3] = vec_out[...] + vec_in[0] + vec_in[1] + vec_in[2]
        for piece in vec_group():
            piece.start()

    def vec_finish():
        rows = vec_in[3, me.own]
        for slot, piece in enumerate(vec_group()):
            piece.wait_recv()
            rows = rows + vec_near[slot]
        o_gains[...] = rows

    def settle_weights():
        for piece in (qkv, out, gate, up, down):
            piece.settle()

    def settle():
        for spread in spread_in + spread_out:
            spread.finish()
        for job in (rs_down, rs_gate, rs_up, rs_out, rs_qkv):
            job.settle()
        for g in range(2):
            for piece in kv_copies(g):
                piece.wait_send()
        for piece in vec_line() + vec_group() + small + first_copies([me.c] * 3):
            piece.wait_send()

    order = (
        (small_begin,),
        (qkv.begin,),
        (make_rope,),
        (small_finish,),
        (first_norm,),
        (qkv.forward,),
        (out.begin,),
        (make_bias, 0),
        (make_bias, 1),
        (qkv.diagonal,),
        (qkv.arrive,),
        (project_kv,),
        (out.forward,),
        (project_q, 0),
        (project_q, 1),
        (save_one.wait,),
        (gate.begin,),
        (up.begin,),
        (down.begin,),
        (kv_arrive,),
        (attend, 0, 0, 4),
        (out.diagonal,),
        (out.arrive,),
        (project_out, 0),
        (sum_att[0].begin,),
        (gate.forward,),
        (attend, 1, 0, 2),
        (sum_att[0].step_one,),
        (attend, 1, 2, 4),
        (sum_att[0].step_two,),
        (project_out, 1),
        (sum_att[1].begin,),
        (second_norm, 0),
        (sum_att[1].step_one,),
        (up.forward,),
        (spread_two[0].step_one,),
        (sum_att[1].step_two,),
        (spread_two[0].step_two,),
        (down.forward,),
        (second_norm, 1),
        (gate.diagonal,),
        (spread_two[0].finish,),
        (spread_two[1].step_one,),
        (up.diagonal,),
        (down.diagonal,),
        (gate.arrive,),
        (up.arrive,),
        (down.arrive,),
        (load_cot.wait,),
        (spread_two[1].step_two,),
        (feed, 0, 0, full_tiles + 1),
        (feed_back, 0),
        (sum_two[0].begin,),
        (spread_two[1].finish,),
        (feed, 1, 0, 3),
        (sum_two[0].step_one,),
        (feed, 1, 3, full_tiles + 1),
        (sum_two[0].step_two,),
        (feed_back, 1),
        (sum_two[1].begin,),
        (settle_weights,),
        (rs_down.partner,),
        (rs_down.own,),
        (rs_down.push_diag,),
        (rs_down.push_near,),
        (middle_back, 0),
        (sum_two[1].step_one,),
        (spread_mid[0].step_one,),
        (rs_gate.partner,),
        (rs_gate.own,),
        (rs_gate.push_diag,),
        (rs_down.relay,),
        (sum_two[1].step_two,),
        (spread_mid[0].step_two,),
        (rs_up.partner,),
        (rs_up.own,),
        (middle_back, 1),
        (feed_out, 0),
        (sum_out[0].begin,),
        (spread_mid[0].finish,),
        (out_back, 0),
        (spread_mid[1].step_one,),
        (attend_back, 0, 0, 2),
        (spread_mid[1].step_two,),
        (attend_back, 0, 2, 4),
        (kv_begin, 0),
        (rs_gate.push_near,),
        (rs_up.push_diag,),
        (rs_gate.relay,),
        (feed_out, 1),
        (sum_out[0].step_one,),
        (spread_mid[1].finish,),
        (out_back, 1),
        (rs_out.partner,),
        (rs_out.own,),
        (load_one.start,),
        (kv_finish, 0),
        (project_back_rows, 0),
        (sum_one[0].begin,),
        (attend_back, 1, 0, 2),
        (sum_one[0].step_one,),
        (sum_out[0].step_two,),
        (attend_back, 1, 2, 4),
        (kv_begin, 1),
        (rs_up.push_near,),
        (rs_up.relay,),
        (rs_out.push_diag,),
        (rs_out.push_near,),
        (sum_one[0].step_two,),
        (result_rows, 0),
        (kv_finish, 1),
        (project_back_rows, 1),
        (sum_one[1].begin,),
        (input_back, 0),
        (load_one.wait,),
        (rs_qkv.partner,),
        (rs_qkv.own,),
        (rs_qkv.push_diag,),
        (rs_qkv.push_near,),
        (rs_out.relay,),
        (sum_out[1].begin,),
        (sum_one[1].step_one,),
        (spread_in[0].step_one,),
        (spread_out[0].step_one,),
        (rs_down.collect, landing, fin_sem),
        (finish_turned, rs_down, o_down),
        (rs_gate.collect, landing, fin_sem),
        (sum_one[1].step_two,),
        (spread_in[0].step_two,),
        (spread_out[0].step_two,),
        (sum_out[1].step_one,),
        (rs_qkv.relay,),
        (finish_rows, rs_gate, [(o_gate, 0, hidden)]),
        (input_back, 1),
        (vec_begin,),
        (rs_up.collect, landing, fin_sem),
        (sum_out[1].step_two,),
        (spread_in[1].step_one,),
        (finish_rows, rs_up, [(o_up, 0, hidden)]),
        (vec_middle,),
        (result_rows, 1),
        (spread_in[1].step_two,),
        (rs_out.collect, landing, fin_sem),
        (finish_turned, rs_out, o_out),
        (rs_qkv.collect, landing, fin_sem),
        (spread_out[1].step_one,),
        (finish_rows, rs_qkv, [(o_query, 0, 512), (o_kv, 512, 128)]),
        (vec_finish,),
        (spread_out[1].step_two,),
        (settle,),
    )
    for action, *values in order:
        action(*values)


def run_layer(
    tokens, attn_gain, w_query, w_key, w_value, w_out, mlp_gain, w_gate, w_up, w_down, cotangent,
    positions, segments,
):
    shape = jax.ShapeDtypeStruct
    width = tokens.shape[1]
    hidden = w_gate.shape[1]
    vmem = pl.BlockSpec(memory_space=pltpu.VMEM)
    anywhere = pl.BlockSpec(memory_space=pl.ANY)
    dma = pltpu.SemaphoreType.DMA
    buffer = pltpu.VMEM
    half_size = HD // 2
    frequency = THETA_BASE ** (-jnp.arange(half_size, dtype=F32) / half_size)
    frequency = jnp.concatenate([frequency] * 4)[None, :]
    return pl.pallas_call(
        layer_kernel,
        name="decoder_layer",
        out_shape=(
            shape((2, 4, 64, width), BF),
            shape((2, 4, 64, width), BF),
            shape((8, 128), F32),
            shape((256, 512), F32),
            shape((256, 128), F32),
            shape((512, 256), F32),
            shape((256, hidden), F32),
            shape((256, hidden), F32),
            shape((hidden, 256), F32),
            shape((2, 256, hidden), BF),
            shape((2, 256, hidden), BF),
            shape((2, 256, hidden), BF),
            shape((2, 256, 512), BF),
            shape((2, 256, 640), BF),
            shape((2, 4, 64, width), BF),
        ),
        in_specs=[anywhere, vmem, vmem, vmem, vmem, anywhere, vmem]
        + [anywhere] * 4
        + [vmem] * 3,
        out_specs=(anywhere,) * 2 + (vmem,) + (anywhere,) * 12,
        scratch_shapes=[
            buffer((256, 640), BF),
            buffer((8, 256), F32),
            buffer((8, 512), jnp.int32),
            buffer((8, 8, 256), F32),
            buffer((4, 8, 512), jnp.int32),
            buffer((512, width), BF),
            buffer((8, 256, hidden), BF),
            buffer((8, 256, hidden), BF),
            buffer((8, hidden, 256), BF),
            buffer((8, 512, 256), BF),
            buffer((8, 256, 640), BF),
            buffer((512, width), BF),
            buffer((2, 4, 64, width), BF),
            buffer((512, hidden), BF),
            buffer((512, hidden), BF),
            buffer((512, hidden), BF),
            buffer((4, 256, hidden), BF),
            buffer((3, 2, 128, hidden), BF),
            buffer((2, 2, 128, 640), BF),
            buffer((4, 256, 512), BF),
            buffer((4, 256, 640), BF),
            buffer((2, 64, hidden), F32),
            buffer((2, 128, 256), F32),
            buffer((2, 4, 64, width), BF),
            buffer((2, 3, 64, width), BF),
            buffer((2, 2, 64, width), BF),
            buffer((2, 3, 64, width), BF),
            buffer((2, 2, 64, width), BF),
            buffer((2, 4, 64, width), BF),
            buffer((64, width), F32),
            buffer((64, width), BF),
            buffer((2, 64, width), F32),
            buffer((2, 64, width), F32),
            buffer((16, 256, 128), BF),
            buffer((2, 1024, 256), BF),
            buffer((16, 1, 256), F32),
            buffer((4, 512, 128), BF),
            buffer((512, 512), BF),
            buffer((512, 256), F32),
            buffer((8, 256, 128), BF),
            buffer((2, 1024, 128), BF),
            buffer((2, HD, 1024), BF),
            buffer((1024, 128), BF),
            buffer((HD, 1024), BF),
            buffer((1024, 128), F32),
            buffer((1024, 128), F32),
            buffer((2, 4, 256, 128), BF),
            buffer((2, 3, 256, 128), BF),
            buffer((512, 640), BF),
            buffer((2, width), F32),
            buffer((4, 8, 8, 128), F32),
            buffer((8, 8, 128), F32),
            buffer((7, 8, 128), F32),
            dma((5, 9)),
            dma((5, 9)),
            dma((5,)),
            dma((10,)),
            dma((10,)),
            dma((3,)),
            dma((3,)),
            dma((4,)),
            dma((8, 3)),
            dma((8, 5)),
            dma((8, 5)),
            dma((8, 4)),
            dma((5, 10)),
            dma((5, 10)),
            pltpu.SemaphoreType.REGULAR((4,)),
            dma((2, 3)),
            dma((2, 3)),
            dma((10,)),
            dma((10,)),
            dma((2,)),
            dma((2, 2)),
            dma((2,)),
        ],
        compiler_params=pltpu.CompilerParams(
            collective_id=0, has_side_effects=True, vmem_limit_bytes=67043328
        ),
    )(
        tokens, attn_gain[None, :], w_query, w_key, w_value, w_out, mlp_gain[None, :], w_gate, w_up,
        w_down, cotangent, positions[None, :], segments[None, :], frequency,
    )


def fast_shards(tokens, *others):
    (result, input_grad, gain_grads, query_g, kv_g, out_g, gate_g, up_g, down_g, *_) = run_layer(
        tokens, *others
    )
    return (
        result.reshape(tokens.shape),
        input_grad.reshape(tokens.shape),
        gain_grads[0:2].reshape(-1),
        query_g,
        kv_g[:, :HD],
        kv_g[:, HD:],
        out_g,
        gain_grads[2:4].reshape(-1),
        gate_g,
        up_g,
        down_g,
    )


def solution(mesh):
    in_specs = (
        P(("fsdp", "ctx"), None),
        P(("fsdp", "ctx")),
        P(("fsdp", "ctx"), "tp"),
        P(("fsdp", "ctx"), "tp"),
        P(("fsdp", "ctx"), "tp"),
        P("tp", ("fsdp", "ctx")),
        P(("fsdp", "ctx")),
        P(("fsdp", "ctx"), "tp"),
        P(("fsdp", "ctx"), "tp"),
        P("tp", ("fsdp", "ctx")),
        P(("fsdp", "ctx"), None),
        P(("fsdp", "ctx")),
        P(("fsdp", "ctx")),
    )
    out_specs = (
        P(("fsdp", "ctx"), None),
        P(("fsdp", "ctx"), None),
        P(("fsdp", "ctx")),
        P(("fsdp", "ctx"), "tp"),
        P(("fsdp", "ctx"), "tp"),
        P(("fsdp", "ctx"), "tp"),
        P("tp", ("fsdp", "ctx")),
        P(("fsdp", "ctx")),
        P(("fsdp", "ctx"), "tp"),
        P(("fsdp", "ctx"), "tp"),
        P("tp", ("fsdp", "ctx")),
    )
    small = (mesh.shape["fsdp"], mesh.shape["ctx"], mesh.shape["tp"]) == (2, 4, 4)
    return jax.shard_map(fast_shards if small else shards, mesh=mesh, in_specs=in_specs, out_specs=out_specs, check_vma=False)
```

```python
import jax
import jax.numpy as jnp
import numpy as np
from jax import lax
from jax.experimental import pallas as pl
from jax.experimental.pallas import tpu as pltpu
from jax.sharding import PartitionSpec as P

H = 32
KVH = 4
HD = 64


EPSILON = 1e-05
THETA_BASE = 10000.0
MASKED_SCORE = -1e30


def shifted(value, axis, steps):
    count = lax.axis_size(axis)
    pairs = [(source, (source + steps) % count) for source in range(count)]
    return lax.ppermute(value, axis, pairs)


def rope_tables(token_pos, half_size):
    frequency = THETA_BASE ** (-jnp.arange(half_size, dtype=jnp.float32) / half_size)
    angles = token_pos.astype(jnp.float32)[:, None] * frequency[None, :]
    return (jnp.cos(angles), jnp.sin(angles))


def rotate(head_rows, cosine, sine):
    half_size = head_rows.shape[-1] // 2
    first_half = head_rows[..., :half_size]
    second_half = head_rows[..., half_size:]
    cos_rows = cosine[:, None, :]
    sin_rows = sine[:, None, :]
    return jnp.concatenate(
        [
            first_half * cos_rows - second_half * sin_rows,
            second_half * cos_rows + first_half * sin_rows,
        ],
        axis=-1,
    )


def rotate_back(head_rows, cosine, sine):
    half_size = head_rows.shape[-1] // 2
    first_half = head_rows[..., :half_size]
    second_half = head_rows[..., half_size:]
    cos_rows = cosine[:, None, :]
    sin_rows = sine[:, None, :]
    return jnp.concatenate(
        [
            first_half * cos_rows + second_half * sin_rows,
            second_half * cos_rows - first_half * sin_rows,
        ],
        axis=-1,
    )


def project(left_side, right_side):
    return jnp.dot(left_side, right_side, preferred_element_type=jnp.float32)


def project_back(left_side, right_side):
    return lax.dot_general(
        left_side, right_side, (((1,), (1,)), ((), ())), preferred_element_type=jnp.float32
    )


def weight_grad(left_side, right_side):
    return lax.dot_general(
        left_side, right_side, (((0,), (0,)), ((), ())), preferred_element_type=jnp.float32
    )


def rms_norm(rows_in, gain_vec):
    inv_rms = lax.rsqrt(jnp.mean(rows_in * rows_in, axis=-1, keepdims=True) + EPSILON)
    unit_rows = rows_in * inv_rms
    return (unit_rows * gain_vec, unit_rows, inv_rms)


def rms_norm_back(gradient, gain_vec, unit_rows, inv_rms):
    gain_grad = jnp.sum(gradient * unit_rows, axis=0)
    scaled_grad = gradient * gain_vec
    return (
        inv_rms
        * (scaled_grad - unit_rows * jnp.mean(scaled_grad * unit_rows, axis=-1, keepdims=True)),
        gain_grad,
    )


def pair_mask(query_pos, query_seg, key_pos, key_seg):
    return (query_seg[:, None] == key_seg[None, :]) & (key_pos[None, :] <= query_pos[:, None])


def split_block(kv_block, kv_heads):
    key_rows = kv_block[:, : kv_heads * HD].reshape(-1, kv_heads, HD)
    value_rows = kv_block[:, kv_heads * HD :].reshape(-1, kv_heads, HD)
    return (key_rows, value_rows)


def attend_block(state_in, queries, kv_block, visible):
    row_top, row_total, output_sum = state_in
    key_rows, value_rows = split_block(kv_block, queries.shape[1])
    scores = jnp.einsum(
        "qkgd,pkd->kgqp", queries, key_rows, preferred_element_type=jnp.float32
    ) * HD ** (-0.5)
    scores = jnp.where(visible, scores, MASKED_SCORE)
    new_top = jnp.maximum(row_top, jnp.max(scores, axis=-1))
    weights = jnp.where(visible, jnp.exp(scores - new_top[..., None]), 0.0)
    decay_factor = jnp.exp(row_top - new_top)
    row_total = row_total * decay_factor + jnp.sum(weights, axis=-1)
    mixed_heads = jnp.einsum(
        "kgqp,pkd->qkgd",
        weights.astype(jnp.bfloat16),
        value_rows,
        preferred_element_type=jnp.float32,
    )
    output_sum = output_sum * jnp.transpose(decay_factor, (2, 0, 1))[..., None] + mixed_heads
    return (new_top, row_total, output_sum)


def block_grads(queries, out_grad, kv_block, visible, log_total, delta_rows):
    key_rows, value_rows = split_block(kv_block, queries.shape[1])
    scale_factor = HD ** (-0.5)
    scores = (
        jnp.einsum("qkgd,pkd->kgqp", queries, key_rows, preferred_element_type=jnp.float32)
        * scale_factor
    )
    probs_full = jnp.where(
        visible, jnp.exp(jnp.where(visible, scores, MASKED_SCORE) - log_total[..., None]), 0.0
    )
    value_grad = jnp.einsum(
        "kgqp,qkgd->pkd",
        probs_full.astype(jnp.bfloat16),
        out_grad,
        preferred_element_type=jnp.float32,
    )
    prob_grad = jnp.einsum(
        "qkgd,pkd->kgqp", out_grad, value_rows, preferred_element_type=jnp.float32
    )
    score_grad = (probs_full * (prob_grad - delta_rows[..., None])).astype(jnp.bfloat16)
    query_grad = (
        jnp.einsum("kgqp,pkd->qkgd", score_grad, key_rows, preferred_element_type=jnp.float32)
        * scale_factor
    )
    key_grad = (
        jnp.einsum("kgqp,qkgd->pkd", score_grad, queries, preferred_element_type=jnp.float32)
        * scale_factor
    )
    block_rows = kv_block.shape[0]
    return (
        query_grad,
        jnp.concatenate(
            [key_grad.reshape(block_rows, -1), value_grad.reshape(block_rows, -1)], axis=-1
        ),
    )


def shards(
    tokens,
    attn_gain,
    w_query,
    w_key,
    w_value,
    w_out,
    mlp_gain,
    w_gate,
    w_up,
    w_down,
    cotangent,
    positions,
    segments,
):
    token_rows = tokens.shape[0]
    gain_one, query_w, key_w, value_w, out_w = (
        lax.all_gather(attn_gain, ("fsdp", "ctx"), axis=0, tiled=True),
        lax.all_gather(w_query, ("fsdp", "ctx"), axis=0, tiled=True),
        lax.all_gather(w_key, ("fsdp", "ctx"), axis=0, tiled=True),
        lax.all_gather(w_value, ("fsdp", "ctx"), axis=0, tiled=True),
        lax.all_gather(w_out, ("fsdp", "ctx"), axis=1, tiled=True),
    )
    gain_two, gate_w, up_w, down_w = (
        lax.all_gather(mlp_gain, ("fsdp", "ctx"), axis=0, tiled=True),
        lax.all_gather(w_gate, ("fsdp", "ctx"), axis=0, tiled=True),
        lax.all_gather(w_up, ("fsdp", "ctx"), axis=0, tiled=True),
        lax.all_gather(w_down, ("fsdp", "ctx"), axis=1, tiled=True),
    )
    head_count = query_w.shape[1] // HD
    kv_heads = key_w.shape[1] // HD
    groups = H // KVH
    cosine, sine = rope_tables(positions, HD // 2)
    token_float = tokens.astype(jnp.float32)
    gain_one_float = gain_one.astype(jnp.float32)
    normed_one, unit_one, inv_one = rms_norm(token_float, gain_one_float)
    normed_low = normed_one.astype(jnp.bfloat16)
    query_lin = project(normed_low, query_w)
    key_lin = project(normed_low, key_w)
    value_low = project(normed_low, value_w).astype(jnp.bfloat16)
    query_rot = rotate(query_lin.reshape(token_rows, head_count, HD), cosine, sine).astype(
        jnp.bfloat16
    )
    key_rot = rotate(key_lin.reshape(token_rows, kv_heads, HD), cosine, sine).astype(jnp.bfloat16)
    queries = query_rot.reshape(token_rows, kv_heads, groups, HD)
    kv_local = jnp.concatenate([key_rot.reshape(token_rows, kv_heads * HD), value_low], axis=-1)
    key_positions, key_segments = (
        lax.all_gather(positions, "ctx", axis=0, tiled=True),
        lax.all_gather(segments, "ctx", axis=0, tiled=True),
    )
    my_index = lax.axis_index("ctx")
    cycle_size = lax.axis_size("ctx")

    def block_marks(source):
        start_row = source * token_rows
        return pair_mask(
            positions,
            segments,
            lax.dynamic_slice_in_dim(key_positions, start_row, token_rows),
            lax.dynamic_slice_in_dim(key_segments, start_row, token_rows),
        )

    start_state = (
        jnp.full((kv_heads, groups, token_rows), MASKED_SCORE, jnp.float32),
        jnp.zeros((kv_heads, groups, token_rows), jnp.float32),
        jnp.zeros((token_rows, kv_heads, groups, HD), jnp.float32),
    )

    def forward_block(state_in, kv_block, source):
        visible = block_marks(source)
        return attend_block(state_in, queries, kv_block, visible)

    def cycle_step(state_in, step_index):
        attn_state, kv_block = state_in
        attn_state = forward_block(attn_state, kv_block, (my_index - step_index) % cycle_size)
        passed = shifted(kv_block, "ctx", 1)
        return ((attn_state, passed), kv_block)

    (attn_state, last_block), kept_blocks = lax.scan(
        cycle_step, (start_state, kv_local), jnp.arange(cycle_size - 1)
    )
    attn_state = forward_block(attn_state, last_block, (my_index + 1) % cycle_size)
    kv_blocks = jnp.concatenate([kept_blocks, last_block[None]], axis=0)
    sources = (my_index - jnp.arange(cycle_size)) % cycle_size
    row_top, row_total, output_sum = attn_state
    attended = output_sum / jnp.transpose(row_total, (2, 0, 1))[..., None]
    log_total = row_top + jnp.log(row_total)
    attended_low = attended.reshape(token_rows, head_count * HD).astype(jnp.bfloat16)
    middle = token_float + lax.psum(project(attended_low, out_w).astype(jnp.bfloat16), "tp").astype(
        jnp.float32
    )
    gain_two_float = gain_two.astype(jnp.float32)
    normed_two, unit_two, inv_two = rms_norm(middle, gain_two_float)
    normed_two_low = normed_two.astype(jnp.bfloat16)
    gate_lin = project(normed_two_low, gate_w)
    up_lin = project(normed_two_low, up_w)
    hidden_low = (jax.nn.silu(gate_lin) * up_lin).astype(jnp.bfloat16)
    result = middle + lax.psum(project(hidden_low, down_w).astype(jnp.bfloat16), "tp").astype(
        jnp.float32
    )
    output = result.astype(jnp.bfloat16)
    hidden_grad = project_back(cotangent, down_w)
    down_w_grad = weight_grad(hidden_low, cotangent)
    sigmoid_gate = jax.nn.sigmoid(gate_lin)
    gate_grad_low = (
        hidden_grad * up_lin * sigmoid_gate * (1.0 + gate_lin * (1.0 - sigmoid_gate))
    ).astype(jnp.bfloat16)
    up_grad_low = (hidden_grad * gate_lin * sigmoid_gate).astype(jnp.bfloat16)
    normed_two_grad = lax.psum(
        (project_back(gate_grad_low, gate_w) + project_back(up_grad_low, up_w)).astype(
            jnp.bfloat16
        ),
        "tp",
    ).astype(jnp.float32)
    gate_w_grad = weight_grad(normed_two_low, gate_grad_low)
    up_w_grad = weight_grad(normed_two_low, up_grad_low)
    norm_back_two, gain_two_grad = rms_norm_back(normed_two_grad, gain_two_float, unit_two, inv_two)
    middle_grad = cotangent.astype(jnp.float32) + norm_back_two
    middle_low = middle_grad.astype(jnp.bfloat16)
    attended_grad_low = project_back(middle_low, out_w).astype(jnp.bfloat16)
    out_w_grad = weight_grad(attended_low, middle_low)
    out_grad = attended_grad_low.reshape(token_rows, kv_heads, groups, HD)
    delta_rows = jnp.transpose(jnp.sum(out_grad.astype(jnp.float32) * attended, axis=-1), (1, 2, 0))

    def backward_block(kv_block, source):
        visible = block_marks(source)
        return block_grads(queries, out_grad, kv_block, visible, log_total, delta_rows)

    query_start = jnp.zeros((token_rows, kv_heads, groups, HD), jnp.float32)

    def back_step(state_in, pieces):
        query_acc, kv_acc = state_in
        query_term, kv_term = backward_block(pieces[0], pieces[1])
        passed = shifted((kv_acc + kv_term).astype(jnp.bfloat16), "ctx", 1).astype(jnp.float32)
        return ((query_acc + query_term, passed), None)

    (query_grad, kv_grad), unused = lax.scan(
        back_step, (query_start, jnp.zeros(kv_local.shape, jnp.float32)), (kv_blocks, sources)
    )
    query_grad_low = (
        rotate_back(query_grad.reshape(token_rows, head_count, HD), cosine, sine)
        .reshape(token_rows, head_count * HD)
        .astype(jnp.bfloat16)
    )
    key_grad_low = (
        rotate_back(kv_grad[:, : kv_heads * HD].reshape(token_rows, kv_heads, HD), cosine, sine)
        .reshape(token_rows, kv_heads * HD)
        .astype(jnp.bfloat16)
    )
    value_grad_low = kv_grad[:, kv_heads * HD :].astype(jnp.bfloat16)
    normed_one_grad = lax.psum(
        (
            project_back(query_grad_low, query_w)
            + project_back(key_grad_low, key_w)
            + project_back(value_grad_low, value_w)
        ).astype(jnp.bfloat16),
        "tp",
    ).astype(jnp.float32)
    query_w_grad = weight_grad(normed_low, query_grad_low)
    key_w_grad = weight_grad(normed_low, key_grad_low)
    value_w_grad = weight_grad(normed_low, value_grad_low)
    norm_back_one, gain_one_grad = rms_norm_back(normed_one_grad, gain_one_float, unit_one, inv_one)
    input_grad = (middle_grad + norm_back_one).astype(jnp.bfloat16)
    summed = (
        lax.psum_scatter(
            gain_one_grad.astype(jnp.bfloat16), ("fsdp", "ctx"), scatter_dimension=0, tiled=True
        ).astype(jnp.float32),
        lax.psum_scatter(
            query_w_grad.astype(jnp.bfloat16), ("fsdp", "ctx"), scatter_dimension=0, tiled=True
        ).astype(jnp.float32),
        lax.psum_scatter(
            key_w_grad.astype(jnp.bfloat16), ("fsdp", "ctx"), scatter_dimension=0, tiled=True
        ).astype(jnp.float32),
        lax.psum_scatter(
            value_w_grad.astype(jnp.bfloat16), ("fsdp", "ctx"), scatter_dimension=0, tiled=True
        ).astype(jnp.float32),
        lax.psum_scatter(
            out_w_grad.astype(jnp.bfloat16), ("fsdp", "ctx"), scatter_dimension=1, tiled=True
        ).astype(jnp.float32),
        lax.psum_scatter(
            gain_two_grad.astype(jnp.bfloat16), ("fsdp", "ctx"), scatter_dimension=0, tiled=True
        ).astype(jnp.float32),
        lax.psum_scatter(
            gate_w_grad.astype(jnp.bfloat16), ("fsdp", "ctx"), scatter_dimension=0, tiled=True
        ).astype(jnp.float32),
        lax.psum_scatter(
            up_w_grad.astype(jnp.bfloat16), ("fsdp", "ctx"), scatter_dimension=0, tiled=True
        ).astype(jnp.float32),
        lax.psum_scatter(
            down_w_grad.astype(jnp.bfloat16), ("fsdp", "ctx"), scatter_dimension=1, tiled=True
        ).astype(jnp.float32),
    )
    return (output, input_grad) + tuple(summed)


MESH = pl.DeviceIdType.MESH
BF = jnp.bfloat16
F32 = jnp.float32


def dotg(left_side, right_side, left_dim, right_dim):
    return lax.dot_general(
        left_side,
        right_side,
        (((left_dim,), (right_dim,)), ((), ())),
        preferred_element_type=F32,
    )


def remote(src, dst, send_sem, recv_sem, device):
    return pltpu.make_async_remote_copy(
        src_ref=src,
        dst_ref=dst,
        send_sem=send_sem,
        recv_sem=recv_sem,
        device_id=device,
        device_id_type=MESH,
    )


class Place:
    def __init__(self):
        self.f = lax.axis_index("fsdp")
        self.c = lax.axis_index("ctx")
        self.z = lax.axis_index("tp")
        self.cx = self.c + 1 - 2 * lax.rem(self.c, 2)
        self.cy = lax.rem(self.c + 2, 4)
        self.cd = 3 - self.c
        self.of = 1 - self.f
        self.own = self.f * 4 + self.c
        self.sx = self.f * 4 + self.cx
        self.sy = self.f * 4 + self.cy
        self.sd = self.f * 4 + self.cd

    def at(self, f=None, c=None, z=None):
        return (
            self.f if f is None else f,
            self.c if c is None else c,
            self.z if z is None else z,
        )


def greet(devices):
    barrier = pltpu.get_barrier_semaphore()
    for device in devices:
        pl.semaphore_signal(barrier, inc=1, device_id=device, device_id_type=MESH)
    pl.semaphore_wait(barrier, len(devices))


def group_devices(me):
    return [
        me.at(c=me.cx),
        me.at(c=me.cy),
        me.at(c=me.cd),
        me.at(f=me.of),
        me.at(f=me.of, c=me.cx),
        me.at(f=me.of, c=me.cy),
        me.at(f=me.of, c=me.cd),
    ]


def column_devices(me):
    return [me.at(z=lax.rem(me.z + step, 4)) for step in (1, 2, 3)]


class Gather:
    def __init__(self, me, index, own, full, send, recv, local_sem):
        self.me, self.full, self.placed = me, full, own is None
        own = full.at[me.own] if own is None else own
        rows = full.shape[1]
        self.half_a = pl.ds(0, rows // 2)
        self.half_b = pl.ds(rows // 2, rows // 2)

        def copy(slot, src, dst, device):
            return remote(src, dst, send.at[index, slot], recv.at[index, slot], device)

        slot_own, slot_x, slot_y = full.at[me.own], full.at[me.sx], full.at[me.sy]
        to_x, to_y, to_core = me.at(c=me.cx), me.at(c=me.cy), me.at(f=me.of)
        diag_a = full.at[me.sd, self.half_a]
        diag_b = full.at[me.sd, self.half_b]
        self.own_x = copy(0, own, slot_own, to_x)
        self.own_y = copy(1, own, slot_own, to_y)
        self.own_core = copy(2, own, slot_own, to_core)
        self.pass_x = copy(3, full.at[me.sy, self.half_a], full.at[me.sy, self.half_a], to_x)
        self.pass_y = copy(4, full.at[me.sx, self.half_b], full.at[me.sx, self.half_b], to_y)
        self.core_x = copy(5, slot_x, slot_x, to_core)
        self.core_y = copy(6, slot_y, slot_y, to_core)
        self.core_a = copy(7, diag_a, diag_a, to_core)
        self.core_b = copy(8, diag_b, diag_b, to_core)
        other = me.of * 4
        into = lambda slot, ref, device: copy(slot, ref, ref, device)
        self.in_x = into(0, slot_x, to_x)
        self.in_y = into(1, slot_y, to_y)
        self.in_a = into(3, diag_a, to_x)
        self.in_b = into(4, diag_b, to_y)
        self.in_core = [
            into(2, full.at[other + me.c], to_core),
            into(5, full.at[other + me.cx], to_core),
            into(6, full.at[other + me.cy], to_core),
            into(7, full.at[other + me.cd, self.half_a], to_core),
            into(8, full.at[other + me.cd, self.half_b], to_core),
        ]
        self.keep = None if self.placed else pltpu.make_async_copy(own, slot_own, local_sem.at[index])

    def begin(self):
        self.own_x.start()
        self.own_y.start()
        self.own_core.start()
        if not self.placed:
            self.keep.start()

    def forward_a(self):
        self.in_y.wait_recv()
        self.pass_x.start()
        self.core_y.start()

    def forward_b(self):
        self.in_x.wait_recv()
        self.pass_y.start()
        self.core_x.start()

    def diagonal_a(self):
        self.in_a.wait_recv()
        self.core_a.start()

    def diagonal_b(self):
        self.in_b.wait_recv()
        self.core_b.start()

    def arrive(self):
        if not self.placed:
            self.keep.wait()
        for piece in self.in_core:
            piece.wait_recv()

    def settle(self):
        for piece in (
            self.own_x,
            self.own_y,
            self.own_core,
            self.pass_x,
            self.pass_y,
            self.core_x,
            self.core_y,
            self.core_a,
            self.core_b,
        ):
            piece.wait_send()


class LineSum:
    def __init__(self, me, part, outer_in, inner_in, send, recv):
        self.me, self.part = me, part
        self.outer_in, self.inner_in = outer_in, inner_in
        self.send, self.recv = send, recv
        z = me.z
        self.is_mid = (z == 1) | (z == 2)
        self.is_end = (z == 0) | (z == 3)
        self.mid_of_end = 1 + z // 3
        self.outer_of_mid = 3 * (z - 1)

    def end_copies(self):
        me, part = self.me, self.part
        mid = self.mid_of_end
        to_mid = me.at(z=mid)
        owners = (3 - me.z, 3 - mid, mid)
        return [
            remote(
                part.at[owner],
                self.outer_in.at[slot],
                self.send.at[slot],
                self.recv.at[slot],
                to_mid,
            )
            for slot, owner in enumerate(owners)
        ]

    def mid_copies(self):
        me, part = self.me, self.part
        far_mid, outer = 3 - me.z, self.outer_of_mid
        far = 3 - outer
        to_mid, to_outer = me.at(z=far_mid), me.at(z=outer)
        return [
            remote(part.at[far], self.inner_in.at[0], self.send.at[0], self.recv.at[3], to_mid),
            remote(part.at[far_mid], self.inner_in.at[1], self.send.at[1], self.recv.at[4], to_mid),
            remote(part.at[outer], self.inner_in.at[0], self.send.at[2], self.recv.at[3], to_outer),
        ]

    def wait_in(self, slot, buffer):
        remote(buffer, buffer, self.send.at[0], self.recv.at[slot], self.me.at(z=3 - self.me.z)).wait_recv()

    def add(self, owner, buffer):
        self.part[owner] = (self.part[owner].astype(F32) + buffer[...].astype(F32)).astype(BF)

    def begin(self):
        @pl.when(self.is_end)
        def _():
            for piece in self.end_copies():
                piece.start()

    def step_one(self):
        @pl.when(self.is_mid)
        def _():
            far = 3 - self.outer_of_mid
            self.wait_in(0, self.outer_in.at[0])
            self.add(far, self.outer_in.at[0])
            self.mid_copies()[0].start()

    def step_two(self):
        @pl.when(self.is_mid)
        def _():
            copies = self.mid_copies()
            self.wait_in(1, self.outer_in.at[1])
            self.add(3 - self.me.z, self.outer_in.at[1])
            copies[1].start()

    def step_three(self):
        @pl.when(self.is_mid)
        def _():
            self.wait_in(3, self.inner_in.at[0])
            self.add(self.outer_of_mid, self.inner_in.at[0])
            self.mid_copies()[2].start()

    def finish(self, total):
        me = self.me

        @pl.when(self.is_mid)
        def _():
            self.wait_in(2, self.outer_in.at[2])
            self.wait_in(4, self.inner_in.at[1])
            total[...] = (
                self.part[me.z].astype(F32)
                + self.outer_in[2].astype(F32)
                + self.inner_in[1].astype(F32)
            )
            for piece in self.mid_copies():
                piece.wait_send()

        @pl.when(self.is_end)
        def _():
            self.wait_in(3, self.inner_in.at[0])
            total[...] = self.part[me.z].astype(F32) + self.inner_in[0].astype(F32)
            for piece in self.end_copies():
                piece.wait_send()


class LineGather:
    def __init__(self, me, blocks, send, recv):
        self.me, self.blocks, self.send, self.recv = me, blocks, send, recv
        z = me.z
        self.is_mid = (z == 1) | (z == 2)
        self.is_end = (z == 0) | (z == 3)
        self.mid_of_end = 1 + z // 3
        self.outer_of_mid = 3 * (z - 1)

    def copy(self, owner, slot, z):
        ref = self.blocks.at[owner]
        return remote(ref, ref, self.send.at[slot], self.recv.at[owner], self.me.at(z=z))

    def wait_in(self, owner):
        ref = self.blocks.at[owner]
        remote(ref, ref, self.send.at[0], self.recv.at[owner], self.me.at(z=3 - self.me.z)).wait_recv()

    def begin(self):
        me = self.me

        @pl.when(self.is_end)
        def _():
            self.copy(me.z, 0, self.mid_of_end).start()

        @pl.when(self.is_mid)
        def _():
            self.copy(me.z, 0, self.outer_of_mid).start()
            self.copy(me.z, 1, 3 - me.z).start()

    def step_one(self):
        me = self.me

        @pl.when(self.is_mid)
        def _():
            self.wait_in(self.outer_of_mid)
            self.copy(self.outer_of_mid, 2, 3 - me.z).start()

    def step_two(self):
        me = self.me

        @pl.when(self.is_mid)
        def _():
            self.wait_in(3 - me.z)
            self.copy(3 - me.z, 3, self.outer_of_mid).start()

    def step_three(self):
        @pl.when(self.is_mid)
        def _():
            far = 3 - self.outer_of_mid
            self.wait_in(far)
            self.copy(far, 4, self.outer_of_mid).start()

    def finish(self):
        me = self.me

        @pl.when(self.is_mid)
        def _():
            self.copy(me.z, 0, self.outer_of_mid).wait_send()
            self.copy(me.z, 1, 3 - me.z).wait_send()
            self.copy(self.outer_of_mid, 2, 3 - me.z).wait_send()
            self.copy(3 - me.z, 3, self.outer_of_mid).wait_send()
            self.copy(3 - self.outer_of_mid, 4, self.outer_of_mid).wait_send()

        @pl.when(self.is_end)
        def _():
            mid = self.mid_of_end
            self.wait_in(mid)
            self.wait_in(3 - mid)
            self.wait_in(3 - me.z)
            self.copy(me.z, 0, mid).wait_send()


def row_of(gains_ref, which):
    return jnp.concatenate([gains_ref[shard, which : which + 1, :] for shard in range(8)], axis=-1)


def swap_halves(rows):
    lane = lax.broadcasted_iota(jnp.int32, rows.shape, 1)
    return jnp.where(
        lax.rem(lane, HD) < HD // 2, pltpu.roll(rows, 96, 1), pltpu.roll(rows, 32, 1)
    )


class Scatter:
    def __init__(self, me, index, last, width, x_of, y_of, chips, refs):
        self.me, self.index, self.last, self.width = me, index, last, width
        self.x_of, self.y_of, self.chips = x_of, y_of, chips
        self.stage, self.core_in, self.diag_in, self.near_in = refs[:4]
        self.send, self.recv, self.credit = refs[4:]
        self.columns = (me.c, me.cx, me.cy, me.cd)
        self.to_x, self.to_y, self.to_core = me.at(c=me.cx), me.at(c=me.cy), me.at(f=me.of)
        self.sent = []

    def copy(self, slot, src, dst, device):
        return remote(
            src, dst, self.send.at[self.index, slot], self.recv.at[self.index, slot], device
        )

    def lanes(self, ref):
        return ref.at[:, pl.ds(0, self.width)]

    def core_copy(self, role):
        return self.copy(
            role, self.stage(self.width, role), self.lanes(self.core_in.at[role]), self.to_core
        )

    def chunk(self, shard):
        return dotg(self.x_of(shard), self.y_of(), 0, 0)

    def partner(self):
        me = self.me
        for role in (3, 1, 2, 0):
            self.stage(self.width, role)[...] = self.chunk(
                me.of * 4 + self.columns[role]
            ).astype(BF)
            if self.index > 0:
                pl.semaphore_wait(self.credit.at[role], 1)
            self.core_copy(role).start()

    def near(self, role, half, slot):
        rows = pl.ds(half * 128, 128)
        side = role - 1
        device = self.to_x if role == 1 else self.to_y
        return self.copy(
            slot, self.chips(role).at[rows, :], self.near_in.at[side, rows, :], device
        )

    def diag(self, half):
        device = self.to_x if half == 0 else self.to_y
        return self.copy(
            4 + half,
            self.chips(3).at[pl.ds(half * 128, 128), :],
            self.lanes(self.diag_in.at[half]),
            device,
        )

    def own(self):
        me = self.me
        for role in (3, 1, 2, 0):
            value = self.chunk(me.f * 4 + self.columns[role])
            self.core_copy(role).wait_recv()
            chip = self.chips(role)
            chip[...] = (value + self.lanes(self.core_in.at[role])[...].astype(F32)).astype(BF)
            if not self.last:
                pl.semaphore_signal(
                    self.credit.at[role], inc=1, device_id=self.to_core, device_id_type=MESH
                )
        for role in range(4):
            self.core_copy(role).wait_send()

    def push_diag(self):
        self.diag(0).start()
        self.diag(1).start()

    def push_near(self):
        self.near(1, 0, 6).start()
        self.near(2, 1, 7).start()

    def relay_a(self):
        first = pl.ds(0, 128)
        self.diag(0).wait_recv()
        rows = self.chips(2).at[first, :]
        rows[...] = (
            rows[...].astype(F32) + self.lanes(self.diag_in.at[0])[...].astype(F32)
        ).astype(BF)
        self.near(2, 0, 8).start()

    def relay_b(self):
        second = pl.ds(128, 128)
        self.diag(1).wait_recv()
        rows = self.chips(1).at[second, :]
        rows[...] = (
            rows[...].astype(F32) + self.lanes(self.diag_in.at[1])[...].astype(F32)
        ).astype(BF)
        self.near(1, 1, 9).start()

    def collect(self, buffer, sem):
        for role, half, slot in ((1, 0, 6), (2, 1, 7), (2, 0, 8), (1, 1, 9)):
            self.near(role, half, slot).wait_recv()
        for side in range(2):
            pltpu.make_async_copy(
                self.near_in.at[side], self.lanes(buffer.at[side]), sem.at[side]
            ).start()

    def collected(self, buffer, sem):
        for side in range(2):
            pltpu.make_async_copy(
                self.near_in.at[side], self.lanes(buffer.at[side]), sem.at[side]
            ).wait()

    def settle(self):
        for half in range(2):
            self.diag(half).wait_send()
        for role, half, slot in ((1, 0, 6), (2, 1, 7), (2, 0, 8), (1, 1, 9)):
            self.near(role, half, slot).wait_send()


def norm_back(gradient, rows_in, gain):
    inv = lax.rsqrt(jnp.mean(rows_in * rows_in, axis=-1, keepdims=True) + EPSILON)
    unit = rows_in * inv
    scaled = gradient * gain
    back = inv * (scaled - unit * jnp.mean(scaled * unit, axis=-1, keepdims=True))
    return back, jnp.sum(gradient * unit, axis=0, keepdims=True)


def layer_kernel(
    tok_h,
    gain_one_in,
    w_query_in,
    w_key_in,
    w_value_in,
    out_h,
    gain_two_in,
    gate_h,
    up_h,
    down_h,
    cot_h,
    pos_in,
    seg_in,
    freq,
    o_result,
    o_input,
    o_gain_one,
    o_gain_two,
    o_query,
    o_key,
    o_value,
    o_out,
    o_gate,
    o_up,
    o_down,
    near_down,
    near_gate,
    near_up,
    near_out,
    near_qkv,
    n_one_h,
    own_gains,
    own_marks,
    gains,
    marks,
    tok,
    w_gate,
    w_up,
    w_down,
    w_out,
    w_qkv,
    cot,
    n_two,
    hid,
    gate_g,
    up_g,
    core_in,
    diag_in,
    diag_low,
    chip_out,
    chip_qkv,
    sum_stage,
    turn_stage,
    part,
    outer_in,
    inner_in,
    outer_two,
    inner_two,
    mlow,
    total,
    own_out,
    mid,
    mid_g,
    q_rot,
    bias,
    lse,
    kv,
    att,
    rope,
    do_rows,
    keys,
    vals_t,
    vals,
    keys_t,
    key_acc,
    val_acc,
    kv_send_buf,
    kv_in,
    d_qkv,
    vec,
    vec_in,
    vec_out,
    vec_near,
    g_send,
    g_recv,
    g_local,
    small_send,
    small_recv,
    first_send,
    first_recv,
    load_sem,
    sum_send,
    sum_recv,
    all_send,
    all_recv,
    rs_send,
    rs_recv,
    credit,
    kv_send,
    kv_recv,
    vec_send,
    vec_recv,
    fin_sem,
    put_sem,
    own_sem,
):
    me = Place()
    group = group_devices(me)
    hidden = hid.shape[1]

    rows_of = [pl.ds(g * 256, 256) for g in range(2)]
    load_tok = pltpu.make_async_copy(tok_h, tok, load_sem.at[0])
    load_cot = pltpu.make_async_copy(cot_h, cot, load_sem.at[1])
    save_one = pltpu.make_async_copy(mlow, n_one_h, load_sem.at[2])
    load_one = pltpu.make_async_copy(n_one_h, mlow, load_sem.at[3])
    load_tok.start()
    load_cot.start()

    w_qkv[me.own, :, 0:512] = w_query_in[...]
    turned = jnp.concatenate([w_key_in[...], w_value_in[...]], axis=0).astype(F32)
    w_qkv[me.own, :, 512:640] = jnp.transpose(turned).astype(BF)
    own_gains[0:1, :] = gain_one_in[...].astype(F32)
    own_gains[1:2, :] = gain_two_in[...].astype(F32)
    own_gains[2:8, :] = jnp.zeros((6, 256), F32)
    own_marks[0:1, :] = pos_in[...]
    own_marks[1:2, :] = seg_in[...]
    own_marks[2:8, :] = jnp.zeros((6, 512), jnp.int32)
    greet(group + column_devices(me))

    qkv = Gather(me, 0, None, w_qkv, g_send, g_recv, g_local)
    out = Gather(me, 1, out_h, w_out, g_send, g_recv, g_local)
    gate = Gather(me, 2, gate_h, w_gate, g_send, g_recv, g_local)
    up = Gather(me, 3, up_h, w_up, g_send, g_recv, g_local)
    down = Gather(me, 4, down_h, w_down, g_send, g_recv, g_local)

    sources = [me.sx, me.sy, me.sd, me.of * 4 + me.c, me.of * 4 + me.cx, me.of * 4 + me.cy, me.of * 4 + me.cd]

    def small_copies(gain_slots, mark_slots):
        return [
            remote(own_gains, gains.at[spot], small_send.at[slot], small_recv.at[slot], group[slot])
            for slot, spot in enumerate(gain_slots)
        ] + [
            remote(
                own_marks, marks.at[spot], small_send.at[7 + slot], small_recv.at[7 + slot], group[slot]
            )
            for slot, spot in enumerate(mark_slots)
        ]

    small = small_copies([me.own] * 7, [me.c] * 3)

    def small_begin():
        for piece in small:
            piece.start()
        gains[me.own] = own_gains[...]
        marks[me.c] = own_marks[...]

    def small_finish():
        for piece in small_copies(sources, (me.cx, me.cy, me.cd)):
            piece.wait_recv()

    def first_norm():
        load_tok.wait()
        gain_one = row_of(gains, 0)

        def body(step, carry):
            values = tok[pl.ds(pl.multiple_of(step * 64, 64), 64), :].astype(F32)
            inv = lax.rsqrt(jnp.mean(values * values, axis=-1, keepdims=True) + EPSILON)
            mlow[step // 4, lax.rem(step, 4)] = (values * inv * gain_one).astype(BF)
            return carry

        lax.fori_loop(0, 8, body, 0)
        save_one.start()

    def make_rope():
        lane = lax.broadcasted_iota(jnp.int32, (128, 128), 1)
        low_half = lax.rem(lane, HD) < HD // 2
        for step in range(4):
            rows = slice(step * 128, (step + 1) * 128)
            places = own_marks[0:1, rows].astype(F32)
            angles = jnp.transpose(jnp.broadcast_to(places, (128, 128))) * freq[...]
            sine = jnp.sin(angles)
            rope[rows, :128] = jnp.cos(angles)
            rope[rows, 128:] = jnp.where(low_half, -sine, sine)

    def make_bias(g):
        own_rows = own_marks[:, g * 256 : (g + 1) * 256].astype(F32)
        for source in range(4):
            key_rows = marks[source, :, g * 256 : (g + 1) * 256].astype(F32)
            key_pos = jnp.transpose(jnp.broadcast_to(key_rows[0:1, :], (128, 256)))
            key_seg = jnp.transpose(jnp.broadcast_to(key_rows[1:2, :], (128, 256)))
            for side in range(2):
                lanes = slice(side * 128, (side + 1) * 128)
                seen = (key_seg == own_rows[1:2, lanes]) & (key_pos <= own_rows[0:1, lanes])
                bias[g, source * 256 : (source + 1) * 256, lanes] = jnp.where(
                    seen, 0.0, MASKED_SCORE
                ).astype(BF)

    lane_pair = lax.broadcasted_iota(jnp.int32, (256, 128), 1)

    def project_in(first, width):
        total_rows = None
        for shard in range(8):
            term = dotg(
                mlow[:, :, :, shard * 256 : (shard + 1) * 256].reshape(512, 256),
                w_qkv[shard, :, first : first + width],
                1,
                0,
            )
            total_rows = term if total_rows is None else total_rows + term
        return total_rows

    def first_copies(places):
        return [
            remote(kv.at[place], kv.at[place], first_send.at[slot], first_recv.at[slot], group[slot])
            for slot, place in enumerate(places)
        ]

    def project_kv():
        rows = project_in(512, 128)
        is_key = lax.broadcasted_iota(jnp.int32, (512, 128), 1) < HD
        cos_rows = jnp.where(is_key, rope[:, :128], 1.0)
        sin_rows = jnp.where(is_key, rope[:, 128:], 0.0)
        kv[me.c] = (rows * cos_rows + swap_halves(rows) * sin_rows).astype(BF)
        for piece in first_copies([me.c] * 3):
            piece.start()

    def project_q(half):
        rows_all = project_in(half * 256, 256)
        for inner in range(2):
            pair = half * 2 + inner
            rows = rows_all[:, inner * 128 : (inner + 1) * 128]
            rot = (rows * rope[:, :128] + swap_halves(rows) * rope[:, 128:]).astype(BF)
            rot = rot * jnp.bfloat16(HD ** (-0.5))
            q_rot[:, pair * 128 : (pair + 1) * 128] = rot

    def kv_arrive():
        for piece in first_copies((me.cx, me.cy, me.cd)):
            piece.wait_recv()
        for g in range(2):
            for source in range(4):
                pairs = kv[source, g * 256 : (g + 1) * 256, :].astype(F32)
                rows = slice(source * 256, (source + 1) * 256)
                keys[g, rows, :] = jnp.where(
                    lane_pair < HD, pairs, pltpu.roll(pairs, HD, 1)
                ).astype(BF)
                vals_t[g, :, rows] = jnp.transpose(pairs)[HD:, :].astype(BF)

    def one_head(pair_rows, odd):
        kept = lane_pair >= HD if odd else lane_pair < HD
        return jnp.where(kept, pair_rows, jnp.zeros_like(pair_rows))

    def attend(step):
        g = step // 4
        pair = step - g * 4
        halves = []
        own = pl.ds(pl.multiple_of(g * 256, 256), 256)
        lanes = pl.ds(pl.multiple_of(pair * 128, 128), 128)
        queries = q_rot[own, lanes]
        for odd in range(2):
            head = step * 2 + odd
            scores = dotg(keys[g], one_head(queries, odd), 1, 1) + bias[g].astype(F32)
            top = jnp.max(scores, axis=0, keepdims=True)
            weights = jnp.exp(scores - top)
            norm = jnp.sum(weights, axis=0, keepdims=True)
            mixed = dotg(vals_t[g], weights.astype(BF), 1, 0)
            halves.append(mixed / norm)
            lse[head] = top + jnp.log(norm)
        rows = jnp.transpose(jnp.concatenate(halves, axis=0))
        att[own, lanes] = rows.astype(BF)

    def project_out(g):
        def body(shard, carry):
            part[g, :, :, pl.ds(pl.multiple_of(shard * 256, 256), 256)] = (
                dotg(att[rows_of[g], :], w_out[shard], 1, 0).astype(BF).reshape(4, 64, 256)
            )
            return carry

        lax.fori_loop(0, 8, body, 0)

    def second_norm(g):
        sum_att[g].finish(total)
        own = pl.ds(pl.multiple_of(g * 256 + me.z * 64, 64), 64)
        mid_rows = tok[own, :].astype(F32) + total[...]
        mid[g] = mid_rows
        inv = lax.rsqrt(jnp.mean(mid_rows * mid_rows, axis=-1, keepdims=True) + EPSILON)
        n_two[g, me.z] = (mid_rows * inv * row_of(gains, 1)).astype(BF)
        spread_two[g].begin()

    def looped(body, count, hooks):
        def step(i, carry):
            for spot, actions in hooks:

                @pl.when(i == spot)
                def _():
                    for action, *values in actions:
                        action(*values)

            body(i)
            return carry

        lax.fori_loop(0, count, step, 0)

    tile_count = (hidden + 255) // 256

    def feed(step):
        g = step // tile_count
        n = step - g * tile_count
        rows = pl.ds(pl.multiple_of(g * 256, 256), 256)
        lanes = pl.ds(pl.multiple_of(jnp.minimum(n * 256, hidden - 256), 128), 256)
        normed = n_two[g].reshape(256, 2048)
        gate = dotg(normed, w_gate[:, :, lanes].reshape(2048, 256), 1, 0)
        up = dotg(normed, w_up[:, :, lanes].reshape(2048, 256), 1, 0)
        hidden_grad = None
        for shard in range(8):
            term = dotg(
                cot[rows, shard * 256 : (shard + 1) * 256], w_down[shard, lanes, :], 1, 1
            )
            hidden_grad = term if hidden_grad is None else hidden_grad + term
        sig = jax.nn.sigmoid(gate)
        silu = gate * sig
        hid[rows, lanes] = (silu * up).astype(BF)
        up_g[rows, lanes] = (hidden_grad * silu).astype(BF)
        gate_g[rows, lanes] = (
            hidden_grad * up * sig * (1.0 + gate * (1.0 - sig))
        ).astype(BF)

    def feed_back(g):
        def body(shard, carry):
            term = dotg(gate_g[rows_of[g], :], w_gate[shard], 1, 1) + dotg(
                up_g[rows_of[g], :], w_up[shard], 1, 1
            )
            part[g, :, :, pl.ds(pl.multiple_of(shard * 256, 256), 256)] = term.astype(BF).reshape(
                4, 64, 256
            )
            return carry

        lax.fori_loop(0, 8, body, 0)

    part_two = n_two

    def feed_out(g):
        def body(shard, carry):
            term = dotg(hid[rows_of[g], :], w_down[shard], 1, 0)
            part_two[g, :, :, pl.ds(pl.multiple_of(shard * 256, 256), 256)] = term.astype(
                BF
            ).reshape(4, 64, 256)
            return carry

        lax.fori_loop(0, 8, body, 0)

    def line_sum(slot, part_ref, outer, inner):
        return LineSum(me, part_ref, outer, inner, sum_send.at[slot], sum_recv.at[slot])

    sum_two = [line_sum(g, part.at[g], outer_in.at[g], inner_in.at[g]) for g in range(2)]
    sum_one = [line_sum(2 + g, part.at[g], outer_in.at[g], inner_in.at[g]) for g in range(2)]

    sum_out = [
        line_sum(4 + g, part_two.at[g], outer_two.at[g], inner_two.at[g]) for g in range(2)
    ]
    sum_att = [line_sum(6 + g, part.at[g], outer_in.at[g], inner_in.at[g]) for g in range(2)]
    spread_two = [LineGather(me, n_two.at[g], all_send.at[6 + g], all_recv.at[6 + g]) for g in range(2)]
    spread_mid = [LineGather(me, mlow.at[g], all_send.at[g], all_recv.at[g]) for g in range(2)]
    spread_in = [LineGather(me, o_input.at[g], all_send.at[2 + g], all_recv.at[2 + g]) for g in range(2)]
    spread_out = [LineGather(me, o_result.at[g], all_send.at[4 + g], all_recv.at[4 + g]) for g in range(2)]

    def middle_back(g):
        sum_two[g].finish(total)
        own = pl.ds(pl.multiple_of(g * 256 + me.z * 64, 64), 64)
        back, gain_grad = norm_back(total[...], mid[g], row_of(gains, 1))
        if g == 0:
            vec[1:2, :] = gain_grad
        else:
            vec[1:2, :] += gain_grad
        grad = cot[own, :].astype(F32) + back
        mid_g[g] = grad
        mlow[g, me.z] = grad.astype(BF)
        spread_mid[g].begin()

    def put_own(g, ref, slot):
        copy = pltpu.make_async_copy(own_out, ref.at[g, me.z], own_sem.at[slot])
        copy.start()
        copy.wait()

    def input_back(g):
        sum_one[g].finish(total)
        own = pl.ds(pl.multiple_of(g * 256 + me.z * 64, 64), 64)
        back, gain_grad = norm_back(total[...], tok[own, :].astype(F32), row_of(gains, 0))
        if g == 0:
            vec[0:1, :] = gain_grad
        else:
            vec[0:1, :] += gain_grad
        own_out[...] = (mid_g[g] + back).astype(BF)
        put_own(g, o_input, 0)
        spread_in[g].begin()

    def result_rows(g):
        sum_out[g].finish(total)
        own_out[...] = (mid[g] + total[...]).astype(BF)
        put_own(g, o_result, 1)
        spread_out[g].begin()

    wide = lambda ref: (lambda shard: ref[:, pl.ds(pl.multiple_of(shard * 256, 256), 256)])

    def blocks_of(ref):
        return lambda shard: ref[
            :, :, :, pl.ds(pl.multiple_of(shard * 256, 256), 256)
        ].reshape(512, 256)

    def stage(width, slot):
        if width > 640:
            return w_up.at[4 + slot]
        return w_up.at[4 + slot // 2, :, pl.ds((slot % 2) * 640, width)]

    landing = w_up.at[pl.ds(6, 2)]

    def scatter(index, width, x_of, y_of, chips, near):
        landed = diag_in.at[index] if index < 3 else diag_low.at[index - 3]
        refs = (stage, core_in, landed, near, rs_send, rs_recv, credit)
        return Scatter(me, index, index == 4, width, x_of, y_of, chips, refs)

    rs_down = scatter(
        0, hidden, wide(cot), lambda: hid[...], lambda role: w_gate.at[4 + role], near_down
    )
    rs_gate = scatter(
        1, hidden, blocks_of(n_two), lambda: gate_g[...], lambda role: w_gate.at[role], near_gate
    )
    rs_up = scatter(
        2, hidden, blocks_of(n_two), lambda: up_g[...], lambda role: w_up.at[role], near_up
    )
    rs_out = scatter(3, 512, blocks_of(mlow), lambda: att[...], lambda role: chip_out.at[role], near_out)
    rs_qkv = scatter(
        4,
        640,
        blocks_of(mlow),
        lambda: d_qkv[...],
        lambda role: chip_qkv.at[role],
        near_qkv,
    )

    def finish_rows(job, outs):
        job.collected(landing, fin_sem)
        width = job.width
        pending = [None, None]
        for step in range(4):
            slot = step % 2
            rows = slice(step * 64, (step + 1) * 64)
            if pending[slot] is not None:
                for piece in pending[slot]:
                    piece.wait()
            sum_stage[slot, :, :width] = (
                job.chips(0)[rows, :].astype(F32)
                + landing[0, rows, :width].astype(F32)
                + landing[1, rows, :width].astype(F32)
            )
            pending[slot] = [
                pltpu.make_async_copy(
                    sum_stage.at[slot, :, pl.ds(first, size)],
                    ref.at[pl.ds(step * 64, 64), :],
                    put_sem.at[slot, number],
                )
                for number, (ref, first, size) in enumerate(outs)
            ]
            for piece in pending[slot]:
                piece.start()
        for slot in range(2):
            for piece in pending[slot]:
                piece.wait()

    def finish_qkv(job):
        finish_rows(job, [(o_query, 0, 512)])
        lanes = slice(512, 640)
        turn_stage[0] = jnp.transpose(
            job.chips(0)[:, lanes].astype(F32)
            + landing[0, :, lanes].astype(F32)
            + landing[1, :, lanes].astype(F32)
        )
        copies = [
            pltpu.make_async_copy(
                turn_stage.at[0, pl.ds(first, HD), :], ref, put_sem.at[0, number]
            )
            for number, (first, ref) in enumerate(((0, o_key), (HD, o_value)))
        ]
        for piece in copies:
            piece.start()
        for piece in copies:
            piece.wait()

    def finish_turned(job, ref):
        job.collected(landing, fin_sem)
        pending = [None, None]
        for step in range(job.width // 128):
            slot = step % 2
            lanes = slice(step * 128, (step + 1) * 128)
            if pending[slot] is not None:
                pending[slot].wait()
            turn_stage[slot] = jnp.transpose(
                job.chips(0)[:, lanes].astype(F32)
                + landing[0, :, lanes].astype(F32)
                + landing[1, :, lanes].astype(F32)
            )
            pending[slot] = pltpu.make_async_copy(
                turn_stage.at[slot], ref.at[pl.ds(step * 128, 128), :], put_sem.at[slot, 0]
            )
            pending[slot].start()
        for piece in pending:
            piece.wait()

    def out_back(g):
        grad = None
        for shard in range(8):
            lanes = slice(shard * 256, (shard + 1) * 256)
            term = dotg(mlow[g, :, :, lanes].reshape(256, 256), w_out[shard], 1, 1)
            grad = term if grad is None else grad + term
        do_rows[...] = grad.astype(BF)
        for source in range(4):
            pairs = kv[source, rows_of[g], :].astype(F32)
            turned = pltpu.roll(pairs, HD, 1)
            rows = slice(source * 256, (source + 1) * 256)
            vals[rows, :] = jnp.where(lane_pair < HD, turned, pairs).astype(BF)
            keys_t[:, rows] = jnp.transpose(pairs)[:HD, :].astype(BF)
        key_acc[...] = jnp.zeros_like(key_acc)
        val_acc[...] = jnp.zeros_like(val_acc)

    def attend_back(step):
        g = step // 4
        pair = step - g * 4
        own = pl.ds(pl.multiple_of(g * 256, 256), 256)
        halves = []
        lanes = pl.ds(pl.multiple_of(pair * 128, 128), 128)
        queries, grads = q_rot[own, lanes], do_rows[:, lanes]
        for odd in range(2):
            query, grad = one_head(queries, odd), one_head(grads, odd)
            scores = dotg(keys[g], query, 1, 1) + bias[g].astype(F32)
            probs = jnp.exp(scores - lse[step * 2 + odd])
            prob_grad = dotg(vals[...], grad, 1, 1)
            delta = jnp.sum(probs * prob_grad, axis=0, keepdims=True)
            score_grad = (probs * (prob_grad - delta)).astype(BF)
            val_acc[...] += dotg(probs.astype(BF), grad, 1, 0)
            key_acc[...] += dotg(score_grad, query, 1, 0)
            halves.append(dotg(keys_t[...], score_grad, 1, 0))
        rows = jnp.transpose(jnp.concatenate(halves, axis=0)) * (HD ** (-0.5))
        rows = rows * rope[own, :128] - swap_halves(rows) * rope[own, 128:]
        d_qkv[own, lanes] = rows.astype(BF)

    def kv_copies(g):
        return [
            remote(
                kv_send_buf.at[g, column],
                kv_in.at[g, slot],
                kv_send.at[g, slot],
                kv_recv.at[g, slot],
                group[slot],
            )
            for slot, column in enumerate((me.cx, me.cy, me.cd))
        ]

    def kv_begin(g):
        for block in range(4):
            rows = slice(block * 256, (block + 1) * 256)
            key_rows, val_rows = key_acc[rows, :], val_acc[rows, :]
            joined = jnp.where(
                lane_pair < HD,
                key_rows + pltpu.roll(key_rows, HD, 1),
                val_rows + pltpu.roll(val_rows, HD, 1),
            )
            kv_send_buf[g, block] = joined.astype(BF)
        for piece in kv_copies(g):
            piece.start()

    def kv_finish(g):
        rows = kv_send_buf[g, me.c].astype(F32)
        for slot, piece in enumerate(kv_copies(g)):
            piece.wait_recv()
            rows = rows + kv_in[g, slot].astype(F32)
        cos_rows = jnp.where(lane_pair < HD, rope[rows_of[g], :128], 1.0)
        sin_rows = jnp.where(lane_pair < HD, rope[rows_of[g], 128:], 0.0)
        rows = rows * cos_rows - swap_halves(rows) * sin_rows
        d_qkv[rows_of[g], 512:640] = rows.astype(BF)

    def project_back_rows(g):
        def body(shard, carry):
            term = dotg(d_qkv[rows_of[g], :], w_qkv[shard], 1, 1)
            part[g, :, :, pl.ds(pl.multiple_of(shard * 256, 256), 256)] = term.astype(BF).reshape(
                4, 64, 256
            )
            return carry

        lax.fori_loop(0, 8, body, 0)

    line = column_devices(me)

    def vec_line():
        return [
            remote(vec_out, vec_in.at[slot], vec_send.at[slot], vec_recv.at[slot], device)
            for slot, device in enumerate(line)
        ]

    targets = [me.sx, me.sy, me.sd, me.of * 4 + me.c, me.of * 4 + me.cx, me.of * 4 + me.cy, me.of * 4 + me.cd]

    def vec_group():
        return [
            remote(
                vec_in.at[3, target],
                vec_near.at[slot],
                vec_send.at[3 + slot],
                vec_recv.at[3 + slot],
                device,
            )
            for slot, (target, device) in enumerate(zip(targets, group))
        ]

    def vec_begin():
        for shard in range(8):
            for which in range(2):
                for half in range(2):
                    first = shard * 256 + half * 128
                    vec_out[shard, 2 * which + half : 2 * which + half + 1, :] = vec[
                        which : which + 1, first : first + 128
                    ]
            vec_out[shard, 4:8, :] = jnp.zeros((4, 128), F32)
        for piece in vec_line():
            piece.start()

    def vec_middle():
        for piece in vec_line():
            piece.wait_recv()
        vec_in[3] = vec_out[...] + vec_in[0] + vec_in[1] + vec_in[2]
        for piece in vec_group():
            piece.start()

    def vec_finish():
        rows = vec_in[3, me.own]
        for slot, piece in enumerate(vec_group()):
            piece.wait_recv()
            rows = rows + vec_near[slot]
        o_gain_one[...] = rows[0:2, :]
        o_gain_two[...] = rows[2:4, :]

    def settle_weights():
        for piece in (qkv, out, gate, up, down):
            piece.settle()

    def settle():
        for spread in spread_in + spread_out:
            spread.finish()
        for job in (rs_down, rs_gate, rs_up, rs_out, rs_qkv):
            job.settle()
        for g in range(2):
            for piece in kv_copies(g):
                piece.wait_send()
        for piece in vec_line() + vec_group() + small + first_copies([me.c] * 3):
            piece.wait_send()

    order = (
        (small_begin,),
        (qkv.begin,),
        (small_finish,),
        (first_norm,),
        (qkv.forward_a,),
        (qkv.forward_b,),
        (out.begin,),
        (make_rope,),
        (qkv.diagonal_a,),
        (qkv.diagonal_b,),
        (make_bias, 0),
        (qkv.arrive,),
        (project_kv,),
        (make_bias, 1),
        (out.forward_a,),
        (out.forward_b,),
        (project_q, 0),
        (project_q, 1),
        (save_one.wait,),
        (down.begin,),
        (kv_arrive,),
        (
            looped,
            attend,
            8,
            (
                (2, ((out.diagonal_a,), (up.begin,), (load_cot.wait,), (out.diagonal_b,), (out.arrive,),)),
                (4, ((project_out, 0), (sum_att[0].begin,), (sum_att[0].step_one,),)),
                (6, ((sum_att[0].step_two,), (gate.begin,),)),
            ),
        ),
        (project_out, 1),
        (sum_att[1].begin,),
        (sum_att[1].step_one,),
        (sum_att[0].step_three,),
        (down.forward_a,),
        (second_norm, 0),
        (sum_att[1].step_two,),
        (sum_att[1].step_three,),
        (spread_two[0].step_two,),
        (up.forward_a,),
        (spread_two[0].step_one,),
        (down.forward_b,),
        (gate.forward_a,),
        (down.diagonal_a,),
        (up.forward_b,),
        (spread_two[0].step_three,),
        (second_norm, 1),
        (down.diagonal_b,),
        (up.diagonal_a,),
        (down.arrive,),
        (spread_two[1].step_one,),
        (gate.forward_b,),
        (up.diagonal_b,),
        (spread_two[1].step_three,),
        (spread_two[0].finish,),
        (spread_two[1].step_two,),
        (gate.diagonal_a,),
        (gate.diagonal_b,),
        (up.arrive,),
        (gate.arrive,),
        (
            looped,
            feed,
            2 * tile_count,
            (
                (6, ((feed_back, 0), (sum_two[0].begin,), (settle_weights,), (spread_two[1].finish,),)),
                (9, ((sum_two[0].step_one,),)),
            ),
        ),
        (feed_back, 1),
        (sum_two[1].begin,),
        (sum_two[0].step_two,),
        (rs_down.partner,),
        (sum_two[0].step_three,),
        (rs_down.own,),
        (rs_gate.partner,),
        (sum_two[1].step_one,),
        (middle_back, 0),
        (rs_down.push_near,),
        (rs_down.push_diag,),
        (rs_gate.own,),
        (sum_two[1].step_three,),
        (sum_two[1].step_two,),
        (rs_up.partner,),
        (rs_up.own,),
        (feed_out, 0),
        (spread_mid[0].step_one,),
        (rs_up.push_near,),
        (spread_mid[0].step_two,),
        (middle_back, 1),
        (rs_gate.push_diag,),
        (spread_mid[0].step_three,),
        (spread_mid[1].step_one,),
        (feed_out, 1),
        (spread_mid[1].step_two,),
        (sum_out[0].begin,),
        (spread_mid[0].finish,),
        (sum_out[0].step_one,),
        (sum_out[1].begin,),
        (out_back, 0),
        (sum_out[0].step_two,),
        (spread_mid[1].step_three,),
        (
            looped,
            attend_back,
            8,
            (
                (2, ((sum_out[0].step_three,),)),
                (4, ((kv_begin, 0), (spread_mid[1].finish,), (sum_out[1].step_one,), (out_back, 1),)),
                (6, ((sum_out[1].step_two,), (result_rows, 0), (kv_finish, 0), (sum_out[1].step_three,), (rs_out.partner,),)),
            ),
        ),
        (project_back_rows, 0),
        (rs_up.push_diag,),
        (sum_one[0].begin,),
        (result_rows, 1),
        (kv_begin, 1),
        (spread_out[0].step_two,),
        (rs_out.own,),
        (spread_out[0].step_one,),
        (sum_one[0].step_one,),
        (rs_gate.push_near,),
        (load_one.start,),
        (kv_finish, 1),
        (spread_out[1].step_two,),
        (sum_one[0].step_two,),
        (rs_out.push_diag,),
        (load_one.wait,),
        (rs_qkv.partner,),
        (rs_qkv.own,),
        (rs_qkv.push_near,),
        (spread_out[0].step_three,),
        (rs_gate.relay_a,),
        (project_back_rows, 1),
        (sum_one[1].begin,),
        (rs_qkv.push_diag,),
        (spread_out[1].step_one,),
        (rs_down.relay_a,),
        (sum_one[0].step_three,),
        (sum_one[1].step_one,),
        (rs_up.relay_a,),
        (rs_out.relay_a,),
        (rs_down.relay_b,),
        (spread_out[1].step_three,),
        (input_back, 0),
        (sum_one[1].step_three,),
        (rs_out.relay_b,),
        (sum_one[1].step_two,),
        (rs_gate.relay_b,),
        (rs_qkv.relay_a,),
        (spread_in[0].step_one,),
        (spread_in[0].step_two,),
        (rs_up.relay_b,),
        (input_back, 1),
        (rs_out.push_near,),
        (rs_down.collect, landing, fin_sem),
        (finish_turned, rs_down, o_down),
        (rs_gate.collect, landing, fin_sem),
        (finish_rows, rs_gate, [(o_gate, 0, hidden)]),
        (rs_qkv.relay_b,),
        (vec_begin,),
        (spread_in[0].step_three,),
        (rs_up.collect, landing, fin_sem),
        (finish_rows, rs_up, [(o_up, 0, hidden)]),
        (spread_in[1].step_one,),
        (spread_in[1].step_two,),
        (rs_out.collect, landing, fin_sem),
        (finish_turned, rs_out, o_out),
        (rs_qkv.collect, landing, fin_sem),
        (finish_qkv, rs_qkv),
        (vec_middle,),
        (vec_finish,),
        (spread_in[1].step_three,),
        (settle,),
    )
    for action, *values in order:
        action(*values)


def run_layer(
    tokens, attn_gain, w_query, w_key, w_value, w_out, mlp_gain, w_gate, w_up, w_down, cotangent,
    positions, segments,
):
    shape = jax.ShapeDtypeStruct
    width = tokens.shape[1]
    hidden = w_gate.shape[1]
    vmem = pl.BlockSpec(memory_space=pltpu.VMEM)
    anywhere = pl.BlockSpec(memory_space=pl.ANY)
    dma = pltpu.SemaphoreType.DMA
    buffer = pltpu.VMEM
    half_size = HD // 2
    frequency = THETA_BASE ** (-np.arange(half_size, dtype=np.float32) / half_size)
    frequency = np.concatenate([frequency] * 4)[None, :].astype(np.float32)
    return pl.pallas_call(
        layer_kernel,
        name="decoder_layer",
        out_shape=(
            shape((2, 4, 64, width), BF),
            shape((2, 4, 64, width), BF),
            shape((2, 128), F32),
            shape((2, 128), F32),
            shape((256, 512), F32),
            shape((HD, 256), F32),
            shape((HD, 256), F32),
            shape((512, 256), F32),
            shape((256, hidden), F32),
            shape((256, hidden), F32),
            shape((hidden, 256), F32),
            shape((2, 256, hidden), BF),
            shape((2, 256, hidden), BF),
            shape((2, 256, hidden), BF),
            shape((2, 256, 512), BF),
            shape((2, 256, 640), BF),
            shape((2, 4, 64, width), BF),
        ),
        in_specs=[anywhere, vmem, vmem, vmem, vmem, anywhere, vmem]
        + [anywhere] * 4
        + [vmem] * 3,
        out_specs=(anywhere,) * 2 + (vmem,) * 2 + (anywhere,) * 13,
        scratch_shapes=[
            buffer((8, 256), F32),
            buffer((8, 512), jnp.int32),
            buffer((8, 8, 256), F32),
            buffer((4, 8, 512), jnp.int32),
            buffer((512, width), BF),
            buffer((8, 256, hidden), BF),
            buffer((8, 256, hidden), BF),
            buffer((8, hidden, 256), BF),
            buffer((8, 512, 256), BF),
            buffer((8, 256, 640), BF),
            buffer((512, width), BF),
            buffer((2, 4, 64, width), BF),
            buffer((512, hidden), BF),
            buffer((512, hidden), BF),
            buffer((512, hidden), BF),
            buffer((4, 256, hidden), BF),
            buffer((3, 2, 128, hidden), BF),
            buffer((2, 2, 128, 640), BF),
            buffer((4, 256, 512), BF),
            buffer((4, 256, 640), BF),
            buffer((2, 64, hidden), F32),
            buffer((2, 128, 256), F32),
            buffer((2, 4, 64, width), BF),
            buffer((2, 3, 64, width), BF),
            buffer((2, 2, 64, width), BF),
            buffer((2, 3, 64, width), BF),
            buffer((2, 2, 64, width), BF),
            buffer((2, 4, 64, width), BF),
            buffer((64, width), F32),
            buffer((64, width), BF),
            buffer((2, 64, width), F32),
            buffer((2, 64, width), F32),
            buffer((512, 512), BF),
            buffer((2, 1024, 256), BF),
            buffer((16, 1, 256), F32),
            buffer((4, 512, 128), BF),
            buffer((512, 512), BF),
            buffer((512, 256), F32),
            buffer((256, 512), BF),
            buffer((2, 1024, 128), BF),
            buffer((2, HD, 1024), BF),
            buffer((1024, 128), BF),
            buffer((HD, 1024), BF),
            buffer((1024, 128), F32),
            buffer((1024, 128), F32),
            buffer((2, 4, 256, 128), BF),
            buffer((2, 3, 256, 128), BF),
            buffer((512, 640), BF),
            buffer((2, width), F32),
            buffer((4, 8, 8, 128), F32),
            buffer((8, 8, 128), F32),
            buffer((7, 8, 128), F32),
            dma((5, 9)),
            dma((5, 9)),
            dma((5,)),
            dma((10,)),
            dma((10,)),
            dma((3,)),
            dma((3,)),
            dma((4,)),
            dma((8, 3)),
            dma((8, 5)),
            dma((8, 5)),
            dma((8, 4)),
            dma((5, 10)),
            dma((5, 10)),
            pltpu.SemaphoreType.REGULAR((4,)),
            dma((2, 3)),
            dma((2, 3)),
            dma((10,)),
            dma((10,)),
            dma((2,)),
            dma((2, 2)),
            dma((2,)),
        ],
        compiler_params=pltpu.CompilerParams(
            collective_id=0, has_side_effects=True, vmem_limit_bytes=67043328
        ),
    )(
        tokens, attn_gain[None, :], w_query, w_key.T, w_value.T, w_out, mlp_gain[None, :], w_gate, w_up,
        w_down, cotangent, positions[None, :], segments[None, :], frequency,
    )


def fast_shards(tokens, *others):
    (
        result, input_grad, gain_one_g, gain_two_g, query_g, key_g, value_g, out_g, gate_g, up_g,
        down_g, *_,
    ) = run_layer(tokens, *others)
    return (
        result.reshape(tokens.shape),
        input_grad.reshape(tokens.shape),
        gain_one_g.reshape(-1),
        query_g,
        key_g.T,
        value_g.T,
        out_g,
        gain_two_g.reshape(-1),
        gate_g,
        up_g,
        down_g,
    )


def solution(mesh):
    in_specs = (
        P(("fsdp", "ctx"), None),
        P(("fsdp", "ctx")),
        P(("fsdp", "ctx"), "tp"),
        P(("fsdp", "ctx"), "tp"),
        P(("fsdp", "ctx"), "tp"),
        P("tp", ("fsdp", "ctx")),
        P(("fsdp", "ctx")),
        P(("fsdp", "ctx"), "tp"),
        P(("fsdp", "ctx"), "tp"),
        P("tp", ("fsdp", "ctx")),
        P(("fsdp", "ctx"), None),
        P(("fsdp", "ctx")),
        P(("fsdp", "ctx")),
    )
    out_specs = (
        P(("fsdp", "ctx"), None),
        P(("fsdp", "ctx"), None),
        P(("fsdp", "ctx")),
        P(("fsdp", "ctx"), "tp"),
        P(("fsdp", "ctx"), "tp"),
        P(("fsdp", "ctx"), "tp"),
        P("tp", ("fsdp", "ctx")),
        P(("fsdp", "ctx")),
        P(("fsdp", "ctx"), "tp"),
        P(("fsdp", "ctx"), "tp"),
        P("tp", ("fsdp", "ctx")),
    )
    small = (mesh.shape["fsdp"], mesh.shape["ctx"], mesh.shape["tp"]) == (2, 4, 4)
    return jax.shard_map(fast_shards if small else shards, mesh=mesh, in_specs=in_specs, out_specs=out_specs, check_vma=False)
```

```python
import jax
import jax.numpy as jnp
import numpy as np
from jax import lax
from jax.experimental import pallas as pl
from jax.experimental.pallas import tpu as pltpu
from jax.sharding import PartitionSpec as P

H = 32
KVH = 4
HD = 64


EPSILON = 1e-05
THETA_BASE = 10000.0
MASKED_SCORE = -1e30


def shifted(value, axis, steps):
    count = lax.axis_size(axis)
    pairs = [(source, (source + steps) % count) for source in range(count)]
    return lax.ppermute(value, axis, pairs)


def rope_tables(token_pos, half_size):
    frequency = THETA_BASE ** (-jnp.arange(half_size, dtype=jnp.float32) / half_size)
    angles = token_pos.astype(jnp.float32)[:, None] * frequency[None, :]
    return (jnp.cos(angles), jnp.sin(angles))


def rotate(head_rows, cosine, sine):
    half_size = head_rows.shape[-1] // 2
    first_half = head_rows[..., :half_size]
    second_half = head_rows[..., half_size:]
    cos_rows = cosine[:, None, :]
    sin_rows = sine[:, None, :]
    return jnp.concatenate(
        [
            first_half * cos_rows - second_half * sin_rows,
            second_half * cos_rows + first_half * sin_rows,
        ],
        axis=-1,
    )


def rotate_back(head_rows, cosine, sine):
    half_size = head_rows.shape[-1] // 2
    first_half = head_rows[..., :half_size]
    second_half = head_rows[..., half_size:]
    cos_rows = cosine[:, None, :]
    sin_rows = sine[:, None, :]
    return jnp.concatenate(
        [
            first_half * cos_rows + second_half * sin_rows,
            second_half * cos_rows - first_half * sin_rows,
        ],
        axis=-1,
    )


def project(left_side, right_side):
    return jnp.dot(left_side, right_side, preferred_element_type=jnp.float32)


def project_back(left_side, right_side):
    return lax.dot_general(
        left_side, right_side, (((1,), (1,)), ((), ())), preferred_element_type=jnp.float32
    )


def weight_grad(left_side, right_side):
    return lax.dot_general(
        left_side, right_side, (((0,), (0,)), ((), ())), preferred_element_type=jnp.float32
    )


def rms_norm(rows_in, gain_vec):
    inv_rms = lax.rsqrt(jnp.mean(rows_in * rows_in, axis=-1, keepdims=True) + EPSILON)
    unit_rows = rows_in * inv_rms
    return (unit_rows * gain_vec, unit_rows, inv_rms)


def rms_norm_back(gradient, gain_vec, unit_rows, inv_rms):
    gain_grad = jnp.sum(gradient * unit_rows, axis=0)
    scaled_grad = gradient * gain_vec
    return (
        inv_rms
        * (scaled_grad - unit_rows * jnp.mean(scaled_grad * unit_rows, axis=-1, keepdims=True)),
        gain_grad,
    )


def pair_mask(query_pos, query_seg, key_pos, key_seg):
    return (query_seg[:, None] == key_seg[None, :]) & (key_pos[None, :] <= query_pos[:, None])


def split_block(kv_block, kv_heads):
    key_rows = kv_block[:, : kv_heads * HD].reshape(-1, kv_heads, HD)
    value_rows = kv_block[:, kv_heads * HD :].reshape(-1, kv_heads, HD)
    return (key_rows, value_rows)


def attend_block(state_in, queries, kv_block, visible):
    row_top, row_total, output_sum = state_in
    key_rows, value_rows = split_block(kv_block, queries.shape[1])
    scores = jnp.einsum(
        "qkgd,pkd->kgqp", queries, key_rows, preferred_element_type=jnp.float32
    ) * HD ** (-0.5)
    scores = jnp.where(visible, scores, MASKED_SCORE)
    new_top = jnp.maximum(row_top, jnp.max(scores, axis=-1))
    weights = jnp.where(visible, jnp.exp(scores - new_top[..., None]), 0.0)
    decay_factor = jnp.exp(row_top - new_top)
    row_total = row_total * decay_factor + jnp.sum(weights, axis=-1)
    mixed_heads = jnp.einsum(
        "kgqp,pkd->qkgd",
        weights.astype(jnp.bfloat16),
        value_rows,
        preferred_element_type=jnp.float32,
    )
    output_sum = output_sum * jnp.transpose(decay_factor, (2, 0, 1))[..., None] + mixed_heads
    return (new_top, row_total, output_sum)


def block_grads(queries, out_grad, kv_block, visible, log_total, delta_rows):
    key_rows, value_rows = split_block(kv_block, queries.shape[1])
    scale_factor = HD ** (-0.5)
    scores = (
        jnp.einsum("qkgd,pkd->kgqp", queries, key_rows, preferred_element_type=jnp.float32)
        * scale_factor
    )
    probs_full = jnp.where(
        visible, jnp.exp(jnp.where(visible, scores, MASKED_SCORE) - log_total[..., None]), 0.0
    )
    value_grad = jnp.einsum(
        "kgqp,qkgd->pkd",
        probs_full.astype(jnp.bfloat16),
        out_grad,
        preferred_element_type=jnp.float32,
    )
    prob_grad = jnp.einsum(
        "qkgd,pkd->kgqp", out_grad, value_rows, preferred_element_type=jnp.float32
    )
    score_grad = (probs_full * (prob_grad - delta_rows[..., None])).astype(jnp.bfloat16)
    query_grad = (
        jnp.einsum("kgqp,pkd->qkgd", score_grad, key_rows, preferred_element_type=jnp.float32)
        * scale_factor
    )
    key_grad = (
        jnp.einsum("kgqp,qkgd->pkd", score_grad, queries, preferred_element_type=jnp.float32)
        * scale_factor
    )
    block_rows = kv_block.shape[0]
    return (
        query_grad,
        jnp.concatenate(
            [key_grad.reshape(block_rows, -1), value_grad.reshape(block_rows, -1)], axis=-1
        ),
    )


def shards(
    tokens,
    attn_gain,
    w_query,
    w_key,
    w_value,
    w_out,
    mlp_gain,
    w_gate,
    w_up,
    w_down,
    cotangent,
    positions,
    segments,
):
    token_rows = tokens.shape[0]
    gain_one, query_w, key_w, value_w, out_w = (
        lax.all_gather(attn_gain, ("fsdp", "ctx"), axis=0, tiled=True),
        lax.all_gather(w_query, ("fsdp", "ctx"), axis=0, tiled=True),
        lax.all_gather(w_key, ("fsdp", "ctx"), axis=0, tiled=True),
        lax.all_gather(w_value, ("fsdp", "ctx"), axis=0, tiled=True),
        lax.all_gather(w_out, ("fsdp", "ctx"), axis=1, tiled=True),
    )
    gain_two, gate_w, up_w, down_w = (
        lax.all_gather(mlp_gain, ("fsdp", "ctx"), axis=0, tiled=True),
        lax.all_gather(w_gate, ("fsdp", "ctx"), axis=0, tiled=True),
        lax.all_gather(w_up, ("fsdp", "ctx"), axis=0, tiled=True),
        lax.all_gather(w_down, ("fsdp", "ctx"), axis=1, tiled=True),
    )
    head_count = query_w.shape[1] // HD
    kv_heads = key_w.shape[1] // HD
    groups = H // KVH
    cosine, sine = rope_tables(positions, HD // 2)
    token_float = tokens.astype(jnp.float32)
    gain_one_float = gain_one.astype(jnp.float32)
    normed_one, unit_one, inv_one = rms_norm(token_float, gain_one_float)
    normed_low = normed_one.astype(jnp.bfloat16)
    query_lin = project(normed_low, query_w)
    key_lin = project(normed_low, key_w)
    value_low = project(normed_low, value_w).astype(jnp.bfloat16)
    query_rot = rotate(query_lin.reshape(token_rows, head_count, HD), cosine, sine).astype(
        jnp.bfloat16
    )
    key_rot = rotate(key_lin.reshape(token_rows, kv_heads, HD), cosine, sine).astype(jnp.bfloat16)
    queries = query_rot.reshape(token_rows, kv_heads, groups, HD)
    kv_local = jnp.concatenate([key_rot.reshape(token_rows, kv_heads * HD), value_low], axis=-1)
    key_positions, key_segments = (
        lax.all_gather(positions, "ctx", axis=0, tiled=True),
        lax.all_gather(segments, "ctx", axis=0, tiled=True),
    )
    my_index = lax.axis_index("ctx")
    cycle_size = lax.axis_size("ctx")

    def block_marks(source):
        start_row = source * token_rows
        return pair_mask(
            positions,
            segments,
            lax.dynamic_slice_in_dim(key_positions, start_row, token_rows),
            lax.dynamic_slice_in_dim(key_segments, start_row, token_rows),
        )

    start_state = (
        jnp.full((kv_heads, groups, token_rows), MASKED_SCORE, jnp.float32),
        jnp.zeros((kv_heads, groups, token_rows), jnp.float32),
        jnp.zeros((token_rows, kv_heads, groups, HD), jnp.float32),
    )

    def forward_block(state_in, kv_block, source):
        visible = block_marks(source)
        return attend_block(state_in, queries, kv_block, visible)

    def cycle_step(state_in, step_index):
        attn_state, kv_block = state_in
        attn_state = forward_block(attn_state, kv_block, (my_index - step_index) % cycle_size)
        passed = shifted(kv_block, "ctx", 1)
        return ((attn_state, passed), kv_block)

    (attn_state, last_block), kept_blocks = lax.scan(
        cycle_step, (start_state, kv_local), jnp.arange(cycle_size - 1)
    )
    attn_state = forward_block(attn_state, last_block, (my_index + 1) % cycle_size)
    kv_blocks = jnp.concatenate([kept_blocks, last_block[None]], axis=0)
    sources = (my_index - jnp.arange(cycle_size)) % cycle_size
    row_top, row_total, output_sum = attn_state
    attended = output_sum / jnp.transpose(row_total, (2, 0, 1))[..., None]
    log_total = row_top + jnp.log(row_total)
    attended_low = attended.reshape(token_rows, head_count * HD).astype(jnp.bfloat16)
    middle = token_float + lax.psum(project(attended_low, out_w).astype(jnp.bfloat16), "tp").astype(
        jnp.float32
    )
    gain_two_float = gain_two.astype(jnp.float32)
    normed_two, unit_two, inv_two = rms_norm(middle, gain_two_float)
    normed_two_low = normed_two.astype(jnp.bfloat16)
    gate_lin = project(normed_two_low, gate_w)
    up_lin = project(normed_two_low, up_w)
    hidden_low = (jax.nn.silu(gate_lin) * up_lin).astype(jnp.bfloat16)
    result = middle + lax.psum(project(hidden_low, down_w).astype(jnp.bfloat16), "tp").astype(
        jnp.float32
    )
    output = result.astype(jnp.bfloat16)
    hidden_grad = project_back(cotangent, down_w)
    down_w_grad = weight_grad(hidden_low, cotangent)
    sigmoid_gate = jax.nn.sigmoid(gate_lin)
    gate_grad_low = (
        hidden_grad * up_lin * sigmoid_gate * (1.0 + gate_lin * (1.0 - sigmoid_gate))
    ).astype(jnp.bfloat16)
    up_grad_low = (hidden_grad * gate_lin * sigmoid_gate).astype(jnp.bfloat16)
    normed_two_grad = lax.psum(
        (project_back(gate_grad_low, gate_w) + project_back(up_grad_low, up_w)).astype(
            jnp.bfloat16
        ),
        "tp",
    ).astype(jnp.float32)
    gate_w_grad = weight_grad(normed_two_low, gate_grad_low)
    up_w_grad = weight_grad(normed_two_low, up_grad_low)
    norm_back_two, gain_two_grad = rms_norm_back(normed_two_grad, gain_two_float, unit_two, inv_two)
    middle_grad = cotangent.astype(jnp.float32) + norm_back_two
    middle_low = middle_grad.astype(jnp.bfloat16)
    attended_grad_low = project_back(middle_low, out_w).astype(jnp.bfloat16)
    out_w_grad = weight_grad(attended_low, middle_low)
    out_grad = attended_grad_low.reshape(token_rows, kv_heads, groups, HD)
    delta_rows = jnp.transpose(jnp.sum(out_grad.astype(jnp.float32) * attended, axis=-1), (1, 2, 0))

    def backward_block(kv_block, source):
        visible = block_marks(source)
        return block_grads(queries, out_grad, kv_block, visible, log_total, delta_rows)

    query_start = jnp.zeros((token_rows, kv_heads, groups, HD), jnp.float32)

    def back_step(state_in, pieces):
        query_acc, kv_acc = state_in
        query_term, kv_term = backward_block(pieces[0], pieces[1])
        passed = shifted((kv_acc + kv_term).astype(jnp.bfloat16), "ctx", 1).astype(jnp.float32)
        return ((query_acc + query_term, passed), None)

    (query_grad, kv_grad), unused = lax.scan(
        back_step, (query_start, jnp.zeros(kv_local.shape, jnp.float32)), (kv_blocks, sources)
    )
    query_grad_low = (
        rotate_back(query_grad.reshape(token_rows, head_count, HD), cosine, sine)
        .reshape(token_rows, head_count * HD)
        .astype(jnp.bfloat16)
    )
    key_grad_low = (
        rotate_back(kv_grad[:, : kv_heads * HD].reshape(token_rows, kv_heads, HD), cosine, sine)
        .reshape(token_rows, kv_heads * HD)
        .astype(jnp.bfloat16)
    )
    value_grad_low = kv_grad[:, kv_heads * HD :].astype(jnp.bfloat16)
    normed_one_grad = lax.psum(
        (
            project_back(query_grad_low, query_w)
            + project_back(key_grad_low, key_w)
            + project_back(value_grad_low, value_w)
        ).astype(jnp.bfloat16),
        "tp",
    ).astype(jnp.float32)
    query_w_grad = weight_grad(normed_low, query_grad_low)
    key_w_grad = weight_grad(normed_low, key_grad_low)
    value_w_grad = weight_grad(normed_low, value_grad_low)
    norm_back_one, gain_one_grad = rms_norm_back(normed_one_grad, gain_one_float, unit_one, inv_one)
    input_grad = (middle_grad + norm_back_one).astype(jnp.bfloat16)
    summed = (
        lax.psum_scatter(
            gain_one_grad.astype(jnp.bfloat16), ("fsdp", "ctx"), scatter_dimension=0, tiled=True
        ).astype(jnp.float32),
        lax.psum_scatter(
            query_w_grad.astype(jnp.bfloat16), ("fsdp", "ctx"), scatter_dimension=0, tiled=True
        ).astype(jnp.float32),
        lax.psum_scatter(
            key_w_grad.astype(jnp.bfloat16), ("fsdp", "ctx"), scatter_dimension=0, tiled=True
        ).astype(jnp.float32),
        lax.psum_scatter(
            value_w_grad.astype(jnp.bfloat16), ("fsdp", "ctx"), scatter_dimension=0, tiled=True
        ).astype(jnp.float32),
        lax.psum_scatter(
            out_w_grad.astype(jnp.bfloat16), ("fsdp", "ctx"), scatter_dimension=1, tiled=True
        ).astype(jnp.float32),
        lax.psum_scatter(
            gain_two_grad.astype(jnp.bfloat16), ("fsdp", "ctx"), scatter_dimension=0, tiled=True
        ).astype(jnp.float32),
        lax.psum_scatter(
            gate_w_grad.astype(jnp.bfloat16), ("fsdp", "ctx"), scatter_dimension=0, tiled=True
        ).astype(jnp.float32),
        lax.psum_scatter(
            up_w_grad.astype(jnp.bfloat16), ("fsdp", "ctx"), scatter_dimension=0, tiled=True
        ).astype(jnp.float32),
        lax.psum_scatter(
            down_w_grad.astype(jnp.bfloat16), ("fsdp", "ctx"), scatter_dimension=1, tiled=True
        ).astype(jnp.float32),
    )
    return (output, input_grad) + tuple(summed)


MESH = pl.DeviceIdType.MESH
BF = jnp.bfloat16
F32 = jnp.float32


def dotg(left_side, right_side, left_dim, right_dim):
    return lax.dot_general(
        left_side,
        right_side,
        (((left_dim,), (right_dim,)), ((), ())),
        preferred_element_type=F32,
    )


def remote(src, dst, send_sem, recv_sem, device):
    return pltpu.make_async_remote_copy(
        src_ref=src,
        dst_ref=dst,
        send_sem=send_sem,
        recv_sem=recv_sem,
        device_id=device,
        device_id_type=MESH,
    )


class Place:
    def __init__(self):
        self.f = lax.axis_index("fsdp")
        self.c = lax.axis_index("ctx")
        self.z = lax.axis_index("tp")
        self.cx = self.c + 1 - 2 * lax.rem(self.c, 2)
        self.cy = lax.rem(self.c + 2, 4)
        self.cd = 3 - self.c
        self.of = 1 - self.f
        self.own = self.f * 4 + self.c
        self.sx = self.f * 4 + self.cx
        self.sy = self.f * 4 + self.cy
        self.sd = self.f * 4 + self.cd

    def at(self, f=None, c=None, z=None):
        return (
            self.f if f is None else f,
            self.c if c is None else c,
            self.z if z is None else z,
        )


def greet(devices):
    barrier = pltpu.get_barrier_semaphore()
    for device in devices:
        pl.semaphore_signal(barrier, inc=1, device_id=device, device_id_type=MESH)
    pl.semaphore_wait(barrier, len(devices))


def group_devices(me):
    return [
        me.at(c=me.cx),
        me.at(c=me.cy),
        me.at(c=me.cd),
        me.at(f=me.of),
        me.at(f=me.of, c=me.cx),
        me.at(f=me.of, c=me.cy),
        me.at(f=me.of, c=me.cd),
    ]


def column_devices(me):
    return [me.at(z=lax.rem(me.z + step, 4)) for step in (1, 2, 3)]


class Gather:
    def __init__(self, me, index, own, full, send, recv, local_sem):
        self.me, self.full, self.placed = me, full, own is None
        own = full.at[me.own] if own is None else own
        rows = full.shape[1]
        self.half_a = pl.ds(0, rows // 2)
        self.half_b = pl.ds(rows // 2, rows // 2)

        def copy(slot, src, dst, device):
            return remote(src, dst, send.at[index, slot], recv.at[index, slot], device)

        slot_own, slot_x, slot_y = full.at[me.own], full.at[me.sx], full.at[me.sy]
        to_x, to_y, to_core = me.at(c=me.cx), me.at(c=me.cy), me.at(f=me.of)
        diag_a = full.at[me.sd, self.half_a]
        diag_b = full.at[me.sd, self.half_b]
        self.own_x = copy(0, own, slot_own, to_x)
        self.own_y = copy(1, own, slot_own, to_y)
        self.own_core = copy(2, own, slot_own, to_core)
        self.pass_x = copy(3, full.at[me.sy, self.half_a], full.at[me.sy, self.half_a], to_x)
        self.pass_y = copy(4, full.at[me.sx, self.half_b], full.at[me.sx, self.half_b], to_y)
        self.core_x = copy(5, slot_x, slot_x, to_core)
        self.core_y = copy(6, slot_y, slot_y, to_core)
        self.core_a = copy(7, diag_a, diag_a, to_core)
        self.core_b = copy(8, diag_b, diag_b, to_core)
        other = me.of * 4
        into = lambda slot, ref, device: copy(slot, ref, ref, device)
        self.in_x = into(0, slot_x, to_x)
        self.in_y = into(1, slot_y, to_y)
        self.in_a = into(3, diag_a, to_x)
        self.in_b = into(4, diag_b, to_y)
        self.in_core = [
            into(2, full.at[other + me.c], to_core),
            into(5, full.at[other + me.cx], to_core),
            into(6, full.at[other + me.cy], to_core),
            into(7, full.at[other + me.cd, self.half_a], to_core),
            into(8, full.at[other + me.cd, self.half_b], to_core),
        ]
        self.keep = None if self.placed else pltpu.make_async_copy(own, slot_own, local_sem.at[index])

    def begin(self):
        self.own_x.start()
        self.own_y.start()
        self.own_core.start()
        if not self.placed:
            self.keep.start()

    def forward_a(self):
        self.in_y.wait_recv()
        self.pass_x.start()
        self.core_y.start()

    def forward_b(self):
        self.in_x.wait_recv()
        self.pass_y.start()
        self.core_x.start()

    def diagonal_a(self):
        self.in_a.wait_recv()
        self.core_a.start()

    def diagonal_b(self):
        self.in_b.wait_recv()
        self.core_b.start()

    def arrive(self):
        if not self.placed:
            self.keep.wait()
        for piece in self.in_core:
            piece.wait_recv()

    def settle(self):
        for piece in (
            self.own_x,
            self.own_y,
            self.own_core,
            self.pass_x,
            self.pass_y,
            self.core_x,
            self.core_y,
            self.core_a,
            self.core_b,
        ):
            piece.wait_send()


class LineSum:
    def __init__(self, me, part, outer_in, inner_in, send, recv):
        self.me, self.part = me, part
        self.outer_in, self.inner_in = outer_in, inner_in
        self.send, self.recv = send, recv
        z = me.z
        self.is_mid = (z == 1) | (z == 2)
        self.is_end = (z == 0) | (z == 3)
        self.mid_of_end = 1 + z // 3
        self.outer_of_mid = 3 * (z - 1)

    def end_copies(self):
        me, part = self.me, self.part
        mid = self.mid_of_end
        to_mid = me.at(z=mid)
        owners = (3 - me.z, 3 - mid, mid)
        return [
            remote(
                part.at[owner],
                self.outer_in.at[slot],
                self.send.at[slot],
                self.recv.at[slot],
                to_mid,
            )
            for slot, owner in enumerate(owners)
        ]

    def mid_copies(self):
        me, part = self.me, self.part
        far_mid, outer = 3 - me.z, self.outer_of_mid
        far = 3 - outer
        to_mid, to_outer = me.at(z=far_mid), me.at(z=outer)
        return [
            remote(part.at[far], self.inner_in.at[0], self.send.at[0], self.recv.at[3], to_mid),
            remote(part.at[far_mid], self.inner_in.at[1], self.send.at[1], self.recv.at[4], to_mid),
            remote(part.at[outer], self.inner_in.at[0], self.send.at[2], self.recv.at[3], to_outer),
        ]

    def wait_in(self, slot, buffer):
        remote(buffer, buffer, self.send.at[0], self.recv.at[slot], self.me.at(z=3 - self.me.z)).wait_recv()

    def add(self, owner, buffer):
        self.part[owner] = (self.part[owner].astype(F32) + buffer[...].astype(F32)).astype(BF)

    def begin(self):
        @pl.when(self.is_end)
        def _():
            for piece in self.end_copies():
                piece.start()

    def step_one(self):
        @pl.when(self.is_mid)
        def _():
            far = 3 - self.outer_of_mid
            self.wait_in(0, self.outer_in.at[0])
            self.add(far, self.outer_in.at[0])
            self.mid_copies()[0].start()

    def step_two(self):
        @pl.when(self.is_mid)
        def _():
            copies = self.mid_copies()
            self.wait_in(1, self.outer_in.at[1])
            self.add(3 - self.me.z, self.outer_in.at[1])
            copies[1].start()

    def step_three(self):
        @pl.when(self.is_mid)
        def _():
            self.wait_in(3, self.inner_in.at[0])
            self.add(self.outer_of_mid, self.inner_in.at[0])
            self.mid_copies()[2].start()

    def finish(self, total):
        me = self.me

        @pl.when(self.is_mid)
        def _():
            self.wait_in(2, self.outer_in.at[2])
            self.wait_in(4, self.inner_in.at[1])
            total[...] = (
                self.part[me.z].astype(F32)
                + self.outer_in[2].astype(F32)
                + self.inner_in[1].astype(F32)
            )
            for piece in self.mid_copies():
                piece.wait_send()

        @pl.when(self.is_end)
        def _():
            self.wait_in(3, self.inner_in.at[0])
            total[...] = self.part[me.z].astype(F32) + self.inner_in[0].astype(F32)
            for piece in self.end_copies():
                piece.wait_send()


class LineGather:
    def __init__(self, me, blocks, send, recv):
        self.me, self.blocks, self.send, self.recv = me, blocks, send, recv
        z = me.z
        self.is_mid = (z == 1) | (z == 2)
        self.is_end = (z == 0) | (z == 3)
        self.mid_of_end = 1 + z // 3
        self.outer_of_mid = 3 * (z - 1)

    def copy(self, owner, slot, z):
        ref = self.blocks.at[owner]
        return remote(ref, ref, self.send.at[slot], self.recv.at[owner], self.me.at(z=z))

    def wait_in(self, owner):
        ref = self.blocks.at[owner]
        remote(ref, ref, self.send.at[0], self.recv.at[owner], self.me.at(z=3 - self.me.z)).wait_recv()

    def begin(self):
        me = self.me

        @pl.when(self.is_end)
        def _():
            self.copy(me.z, 0, self.mid_of_end).start()

        @pl.when(self.is_mid)
        def _():
            self.copy(me.z, 0, self.outer_of_mid).start()
            self.copy(me.z, 1, 3 - me.z).start()

    def step_one(self):
        me = self.me

        @pl.when(self.is_mid)
        def _():
            self.wait_in(self.outer_of_mid)
            self.copy(self.outer_of_mid, 2, 3 - me.z).start()

    def step_two(self):
        me = self.me

        @pl.when(self.is_mid)
        def _():
            self.wait_in(3 - me.z)
            self.copy(3 - me.z, 3, self.outer_of_mid).start()

    def step_three(self):
        @pl.when(self.is_mid)
        def _():
            far = 3 - self.outer_of_mid
            self.wait_in(far)
            self.copy(far, 4, self.outer_of_mid).start()

    def finish(self):
        me = self.me

        @pl.when(self.is_mid)
        def _():
            self.copy(me.z, 0, self.outer_of_mid).wait_send()
            self.copy(me.z, 1, 3 - me.z).wait_send()
            self.copy(self.outer_of_mid, 2, 3 - me.z).wait_send()
            self.copy(3 - me.z, 3, self.outer_of_mid).wait_send()
            self.copy(3 - self.outer_of_mid, 4, self.outer_of_mid).wait_send()

        @pl.when(self.is_end)
        def _():
            mid = self.mid_of_end
            self.wait_in(mid)
            self.wait_in(3 - mid)
            self.wait_in(3 - me.z)
            self.copy(me.z, 0, mid).wait_send()


def row_of(gains_ref, which):
    return jnp.concatenate([gains_ref[shard, which : which + 1, :] for shard in range(8)], axis=-1)


def swap_halves(rows):
    lane = lax.broadcasted_iota(jnp.int32, rows.shape, 1)
    return jnp.where(
        lax.rem(lane, HD) < HD // 2, pltpu.roll(rows, 96, 1), pltpu.roll(rows, 32, 1)
    )


class Scatter:
    def __init__(self, me, index, last, width, x_of, y_of, chips, refs):
        self.me, self.index, self.last, self.width = me, index, last, width
        self.x_of, self.y_of, self.chips = x_of, y_of, chips
        self.stage, self.core_in, self.diag_in, self.near_in = refs[:4]
        self.send, self.recv, self.credit = refs[4:]
        self.to_x, self.to_y, self.to_core = me.at(c=me.cx), me.at(c=me.cy), me.at(f=me.of)
        self.sent = []

    def copy(self, slot, src, dst, device):
        return remote(
            src, dst, self.send.at[self.index, slot], self.recv.at[self.index, slot], device
        )

    def lanes(self, ref):
        return ref.at[:, pl.ds(0, self.width)]

    def core_copy(self, role):
        return self.copy(
            role, self.stage(self.width, role), self.lanes(self.core_in.at[role]), self.to_core
        )

    def chunk(self, core, role):
        c = self.me.c
        high = lax.rem(c // 2 + role // 2, 2)
        low = lax.rem(lax.rem(c, 2) + lax.rem(role, 2), 2)
        return dotg(self.x_of(core * 4 + 2 * high + low), self.y_of(), 0, 0)

    def roles(self, body):
        def pair(step, carry):
            body(3 - step)
            body(1 - step)
            return carry

        lax.fori_loop(0, 2, pair, 0)

    def partner(self):
        def body(role):
            self.stage(self.width, role)[...] = self.chunk(self.me.of, role).astype(BF)
            if self.index > 0:
                pl.semaphore_wait(self.credit.at[role], 1)
            self.core_copy(role).start()

        self.roles(body)

    def own(self):
        def body(role):
            value = self.chunk(self.me.f, role)
            self.core_copy(role).wait_recv()
            chip = self.chips(role)
            chip[...] = (value + self.lanes(self.core_in.at[role])[...].astype(F32)).astype(BF)
            if not self.last:
                pl.semaphore_signal(
                    self.credit.at[role], inc=1, device_id=self.to_core, device_id_type=MESH
                )

        self.roles(body)
        for role in range(4):
            self.core_copy(role).wait_send()

    def near(self, role, half, slot):
        rows = pl.ds(half * 128, 128)
        side = role - 1
        device = self.to_x if role == 1 else self.to_y
        return self.copy(
            slot, self.chips(role).at[rows, :], self.near_in.at[side, rows, :], device
        )

    def diag(self, half):
        device = self.to_x if half == 0 else self.to_y
        return self.copy(
            4 + half,
            self.chips(3).at[pl.ds(half * 128, 128), :],
            self.lanes(self.diag_in.at[half]),
            device,
        )

    def push_diag(self):
        self.diag(0).start()
        self.diag(1).start()

    def push_near(self):
        self.near(1, 0, 6).start()
        self.near(2, 1, 7).start()

    def relay_a(self):
        first = pl.ds(0, 128)
        self.diag(0).wait_recv()
        rows = self.chips(2).at[first, :]
        rows[...] = (
            rows[...].astype(F32) + self.lanes(self.diag_in.at[0])[...].astype(F32)
        ).astype(BF)
        self.near(2, 0, 8).start()

    def relay_b(self):
        second = pl.ds(128, 128)
        self.diag(1).wait_recv()
        rows = self.chips(1).at[second, :]
        rows[...] = (
            rows[...].astype(F32) + self.lanes(self.diag_in.at[1])[...].astype(F32)
        ).astype(BF)
        self.near(1, 1, 9).start()

    def collect(self, buffer, sem):
        for role, half, slot in ((1, 0, 6), (2, 1, 7), (2, 0, 8), (1, 1, 9)):
            self.near(role, half, slot).wait_recv()
        for side in range(2):
            pltpu.make_async_copy(
                self.near_in.at[side], self.lanes(buffer.at[side]), sem.at[side]
            ).start()

    def collected(self, buffer, sem):
        for side in range(2):
            pltpu.make_async_copy(
                self.near_in.at[side], self.lanes(buffer.at[side]), sem.at[side]
            ).wait()

    def settle(self):
        for half in range(2):
            self.diag(half).wait_send()
        for role, half, slot in ((1, 0, 6), (2, 1, 7), (2, 0, 8), (1, 1, 9)):
            self.near(role, half, slot).wait_send()


def norm_back(gradient, rows_in, gain):
    inv = lax.rsqrt(jnp.mean(rows_in * rows_in, axis=-1, keepdims=True) + EPSILON)
    unit = rows_in * inv
    scaled = gradient * gain
    back = inv * (scaled - unit * jnp.mean(scaled * unit, axis=-1, keepdims=True))
    return back, jnp.sum(gradient * unit, axis=0, keepdims=True)


def layer_kernel(
    tok_h,
    gains_in,
    w_query_in,
    w_key_in,
    w_value_in,
    out_h,
    gate_h,
    up_h,
    down_h,
    cot_h,
    pos_in,
    seg_in,
    freq,
    o_result,
    o_input,
    o_gain_one,
    o_gain_two,
    o_query,
    o_key,
    o_value,
    o_out,
    o_gate,
    o_up,
    o_down,
    near_down,
    near_gate,
    near_up,
    near_out,
    near_qkv,
    n_one_h,
    own_gains,
    own_marks,
    gains,
    marks,
    tok,
    w_gate,
    w_up,
    w_down,
    w_out,
    w_qkv,
    cot,
    n_two,
    hid,
    gate_g,
    up_g,
    core_in,
    diag_in,
    diag_low,
    chip_out,
    chip_qkv,
    sum_stage,
    turn_stage,
    part,
    outer_in,
    inner_in,
    outer_two,
    inner_two,
    mlow,
    total,
    own_out,
    mid,
    mid_g,
    q_rot,
    bias,
    lse,
    kv,
    att,
    rope,
    do_rows,
    keys,
    vals_t,
    vals,
    keys_t,
    key_acc,
    val_acc,
    kv_send_buf,
    kv_in,
    d_qkv,
    vec,
    vec_in,
    vec_out,
    vec_near,
    g_send,
    g_recv,
    g_local,
    small_send,
    small_recv,
    first_send,
    first_recv,
    load_sem,
    sum_send,
    sum_recv,
    all_send,
    all_recv,
    rs_send,
    rs_recv,
    credit,
    kv_send,
    kv_recv,
    vec_send,
    vec_recv,
    fin_sem,
    put_sem,
    own_sem,
):
    me = Place()
    group = group_devices(me)
    hidden = hid.shape[1]

    rows_of = [pl.ds(g * 256, 256) for g in range(2)]
    load_tok = pltpu.make_async_copy(tok_h, tok, load_sem.at[0])
    load_cot = pltpu.make_async_copy(cot_h, cot, load_sem.at[1])
    save_one = pltpu.make_async_copy(mlow, n_one_h, load_sem.at[2])
    load_one = pltpu.make_async_copy(n_one_h, mlow, load_sem.at[3])
    load_tok.start()
    load_cot.start()

    w_qkv[me.own, :, 0:512] = w_query_in[...]
    turned = jnp.concatenate([w_key_in[...], w_value_in[...]], axis=0).astype(F32)
    w_qkv[me.own, :, 512:640] = jnp.transpose(turned).astype(BF)
    own_gains[0:2, :] = gains_in[...].astype(F32)
    own_gains[2:8, :] = jnp.zeros((6, 256), F32)
    own_marks[0:1, :] = pos_in[...]
    own_marks[1:2, :] = seg_in[...]
    own_marks[2:8, :] = jnp.zeros((6, 512), jnp.int32)
    greet(group + column_devices(me))

    qkv = Gather(me, 0, None, w_qkv, g_send, g_recv, g_local)
    out = Gather(me, 1, out_h, w_out, g_send, g_recv, g_local)
    gate = Gather(me, 2, gate_h, w_gate, g_send, g_recv, g_local)
    up = Gather(me, 3, up_h, w_up, g_send, g_recv, g_local)
    down = Gather(me, 4, down_h, w_down, g_send, g_recv, g_local)

    sources = [me.sx, me.sy, me.sd, me.of * 4 + me.c, me.of * 4 + me.cx, me.of * 4 + me.cy, me.of * 4 + me.cd]

    def small_copies(gain_slots, mark_slots):
        return [
            remote(own_gains, gains.at[spot], small_send.at[slot], small_recv.at[slot], group[slot])
            for slot, spot in enumerate(gain_slots)
        ] + [
            remote(
                own_marks, marks.at[spot], small_send.at[7 + slot], small_recv.at[7 + slot], group[slot]
            )
            for slot, spot in enumerate(mark_slots)
        ]

    small = small_copies([me.own] * 7, [me.c] * 3)

    def small_begin():
        for piece in small:
            piece.start()
        gains[me.own] = own_gains[...]
        marks[me.c] = own_marks[...]

    def small_finish():
        for piece in small_copies(sources, (me.cx, me.cy, me.cd)):
            piece.wait_recv()

    def first_norm():
        load_tok.wait()
        gain_one = row_of(gains, 0)

        def body(step, carry):
            values = tok[pl.ds(pl.multiple_of(step * 64, 64), 64), :].astype(F32)
            inv = lax.rsqrt(jnp.mean(values * values, axis=-1, keepdims=True) + EPSILON)
            mlow[step // 4, lax.rem(step, 4)] = (values * inv * gain_one).astype(BF)
            return carry

        lax.fori_loop(0, 8, body, 0)
        save_one.start()

    def make_rope():
        lane = lax.broadcasted_iota(jnp.int32, (128, 128), 1)
        low_half = lax.rem(lane, HD) < HD // 2
        for step in range(4):
            rows = slice(step * 128, (step + 1) * 128)
            places = own_marks[0:1, rows].astype(F32)
            angles = jnp.transpose(jnp.broadcast_to(places, (128, 128))) * freq[...]
            sine = jnp.sin(angles)
            rope[rows, :128] = jnp.cos(angles)
            rope[rows, 128:] = jnp.where(low_half, -sine, sine)

    def make_bias(g):
        own_rows = own_marks[:, g * 256 : (g + 1) * 256].astype(F32)
        for source in range(4):
            key_rows = marks[source, :, g * 256 : (g + 1) * 256].astype(F32)
            key_pos = jnp.transpose(jnp.broadcast_to(key_rows[0:1, :], (128, 256)))
            key_seg = jnp.transpose(jnp.broadcast_to(key_rows[1:2, :], (128, 256)))
            for side in range(2):
                lanes = slice(side * 128, (side + 1) * 128)
                seen = (key_seg == own_rows[1:2, lanes]) & (key_pos <= own_rows[0:1, lanes])
                bias[g, source * 256 : (source + 1) * 256, lanes] = jnp.where(
                    seen, 0.0, MASKED_SCORE
                ).astype(BF)

    lane_pair = lax.broadcasted_iota(jnp.int32, (256, 128), 1)

    def project_in(first, width):
        total_rows = None
        for shard in range(8):
            term = dotg(
                mlow[:, :, :, shard * 256 : (shard + 1) * 256].reshape(512, 256),
                w_qkv[shard, :, first : first + width],
                1,
                0,
            )
            total_rows = term if total_rows is None else total_rows + term
        return total_rows

    def first_copies(places):
        return [
            remote(kv.at[place], kv.at[place], first_send.at[slot], first_recv.at[slot], group[slot])
            for slot, place in enumerate(places)
        ]

    def project_kv():
        rows = project_in(512, 128)
        is_key = lax.broadcasted_iota(jnp.int32, (512, 128), 1) < HD
        cos_rows = jnp.where(is_key, rope[:, :128], 1.0)
        sin_rows = jnp.where(is_key, rope[:, 128:], 0.0)
        kv[me.c] = (rows * cos_rows + swap_halves(rows) * sin_rows).astype(BF)
        for piece in first_copies([me.c] * 3):
            piece.start()

    def project_q(half):
        rows_all = project_in(half * 256, 256)
        for inner in range(2):
            pair = half * 2 + inner
            rows = rows_all[:, inner * 128 : (inner + 1) * 128]
            rot = (rows * rope[:, :128] + swap_halves(rows) * rope[:, 128:]).astype(BF)
            rot = rot * jnp.bfloat16(HD ** (-0.5))
            q_rot[:, pair * 128 : (pair + 1) * 128] = rot

    def kv_arrive():
        for piece in first_copies((me.cx, me.cy, me.cd)):
            piece.wait_recv()
        for g in range(2):
            for source in range(4):
                pairs = kv[source, g * 256 : (g + 1) * 256, :].astype(F32)
                rows = slice(source * 256, (source + 1) * 256)
                keys[g, rows, :] = jnp.where(
                    lane_pair < HD, pairs, pltpu.roll(pairs, HD, 1)
                ).astype(BF)
                vals_t[g, :, rows] = jnp.transpose(pairs)[HD:, :].astype(BF)

    def one_head(pair_rows, odd):
        kept = lane_pair >= HD if odd else lane_pair < HD
        return jnp.where(kept, pair_rows, jnp.zeros_like(pair_rows))

    def attend(step):
        g = step // 4
        pair = step - g * 4
        halves = []
        own = pl.ds(pl.multiple_of(g * 256, 256), 256)
        lanes = pl.ds(pl.multiple_of(pair * 128, 128), 128)
        queries = q_rot[own, lanes]
        for odd in range(2):
            head = step * 2 + odd
            scores = dotg(keys[g], one_head(queries, odd), 1, 1) + bias[g].astype(F32)
            top = jnp.max(scores, axis=0, keepdims=True)
            weights = jnp.exp(scores - top)
            norm = jnp.sum(weights, axis=0, keepdims=True)
            mixed = dotg(vals_t[g], weights.astype(BF), 1, 0)
            halves.append(mixed / norm)
            lse[head] = top + jnp.log(norm)
        rows = jnp.transpose(jnp.concatenate(halves, axis=0))
        att[own, lanes] = rows.astype(BF)

    def project_out(g):
        def body(shard, carry):
            part[g, :, :, pl.ds(pl.multiple_of(shard * 256, 256), 256)] = (
                dotg(att[rows_of[g], :], w_out[shard], 1, 0).astype(BF).reshape(4, 64, 256)
            )
            return carry

        lax.fori_loop(0, 8, body, 0)

    def second_norm(g):
        sum_att[g].finish(total)
        own = pl.ds(pl.multiple_of(g * 256 + me.z * 64, 64), 64)
        mid_rows = tok[own, :].astype(F32) + total[...]
        mid[g] = mid_rows
        inv = lax.rsqrt(jnp.mean(mid_rows * mid_rows, axis=-1, keepdims=True) + EPSILON)
        n_two[g, me.z] = (mid_rows * inv * row_of(gains, 1)).astype(BF)
        spread_two[g].begin()

    def looped(body, count, hooks):
        def step(i, carry):
            for spot, actions in hooks:

                @pl.when(i == spot)
                def _():
                    for action, *values in actions:
                        action(*values)

            body(i)
            return carry

        lax.fori_loop(0, count, step, 0)

    tile_count = (hidden + 255) // 256

    def feed(step):
        g = step // tile_count
        n = step - g * tile_count
        rows = pl.ds(pl.multiple_of(g * 256, 256), 256)
        lanes = pl.ds(pl.multiple_of(jnp.minimum(n * 256, hidden - 256), 128), 256)
        normed = n_two[g].reshape(256, 2048)
        gate = dotg(normed, w_gate[:, :, lanes].reshape(2048, 256), 1, 0)
        up = dotg(normed, w_up[:, :, lanes].reshape(2048, 256), 1, 0)
        hidden_grad = None
        for shard in range(8):
            term = dotg(
                cot[rows, shard * 256 : (shard + 1) * 256], w_down[shard, lanes, :], 1, 1
            )
            hidden_grad = term if hidden_grad is None else hidden_grad + term
        sig = jax.nn.sigmoid(gate)
        silu = gate * sig
        hid[rows, lanes] = (silu * up).astype(BF)
        up_g[rows, lanes] = (hidden_grad * silu).astype(BF)
        gate_g[rows, lanes] = (
            hidden_grad * up * sig * (1.0 + gate * (1.0 - sig))
        ).astype(BF)

    def feed_back(g):
        def body(shard, carry):
            term = dotg(gate_g[rows_of[g], :], w_gate[shard], 1, 1) + dotg(
                up_g[rows_of[g], :], w_up[shard], 1, 1
            )
            part[g, :, :, pl.ds(pl.multiple_of(shard * 256, 256), 256)] = term.astype(BF).reshape(
                4, 64, 256
            )
            return carry

        lax.fori_loop(0, 8, body, 0)

    part_two = n_two

    def feed_out(g):
        def body(shard, carry):
            term = dotg(hid[rows_of[g], :], w_down[shard], 1, 0)
            part_two[g, :, :, pl.ds(pl.multiple_of(shard * 256, 256), 256)] = term.astype(
                BF
            ).reshape(4, 64, 256)
            return carry

        lax.fori_loop(0, 8, body, 0)

    def line_sum(slot, part_ref, outer, inner):
        return LineSum(me, part_ref, outer, inner, sum_send.at[slot], sum_recv.at[slot])

    sum_two = [line_sum(g, part.at[g], outer_in.at[g], inner_in.at[g]) for g in range(2)]
    sum_one = [line_sum(2 + g, part.at[g], outer_in.at[g], inner_in.at[g]) for g in range(2)]

    sum_out = [
        line_sum(4 + g, part_two.at[g], outer_two.at[g], inner_two.at[g]) for g in range(2)
    ]
    sum_att = [line_sum(6 + g, part.at[g], outer_in.at[g], inner_in.at[g]) for g in range(2)]
    spread_two = [LineGather(me, n_two.at[g], all_send.at[6 + g], all_recv.at[6 + g]) for g in range(2)]
    spread_mid = [LineGather(me, mlow.at[g], all_send.at[g], all_recv.at[g]) for g in range(2)]
    spread_in = [LineGather(me, o_input.at[g], all_send.at[2 + g], all_recv.at[2 + g]) for g in range(2)]
    spread_out = [LineGather(me, o_result.at[g], all_send.at[4 + g], all_recv.at[4 + g]) for g in range(2)]

    def middle_back(g):
        sum_two[g].finish(total)
        own = pl.ds(pl.multiple_of(g * 256 + me.z * 64, 64), 64)
        back, gain_grad = norm_back(total[...], mid[g], row_of(gains, 1))
        if g == 0:
            vec[1:2, :] = gain_grad
        else:
            vec[1:2, :] += gain_grad
        grad = cot[own, :].astype(F32) + back
        mid_g[g] = grad
        mlow[g, me.z] = grad.astype(BF)
        spread_mid[g].begin()

    def put_own(g, ref, slot):
        copy = pltpu.make_async_copy(own_out, ref.at[g, me.z], own_sem.at[slot])
        copy.start()
        copy.wait()

    def input_back(g):
        sum_one[g].finish(total)
        own = pl.ds(pl.multiple_of(g * 256 + me.z * 64, 64), 64)
        back, gain_grad = norm_back(total[...], tok[own, :].astype(F32), row_of(gains, 0))
        if g == 0:
            vec[0:1, :] = gain_grad
        else:
            vec[0:1, :] += gain_grad
        own_out[...] = (mid_g[g] + back).astype(BF)
        put_own(g, o_input, 0)
        spread_in[g].begin()

    def result_rows(g):
        sum_out[g].finish(total)
        own_out[...] = (mid[g] + total[...]).astype(BF)
        put_own(g, o_result, 1)
        spread_out[g].begin()

    wide = lambda ref: (lambda shard: ref[:, pl.ds(pl.multiple_of(shard * 256, 256), 256)])

    def blocks_of(ref):
        return lambda shard: ref[
            :, :, :, pl.ds(pl.multiple_of(shard * 256, 256), 256)
        ].reshape(512, 256)

    def stage(width, slot):
        if width > 640:
            return w_up.at[4 + slot]
        first = lax.rem(slot, 2) * 640
        if not isinstance(slot, int):
            first = pl.multiple_of(first, 128)
        return w_up.at[4 + slot // 2, :, pl.ds(first, width)]

    landing = w_up.at[pl.ds(6, 2)]

    def scatter(index, width, x_of, y_of, chips, near):
        landed = diag_in.at[index] if index < 3 else diag_low.at[index - 3]
        refs = (stage, core_in, landed, near, rs_send, rs_recv, credit)
        return Scatter(me, index, index == 4, width, x_of, y_of, chips, refs)

    rs_down = scatter(
        0, hidden, wide(cot), lambda: hid[...], lambda role: w_gate.at[4 + role], near_down
    )
    rs_gate = scatter(
        1, hidden, blocks_of(n_two), lambda: gate_g[...], lambda role: w_gate.at[role], near_gate
    )
    rs_up = scatter(
        2, hidden, blocks_of(n_two), lambda: up_g[...], lambda role: w_up.at[role], near_up
    )
    rs_out = scatter(3, 512, blocks_of(mlow), lambda: att[...], lambda role: chip_out.at[role], near_out)
    rs_qkv = scatter(
        4,
        640,
        blocks_of(mlow),
        lambda: d_qkv[...],
        lambda role: chip_qkv.at[role],
        near_qkv,
    )

    def finish_rows(job, outs):
        job.collected(landing, fin_sem)
        width = job.width
        pending = [None, None]
        for step in range(4):
            slot = step % 2
            rows = slice(step * 64, (step + 1) * 64)
            if pending[slot] is not None:
                for piece in pending[slot]:
                    piece.wait()
            sum_stage[slot, :, :width] = (
                job.chips(0)[rows, :].astype(F32)
                + landing[0, rows, :width].astype(F32)
                + landing[1, rows, :width].astype(F32)
            )
            pending[slot] = [
                pltpu.make_async_copy(
                    sum_stage.at[slot, :, pl.ds(first, size)],
                    ref.at[pl.ds(step * 64, 64), :],
                    put_sem.at[slot, number],
                )
                for number, (ref, first, size) in enumerate(outs)
            ]
            for piece in pending[slot]:
                piece.start()
        for slot in range(2):
            for piece in pending[slot]:
                piece.wait()

    def finish_qkv(job):
        finish_rows(job, [(o_query, 0, 512)])
        lanes = slice(512, 640)
        turn_stage[0] = jnp.transpose(
            job.chips(0)[:, lanes].astype(F32)
            + landing[0, :, lanes].astype(F32)
            + landing[1, :, lanes].astype(F32)
        )
        copies = [
            pltpu.make_async_copy(
                turn_stage.at[0, pl.ds(first, HD), :], ref, put_sem.at[0, number]
            )
            for number, (first, ref) in enumerate(((0, o_key), (HD, o_value)))
        ]
        for piece in copies:
            piece.start()
        for piece in copies:
            piece.wait()

    def finish_turned(job, ref):
        job.collected(landing, fin_sem)

        def put(step, slot):
            rows = pl.ds(pl.multiple_of(step * 128, 128), 128)
            return pltpu.make_async_copy(turn_stage.at[slot], ref.at[rows, :], put_sem.at[slot, 0])

        def body(step, carry):
            slot = lax.rem(step, 2)
            lanes = pl.ds(pl.multiple_of(step * 128, 128), 128)

            @pl.when(step >= 2)
            def _():
                put(step, slot).wait()

            turn_stage[slot] = jnp.transpose(
                job.chips(0)[:, lanes].astype(F32)
                + landing[0, :, lanes].astype(F32)
                + landing[1, :, lanes].astype(F32)
            )
            put(step, slot).start()
            return carry

        lax.fori_loop(0, job.width // 128, body, 0)
        for slot in range(2):
            put(slot, slot).wait()

    def out_back(g):
        grad = None
        for shard in range(8):
            lanes = slice(shard * 256, (shard + 1) * 256)
            term = dotg(mlow[g, :, :, lanes].reshape(256, 256), w_out[shard], 1, 1)
            grad = term if grad is None else grad + term
        do_rows[...] = grad.astype(BF)
        for source in range(4):
            pairs = kv[source, rows_of[g], :].astype(F32)
            turned = pltpu.roll(pairs, HD, 1)
            rows = slice(source * 256, (source + 1) * 256)
            vals[rows, :] = jnp.where(lane_pair < HD, turned, pairs).astype(BF)
            keys_t[:, rows] = jnp.transpose(pairs)[:HD, :].astype(BF)
        key_acc[...] = jnp.zeros_like(key_acc)
        val_acc[...] = jnp.zeros_like(val_acc)

    def attend_back(step):
        g = step // 4
        pair = step - g * 4
        own = pl.ds(pl.multiple_of(g * 256, 256), 256)
        halves = []
        lanes = pl.ds(pl.multiple_of(pair * 128, 128), 128)
        queries, grads = q_rot[own, lanes], do_rows[:, lanes]
        for odd in range(2):
            query, grad = one_head(queries, odd), one_head(grads, odd)
            scores = dotg(keys[g], query, 1, 1) + bias[g].astype(F32)
            probs = jnp.exp(scores - lse[step * 2 + odd])
            prob_grad = dotg(vals[...], grad, 1, 1)
            delta = jnp.sum(probs * prob_grad, axis=0, keepdims=True)
            score_grad = (probs * (prob_grad - delta)).astype(BF)
            val_acc[...] += dotg(probs.astype(BF), grad, 1, 0)
            key_acc[...] += dotg(score_grad, query, 1, 0)
            halves.append(dotg(keys_t[...], score_grad, 1, 0))
        rows = jnp.transpose(jnp.concatenate(halves, axis=0)) * (HD ** (-0.5))
        rows = rows * rope[own, :128] - swap_halves(rows) * rope[own, 128:]
        d_qkv[own, lanes] = rows.astype(BF)

    def kv_copies(g):
        return [
            remote(
                kv_send_buf.at[g, column],
                kv_in.at[g, slot],
                kv_send.at[g, slot],
                kv_recv.at[g, slot],
                group[slot],
            )
            for slot, column in enumerate((me.cx, me.cy, me.cd))
        ]

    def kv_begin(g):
        for block in range(4):
            rows = slice(block * 256, (block + 1) * 256)
            key_rows, val_rows = key_acc[rows, :], val_acc[rows, :]
            joined = jnp.where(
                lane_pair < HD,
                key_rows + pltpu.roll(key_rows, HD, 1),
                val_rows + pltpu.roll(val_rows, HD, 1),
            )
            kv_send_buf[g, block] = joined.astype(BF)
        for piece in kv_copies(g):
            piece.start()

    def kv_finish(g):
        rows = kv_send_buf[g, me.c].astype(F32)
        for slot, piece in enumerate(kv_copies(g)):
            piece.wait_recv()
            rows = rows + kv_in[g, slot].astype(F32)
        cos_rows = jnp.where(lane_pair < HD, rope[rows_of[g], :128], 1.0)
        sin_rows = jnp.where(lane_pair < HD, rope[rows_of[g], 128:], 0.0)
        rows = rows * cos_rows - swap_halves(rows) * sin_rows
        d_qkv[rows_of[g], 512:640] = rows.astype(BF)

    def project_back_rows(g):
        def body(shard, carry):
            term = dotg(d_qkv[rows_of[g], :], w_qkv[shard], 1, 1)
            part[g, :, :, pl.ds(pl.multiple_of(shard * 256, 256), 256)] = term.astype(BF).reshape(
                4, 64, 256
            )
            return carry

        lax.fori_loop(0, 8, body, 0)

    line = column_devices(me)

    def vec_line():
        return [
            remote(vec_out, vec_in.at[slot], vec_send.at[slot], vec_recv.at[slot], device)
            for slot, device in enumerate(line)
        ]

    targets = [me.sx, me.sy, me.sd, me.of * 4 + me.c, me.of * 4 + me.cx, me.of * 4 + me.cy, me.of * 4 + me.cd]

    def vec_group():
        return [
            remote(
                vec_in.at[3, target],
                vec_near.at[slot],
                vec_send.at[3 + slot],
                vec_recv.at[3 + slot],
                device,
            )
            for slot, (target, device) in enumerate(zip(targets, group))
        ]

    def vec_begin():
        for shard in range(8):
            for which in range(2):
                for half in range(2):
                    first = shard * 256 + half * 128
                    vec_out[shard, 2 * which + half : 2 * which + half + 1, :] = vec[
                        which : which + 1, first : first + 128
                    ]
            vec_out[shard, 4:8, :] = jnp.zeros((4, 128), F32)
        for piece in vec_line():
            piece.start()

    def vec_middle():
        for piece in vec_line():
            piece.wait_recv()
        vec_in[3] = vec_out[...] + vec_in[0] + vec_in[1] + vec_in[2]
        for piece in vec_group():
            piece.start()

    def vec_finish():
        rows = vec_in[3, me.own]
        for slot, piece in enumerate(vec_group()):
            piece.wait_recv()
            rows = rows + vec_near[slot]
        o_gain_one[...] = rows[0:2, :]
        o_gain_two[...] = rows[2:4, :]

    def settle_weights():
        for piece in (qkv, out, gate, up, down):
            piece.settle()

    def settle():
        for spread in spread_in + spread_out:
            spread.finish()
        for job in (rs_down, rs_gate, rs_up, rs_out, rs_qkv):
            job.settle()
        for g in range(2):
            for piece in kv_copies(g):
                piece.wait_send()
        for piece in vec_line() + vec_group() + small + first_copies([me.c] * 3):
            piece.wait_send()

    order = (
        (small_begin,),
        (qkv.begin,),
        (make_rope,),
        (qkv.forward_a,),
        (qkv.forward_b,),
        (small_finish,),
        (first_norm,),
        (out.begin,),
        (qkv.diagonal_a,),
        (qkv.diagonal_b,),
        (qkv.arrive,),
        (project_kv,),
        (project_q, 0),
        (out.forward_a,),
        (make_bias, 0),
        (out.forward_b,),
        (project_q, 1),
        (save_one.wait,),
        (up.begin,),
        (kv_arrive,),
        (make_bias, 1),
        (down.begin,),
        (
            looped,
            attend,
            8,
            (
                (2, ((out.diagonal_a,), (out.diagonal_b,),)),
                (4, ((out.arrive,),)),
                (6, ((project_out, 0), (sum_att[0].begin,), (sum_att[0].step_one,),)),
            ),
        ),
        (project_out, 1),
        (load_cot.wait,),
        (gate.begin,),
        (sum_att[1].begin,),
        (sum_att[0].step_two,),
        (sum_att[0].step_three,),
        (second_norm, 0),
        (down.forward_a,),
        (down.forward_b,),
        (up.forward_a,),
        (sum_att[1].step_one,),
        (sum_att[1].step_two,),
        (spread_two[0].step_two,),
        (sum_att[1].step_three,),
        (second_norm, 1),
        (up.forward_b,),
        (down.diagonal_a,),
        (down.diagonal_b,),
        (spread_two[0].step_one,),
        (down.arrive,),
        (up.diagonal_a,),
        (gate.forward_a,),
        (spread_two[1].step_one,),
        (gate.forward_b,),
        (spread_two[0].step_three,),
        (up.diagonal_b,),
        (up.arrive,),
        (gate.diagonal_a,),
        (spread_two[1].step_two,),
        (gate.diagonal_b,),
        (spread_two[0].finish,),
        (gate.arrive,),
        (settle_weights,),
        (
            looped,
            feed,
            2 * tile_count,
            (
                (3, ((spread_two[1].step_three,),)),
                (6, ((feed_back, 0), (sum_two[0].begin,), (spread_two[1].finish,),)),
            ),
        ),
        (feed_back, 1),
        (sum_two[0].step_one,),
        (sum_two[0].step_two,),
        (sum_two[1].begin,),
        (rs_down.partner,),
        (sum_two[0].step_three,),
        (rs_down.own,),
        (rs_gate.partner,),
        (sum_two[1].step_one,),
        (middle_back, 0),
        (rs_gate.own,),
        (rs_up.partner,),
        (sum_two[1].step_three,),
        (sum_two[1].step_two,),
        (rs_up.own,),
        (spread_mid[0].step_one,),
        (spread_mid[0].step_two,),
        (rs_up.push_near,),
        (middle_back, 1),
        (rs_down.push_near,),
        (feed_out, 1),
        (spread_mid[1].step_one,),
        (rs_gate.push_near,),
        (feed_out, 0),
        (spread_mid[0].step_three,),
        (sum_out[1].begin,),
        (sum_out[1].step_one,),
        (sum_out[0].begin,),
        (spread_mid[0].finish,),
        (out_back, 0),
        (rs_gate.push_diag,),
        (spread_mid[1].step_two,),
        (
            looped,
            attend_back,
            8,
            (
                (4, ((spread_mid[1].step_three,), (spread_mid[1].finish,), (kv_begin, 0), (sum_out[1].step_two,), (out_back, 1),)),
                (6, ((sum_out[1].step_three,), (rs_out.partner,), (sum_out[0].step_one,), (result_rows, 1), (rs_down.push_diag,),)),
            ),
        ),
        (kv_begin, 1),
        (rs_up.push_diag,),
        (kv_finish, 0),
        (project_back_rows, 0),
        (sum_out[0].step_three,),
        (sum_out[0].step_two,),
        (spread_out[1].step_two,),
        (sum_one[0].begin,),
        (rs_out.own,),
        (rs_out.push_diag,),
        (spread_out[1].step_one,),
        (kv_finish, 1),
        (project_back_rows, 1),
        (sum_one[1].begin,),
        (rs_gate.relay_a,),
        (result_rows, 0),
        (load_one.start,),
        (sum_one[0].step_one,),
        (spread_out[1].step_three,),
        (load_one.wait,),
        (rs_down.relay_a,),
        (sum_one[0].step_two,),
        (rs_qkv.partner,),
        (spread_out[0].step_two,),
        (sum_one[0].step_three,),
        (rs_out.relay_a,),
        (rs_up.relay_a,),
        (rs_up.relay_b,),
        (rs_down.relay_b,),
        (sum_one[1].step_one,),
        (rs_qkv.own,),
        (input_back, 0),
        (sum_one[1].step_two,),
        (sum_one[1].step_three,),
        (rs_qkv.push_diag,),
        (spread_in[0].step_two,),
        (spread_out[0].step_one,),
        (rs_gate.relay_b,),
        (input_back, 1),
        (rs_out.push_near,),
        (spread_in[0].step_one,),
        (rs_qkv.push_near,),
        (vec_begin,),
        (rs_down.collect, landing, fin_sem),
        (finish_turned, rs_down, o_down),
        (spread_out[0].step_three,),
        (rs_qkv.relay_a,),
        (spread_in[1].step_one,),
        (spread_in[1].step_two,),
        (rs_out.relay_b,),
        (rs_gate.collect, landing, fin_sem),
        (finish_rows, rs_gate, [(o_gate, 0, hidden)]),
        (rs_up.collect, landing, fin_sem),
        (finish_rows, rs_up, [(o_up, 0, hidden)]),
        (spread_in[0].step_three,),
        (rs_out.collect, landing, fin_sem),
        (finish_turned, rs_out, o_out),
        (rs_qkv.relay_b,),
        (spread_in[1].step_three,),
        (vec_middle,),
        (vec_finish,),
        (rs_qkv.collect, landing, fin_sem),
        (finish_qkv, rs_qkv),
        (settle,),
    )
    for action, *values in order:
        action(*values)


def run_layer(
    tokens, attn_gain, w_query, w_key, w_value, w_out, mlp_gain, w_gate, w_up, w_down, cotangent,
    positions, segments,
):
    shape = jax.ShapeDtypeStruct
    width = tokens.shape[1]
    hidden = w_gate.shape[1]
    vmem = pl.BlockSpec(memory_space=pltpu.VMEM)
    anywhere = pl.BlockSpec(memory_space=pl.ANY)
    dma = pltpu.SemaphoreType.DMA
    buffer = pltpu.VMEM
    half_size = HD // 2
    frequency = THETA_BASE ** (-np.arange(half_size, dtype=np.float32) / half_size)
    frequency = np.concatenate([frequency] * 4)[None, :].astype(np.float32)
    return pl.pallas_call(
        layer_kernel,
        name="decoder_layer",
        out_shape=(
            shape((2, 4, 64, width), BF),
            shape((2, 4, 64, width), BF),
            shape((2, 128), F32),
            shape((2, 128), F32),
            shape((256, 512), F32),
            shape((HD, 256), F32),
            shape((HD, 256), F32),
            shape((512, 256), F32),
            shape((256, hidden), F32),
            shape((256, hidden), F32),
            shape((hidden, 256), F32),
            shape((2, 256, hidden), BF),
            shape((2, 256, hidden), BF),
            shape((2, 256, hidden), BF),
            shape((2, 256, 512), BF),
            shape((2, 256, 640), BF),
            shape((2, 4, 64, width), BF),
        ),
        in_specs=[anywhere, vmem, vmem, vmem, vmem]
        + [anywhere] * 5
        + [vmem] * 3,
        out_specs=(anywhere,) * 2 + (vmem,) * 2 + (anywhere,) * 13,
        scratch_shapes=[
            buffer((8, 256), F32),
            buffer((8, 512), jnp.int32),
            buffer((8, 8, 256), F32),
            buffer((4, 8, 512), jnp.int32),
            buffer((512, width), BF),
            buffer((8, 256, hidden), BF),
            buffer((8, 256, hidden), BF),
            buffer((8, hidden, 256), BF),
            buffer((8, 512, 256), BF),
            buffer((8, 256, 640), BF),
            buffer((512, width), BF),
            buffer((2, 4, 64, width), BF),
            buffer((512, hidden), BF),
            buffer((512, hidden), BF),
            buffer((512, hidden), BF),
            buffer((4, 256, hidden), BF),
            buffer((3, 2, 128, hidden), BF),
            buffer((2, 2, 128, 640), BF),
            buffer((4, 256, 512), BF),
            buffer((4, 256, 640), BF),
            buffer((2, 64, hidden), F32),
            buffer((2, 128, 256), F32),
            buffer((2, 4, 64, width), BF),
            buffer((2, 3, 64, width), BF),
            buffer((2, 2, 64, width), BF),
            buffer((2, 3, 64, width), BF),
            buffer((2, 2, 64, width), BF),
            buffer((2, 4, 64, width), BF),
            buffer((64, width), F32),
            buffer((64, width), BF),
            buffer((2, 64, width), F32),
            buffer((2, 64, width), F32),
            buffer((512, 512), BF),
            buffer((2, 1024, 256), BF),
            buffer((16, 1, 256), F32),
            buffer((4, 512, 128), BF),
            buffer((512, 512), BF),
            buffer((512, 256), F32),
            buffer((256, 512), BF),
            buffer((2, 1024, 128), BF),
            buffer((2, HD, 1024), BF),
            buffer((1024, 128), BF),
            buffer((HD, 1024), BF),
            buffer((1024, 128), F32),
            buffer((1024, 128), F32),
            buffer((2, 4, 256, 128), BF),
            buffer((2, 3, 256, 128), BF),
            buffer((512, 640), BF),
            buffer((2, width), F32),
            buffer((4, 8, 8, 128), F32),
            buffer((8, 8, 128), F32),
            buffer((7, 8, 128), F32),
            dma((5, 9)),
            dma((5, 9)),
            dma((5,)),
            dma((10,)),
            dma((10,)),
            dma((3,)),
            dma((3,)),
            dma((4,)),
            dma((8, 3)),
            dma((8, 5)),
            dma((8, 5)),
            dma((8, 4)),
            dma((5, 10)),
            dma((5, 10)),
            pltpu.SemaphoreType.REGULAR((4,)),
            dma((2, 3)),
            dma((2, 3)),
            dma((10,)),
            dma((10,)),
            dma((2,)),
            dma((2, 2)),
            dma((2,)),
        ],
        compiler_params=pltpu.CompilerParams(
            collective_id=0, has_side_effects=True, vmem_limit_bytes=67043328
        ),
    )(
        tokens, jnp.stack([attn_gain, mlp_gain]), w_query, w_key.T, w_value.T, w_out, w_gate, w_up,
        w_down, cotangent, positions[None, :], segments[None, :], frequency,
    )


def hand_over_kernel(*refs):
    count = (len(refs) - 2) // 3
    sources, targets, buffers = refs[:count], refs[count : 2 * count], refs[2 * count : 3 * count]
    in_sem, out_sem = refs[3 * count :]
    fetch = [
        pltpu.make_async_copy(source, buffers[n], in_sem.at[n]) for n, source in enumerate(sources)
    ]
    store = [
        pltpu.make_async_copy(buffers[n], target, out_sem.at[n]) for n, target in enumerate(targets)
    ]
    for piece in fetch:
        piece.start()
    for n in range(count):
        fetch[n].wait()
        store[n].start()
    for piece in store:
        piece.wait()


def hand_over(values):
    anywhere = pl.BlockSpec(memory_space=pl.ANY)
    dma = pltpu.SemaphoreType.DMA
    return pl.pallas_call(
        hand_over_kernel,
        name="hand_over",
        out_shape=tuple(jax.ShapeDtypeStruct(value.shape, value.dtype) for value in values),
        in_specs=[anywhere] * len(values),
        out_specs=(anywhere,) * len(values),
        scratch_shapes=[pltpu.VMEM(value.shape, value.dtype) for value in values]
        + [dma((len(values),)), dma((len(values),))],
        compiler_params=pltpu.CompilerParams(vmem_limit_bytes=67043328),
    )(*values)


def fast_shards(tokens, *others):
    made = run_layer(tokens, *others)
    (
        query_g, out_g, gate_g, up_g, down_g, key_g, value_g, gain_one_g, gain_two_g, result, input_grad,
    ) = hand_over(made[4:5] + made[7:11] + made[5:7] + made[2:4] + made[0:2])
    return (
        result.reshape(tokens.shape),
        input_grad.reshape(tokens.shape),
        gain_one_g.reshape(-1),
        query_g,
        key_g.T,
        value_g.T,
        out_g,
        gain_two_g.reshape(-1),
        gate_g,
        up_g,
        down_g,
    )


def solution(mesh):
    in_specs = (
        P(("fsdp", "ctx"), None),
        P(("fsdp", "ctx")),
        P(("fsdp", "ctx"), "tp"),
        P(("fsdp", "ctx"), "tp"),
        P(("fsdp", "ctx"), "tp"),
        P("tp", ("fsdp", "ctx")),
        P(("fsdp", "ctx")),
        P(("fsdp", "ctx"), "tp"),
        P(("fsdp", "ctx"), "tp"),
        P("tp", ("fsdp", "ctx")),
        P(("fsdp", "ctx"), None),
        P(("fsdp", "ctx")),
        P(("fsdp", "ctx")),
    )
    out_specs = (
        P(("fsdp", "ctx"), None),
        P(("fsdp", "ctx"), None),
        P(("fsdp", "ctx")),
        P(("fsdp", "ctx"), "tp"),
        P(("fsdp", "ctx"), "tp"),
        P(("fsdp", "ctx"), "tp"),
        P("tp", ("fsdp", "ctx")),
        P(("fsdp", "ctx")),
        P(("fsdp", "ctx"), "tp"),
        P(("fsdp", "ctx"), "tp"),
        P("tp", ("fsdp", "ctx")),
    )
    small = (mesh.shape["fsdp"], mesh.shape["ctx"], mesh.shape["tp"]) == (2, 4, 4)
    return jax.shard_map(fast_shards if small else shards, mesh=mesh, in_specs=in_specs, out_specs=out_specs, check_vma=False)
```

```python
import jax
import jax.numpy as jnp
import numpy as np
from jax import lax
from jax.experimental import pallas as pl
from jax.experimental.pallas import tpu as pltpu
from jax.sharding import PartitionSpec as P

H = 32
KVH = 4
HD = 64


EPSILON = 1e-05
THETA_BASE = 10000.0
MASKED_SCORE = -1e30


def shifted(value, axis, steps):
    count = lax.axis_size(axis)
    pairs = [(source, (source + steps) % count) for source in range(count)]
    return lax.ppermute(value, axis, pairs)


def rope_tables(token_pos, half_size):
    frequency = THETA_BASE ** (-jnp.arange(half_size, dtype=jnp.float32) / half_size)
    angles = token_pos.astype(jnp.float32)[:, None] * frequency[None, :]
    return (jnp.cos(angles), jnp.sin(angles))


def rotate(head_rows, cosine, sine):
    half_size = head_rows.shape[-1] // 2
    first_half = head_rows[..., :half_size]
    second_half = head_rows[..., half_size:]
    cos_rows = cosine[:, None, :]
    sin_rows = sine[:, None, :]
    return jnp.concatenate(
        [
            first_half * cos_rows - second_half * sin_rows,
            second_half * cos_rows + first_half * sin_rows,
        ],
        axis=-1,
    )


def rotate_back(head_rows, cosine, sine):
    half_size = head_rows.shape[-1] // 2
    first_half = head_rows[..., :half_size]
    second_half = head_rows[..., half_size:]
    cos_rows = cosine[:, None, :]
    sin_rows = sine[:, None, :]
    return jnp.concatenate(
        [
            first_half * cos_rows + second_half * sin_rows,
            second_half * cos_rows - first_half * sin_rows,
        ],
        axis=-1,
    )


def project(left_side, right_side):
    return jnp.dot(left_side, right_side, preferred_element_type=jnp.float32)


def project_back(left_side, right_side):
    return lax.dot_general(
        left_side, right_side, (((1,), (1,)), ((), ())), preferred_element_type=jnp.float32
    )


def weight_grad(left_side, right_side):
    return lax.dot_general(
        left_side, right_side, (((0,), (0,)), ((), ())), preferred_element_type=jnp.float32
    )


def rms_norm(rows_in, gain_vec):
    inv_rms = lax.rsqrt(jnp.mean(rows_in * rows_in, axis=-1, keepdims=True) + EPSILON)
    unit_rows = rows_in * inv_rms
    return (unit_rows * gain_vec, unit_rows, inv_rms)


def rms_norm_back(gradient, gain_vec, unit_rows, inv_rms):
    gain_grad = jnp.sum(gradient * unit_rows, axis=0)
    scaled_grad = gradient * gain_vec
    return (
        inv_rms
        * (scaled_grad - unit_rows * jnp.mean(scaled_grad * unit_rows, axis=-1, keepdims=True)),
        gain_grad,
    )


def pair_mask(query_pos, query_seg, key_pos, key_seg):
    return (query_seg[:, None] == key_seg[None, :]) & (key_pos[None, :] <= query_pos[:, None])


def split_block(kv_block, kv_heads):
    key_rows = kv_block[:, : kv_heads * HD].reshape(-1, kv_heads, HD)
    value_rows = kv_block[:, kv_heads * HD :].reshape(-1, kv_heads, HD)
    return (key_rows, value_rows)


def attend_block(state_in, queries, kv_block, visible):
    row_top, row_total, output_sum = state_in
    key_rows, value_rows = split_block(kv_block, queries.shape[1])
    scores = jnp.einsum(
        "qkgd,pkd->kgqp", queries, key_rows, preferred_element_type=jnp.float32
    ) * HD ** (-0.5)
    scores = jnp.where(visible, scores, MASKED_SCORE)
    new_top = jnp.maximum(row_top, jnp.max(scores, axis=-1))
    weights = jnp.where(visible, jnp.exp(scores - new_top[..., None]), 0.0)
    decay_factor = jnp.exp(row_top - new_top)
    row_total = row_total * decay_factor + jnp.sum(weights, axis=-1)
    mixed_heads = jnp.einsum(
        "kgqp,pkd->qkgd",
        weights.astype(jnp.bfloat16),
        value_rows,
        preferred_element_type=jnp.float32,
    )
    output_sum = output_sum * jnp.transpose(decay_factor, (2, 0, 1))[..., None] + mixed_heads
    return (new_top, row_total, output_sum)


def block_grads(queries, out_grad, kv_block, visible, log_total, delta_rows):
    key_rows, value_rows = split_block(kv_block, queries.shape[1])
    scale_factor = HD ** (-0.5)
    scores = (
        jnp.einsum("qkgd,pkd->kgqp", queries, key_rows, preferred_element_type=jnp.float32)
        * scale_factor
    )
    probs_full = jnp.where(
        visible, jnp.exp(jnp.where(visible, scores, MASKED_SCORE) - log_total[..., None]), 0.0
    )
    value_grad = jnp.einsum(
        "kgqp,qkgd->pkd",
        probs_full.astype(jnp.bfloat16),
        out_grad,
        preferred_element_type=jnp.float32,
    )
    prob_grad = jnp.einsum(
        "qkgd,pkd->kgqp", out_grad, value_rows, preferred_element_type=jnp.float32
    )
    score_grad = (probs_full * (prob_grad - delta_rows[..., None])).astype(jnp.bfloat16)
    query_grad = (
        jnp.einsum("kgqp,pkd->qkgd", score_grad, key_rows, preferred_element_type=jnp.float32)
        * scale_factor
    )
    key_grad = (
        jnp.einsum("kgqp,qkgd->pkd", score_grad, queries, preferred_element_type=jnp.float32)
        * scale_factor
    )
    block_rows = kv_block.shape[0]
    return (
        query_grad,
        jnp.concatenate(
            [key_grad.reshape(block_rows, -1), value_grad.reshape(block_rows, -1)], axis=-1
        ),
    )


def shards(
    tokens,
    attn_gain,
    w_query,
    w_key,
    w_value,
    w_out,
    mlp_gain,
    w_gate,
    w_up,
    w_down,
    cotangent,
    positions,
    segments,
):
    token_rows = tokens.shape[0]
    gain_one, query_w, key_w, value_w, out_w = (
        lax.all_gather(attn_gain, ("fsdp", "ctx"), axis=0, tiled=True),
        lax.all_gather(w_query, ("fsdp", "ctx"), axis=0, tiled=True),
        lax.all_gather(w_key, ("fsdp", "ctx"), axis=0, tiled=True),
        lax.all_gather(w_value, ("fsdp", "ctx"), axis=0, tiled=True),
        lax.all_gather(w_out, ("fsdp", "ctx"), axis=1, tiled=True),
    )
    gain_two, gate_w, up_w, down_w = (
        lax.all_gather(mlp_gain, ("fsdp", "ctx"), axis=0, tiled=True),
        lax.all_gather(w_gate, ("fsdp", "ctx"), axis=0, tiled=True),
        lax.all_gather(w_up, ("fsdp", "ctx"), axis=0, tiled=True),
        lax.all_gather(w_down, ("fsdp", "ctx"), axis=1, tiled=True),
    )
    head_count = query_w.shape[1] // HD
    kv_heads = key_w.shape[1] // HD
    groups = H // KVH
    cosine, sine = rope_tables(positions, HD // 2)
    token_float = tokens.astype(jnp.float32)
    gain_one_float = gain_one.astype(jnp.float32)
    normed_one, unit_one, inv_one = rms_norm(token_float, gain_one_float)
    normed_low = normed_one.astype(jnp.bfloat16)
    query_lin = project(normed_low, query_w)
    key_lin = project(normed_low, key_w)
    value_low = project(normed_low, value_w).astype(jnp.bfloat16)
    query_rot = rotate(query_lin.reshape(token_rows, head_count, HD), cosine, sine).astype(
        jnp.bfloat16
    )
    key_rot = rotate(key_lin.reshape(token_rows, kv_heads, HD), cosine, sine).astype(jnp.bfloat16)
    queries = query_rot.reshape(token_rows, kv_heads, groups, HD)
    kv_local = jnp.concatenate([key_rot.reshape(token_rows, kv_heads * HD), value_low], axis=-1)
    key_positions, key_segments = (
        lax.all_gather(positions, "ctx", axis=0, tiled=True),
        lax.all_gather(segments, "ctx", axis=0, tiled=True),
    )
    my_index = lax.axis_index("ctx")
    cycle_size = lax.axis_size("ctx")

    def block_marks(source):
        start_row = source * token_rows
        return pair_mask(
            positions,
            segments,
            lax.dynamic_slice_in_dim(key_positions, start_row, token_rows),
            lax.dynamic_slice_in_dim(key_segments, start_row, token_rows),
        )

    start_state = (
        jnp.full((kv_heads, groups, token_rows), MASKED_SCORE, jnp.float32),
        jnp.zeros((kv_heads, groups, token_rows), jnp.float32),
        jnp.zeros((token_rows, kv_heads, groups, HD), jnp.float32),
    )

    def forward_block(state_in, kv_block, source):
        visible = block_marks(source)
        return attend_block(state_in, queries, kv_block, visible)

    def cycle_step(state_in, step_index):
        attn_state, kv_block = state_in
        attn_state = forward_block(attn_state, kv_block, (my_index - step_index) % cycle_size)
        passed = shifted(kv_block, "ctx", 1)
        return ((attn_state, passed), kv_block)

    (attn_state, last_block), kept_blocks = lax.scan(
        cycle_step, (start_state, kv_local), jnp.arange(cycle_size - 1)
    )
    attn_state = forward_block(attn_state, last_block, (my_index + 1) % cycle_size)
    kv_blocks = jnp.concatenate([kept_blocks, last_block[None]], axis=0)
    sources = (my_index - jnp.arange(cycle_size)) % cycle_size
    row_top, row_total, output_sum = attn_state
    attended = output_sum / jnp.transpose(row_total, (2, 0, 1))[..., None]
    log_total = row_top + jnp.log(row_total)
    attended_low = attended.reshape(token_rows, head_count * HD).astype(jnp.bfloat16)
    middle = token_float + lax.psum(project(attended_low, out_w).astype(jnp.bfloat16), "tp").astype(
        jnp.float32
    )
    gain_two_float = gain_two.astype(jnp.float32)
    normed_two, unit_two, inv_two = rms_norm(middle, gain_two_float)
    normed_two_low = normed_two.astype(jnp.bfloat16)
    gate_lin = project(normed_two_low, gate_w)
    up_lin = project(normed_two_low, up_w)
    hidden_low = (jax.nn.silu(gate_lin) * up_lin).astype(jnp.bfloat16)
    result = middle + lax.psum(project(hidden_low, down_w).astype(jnp.bfloat16), "tp").astype(
        jnp.float32
    )
    output = result.astype(jnp.bfloat16)
    hidden_grad = project_back(cotangent, down_w)
    down_w_grad = weight_grad(hidden_low, cotangent)
    sigmoid_gate = jax.nn.sigmoid(gate_lin)
    gate_grad_low = (
        hidden_grad * up_lin * sigmoid_gate * (1.0 + gate_lin * (1.0 - sigmoid_gate))
    ).astype(jnp.bfloat16)
    up_grad_low = (hidden_grad * gate_lin * sigmoid_gate).astype(jnp.bfloat16)
    normed_two_grad = lax.psum(
        (project_back(gate_grad_low, gate_w) + project_back(up_grad_low, up_w)).astype(
            jnp.bfloat16
        ),
        "tp",
    ).astype(jnp.float32)
    gate_w_grad = weight_grad(normed_two_low, gate_grad_low)
    up_w_grad = weight_grad(normed_two_low, up_grad_low)
    norm_back_two, gain_two_grad = rms_norm_back(normed_two_grad, gain_two_float, unit_two, inv_two)
    middle_grad = cotangent.astype(jnp.float32) + norm_back_two
    middle_low = middle_grad.astype(jnp.bfloat16)
    attended_grad_low = project_back(middle_low, out_w).astype(jnp.bfloat16)
    out_w_grad = weight_grad(attended_low, middle_low)
    out_grad = attended_grad_low.reshape(token_rows, kv_heads, groups, HD)
    delta_rows = jnp.transpose(jnp.sum(out_grad.astype(jnp.float32) * attended, axis=-1), (1, 2, 0))

    def backward_block(kv_block, source):
        visible = block_marks(source)
        return block_grads(queries, out_grad, kv_block, visible, log_total, delta_rows)

    query_start = jnp.zeros((token_rows, kv_heads, groups, HD), jnp.float32)

    def back_step(state_in, pieces):
        query_acc, kv_acc = state_in
        query_term, kv_term = backward_block(pieces[0], pieces[1])
        passed = shifted((kv_acc + kv_term).astype(jnp.bfloat16), "ctx", 1).astype(jnp.float32)
        return ((query_acc + query_term, passed), None)

    (query_grad, kv_grad), unused = lax.scan(
        back_step, (query_start, jnp.zeros(kv_local.shape, jnp.float32)), (kv_blocks, sources)
    )
    query_grad_low = (
        rotate_back(query_grad.reshape(token_rows, head_count, HD), cosine, sine)
        .reshape(token_rows, head_count * HD)
        .astype(jnp.bfloat16)
    )
    key_grad_low = (
        rotate_back(kv_grad[:, : kv_heads * HD].reshape(token_rows, kv_heads, HD), cosine, sine)
        .reshape(token_rows, kv_heads * HD)
        .astype(jnp.bfloat16)
    )
    value_grad_low = kv_grad[:, kv_heads * HD :].astype(jnp.bfloat16)
    normed_one_grad = lax.psum(
        (
            project_back(query_grad_low, query_w)
            + project_back(key_grad_low, key_w)
            + project_back(value_grad_low, value_w)
        ).astype(jnp.bfloat16),
        "tp",
    ).astype(jnp.float32)
    query_w_grad = weight_grad(normed_low, query_grad_low)
    key_w_grad = weight_grad(normed_low, key_grad_low)
    value_w_grad = weight_grad(normed_low, value_grad_low)
    norm_back_one, gain_one_grad = rms_norm_back(normed_one_grad, gain_one_float, unit_one, inv_one)
    input_grad = (middle_grad + norm_back_one).astype(jnp.bfloat16)
    summed = (
        lax.psum_scatter(
            gain_one_grad.astype(jnp.bfloat16), ("fsdp", "ctx"), scatter_dimension=0, tiled=True
        ).astype(jnp.float32),
        lax.psum_scatter(
            query_w_grad.astype(jnp.bfloat16), ("fsdp", "ctx"), scatter_dimension=0, tiled=True
        ).astype(jnp.float32),
        lax.psum_scatter(
            key_w_grad.astype(jnp.bfloat16), ("fsdp", "ctx"), scatter_dimension=0, tiled=True
        ).astype(jnp.float32),
        lax.psum_scatter(
            value_w_grad.astype(jnp.bfloat16), ("fsdp", "ctx"), scatter_dimension=0, tiled=True
        ).astype(jnp.float32),
        lax.psum_scatter(
            out_w_grad.astype(jnp.bfloat16), ("fsdp", "ctx"), scatter_dimension=1, tiled=True
        ).astype(jnp.float32),
        lax.psum_scatter(
            gain_two_grad.astype(jnp.bfloat16), ("fsdp", "ctx"), scatter_dimension=0, tiled=True
        ).astype(jnp.float32),
        lax.psum_scatter(
            gate_w_grad.astype(jnp.bfloat16), ("fsdp", "ctx"), scatter_dimension=0, tiled=True
        ).astype(jnp.float32),
        lax.psum_scatter(
            up_w_grad.astype(jnp.bfloat16), ("fsdp", "ctx"), scatter_dimension=0, tiled=True
        ).astype(jnp.float32),
        lax.psum_scatter(
            down_w_grad.astype(jnp.bfloat16), ("fsdp", "ctx"), scatter_dimension=1, tiled=True
        ).astype(jnp.float32),
    )
    return (output, input_grad) + tuple(summed)


MESH = pl.DeviceIdType.MESH
BF = jnp.bfloat16
F32 = jnp.float32


def dotg(left_side, right_side, left_dim, right_dim):
    return lax.dot_general(
        left_side,
        right_side,
        (((left_dim,), (right_dim,)), ((), ())),
        preferred_element_type=F32,
    )


def remote(src, dst, send_sem, recv_sem, device):
    return pltpu.make_async_remote_copy(
        src_ref=src,
        dst_ref=dst,
        send_sem=send_sem,
        recv_sem=recv_sem,
        device_id=device,
        device_id_type=MESH,
    )


class Place:
    def __init__(self):
        self.f = lax.axis_index("fsdp")
        self.c = lax.axis_index("ctx")
        self.z = lax.axis_index("tp")
        self.cx = self.c + 1 - 2 * lax.rem(self.c, 2)
        self.cy = lax.rem(self.c + 2, 4)
        self.cd = 3 - self.c
        self.of = 1 - self.f
        self.own = self.f * 4 + self.c
        self.sx = self.f * 4 + self.cx
        self.sy = self.f * 4 + self.cy
        self.sd = self.f * 4 + self.cd

    def at(self, f=None, c=None, z=None):
        return (
            self.f if f is None else f,
            self.c if c is None else c,
            self.z if z is None else z,
        )


def group_devices(me):
    return [
        me.at(c=me.cx),
        me.at(c=me.cy),
        me.at(c=me.cd),
        me.at(f=me.of),
        me.at(f=me.of, c=me.cx),
        me.at(f=me.of, c=me.cy),
        me.at(f=me.of, c=me.cd),
    ]


def column_devices(me):
    return [me.at(z=lax.rem(me.z + step, 4)) for step in (1, 2, 3)]


class Gather:
    def __init__(self, me, index, own, full, send, recv, local_sem):
        self.me, self.full, self.placed = me, full, own is None
        own = full.at[me.own] if own is None else own
        rows = full.shape[1]
        self.half_a = pl.ds(0, rows // 2)
        self.half_b = pl.ds(rows // 2, rows // 2)

        def copy(slot, src, dst, device):
            return remote(src, dst, send.at[index, slot], recv.at[index, slot], device)

        slot_own, slot_x, slot_y = full.at[me.own], full.at[me.sx], full.at[me.sy]
        to_x, to_y, to_core = me.at(c=me.cx), me.at(c=me.cy), me.at(f=me.of)
        diag_a = full.at[me.sd, self.half_a]
        diag_b = full.at[me.sd, self.half_b]
        self.own_x = copy(0, own, slot_own, to_x)
        self.own_y = copy(1, own, slot_own, to_y)
        self.own_core = copy(2, own, slot_own, to_core)
        self.pass_x = copy(3, full.at[me.sy, self.half_a], full.at[me.sy, self.half_a], to_x)
        self.pass_y = copy(4, full.at[me.sx, self.half_b], full.at[me.sx, self.half_b], to_y)
        self.core_x = copy(5, slot_x, slot_x, to_core)
        self.core_y = copy(6, slot_y, slot_y, to_core)
        self.core_a = copy(7, diag_a, diag_a, to_core)
        self.core_b = copy(8, diag_b, diag_b, to_core)
        other = me.of * 4
        into = lambda slot, ref, device: copy(slot, ref, ref, device)
        self.in_x = into(0, slot_x, to_x)
        self.in_y = into(1, slot_y, to_y)
        self.in_a = into(3, diag_a, to_x)
        self.in_b = into(4, diag_b, to_y)
        self.in_core = [
            into(2, full.at[other + me.c], to_core),
            into(5, full.at[other + me.cx], to_core),
            into(6, full.at[other + me.cy], to_core),
            into(7, full.at[other + me.cd, self.half_a], to_core),
            into(8, full.at[other + me.cd, self.half_b], to_core),
        ]
        self.keep = None if self.placed else pltpu.make_async_copy(own, slot_own, local_sem.at[index])

    def begin(self):
        self.own_x.start()
        self.own_y.start()
        self.own_core.start()
        if not self.placed:
            self.keep.start()

    def forward_a(self):
        self.in_y.wait_recv()
        self.pass_x.start()
        self.core_y.start()

    def forward_b(self):
        self.in_x.wait_recv()
        self.pass_y.start()
        self.core_x.start()

    def diagonal_a(self):
        self.in_a.wait_recv()
        self.core_a.start()

    def diagonal_b(self):
        self.in_b.wait_recv()
        self.core_b.start()

    def arrive(self):
        if not self.placed:
            self.keep.wait()
        for piece in self.in_core:
            piece.wait_recv()

    def settle(self):
        for piece in (
            self.own_x,
            self.own_y,
            self.own_core,
            self.pass_x,
            self.pass_y,
            self.core_x,
            self.core_y,
            self.core_a,
            self.core_b,
        ):
            piece.wait_send()


class LineSum:
    def __init__(self, me, part, outer_in, inner_in, send, recv):
        self.me, self.part = me, part
        self.outer_in, self.inner_in = outer_in, inner_in
        self.send, self.recv = send, recv
        z = me.z
        self.is_mid = (z == 1) | (z == 2)
        self.is_end = (z == 0) | (z == 3)
        self.mid_of_end = 1 + z // 3
        self.outer_of_mid = 3 * (z - 1)

    def end_copies(self):
        me, part = self.me, self.part
        mid = self.mid_of_end
        to_mid = me.at(z=mid)
        owners = (3 - me.z, 3 - mid, mid)
        return [
            remote(
                part.at[owner],
                self.outer_in.at[slot],
                self.send.at[slot],
                self.recv.at[slot],
                to_mid,
            )
            for slot, owner in enumerate(owners)
        ]

    def mid_copies(self):
        me, part = self.me, self.part
        far_mid, outer = 3 - me.z, self.outer_of_mid
        far = 3 - outer
        to_mid, to_outer = me.at(z=far_mid), me.at(z=outer)
        return [
            remote(part.at[far], self.inner_in.at[0], self.send.at[0], self.recv.at[3], to_mid),
            remote(part.at[far_mid], self.inner_in.at[1], self.send.at[1], self.recv.at[4], to_mid),
            remote(part.at[outer], self.inner_in.at[0], self.send.at[2], self.recv.at[3], to_outer),
        ]

    def wait_in(self, slot, buffer):
        remote(buffer, buffer, self.send.at[0], self.recv.at[slot], self.me.at(z=3 - self.me.z)).wait_recv()

    def add(self, owner, buffer):
        self.part[owner] = (self.part[owner].astype(F32) + buffer[...].astype(F32)).astype(BF)

    def begin(self):
        @pl.when(self.is_end)
        def _():
            for piece in self.end_copies():
                piece.start()

    def step_one(self):
        @pl.when(self.is_mid)
        def _():
            far = 3 - self.outer_of_mid
            self.wait_in(0, self.outer_in.at[0])
            self.add(far, self.outer_in.at[0])
            self.mid_copies()[0].start()

    def step_two(self):
        @pl.when(self.is_mid)
        def _():
            copies = self.mid_copies()
            self.wait_in(1, self.outer_in.at[1])
            self.add(3 - self.me.z, self.outer_in.at[1])
            copies[1].start()

    def step_three(self):
        @pl.when(self.is_mid)
        def _():
            self.wait_in(3, self.inner_in.at[0])
            self.add(self.outer_of_mid, self.inner_in.at[0])
            self.mid_copies()[2].start()

    def finish(self, total):
        me = self.me

        @pl.when(self.is_mid)
        def _():
            self.wait_in(2, self.outer_in.at[2])
            self.wait_in(4, self.inner_in.at[1])
            total[...] = (
                self.part[me.z].astype(F32)
                + self.outer_in[2].astype(F32)
                + self.inner_in[1].astype(F32)
            )
            for piece in self.mid_copies():
                piece.wait_send()

        @pl.when(self.is_end)
        def _():
            self.wait_in(3, self.inner_in.at[0])
            total[...] = self.part[me.z].astype(F32) + self.inner_in[0].astype(F32)
            for piece in self.end_copies():
                piece.wait_send()


class LineGather:
    def __init__(self, me, blocks, send, recv):
        self.me, self.blocks, self.send, self.recv = me, blocks, send, recv
        z = me.z
        self.is_mid = (z == 1) | (z == 2)
        self.is_end = (z == 0) | (z == 3)
        self.mid_of_end = 1 + z // 3
        self.outer_of_mid = 3 * (z - 1)

    def copy(self, owner, slot, z):
        ref = self.blocks.at[owner]
        return remote(ref, ref, self.send.at[slot], self.recv.at[owner], self.me.at(z=z))

    def wait_in(self, owner):
        ref = self.blocks.at[owner]
        remote(ref, ref, self.send.at[0], self.recv.at[owner], self.me.at(z=3 - self.me.z)).wait_recv()

    def begin(self):
        me = self.me

        @pl.when(self.is_end)
        def _():
            self.copy(me.z, 0, self.mid_of_end).start()

        @pl.when(self.is_mid)
        def _():
            self.copy(me.z, 0, self.outer_of_mid).start()
            self.copy(me.z, 1, 3 - me.z).start()

    def step_one(self):
        me = self.me

        @pl.when(self.is_mid)
        def _():
            self.wait_in(self.outer_of_mid)
            self.copy(self.outer_of_mid, 2, 3 - me.z).start()

    def step_two(self):
        me = self.me

        @pl.when(self.is_mid)
        def _():
            self.wait_in(3 - me.z)
            self.copy(3 - me.z, 3, self.outer_of_mid).start()

    def step_three(self):
        @pl.when(self.is_mid)
        def _():
            far = 3 - self.outer_of_mid
            self.wait_in(far)
            self.copy(far, 4, self.outer_of_mid).start()

    def finish(self):
        me = self.me

        @pl.when(self.is_mid)
        def _():
            self.copy(me.z, 0, self.outer_of_mid).wait_send()
            self.copy(me.z, 1, 3 - me.z).wait_send()
            self.copy(self.outer_of_mid, 2, 3 - me.z).wait_send()
            self.copy(3 - me.z, 3, self.outer_of_mid).wait_send()
            self.copy(3 - self.outer_of_mid, 4, self.outer_of_mid).wait_send()

        @pl.when(self.is_end)
        def _():
            mid = self.mid_of_end
            self.wait_in(mid)
            self.wait_in(3 - mid)
            self.wait_in(3 - me.z)
            self.copy(me.z, 0, mid).wait_send()


def row_of(gains_ref, which):
    return jnp.concatenate([gains_ref[shard, which : which + 1, :] for shard in range(8)], axis=-1)


def swap_halves(rows):
    lane = lax.broadcasted_iota(jnp.int32, rows.shape, 1)
    return jnp.where(
        lax.rem(lane, HD) < HD // 2, pltpu.roll(rows, 96, 1), pltpu.roll(rows, 32, 1)
    )


class Scatter:
    def __init__(self, me, index, last, width, x_of, y_of, chips, refs):
        self.me, self.index, self.last, self.width = me, index, last, width
        self.x_of, self.y_of, self.chips = x_of, y_of, chips
        self.stage, self.core_in, self.diag_in, self.near_in = refs[:4]
        self.send, self.recv, self.credit = refs[4:]
        self.to_x, self.to_y, self.to_core = me.at(c=me.cx), me.at(c=me.cy), me.at(f=me.of)
        self.sent = []

    def copy(self, slot, src, dst, device):
        return remote(
            src, dst, self.send.at[self.index, slot], self.recv.at[self.index, slot], device
        )

    def lanes(self, ref):
        return ref.at[:, pl.ds(0, self.width)]

    def core_copy(self, role):
        return self.copy(
            role, self.stage(self.width, role), self.lanes(self.core_in.at[role]), self.to_core
        )

    def chunk(self, core, role):
        c = self.me.c
        high = lax.rem(c // 2 + role // 2, 2)
        low = lax.rem(lax.rem(c, 2) + lax.rem(role, 2), 2)
        return dotg(self.x_of(core * 4 + 2 * high + low), self.y_of(), 0, 0)

    def roles(self, body):
        def pair(step, carry):
            body(3 - step)
            body(1 - step)
            return carry

        lax.fori_loop(0, 2, pair, 0)

    def partner(self):
        def body(role):
            self.stage(self.width, role)[...] = self.chunk(self.me.of, role).astype(BF)
            if self.index > 0:
                pl.semaphore_wait(self.credit.at[role], 1)
            self.core_copy(role).start()

        self.roles(body)

    def own(self):
        def body(role):
            value = self.chunk(self.me.f, role)
            self.core_copy(role).wait_recv()
            chip = self.chips(role)
            chip[...] = (value + self.lanes(self.core_in.at[role])[...].astype(F32)).astype(BF)
            if not self.last:
                pl.semaphore_signal(
                    self.credit.at[role], inc=1, device_id=self.to_core, device_id_type=MESH
                )

        self.roles(body)
        for role in range(4):
            self.core_copy(role).wait_send()

    def near(self, role, half, slot):
        rows = pl.ds(half * 128, 128)
        side = role - 1
        device = self.to_x if role == 1 else self.to_y
        return self.copy(
            slot, self.chips(role).at[rows, :], self.near_in.at[side, rows, :], device
        )

    def diag(self, half):
        device = self.to_x if half == 0 else self.to_y
        return self.copy(
            4 + half,
            self.chips(3).at[pl.ds(half * 128, 128), :],
            self.lanes(self.diag_in.at[half]),
            device,
        )

    def push_diag(self):
        self.diag(0).start()
        self.diag(1).start()

    def push_near(self):
        self.near(1, 0, 6).start()
        self.near(2, 1, 7).start()

    def relay_a(self):
        first = pl.ds(0, 128)
        self.diag(0).wait_recv()
        rows = self.chips(2).at[first, :]
        rows[...] = (
            rows[...].astype(F32) + self.lanes(self.diag_in.at[0])[...].astype(F32)
        ).astype(BF)
        self.near(2, 0, 8).start()

    def relay_b(self):
        second = pl.ds(128, 128)
        self.diag(1).wait_recv()
        rows = self.chips(1).at[second, :]
        rows[...] = (
            rows[...].astype(F32) + self.lanes(self.diag_in.at[1])[...].astype(F32)
        ).astype(BF)
        self.near(1, 1, 9).start()

    def collect(self, buffer, sem):
        for role, half, slot in ((1, 0, 6), (2, 1, 7), (2, 0, 8), (1, 1, 9)):
            self.near(role, half, slot).wait_recv()
        for side in range(2):
            pltpu.make_async_copy(
                self.near_in.at[side], self.lanes(buffer.at[side]), sem.at[side]
            ).start()

    def collected(self, buffer, sem):
        for side in range(2):
            pltpu.make_async_copy(
                self.near_in.at[side], self.lanes(buffer.at[side]), sem.at[side]
            ).wait()

    def settle(self):
        for half in range(2):
            self.diag(half).wait_send()
        for role, half, slot in ((1, 0, 6), (2, 1, 7), (2, 0, 8), (1, 1, 9)):
            self.near(role, half, slot).wait_send()


def norm_back(gradient, rows_in, gain):
    inv = lax.rsqrt(jnp.mean(rows_in * rows_in, axis=-1, keepdims=True) + EPSILON)
    unit = rows_in * inv
    scaled = gradient * gain
    back = inv * (scaled - unit * jnp.mean(scaled * unit, axis=-1, keepdims=True))
    return back, jnp.sum(gradient * unit, axis=0, keepdims=True)


def layer_kernel(
    tok_h,
    gain_one_in,
    gain_two_in,
    w_query_in,
    w_key_in,
    w_value_in,
    out_h,
    gate_h,
    up_h,
    down_h,
    cot_h,
    pos_in,
    seg_in,
    freq,
    o_result,
    o_input,
    o_gain_one,
    o_gain_two,
    o_query,
    o_key,
    o_value,
    o_out,
    o_gate,
    o_up,
    o_down,
    near_down,
    near_gate,
    near_up,
    near_out,
    near_qkv,
    n_one_h,
    own_gains,
    own_marks,
    gains,
    marks,
    tok,
    w_gate,
    w_up,
    w_down,
    w_out,
    w_qkv,
    cot,
    n_two,
    hid,
    gate_g,
    up_g,
    core_in,
    diag_in,
    diag_low,
    chip_out,
    chip_qkv,
    sum_stage,
    turn_stage,
    part,
    outer_in,
    inner_in,
    outer_two,
    inner_two,
    mlow,
    total,
    own_out,
    mid,
    mid_g,
    q_rot,
    bias,
    lse,
    kv,
    att,
    rope,
    do_rows,
    keys,
    vals_t,
    vals,
    keys_t,
    key_acc,
    val_acc,
    kv_send_buf,
    kv_in,
    d_qkv,
    vec,
    vec_in,
    vec_out,
    vec_near,
    g_send,
    g_recv,
    g_local,
    small_send,
    small_recv,
    first_send,
    first_recv,
    load_sem,
    sum_send,
    sum_recv,
    all_send,
    all_recv,
    rs_send,
    rs_recv,
    credit,
    kv_send,
    kv_recv,
    vec_send,
    vec_recv,
    fin_sem,
    put_sem,
    own_sem,
):
    me = Place()
    group = group_devices(me)
    hidden = hid.shape[1]

    rows_of = [pl.ds(g * 256, 256) for g in range(2)]
    load_tok = pltpu.make_async_copy(tok_h, tok, load_sem.at[0])
    load_cot = pltpu.make_async_copy(cot_h, cot, load_sem.at[1])
    save_one = pltpu.make_async_copy(mlow, n_one_h, load_sem.at[2])
    load_one = pltpu.make_async_copy(n_one_h, mlow, load_sem.at[3])
    load_tok.start()
    load_cot.start()
    barrier = pltpu.get_barrier_semaphore()
    for device in group + column_devices(me):
        pl.semaphore_signal(barrier, inc=1, device_id=device, device_id_type=MESH)

    w_qkv[me.own, :, 0:512] = w_query_in[...]
    turned = jnp.concatenate([w_key_in[...], w_value_in[...]], axis=0).astype(F32)
    w_qkv[me.own, :, 512:640] = jnp.transpose(turned).astype(BF)
    own_gains[0:1, :] = gain_one_in[...].reshape(1, 256).astype(F32)
    own_gains[1:2, :] = gain_two_in[...].reshape(1, 256).astype(F32)
    own_gains[2:8, :] = jnp.zeros((6, 256), F32)
    own_marks[0:1, :] = pos_in[...]
    own_marks[1:2, :] = seg_in[...]
    own_marks[2:8, :] = jnp.zeros((6, 512), jnp.int32)
    pl.semaphore_wait(barrier, 10)

    qkv = Gather(me, 0, None, w_qkv, g_send, g_recv, g_local)
    out = Gather(me, 1, out_h, w_out, g_send, g_recv, g_local)
    gate = Gather(me, 2, gate_h, w_gate, g_send, g_recv, g_local)
    up = Gather(me, 3, up_h, w_up, g_send, g_recv, g_local)
    down = Gather(me, 4, down_h, w_down, g_send, g_recv, g_local)

    sources = [me.sx, me.sy, me.sd, me.of * 4 + me.c, me.of * 4 + me.cx, me.of * 4 + me.cy, me.of * 4 + me.cd]

    def small_copies(gain_slots, mark_slots):
        return [
            remote(own_gains, gains.at[spot], small_send.at[slot], small_recv.at[slot], group[slot])
            for slot, spot in enumerate(gain_slots)
        ] + [
            remote(
                own_marks, marks.at[spot], small_send.at[7 + slot], small_recv.at[7 + slot], group[slot]
            )
            for slot, spot in enumerate(mark_slots)
        ]

    small = small_copies([me.own] * 7, [me.c] * 3)

    def small_begin():
        for piece in small:
            piece.start()
        gains[me.own] = own_gains[...]
        marks[me.c] = own_marks[...]

    def small_finish():
        for piece in small_copies(sources, (me.cx, me.cy, me.cd)):
            piece.wait_recv()

    def first_norm():
        load_tok.wait()
        gain_one = row_of(gains, 0)

        def body(step, carry):
            values = tok[pl.ds(pl.multiple_of(step * 64, 64), 64), :].astype(F32)
            inv = lax.rsqrt(jnp.mean(values * values, axis=-1, keepdims=True) + EPSILON)
            mlow[step // 4, lax.rem(step, 4)] = (values * inv * gain_one).astype(BF)
            return carry

        lax.fori_loop(0, 8, body, 0)
        save_one.start()

    def make_rope():
        lane = lax.broadcasted_iota(jnp.int32, (128, 128), 1)
        low_half = lax.rem(lane, HD) < HD // 2
        for step in range(4):
            rows = slice(step * 128, (step + 1) * 128)
            places = own_marks[0:1, rows].astype(F32)
            angles = jnp.transpose(jnp.broadcast_to(places, (128, 128))) * freq[...]
            sine = jnp.sin(angles)
            rope[rows, :128] = jnp.cos(angles)
            rope[rows, 128:] = jnp.where(low_half, -sine, sine)

    def make_bias(g):
        own_rows = own_marks[:, g * 256 : (g + 1) * 256].astype(F32)
        for source in range(4):
            key_rows = marks[source, :, g * 256 : (g + 1) * 256].astype(F32)
            key_pos = jnp.transpose(jnp.broadcast_to(key_rows[0:1, :], (128, 256)))
            key_seg = jnp.transpose(jnp.broadcast_to(key_rows[1:2, :], (128, 256)))
            for side in range(2):
                lanes = slice(side * 128, (side + 1) * 128)
                seen = (key_seg == own_rows[1:2, lanes]) & (key_pos <= own_rows[0:1, lanes])
                bias[g, source * 256 : (source + 1) * 256, lanes] = jnp.where(
                    seen, 0.0, MASKED_SCORE
                ).astype(BF)

    lane_pair = lax.broadcasted_iota(jnp.int32, (256, 128), 1)

    def project_in(first, width):
        total_rows = None
        for shard in range(8):
            term = dotg(
                mlow[:, :, :, shard * 256 : (shard + 1) * 256].reshape(512, 256),
                w_qkv[shard, :, first : first + width],
                1,
                0,
            )
            total_rows = term if total_rows is None else total_rows + term
        return total_rows

    def first_copies(places):
        return [
            remote(kv.at[place], kv.at[place], first_send.at[slot], first_recv.at[slot], group[slot])
            for slot, place in enumerate(places)
        ]

    def project_kv():
        rows = project_in(512, 128)
        is_key = lax.broadcasted_iota(jnp.int32, (512, 128), 1) < HD
        cos_rows = jnp.where(is_key, rope[:, :128], 1.0)
        sin_rows = jnp.where(is_key, rope[:, 128:], 0.0)
        kv[me.c] = (rows * cos_rows + swap_halves(rows) * sin_rows).astype(BF)
        for piece in first_copies([me.c] * 3):
            piece.start()

    def project_q(half):
        rows_all = project_in(half * 256, 256)
        for inner in range(2):
            pair = half * 2 + inner
            rows = rows_all[:, inner * 128 : (inner + 1) * 128]
            rot = (rows * rope[:, :128] + swap_halves(rows) * rope[:, 128:]).astype(BF)
            rot = rot * jnp.bfloat16(HD ** (-0.5))
            q_rot[:, pair * 128 : (pair + 1) * 128] = rot

    def kv_arrive():
        for piece in first_copies((me.cx, me.cy, me.cd)):
            piece.wait_recv()
        for g in range(2):
            for source in range(4):
                pairs = kv[source, g * 256 : (g + 1) * 256, :].astype(F32)
                rows = slice(source * 256, (source + 1) * 256)
                keys[g, rows, :] = jnp.where(
                    lane_pair < HD, pairs, pltpu.roll(pairs, HD, 1)
                ).astype(BF)
                vals_t[g, :, rows] = jnp.transpose(pairs)[HD:, :].astype(BF)

    def one_head(pair_rows, odd):
        kept = lane_pair >= HD if odd else lane_pair < HD
        return jnp.where(kept, pair_rows, jnp.zeros_like(pair_rows))

    def attend(step):
        g = step // 4
        pair = step - g * 4
        halves = []
        own = pl.ds(pl.multiple_of(g * 256, 256), 256)
        lanes = pl.ds(pl.multiple_of(pair * 128, 128), 128)
        queries = q_rot[own, lanes]
        for odd in range(2):
            head = step * 2 + odd
            scores = dotg(keys[g], one_head(queries, odd), 1, 1) + bias[g].astype(F32)
            top = jnp.max(scores, axis=0, keepdims=True)
            weights = jnp.exp(scores - top)
            norm = jnp.sum(weights, axis=0, keepdims=True)
            mixed = dotg(vals_t[g], weights.astype(BF), 1, 0)
            halves.append(mixed / norm)
            lse[head] = top + jnp.log(norm)
        rows = jnp.transpose(jnp.concatenate(halves, axis=0))
        att[own, lanes] = rows.astype(BF)

    def project_out(g):
        def body(shard, carry):
            part[g, :, :, pl.ds(pl.multiple_of(shard * 256, 256), 256)] = (
                dotg(att[rows_of[g], :], w_out[shard], 1, 0).astype(BF).reshape(4, 64, 256)
            )
            return carry

        lax.fori_loop(0, 8, body, 0)

    def second_norm(g):
        sum_att[g].finish(total)
        own = pl.ds(pl.multiple_of(g * 256 + me.z * 64, 64), 64)
        mid_rows = tok[own, :].astype(F32) + total[...]
        mid[g] = mid_rows
        inv = lax.rsqrt(jnp.mean(mid_rows * mid_rows, axis=-1, keepdims=True) + EPSILON)
        n_two[g, me.z] = (mid_rows * inv * row_of(gains, 1)).astype(BF)
        spread_two[g].begin()

    def looped(body, count, hooks):
        def step(i, carry):
            for spot, actions in hooks:

                @pl.when(i == spot)
                def _():
                    for action, *values in actions:
                        action(*values)

            body(i)
            return carry

        lax.fori_loop(0, count, step, 0)

    tile_count = (hidden + 255) // 256

    def feed(step):
        g = step // tile_count
        n = step - g * tile_count
        rows = pl.ds(pl.multiple_of(g * 256, 256), 256)
        lanes = pl.ds(pl.multiple_of(jnp.minimum(n * 256, hidden - 256), 128), 256)
        normed = n_two[g].reshape(256, 2048)
        gate = dotg(normed, w_gate[:, :, lanes].reshape(2048, 256), 1, 0)
        up = dotg(normed, w_up[:, :, lanes].reshape(2048, 256), 1, 0)
        hidden_grad = None
        for shard in range(8):
            term = dotg(
                cot[rows, shard * 256 : (shard + 1) * 256], w_down[shard, lanes, :], 1, 1
            )
            hidden_grad = term if hidden_grad is None else hidden_grad + term
        sig = jax.nn.sigmoid(gate)
        silu = gate * sig
        hid[rows, lanes] = (silu * up).astype(BF)
        up_g[rows, lanes] = (hidden_grad * silu).astype(BF)
        gate_g[rows, lanes] = (
            hidden_grad * up * sig * (1.0 + gate * (1.0 - sig))
        ).astype(BF)

    def feed_back(g):
        def body(shard, carry):
            term = dotg(gate_g[rows_of[g], :], w_gate[shard], 1, 1) + dotg(
                up_g[rows_of[g], :], w_up[shard], 1, 1
            )
            part[g, :, :, pl.ds(pl.multiple_of(shard * 256, 256), 256)] = term.astype(BF).reshape(
                4, 64, 256
            )
            return carry

        lax.fori_loop(0, 8, body, 0)

    part_two = n_two

    def feed_out(g):
        def body(shard, carry):
            term = dotg(hid[rows_of[g], :], w_down[shard], 1, 0)
            part_two[g, :, :, pl.ds(pl.multiple_of(shard * 256, 256), 256)] = term.astype(
                BF
            ).reshape(4, 64, 256)
            return carry

        lax.fori_loop(0, 8, body, 0)

    def line_sum(slot, part_ref, outer, inner):
        return LineSum(me, part_ref, outer, inner, sum_send.at[slot], sum_recv.at[slot])

    sum_two = [line_sum(g, part.at[g], outer_in.at[g], inner_in.at[g]) for g in range(2)]
    sum_one = [line_sum(2 + g, part.at[g], outer_in.at[g], inner_in.at[g]) for g in range(2)]

    sum_out = [
        line_sum(4 + g, part_two.at[g], outer_two.at[g], inner_two.at[g]) for g in range(2)
    ]
    sum_att = [line_sum(6 + g, part.at[g], outer_in.at[g], inner_in.at[g]) for g in range(2)]
    spread_two = [LineGather(me, n_two.at[g], all_send.at[6 + g], all_recv.at[6 + g]) for g in range(2)]
    spread_mid = [LineGather(me, mlow.at[g], all_send.at[g], all_recv.at[g]) for g in range(2)]
    spread_in = [LineGather(me, o_input.at[g], all_send.at[2 + g], all_recv.at[2 + g]) for g in range(2)]
    spread_out = [LineGather(me, o_result.at[g], all_send.at[4 + g], all_recv.at[4 + g]) for g in range(2)]

    def middle_back(g):
        sum_two[g].finish(total)
        own = pl.ds(pl.multiple_of(g * 256 + me.z * 64, 64), 64)
        back, gain_grad = norm_back(total[...], mid[g], row_of(gains, 1))
        if g == 0:
            vec[1:2, :] = gain_grad
        else:
            vec[1:2, :] += gain_grad
        grad = cot[own, :].astype(F32) + back
        mid_g[g] = grad
        mlow[g, me.z] = grad.astype(BF)
        spread_mid[g].begin()

    def put_own(g, ref, slot):
        copy = pltpu.make_async_copy(own_out, ref.at[g, me.z], own_sem.at[slot])
        copy.start()
        copy.wait()

    def input_back(g):
        sum_one[g].finish(total)
        own = pl.ds(pl.multiple_of(g * 256 + me.z * 64, 64), 64)
        back, gain_grad = norm_back(total[...], tok[own, :].astype(F32), row_of(gains, 0))
        if g == 0:
            vec[0:1, :] = gain_grad
        else:
            vec[0:1, :] += gain_grad
        own_out[...] = (mid_g[g] + back).astype(BF)
        put_own(g, o_input, 0)
        spread_in[g].begin()

    def result_rows(g):
        sum_out[g].finish(total)
        own_out[...] = (mid[g] + total[...]).astype(BF)
        put_own(g, o_result, 1)
        spread_out[g].begin()

    wide = lambda ref: (lambda shard: ref[:, pl.ds(pl.multiple_of(shard * 256, 256), 256)])

    def blocks_of(ref):
        return lambda shard: ref[
            :, :, :, pl.ds(pl.multiple_of(shard * 256, 256), 256)
        ].reshape(512, 256)

    def stage(width, slot):
        if width > 640:
            return w_up.at[4 + slot]
        first = lax.rem(slot, 2) * 640
        if not isinstance(slot, int):
            first = pl.multiple_of(first, 128)
        return w_up.at[4 + slot // 2, :, pl.ds(first, width)]

    landing = w_up.at[pl.ds(6, 2)]

    def scatter(index, width, x_of, y_of, chips, near):
        landed = diag_in.at[index] if index < 3 else diag_low.at[index - 3]
        refs = (stage, core_in, landed, near, rs_send, rs_recv, credit)
        return Scatter(me, index, index == 4, width, x_of, y_of, chips, refs)

    rs_down = scatter(
        0, hidden, wide(cot), lambda: hid[...], lambda role: w_gate.at[4 + role], near_down
    )
    rs_gate = scatter(
        1, hidden, blocks_of(n_two), lambda: gate_g[...], lambda role: w_gate.at[role], near_gate
    )
    rs_up = scatter(
        2, hidden, blocks_of(n_two), lambda: up_g[...], lambda role: w_up.at[role], near_up
    )
    rs_out = scatter(3, 512, blocks_of(mlow), lambda: att[...], lambda role: chip_out.at[role], near_out)
    rs_qkv = scatter(
        4,
        640,
        blocks_of(mlow),
        lambda: d_qkv[...],
        lambda role: chip_qkv.at[role],
        near_qkv,
    )

    def finish_rows(job, outs):
        job.collected(landing, fin_sem)
        width = job.width
        pending = [None, None]
        for step in range(4):
            slot = step % 2
            rows = slice(step * 64, (step + 1) * 64)
            if pending[slot] is not None:
                for piece in pending[slot]:
                    piece.wait()
            sum_stage[slot, :, :width] = (
                job.chips(0)[rows, :].astype(F32)
                + landing[0, rows, :width].astype(F32)
                + landing[1, rows, :width].astype(F32)
            )
            pending[slot] = [
                pltpu.make_async_copy(
                    sum_stage.at[slot, :, pl.ds(first, size)],
                    ref.at[pl.ds(step * 64, 64), :],
                    put_sem.at[slot, number],
                )
                for number, (ref, first, size) in enumerate(outs)
            ]
            for piece in pending[slot]:
                piece.start()
        for slot in range(2):
            for piece in pending[slot]:
                piece.wait()

    def finish_qkv(job):
        finish_rows(job, [(o_query, 0, 512)])
        lanes = slice(512, 640)
        turn_stage[0] = jnp.transpose(
            job.chips(0)[:, lanes].astype(F32)
            + landing[0, :, lanes].astype(F32)
            + landing[1, :, lanes].astype(F32)
        )
        copies = [
            pltpu.make_async_copy(
                turn_stage.at[0, pl.ds(first, HD), :], ref, put_sem.at[0, number]
            )
            for number, (first, ref) in enumerate(((0, o_key), (HD, o_value)))
        ]
        for piece in copies:
            piece.start()
        for piece in copies:
            piece.wait()

    def finish_turned(job, ref):
        job.collected(landing, fin_sem)

        def put(step, slot):
            rows = pl.ds(pl.multiple_of(step * 128, 128), 128)
            return pltpu.make_async_copy(turn_stage.at[slot], ref.at[rows, :], put_sem.at[slot, 0])

        def body(step, carry):
            slot = lax.rem(step, 2)
            lanes = pl.ds(pl.multiple_of(step * 128, 128), 128)

            @pl.when(step >= 2)
            def _():
                put(step, slot).wait()

            turn_stage[slot] = jnp.transpose(
                job.chips(0)[:, lanes].astype(F32)
                + landing[0, :, lanes].astype(F32)
                + landing[1, :, lanes].astype(F32)
            )
            put(step, slot).start()
            return carry

        lax.fori_loop(0, job.width // 128, body, 0)
        for slot in range(2):
            put(slot, slot).wait()

    def out_back(g):
        grad = None
        for shard in range(8):
            lanes = slice(shard * 256, (shard + 1) * 256)
            term = dotg(mlow[g, :, :, lanes].reshape(256, 256), w_out[shard], 1, 1)
            grad = term if grad is None else grad + term
        do_rows[...] = grad.astype(BF)
        for source in range(4):
            pairs = kv[source, rows_of[g], :].astype(F32)
            turned = pltpu.roll(pairs, HD, 1)
            rows = slice(source * 256, (source + 1) * 256)
            vals[rows, :] = jnp.where(lane_pair < HD, turned, pairs).astype(BF)
            keys_t[:, rows] = jnp.transpose(pairs)[:HD, :].astype(BF)
        key_acc[...] = jnp.zeros_like(key_acc)
        val_acc[...] = jnp.zeros_like(val_acc)

    def attend_back(step):
        g = step // 4
        pair = step - g * 4
        own = pl.ds(pl.multiple_of(g * 256, 256), 256)
        halves = []
        lanes = pl.ds(pl.multiple_of(pair * 128, 128), 128)
        queries, grads = q_rot[own, lanes], do_rows[:, lanes]
        for odd in range(2):
            query, grad = one_head(queries, odd), one_head(grads, odd)
            scores = dotg(keys[g], query, 1, 1) + bias[g].astype(F32)
            probs = jnp.exp(scores - lse[step * 2 + odd])
            prob_grad = dotg(vals[...], grad, 1, 1)
            delta = jnp.sum(probs * prob_grad, axis=0, keepdims=True)
            score_grad = (probs * (prob_grad - delta)).astype(BF)
            val_acc[...] += dotg(probs.astype(BF), grad, 1, 0)
            key_acc[...] += dotg(score_grad, query, 1, 0)
            halves.append(dotg(keys_t[...], score_grad, 1, 0))
        rows = jnp.transpose(jnp.concatenate(halves, axis=0)) * (HD ** (-0.5))
        rows = rows * rope[own, :128] - swap_halves(rows) * rope[own, 128:]
        d_qkv[own, lanes] = rows.astype(BF)

    def kv_copies(g):
        return [
            remote(
                kv_send_buf.at[g, column],
                kv_in.at[g, slot],
                kv_send.at[g, slot],
                kv_recv.at[g, slot],
                group[slot],
            )
            for slot, column in enumerate((me.cx, me.cy, me.cd))
        ]

    def kv_begin(g):
        for block in range(4):
            rows = slice(block * 256, (block + 1) * 256)
            key_rows, val_rows = key_acc[rows, :], val_acc[rows, :]
            joined = jnp.where(
                lane_pair < HD,
                key_rows + pltpu.roll(key_rows, HD, 1),
                val_rows + pltpu.roll(val_rows, HD, 1),
            )
            kv_send_buf[g, block] = joined.astype(BF)
        for piece in kv_copies(g):
            piece.start()

    def kv_finish(g):
        rows = kv_send_buf[g, me.c].astype(F32)
        for slot, piece in enumerate(kv_copies(g)):
            piece.wait_recv()
            rows = rows + kv_in[g, slot].astype(F32)
        cos_rows = jnp.where(lane_pair < HD, rope[rows_of[g], :128], 1.0)
        sin_rows = jnp.where(lane_pair < HD, rope[rows_of[g], 128:], 0.0)
        rows = rows * cos_rows - swap_halves(rows) * sin_rows
        d_qkv[rows_of[g], 512:640] = rows.astype(BF)

    def project_back_rows(g):
        def body(shard, carry):
            term = dotg(d_qkv[rows_of[g], :], w_qkv[shard], 1, 1)
            part[g, :, :, pl.ds(pl.multiple_of(shard * 256, 256), 256)] = term.astype(BF).reshape(
                4, 64, 256
            )
            return carry

        lax.fori_loop(0, 8, body, 0)

    line = column_devices(me)

    def vec_line():
        return [
            remote(vec_out, vec_in.at[slot], vec_send.at[slot], vec_recv.at[slot], device)
            for slot, device in enumerate(line)
        ]

    targets = [me.sx, me.sy, me.sd, me.of * 4 + me.c, me.of * 4 + me.cx, me.of * 4 + me.cy, me.of * 4 + me.cd]

    def vec_group():
        return [
            remote(
                vec_in.at[3, target],
                vec_near.at[slot],
                vec_send.at[3 + slot],
                vec_recv.at[3 + slot],
                device,
            )
            for slot, (target, device) in enumerate(zip(targets, group))
        ]

    def vec_begin():
        for shard in range(8):
            for which in range(2):
                for half in range(2):
                    first = shard * 256 + half * 128
                    vec_out[shard, 2 * which + half : 2 * which + half + 1, :] = vec[
                        which : which + 1, first : first + 128
                    ]
            vec_out[shard, 4:8, :] = jnp.zeros((4, 128), F32)
        for piece in vec_line():
            piece.start()

    def vec_middle():
        for piece in vec_line():
            piece.wait_recv()
        vec_in[3] = vec_out[...] + vec_in[0] + vec_in[1] + vec_in[2]
        for piece in vec_group():
            piece.start()

    def vec_finish():
        rows = vec_in[3, me.own]
        for slot, piece in enumerate(vec_group()):
            piece.wait_recv()
            rows = rows + vec_near[slot]
        o_gain_one[...] = rows[0:2, :]
        o_gain_two[...] = rows[2:4, :]

    def settle_weights():
        for piece in (qkv, out, gate, up, down):
            piece.settle()

    def settle():
        for spread in spread_in + spread_out:
            spread.finish()
        for job in (rs_down, rs_gate, rs_up, rs_out, rs_qkv):
            job.settle()
        for g in range(2):
            for piece in kv_copies(g):
                piece.wait_send()
        for piece in vec_line() + vec_group() + small + first_copies([me.c] * 3):
            piece.wait_send()

    order = (
        (qkv.begin,),
        (small_begin,),
        (make_rope,),
        (qkv.forward_a,),
        (qkv.forward_b,),
        (small_finish,),
        (first_norm,),
        (out.begin,),
        (qkv.diagonal_a,),
        (qkv.diagonal_b,),
        (qkv.arrive,),
        (project_kv,),
        (project_q, 0),
        (out.forward_a,),
        (make_bias, 0),
        (out.forward_b,),
        (project_q, 1),
        (save_one.wait,),
        (up.begin,),
        (kv_arrive,),
        (make_bias, 1),
        (down.begin,),
        (
            looped,
            attend,
            8,
            (
                (2, ((out.diagonal_a,), (out.diagonal_b,),)),
                (4, ((out.arrive,),)),
                (6, ((project_out, 0), (sum_att[0].begin,), (sum_att[0].step_one,),)),
            ),
        ),
        (project_out, 1),
        (load_cot.wait,),
        (gate.begin,),
        (sum_att[1].begin,),
        (sum_att[0].step_two,),
        (sum_att[0].step_three,),
        (second_norm, 0),
        (down.forward_a,),
        (down.forward_b,),
        (up.forward_a,),
        (sum_att[1].step_one,),
        (sum_att[1].step_two,),
        (spread_two[0].step_two,),
        (sum_att[1].step_three,),
        (second_norm, 1),
        (up.forward_b,),
        (down.diagonal_a,),
        (down.diagonal_b,),
        (spread_two[0].step_one,),
        (down.arrive,),
        (up.diagonal_a,),
        (gate.forward_a,),
        (spread_two[1].step_one,),
        (gate.forward_b,),
        (spread_two[0].step_three,),
        (up.diagonal_b,),
        (up.arrive,),
        (gate.diagonal_a,),
        (spread_two[1].step_two,),
        (gate.diagonal_b,),
        (spread_two[0].finish,),
        (gate.arrive,),
        (settle_weights,),
        (
            looped,
            feed,
            2 * tile_count,
            (
                (3, ((spread_two[1].step_three,),)),
                (6, ((feed_back, 0), (sum_two[0].begin,), (spread_two[1].finish,),)),
            ),
        ),
        (feed_back, 1),
        (sum_two[0].step_one,),
        (sum_two[0].step_two,),
        (sum_two[1].begin,),
        (rs_down.partner,),
        (sum_two[0].step_three,),
        (rs_down.own,),
        (rs_gate.partner,),
        (sum_two[1].step_one,),
        (middle_back, 0),
        (rs_gate.own,),
        (rs_up.partner,),
        (sum_two[1].step_three,),
        (sum_two[1].step_two,),
        (rs_up.own,),
        (spread_mid[0].step_one,),
        (spread_mid[0].step_two,),
        (rs_up.push_near,),
        (middle_back, 1),
        (rs_down.push_near,),
        (feed_out, 1),
        (spread_mid[1].step_one,),
        (rs_gate.push_near,),
        (feed_out, 0),
        (spread_mid[0].step_three,),
        (sum_out[1].begin,),
        (sum_out[1].step_one,),
        (sum_out[0].begin,),
        (spread_mid[0].finish,),
        (out_back, 0),
        (rs_gate.push_diag,),
        (spread_mid[1].step_two,),
        (
            looped,
            attend_back,
            8,
            (
                (4, ((spread_mid[1].step_three,), (spread_mid[1].finish,), (kv_begin, 0), (sum_out[1].step_two,), (out_back, 1),)),
                (6, ((sum_out[1].step_three,), (rs_out.partner,), (sum_out[0].step_one,), (result_rows, 1), (rs_down.push_diag,),)),
            ),
        ),
        (kv_begin, 1),
        (rs_up.push_diag,),
        (kv_finish, 0),
        (project_back_rows, 0),
        (sum_out[0].step_three,),
        (sum_out[0].step_two,),
        (spread_out[1].step_two,),
        (sum_one[0].begin,),
        (rs_out.own,),
        (rs_out.push_diag,),
        (spread_out[1].step_one,),
        (kv_finish, 1),
        (project_back_rows, 1),
        (sum_one[1].begin,),
        (rs_gate.relay_a,),
        (result_rows, 0),
        (load_one.start,),
        (sum_one[0].step_one,),
        (spread_out[1].step_three,),
        (load_one.wait,),
        (rs_down.relay_a,),
        (sum_one[0].step_two,),
        (rs_qkv.partner,),
        (spread_out[0].step_two,),
        (sum_one[0].step_three,),
        (rs_out.relay_a,),
        (rs_up.relay_a,),
        (rs_up.relay_b,),
        (rs_down.relay_b,),
        (sum_one[1].step_one,),
        (rs_qkv.own,),
        (input_back, 0),
        (sum_one[1].step_two,),
        (sum_one[1].step_three,),
        (rs_qkv.push_diag,),
        (spread_in[0].step_two,),
        (spread_out[0].step_one,),
        (rs_gate.relay_b,),
        (input_back, 1),
        (rs_out.push_near,),
        (spread_in[0].step_one,),
        (rs_qkv.push_near,),
        (vec_begin,),
        (rs_down.collect, landing, fin_sem),
        (finish_turned, rs_down, o_down),
        (spread_out[0].step_three,),
        (rs_qkv.relay_a,),
        (spread_in[1].step_one,),
        (spread_in[1].step_two,),
        (rs_out.relay_b,),
        (rs_gate.collect, landing, fin_sem),
        (finish_rows, rs_gate, [(o_gate, 0, hidden)]),
        (rs_up.collect, landing, fin_sem),
        (finish_rows, rs_up, [(o_up, 0, hidden)]),
        (spread_in[0].step_three,),
        (rs_out.collect, landing, fin_sem),
        (finish_turned, rs_out, o_out),
        (rs_qkv.relay_b,),
        (spread_in[1].step_three,),
        (vec_middle,),
        (vec_finish,),
        (rs_qkv.collect, landing, fin_sem),
        (finish_qkv, rs_qkv),
        (settle,),
    )
    for action, *values in order:
        action(*values)


def run_layer(
    tokens, attn_gain, w_query, w_key, w_value, w_out, mlp_gain, w_gate, w_up, w_down, cotangent,
    positions, segments,
):
    shape = jax.ShapeDtypeStruct
    width = tokens.shape[1]
    hidden = w_gate.shape[1]
    vmem = pl.BlockSpec(memory_space=pltpu.VMEM)
    anywhere = pl.BlockSpec(memory_space=pl.ANY)
    dma = pltpu.SemaphoreType.DMA
    buffer = pltpu.VMEM
    half_size = HD // 2
    frequency = THETA_BASE ** (-np.arange(half_size, dtype=np.float32) / half_size)
    frequency = np.concatenate([frequency] * 4)[None, :].astype(np.float32)
    return pl.pallas_call(
        layer_kernel,
        name="decoder_layer",
        out_shape=(
            shape((2, 4, 64, width), BF),
            shape((2, 4, 64, width), BF),
            shape((2, 128), F32),
            shape((2, 128), F32),
            shape((256, 512), F32),
            shape((HD, 256), F32),
            shape((HD, 256), F32),
            shape((512, 256), F32),
            shape((256, hidden), F32),
            shape((256, hidden), F32),
            shape((hidden, 256), F32),
            shape((2, 256, hidden), BF),
            shape((2, 256, hidden), BF),
            shape((2, 256, hidden), BF),
            shape((2, 256, 512), BF),
            shape((2, 256, 640), BF),
            shape((2, 4, 64, width), BF),
        ),
        in_specs=[anywhere, vmem, vmem, vmem, vmem, vmem]
        + [anywhere] * 5
        + [vmem] * 3,
        out_specs=(anywhere,) * 2 + (vmem,) * 2 + (anywhere,) * 13,
        scratch_shapes=[
            buffer((8, 256), F32),
            buffer((8, 512), jnp.int32),
            buffer((8, 8, 256), F32),
            buffer((4, 8, 512), jnp.int32),
            buffer((512, width), BF),
            buffer((8, 256, hidden), BF),
            buffer((8, 256, hidden), BF),
            buffer((8, hidden, 256), BF),
            buffer((8, 512, 256), BF),
            buffer((8, 256, 640), BF),
            buffer((512, width), BF),
            buffer((2, 4, 64, width), BF),
            buffer((512, hidden), BF),
            buffer((512, hidden), BF),
            buffer((512, hidden), BF),
            buffer((4, 256, hidden), BF),
            buffer((3, 2, 128, hidden), BF),
            buffer((2, 2, 128, 640), BF),
            buffer((4, 256, 512), BF),
            buffer((4, 256, 640), BF),
            buffer((2, 64, hidden), F32),
            buffer((2, 128, 256), F32),
            buffer((2, 4, 64, width), BF),
            buffer((2, 3, 64, width), BF),
            buffer((2, 2, 64, width), BF),
            buffer((2, 3, 64, width), BF),
            buffer((2, 2, 64, width), BF),
            buffer((2, 4, 64, width), BF),
            buffer((64, width), F32),
            buffer((64, width), BF),
            buffer((2, 64, width), F32),
            buffer((2, 64, width), F32),
            buffer((512, 512), BF),
            buffer((2, 1024, 256), BF),
            buffer((16, 1, 256), F32),
            buffer((4, 512, 128), BF),
            buffer((512, 512), BF),
            buffer((512, 256), F32),
            buffer((256, 512), BF),
            buffer((2, 1024, 128), BF),
            buffer((2, HD, 1024), BF),
            buffer((1024, 128), BF),
            buffer((HD, 1024), BF),
            buffer((1024, 128), F32),
            buffer((1024, 128), F32),
            buffer((2, 4, 256, 128), BF),
            buffer((2, 3, 256, 128), BF),
            buffer((512, 640), BF),
            buffer((2, width), F32),
            buffer((4, 8, 8, 128), F32),
            buffer((8, 8, 128), F32),
            buffer((7, 8, 128), F32),
            dma((5, 9)),
            dma((5, 9)),
            dma((5,)),
            dma((10,)),
            dma((10,)),
            dma((3,)),
            dma((3,)),
            dma((4,)),
            dma((8, 3)),
            dma((8, 5)),
            dma((8, 5)),
            dma((8, 4)),
            dma((5, 10)),
            dma((5, 10)),
            pltpu.SemaphoreType.REGULAR((4,)),
            dma((2, 3)),
            dma((2, 3)),
            dma((10,)),
            dma((10,)),
            dma((2,)),
            dma((2, 2)),
            dma((2,)),
        ],
        compiler_params=pltpu.CompilerParams(
            collective_id=0, has_side_effects=True, vmem_limit_bytes=67043328
        ),
    )(
        tokens, attn_gain, mlp_gain, w_query, w_key.T, w_value.T, w_out, w_gate, w_up,
        w_down, cotangent, positions[None, :], segments[None, :], frequency,
    )


def hand_over_kernel(*refs):
    count = (len(refs) - 2) // 3
    sources, targets, buffers = refs[:count], refs[count : 2 * count], refs[2 * count : 3 * count]
    in_sem, out_sem = refs[3 * count :]
    fetch = [
        pltpu.make_async_copy(source, buffers[n], in_sem.at[n]) for n, source in enumerate(sources)
    ]
    store = [
        pltpu.make_async_copy(buffers[n], target, out_sem.at[n]) for n, target in enumerate(targets)
    ]
    for piece in fetch:
        piece.start()
    for n in range(count):
        fetch[n].wait()
        store[n].start()
    for piece in store:
        piece.wait()


def hand_over(values):
    anywhere = pl.BlockSpec(memory_space=pl.ANY)
    dma = pltpu.SemaphoreType.DMA
    return pl.pallas_call(
        hand_over_kernel,
        name="hand_over",
        out_shape=tuple(jax.ShapeDtypeStruct(value.shape, value.dtype) for value in values),
        in_specs=[anywhere] * len(values),
        out_specs=(anywhere,) * len(values),
        scratch_shapes=[pltpu.VMEM(value.shape, value.dtype) for value in values]
        + [dma((len(values),)), dma((len(values),))],
        compiler_params=pltpu.CompilerParams(vmem_limit_bytes=67043328),
    )(*values)


def fast_shards(tokens, *others):
    made = run_layer(tokens, *others)
    (
        query_g, out_g, gate_g, up_g, down_g, key_g, value_g, gain_one_g, gain_two_g, result, input_grad,
    ) = hand_over(made[4:5] + made[7:11] + made[5:7] + made[2:4] + made[0:2])
    return (
        result.reshape(tokens.shape),
        input_grad.reshape(tokens.shape),
        gain_one_g.reshape(-1),
        query_g,
        key_g.T,
        value_g.T,
        out_g,
        gain_two_g.reshape(-1),
        gate_g,
        up_g,
        down_g,
    )


def solution(mesh):
    in_specs = (
        P(("fsdp", "ctx"), None),
        P(("fsdp", "ctx")),
        P(("fsdp", "ctx"), "tp"),
        P(("fsdp", "ctx"), "tp"),
        P(("fsdp", "ctx"), "tp"),
        P("tp", ("fsdp", "ctx")),
        P(("fsdp", "ctx")),
        P(("fsdp", "ctx"), "tp"),
        P(("fsdp", "ctx"), "tp"),
        P("tp", ("fsdp", "ctx")),
        P(("fsdp", "ctx"), None),
        P(("fsdp", "ctx")),
        P(("fsdp", "ctx")),
    )
    out_specs = (
        P(("fsdp", "ctx"), None),
        P(("fsdp", "ctx"), None),
        P(("fsdp", "ctx")),
        P(("fsdp", "ctx"), "tp"),
        P(("fsdp", "ctx"), "tp"),
        P(("fsdp", "ctx"), "tp"),
        P("tp", ("fsdp", "ctx")),
        P(("fsdp", "ctx")),
        P(("fsdp", "ctx"), "tp"),
        P(("fsdp", "ctx"), "tp"),
        P("tp", ("fsdp", "ctx")),
    )
    small = (mesh.shape["fsdp"], mesh.shape["ctx"], mesh.shape["tp"]) == (2, 4, 4)
    return jax.shard_map(fast_shards if small else shards, mesh=mesh, in_specs=in_specs, out_specs=out_specs, check_vma=False)
```

```python
import jax
import jax.numpy as jnp
import numpy as np
from jax import lax
from jax.experimental import pallas as pl
from jax.experimental.pallas import tpu as pltpu
from jax.sharding import PartitionSpec as P

H = 32
KVH = 4
HD = 64


EPSILON = 1e-05
THETA_BASE = 10000.0
MASKED_SCORE = -1e30


def shifted(value, axis, steps):
    count = lax.axis_size(axis)
    pairs = [(source, (source + steps) % count) for source in range(count)]
    return lax.ppermute(value, axis, pairs)


def rope_tables(token_pos, half_size):
    frequency = THETA_BASE ** (-jnp.arange(half_size, dtype=jnp.float32) / half_size)
    angles = token_pos.astype(jnp.float32)[:, None] * frequency[None, :]
    return (jnp.cos(angles), jnp.sin(angles))


def rotate(head_rows, cosine, sine):
    half_size = head_rows.shape[-1] // 2
    first_half = head_rows[..., :half_size]
    second_half = head_rows[..., half_size:]
    cos_rows = cosine[:, None, :]
    sin_rows = sine[:, None, :]
    return jnp.concatenate(
        [
            first_half * cos_rows - second_half * sin_rows,
            second_half * cos_rows + first_half * sin_rows,
        ],
        axis=-1,
    )


def rotate_back(head_rows, cosine, sine):
    half_size = head_rows.shape[-1] // 2
    first_half = head_rows[..., :half_size]
    second_half = head_rows[..., half_size:]
    cos_rows = cosine[:, None, :]
    sin_rows = sine[:, None, :]
    return jnp.concatenate(
        [
            first_half * cos_rows + second_half * sin_rows,
            second_half * cos_rows - first_half * sin_rows,
        ],
        axis=-1,
    )


def project(left_side, right_side):
    return jnp.dot(left_side, right_side, preferred_element_type=jnp.float32)


def project_back(left_side, right_side):
    return lax.dot_general(
        left_side, right_side, (((1,), (1,)), ((), ())), preferred_element_type=jnp.float32
    )


def weight_grad(left_side, right_side):
    return lax.dot_general(
        left_side, right_side, (((0,), (0,)), ((), ())), preferred_element_type=jnp.float32
    )


def rms_norm(rows_in, gain_vec):
    inv_rms = lax.rsqrt(jnp.mean(rows_in * rows_in, axis=-1, keepdims=True) + EPSILON)
    unit_rows = rows_in * inv_rms
    return (unit_rows * gain_vec, unit_rows, inv_rms)


def rms_norm_back(gradient, gain_vec, unit_rows, inv_rms):
    gain_grad = jnp.sum(gradient * unit_rows, axis=0)
    scaled_grad = gradient * gain_vec
    return (
        inv_rms
        * (scaled_grad - unit_rows * jnp.mean(scaled_grad * unit_rows, axis=-1, keepdims=True)),
        gain_grad,
    )


def pair_mask(query_pos, query_seg, key_pos, key_seg):
    return (query_seg[:, None] == key_seg[None, :]) & (key_pos[None, :] <= query_pos[:, None])


def split_block(kv_block, kv_heads):
    key_rows = kv_block[:, : kv_heads * HD].reshape(-1, kv_heads, HD)
    value_rows = kv_block[:, kv_heads * HD :].reshape(-1, kv_heads, HD)
    return (key_rows, value_rows)


def attend_block(state_in, queries, kv_block, visible):
    row_top, row_total, output_sum = state_in
    key_rows, value_rows = split_block(kv_block, queries.shape[1])
    scores = jnp.einsum(
        "qkgd,pkd->kgqp", queries, key_rows, preferred_element_type=jnp.float32
    ) * HD ** (-0.5)
    scores = jnp.where(visible, scores, MASKED_SCORE)
    new_top = jnp.maximum(row_top, jnp.max(scores, axis=-1))
    weights = jnp.where(visible, jnp.exp(scores - new_top[..., None]), 0.0)
    decay_factor = jnp.exp(row_top - new_top)
    row_total = row_total * decay_factor + jnp.sum(weights, axis=-1)
    mixed_heads = jnp.einsum(
        "kgqp,pkd->qkgd",
        weights.astype(jnp.bfloat16),
        value_rows,
        preferred_element_type=jnp.float32,
    )
    output_sum = output_sum * jnp.transpose(decay_factor, (2, 0, 1))[..., None] + mixed_heads
    return (new_top, row_total, output_sum)


def block_grads(queries, out_grad, kv_block, visible, log_total, delta_rows):
    key_rows, value_rows = split_block(kv_block, queries.shape[1])
    scale_factor = HD ** (-0.5)
    scores = (
        jnp.einsum("qkgd,pkd->kgqp", queries, key_rows, preferred_element_type=jnp.float32)
        * scale_factor
    )
    probs_full = jnp.where(
        visible, jnp.exp(jnp.where(visible, scores, MASKED_SCORE) - log_total[..., None]), 0.0
    )
    value_grad = jnp.einsum(
        "kgqp,qkgd->pkd",
        probs_full.astype(jnp.bfloat16),
        out_grad,
        preferred_element_type=jnp.float32,
    )
    prob_grad = jnp.einsum(
        "qkgd,pkd->kgqp", out_grad, value_rows, preferred_element_type=jnp.float32
    )
    score_grad = (probs_full * (prob_grad - delta_rows[..., None])).astype(jnp.bfloat16)
    query_grad = (
        jnp.einsum("kgqp,pkd->qkgd", score_grad, key_rows, preferred_element_type=jnp.float32)
        * scale_factor
    )
    key_grad = (
        jnp.einsum("kgqp,qkgd->pkd", score_grad, queries, preferred_element_type=jnp.float32)
        * scale_factor
    )
    block_rows = kv_block.shape[0]
    return (
        query_grad,
        jnp.concatenate(
            [key_grad.reshape(block_rows, -1), value_grad.reshape(block_rows, -1)], axis=-1
        ),
    )


def shards(
    tokens,
    attn_gain,
    w_query,
    w_key,
    w_value,
    w_out,
    mlp_gain,
    w_gate,
    w_up,
    w_down,
    cotangent,
    positions,
    segments,
):
    token_rows = tokens.shape[0]
    gain_one, query_w, key_w, value_w, out_w = (
        lax.all_gather(attn_gain, ("fsdp", "ctx"), axis=0, tiled=True),
        lax.all_gather(w_query, ("fsdp", "ctx"), axis=0, tiled=True),
        lax.all_gather(w_key, ("fsdp", "ctx"), axis=0, tiled=True),
        lax.all_gather(w_value, ("fsdp", "ctx"), axis=0, tiled=True),
        lax.all_gather(w_out, ("fsdp", "ctx"), axis=1, tiled=True),
    )
    gain_two, gate_w, up_w, down_w = (
        lax.all_gather(mlp_gain, ("fsdp", "ctx"), axis=0, tiled=True),
        lax.all_gather(w_gate, ("fsdp", "ctx"), axis=0, tiled=True),
        lax.all_gather(w_up, ("fsdp", "ctx"), axis=0, tiled=True),
        lax.all_gather(w_down, ("fsdp", "ctx"), axis=1, tiled=True),
    )
    head_count = query_w.shape[1] // HD
    kv_heads = key_w.shape[1] // HD
    groups = H // KVH
    cosine, sine = rope_tables(positions, HD // 2)
    token_float = tokens.astype(jnp.float32)
    gain_one_float = gain_one.astype(jnp.float32)
    normed_one, unit_one, inv_one = rms_norm(token_float, gain_one_float)
    normed_low = normed_one.astype(jnp.bfloat16)
    query_lin = project(normed_low, query_w)
    key_lin = project(normed_low, key_w)
    value_low = project(normed_low, value_w).astype(jnp.bfloat16)
    query_rot = rotate(query_lin.reshape(token_rows, head_count, HD), cosine, sine).astype(
        jnp.bfloat16
    )
    key_rot = rotate(key_lin.reshape(token_rows, kv_heads, HD), cosine, sine).astype(jnp.bfloat16)
    queries = query_rot.reshape(token_rows, kv_heads, groups, HD)
    kv_local = jnp.concatenate([key_rot.reshape(token_rows, kv_heads * HD), value_low], axis=-1)
    key_positions, key_segments = (
        lax.all_gather(positions, "ctx", axis=0, tiled=True),
        lax.all_gather(segments, "ctx", axis=0, tiled=True),
    )
    my_index = lax.axis_index("ctx")
    cycle_size = lax.axis_size("ctx")

    def block_marks(source):
        start_row = source * token_rows
        return pair_mask(
            positions,
            segments,
            lax.dynamic_slice_in_dim(key_positions, start_row, token_rows),
            lax.dynamic_slice_in_dim(key_segments, start_row, token_rows),
        )

    start_state = (
        jnp.full((kv_heads, groups, token_rows), MASKED_SCORE, jnp.float32),
        jnp.zeros((kv_heads, groups, token_rows), jnp.float32),
        jnp.zeros((token_rows, kv_heads, groups, HD), jnp.float32),
    )

    def forward_block(state_in, kv_block, source):
        visible = block_marks(source)
        return attend_block(state_in, queries, kv_block, visible)

    def cycle_step(state_in, step_index):
        attn_state, kv_block = state_in
        attn_state = forward_block(attn_state, kv_block, (my_index - step_index) % cycle_size)
        passed = shifted(kv_block, "ctx", 1)
        return ((attn_state, passed), kv_block)

    (attn_state, last_block), kept_blocks = lax.scan(
        cycle_step, (start_state, kv_local), jnp.arange(cycle_size - 1)
    )
    attn_state = forward_block(attn_state, last_block, (my_index + 1) % cycle_size)
    kv_blocks = jnp.concatenate([kept_blocks, last_block[None]], axis=0)
    sources = (my_index - jnp.arange(cycle_size)) % cycle_size
    row_top, row_total, output_sum = attn_state
    attended = output_sum / jnp.transpose(row_total, (2, 0, 1))[..., None]
    log_total = row_top + jnp.log(row_total)
    attended_low = attended.reshape(token_rows, head_count * HD).astype(jnp.bfloat16)
    middle = token_float + lax.psum(project(attended_low, out_w).astype(jnp.bfloat16), "tp").astype(
        jnp.float32
    )
    gain_two_float = gain_two.astype(jnp.float32)
    normed_two, unit_two, inv_two = rms_norm(middle, gain_two_float)
    normed_two_low = normed_two.astype(jnp.bfloat16)
    gate_lin = project(normed_two_low, gate_w)
    up_lin = project(normed_two_low, up_w)
    hidden_low = (jax.nn.silu(gate_lin) * up_lin).astype(jnp.bfloat16)
    result = middle + lax.psum(project(hidden_low, down_w).astype(jnp.bfloat16), "tp").astype(
        jnp.float32
    )
    output = result.astype(jnp.bfloat16)
    hidden_grad = project_back(cotangent, down_w)
    down_w_grad = weight_grad(hidden_low, cotangent)
    sigmoid_gate = jax.nn.sigmoid(gate_lin)
    gate_grad_low = (
        hidden_grad * up_lin * sigmoid_gate * (1.0 + gate_lin * (1.0 - sigmoid_gate))
    ).astype(jnp.bfloat16)
    up_grad_low = (hidden_grad * gate_lin * sigmoid_gate).astype(jnp.bfloat16)
    normed_two_grad = lax.psum(
        (project_back(gate_grad_low, gate_w) + project_back(up_grad_low, up_w)).astype(
            jnp.bfloat16
        ),
        "tp",
    ).astype(jnp.float32)
    gate_w_grad = weight_grad(normed_two_low, gate_grad_low)
    up_w_grad = weight_grad(normed_two_low, up_grad_low)
    norm_back_two, gain_two_grad = rms_norm_back(normed_two_grad, gain_two_float, unit_two, inv_two)
    middle_grad = cotangent.astype(jnp.float32) + norm_back_two
    middle_low = middle_grad.astype(jnp.bfloat16)
    attended_grad_low = project_back(middle_low, out_w).astype(jnp.bfloat16)
    out_w_grad = weight_grad(attended_low, middle_low)
    out_grad = attended_grad_low.reshape(token_rows, kv_heads, groups, HD)
    delta_rows = jnp.transpose(jnp.sum(out_grad.astype(jnp.float32) * attended, axis=-1), (1, 2, 0))

    def backward_block(kv_block, source):
        visible = block_marks(source)
        return block_grads(queries, out_grad, kv_block, visible, log_total, delta_rows)

    query_start = jnp.zeros((token_rows, kv_heads, groups, HD), jnp.float32)

    def back_step(state_in, pieces):
        query_acc, kv_acc = state_in
        query_term, kv_term = backward_block(pieces[0], pieces[1])
        passed = shifted((kv_acc + kv_term).astype(jnp.bfloat16), "ctx", 1).astype(jnp.float32)
        return ((query_acc + query_term, passed), None)

    (query_grad, kv_grad), unused = lax.scan(
        back_step, (query_start, jnp.zeros(kv_local.shape, jnp.float32)), (kv_blocks, sources)
    )
    query_grad_low = (
        rotate_back(query_grad.reshape(token_rows, head_count, HD), cosine, sine)
        .reshape(token_rows, head_count * HD)
        .astype(jnp.bfloat16)
    )
    key_grad_low = (
        rotate_back(kv_grad[:, : kv_heads * HD].reshape(token_rows, kv_heads, HD), cosine, sine)
        .reshape(token_rows, kv_heads * HD)
        .astype(jnp.bfloat16)
    )
    value_grad_low = kv_grad[:, kv_heads * HD :].astype(jnp.bfloat16)
    normed_one_grad = lax.psum(
        (
            project_back(query_grad_low, query_w)
            + project_back(key_grad_low, key_w)
            + project_back(value_grad_low, value_w)
        ).astype(jnp.bfloat16),
        "tp",
    ).astype(jnp.float32)
    query_w_grad = weight_grad(normed_low, query_grad_low)
    key_w_grad = weight_grad(normed_low, key_grad_low)
    value_w_grad = weight_grad(normed_low, value_grad_low)
    norm_back_one, gain_one_grad = rms_norm_back(normed_one_grad, gain_one_float, unit_one, inv_one)
    input_grad = (middle_grad + norm_back_one).astype(jnp.bfloat16)
    summed = (
        lax.psum_scatter(
            gain_one_grad.astype(jnp.bfloat16), ("fsdp", "ctx"), scatter_dimension=0, tiled=True
        ).astype(jnp.float32),
        lax.psum_scatter(
            query_w_grad.astype(jnp.bfloat16), ("fsdp", "ctx"), scatter_dimension=0, tiled=True
        ).astype(jnp.float32),
        lax.psum_scatter(
            key_w_grad.astype(jnp.bfloat16), ("fsdp", "ctx"), scatter_dimension=0, tiled=True
        ).astype(jnp.float32),
        lax.psum_scatter(
            value_w_grad.astype(jnp.bfloat16), ("fsdp", "ctx"), scatter_dimension=0, tiled=True
        ).astype(jnp.float32),
        lax.psum_scatter(
            out_w_grad.astype(jnp.bfloat16), ("fsdp", "ctx"), scatter_dimension=1, tiled=True
        ).astype(jnp.float32),
        lax.psum_scatter(
            gain_two_grad.astype(jnp.bfloat16), ("fsdp", "ctx"), scatter_dimension=0, tiled=True
        ).astype(jnp.float32),
        lax.psum_scatter(
            gate_w_grad.astype(jnp.bfloat16), ("fsdp", "ctx"), scatter_dimension=0, tiled=True
        ).astype(jnp.float32),
        lax.psum_scatter(
            up_w_grad.astype(jnp.bfloat16), ("fsdp", "ctx"), scatter_dimension=0, tiled=True
        ).astype(jnp.float32),
        lax.psum_scatter(
            down_w_grad.astype(jnp.bfloat16), ("fsdp", "ctx"), scatter_dimension=1, tiled=True
        ).astype(jnp.float32),
    )
    return (output, input_grad) + tuple(summed)


MESH = pl.DeviceIdType.MESH
BF = jnp.bfloat16
F32 = jnp.float32


def dotg(left_side, right_side, left_dim, right_dim):
    return lax.dot_general(
        left_side,
        right_side,
        (((left_dim,), (right_dim,)), ((), ())),
        preferred_element_type=F32,
    )


def remote(src, dst, send_sem, recv_sem, device):
    return pltpu.make_async_remote_copy(
        src_ref=src,
        dst_ref=dst,
        send_sem=send_sem,
        recv_sem=recv_sem,
        device_id=device,
        device_id_type=MESH,
    )


class Place:
    def __init__(self):
        self.f = lax.axis_index("fsdp")
        self.c = lax.axis_index("ctx")
        self.z = lax.axis_index("tp")
        self.cx = self.c + 1 - 2 * lax.rem(self.c, 2)
        self.cy = lax.rem(self.c + 2, 4)
        self.cd = 3 - self.c
        self.of = 1 - self.f
        self.own = self.f * 4 + self.c
        self.sx = self.f * 4 + self.cx
        self.sy = self.f * 4 + self.cy
        self.sd = self.f * 4 + self.cd

    def at(self, f=None, c=None, z=None):
        return (
            self.f if f is None else f,
            self.c if c is None else c,
            self.z if z is None else z,
        )


def group_devices(me):
    return [
        me.at(c=me.cx),
        me.at(c=me.cy),
        me.at(c=me.cd),
        me.at(f=me.of),
        me.at(f=me.of, c=me.cx),
        me.at(f=me.of, c=me.cy),
        me.at(f=me.of, c=me.cd),
    ]


def column_devices(me):
    return [me.at(z=lax.rem(me.z + step, 4)) for step in (1, 2, 3)]


class Gather:
    def __init__(self, me, index, own, full, send, recv, local_sem):
        self.me, self.full, self.placed = me, full, own is None
        own = full.at[me.own] if own is None else own
        rows = full.shape[1]
        self.half_a = pl.ds(0, rows // 2)
        self.half_b = pl.ds(rows // 2, rows // 2)

        def copy(slot, src, dst, device):
            return remote(src, dst, send.at[index, slot], recv.at[index, slot], device)

        slot_own, slot_x, slot_y = full.at[me.own], full.at[me.sx], full.at[me.sy]
        to_x, to_y, to_core = me.at(c=me.cx), me.at(c=me.cy), me.at(f=me.of)
        diag_a = full.at[me.sd, self.half_a]
        diag_b = full.at[me.sd, self.half_b]
        self.own_x = copy(0, own, slot_own, to_x)
        self.own_y = copy(1, own, slot_own, to_y)
        self.own_core = copy(2, own, slot_own, to_core)
        self.pass_x = copy(3, full.at[me.sy, self.half_a], full.at[me.sy, self.half_a], to_x)
        self.pass_y = copy(4, full.at[me.sx, self.half_b], full.at[me.sx, self.half_b], to_y)
        self.core_x = copy(5, slot_x, slot_x, to_core)
        self.core_y = copy(6, slot_y, slot_y, to_core)
        self.core_a = copy(7, diag_a, diag_a, to_core)
        self.core_b = copy(8, diag_b, diag_b, to_core)
        other = me.of * 4
        into = lambda slot, ref, device: copy(slot, ref, ref, device)
        self.in_x = into(0, slot_x, to_x)
        self.in_y = into(1, slot_y, to_y)
        self.in_a = into(3, diag_a, to_x)
        self.in_b = into(4, diag_b, to_y)
        self.in_core = [
            into(2, full.at[other + me.c], to_core),
            into(5, full.at[other + me.cx], to_core),
            into(6, full.at[other + me.cy], to_core),
            into(7, full.at[other + me.cd, self.half_a], to_core),
            into(8, full.at[other + me.cd, self.half_b], to_core),
        ]
        self.keep = None if self.placed else pltpu.make_async_copy(own, slot_own, local_sem.at[index])

    def begin(self):
        self.own_x.start()
        self.own_y.start()
        self.own_core.start()
        if not self.placed:
            self.keep.start()

    def forward_a(self):
        self.in_y.wait_recv()
        self.pass_x.start()
        self.core_y.start()

    def forward_b(self):
        self.in_x.wait_recv()
        self.pass_y.start()
        self.core_x.start()

    def diagonal_a(self):
        self.in_a.wait_recv()
        self.core_a.start()

    def diagonal_b(self):
        self.in_b.wait_recv()
        self.core_b.start()

    def arrive(self):
        if not self.placed:
            self.keep.wait()
        for piece in self.in_core:
            piece.wait_recv()

    def settle(self):
        for piece in (
            self.own_x,
            self.own_y,
            self.own_core,
            self.pass_x,
            self.pass_y,
            self.core_x,
            self.core_y,
            self.core_a,
            self.core_b,
        ):
            piece.wait_send()


class LineSum:
    def __init__(self, me, part, outer_in, inner_in, send, recv):
        self.me, self.part = me, part
        self.outer_in, self.inner_in = outer_in, inner_in
        self.send, self.recv = send, recv
        z = me.z
        self.is_mid = (z == 1) | (z == 2)
        self.is_end = (z == 0) | (z == 3)
        self.mid_of_end = 1 + z // 3
        self.outer_of_mid = 3 * (z - 1)

    def end_copies(self):
        me, part = self.me, self.part
        mid = self.mid_of_end
        to_mid = me.at(z=mid)
        owners = (3 - me.z, 3 - mid, mid)
        return [
            remote(
                part.at[owner],
                self.outer_in.at[slot],
                self.send.at[slot],
                self.recv.at[slot],
                to_mid,
            )
            for slot, owner in enumerate(owners)
        ]

    def mid_copies(self):
        me, part = self.me, self.part
        far_mid, outer = 3 - me.z, self.outer_of_mid
        far = 3 - outer
        to_mid, to_outer = me.at(z=far_mid), me.at(z=outer)
        return [
            remote(part.at[far], self.inner_in.at[0], self.send.at[0], self.recv.at[3], to_mid),
            remote(part.at[far_mid], self.inner_in.at[1], self.send.at[1], self.recv.at[4], to_mid),
            remote(part.at[outer], self.inner_in.at[0], self.send.at[2], self.recv.at[3], to_outer),
        ]

    def wait_in(self, slot, buffer):
        remote(buffer, buffer, self.send.at[0], self.recv.at[slot], self.me.at(z=3 - self.me.z)).wait_recv()

    def add(self, owner, buffer):
        self.part[owner] = (self.part[owner].astype(F32) + buffer[...].astype(F32)).astype(BF)

    def begin(self):
        @pl.when(self.is_end)
        def _():
            for piece in self.end_copies():
                piece.start()

    def step_one(self):
        @pl.when(self.is_mid)
        def _():
            far = 3 - self.outer_of_mid
            self.wait_in(0, self.outer_in.at[0])
            self.add(far, self.outer_in.at[0])
            self.mid_copies()[0].start()

    def step_two(self):
        @pl.when(self.is_mid)
        def _():
            copies = self.mid_copies()
            self.wait_in(1, self.outer_in.at[1])
            self.add(3 - self.me.z, self.outer_in.at[1])
            copies[1].start()

    def step_three(self):
        @pl.when(self.is_mid)
        def _():
            self.wait_in(3, self.inner_in.at[0])
            self.add(self.outer_of_mid, self.inner_in.at[0])
            self.mid_copies()[2].start()

    def finish(self, total):
        me = self.me

        @pl.when(self.is_mid)
        def _():
            self.wait_in(2, self.outer_in.at[2])
            self.wait_in(4, self.inner_in.at[1])
            total[...] = (
                self.part[me.z].astype(F32)
                + self.outer_in[2].astype(F32)
                + self.inner_in[1].astype(F32)
            )

        @pl.when(self.is_end)
        def _():
            self.wait_in(3, self.inner_in.at[0])
            total[...] = self.part[me.z].astype(F32) + self.inner_in[0].astype(F32)
            for piece in self.end_copies():
                piece.wait_send()

    def drain(self):
        @pl.when(self.is_mid)
        def _():
            for piece in self.mid_copies():
                piece.wait_send()


class LineGather:
    def __init__(self, me, blocks, send, recv):
        self.me, self.blocks, self.send, self.recv = me, blocks, send, recv
        z = me.z
        self.is_mid = (z == 1) | (z == 2)
        self.is_end = (z == 0) | (z == 3)
        self.mid_of_end = 1 + z // 3
        self.outer_of_mid = 3 * (z - 1)

    def copy(self, owner, slot, z):
        ref = self.blocks.at[owner]
        return remote(ref, ref, self.send.at[slot], self.recv.at[owner], self.me.at(z=z))

    def wait_in(self, owner):
        ref = self.blocks.at[owner]
        remote(ref, ref, self.send.at[0], self.recv.at[owner], self.me.at(z=3 - self.me.z)).wait_recv()

    def begin(self):
        me = self.me

        @pl.when(self.is_end)
        def _():
            self.copy(me.z, 0, self.mid_of_end).start()

        @pl.when(self.is_mid)
        def _():
            self.copy(me.z, 0, self.outer_of_mid).start()
            self.copy(me.z, 1, 3 - me.z).start()

    def step_one(self):
        me = self.me

        @pl.when(self.is_mid)
        def _():
            self.wait_in(self.outer_of_mid)
            self.copy(self.outer_of_mid, 2, 3 - me.z).start()

    def step_two(self):
        me = self.me

        @pl.when(self.is_mid)
        def _():
            self.wait_in(3 - me.z)
            self.copy(3 - me.z, 3, self.outer_of_mid).start()

    def step_three(self):
        @pl.when(self.is_mid)
        def _():
            far = 3 - self.outer_of_mid
            self.wait_in(far)
            self.copy(far, 4, self.outer_of_mid).start()

    def finish(self):
        me = self.me

        @pl.when(self.is_mid)
        def _():
            self.copy(me.z, 0, self.outer_of_mid).wait_send()
            self.copy(me.z, 1, 3 - me.z).wait_send()
            self.copy(self.outer_of_mid, 2, 3 - me.z).wait_send()
            self.copy(3 - me.z, 3, self.outer_of_mid).wait_send()
            self.copy(3 - self.outer_of_mid, 4, self.outer_of_mid).wait_send()

        @pl.when(self.is_end)
        def _():
            mid = self.mid_of_end
            self.wait_in(mid)
            self.wait_in(3 - mid)
            self.wait_in(3 - me.z)
            self.copy(me.z, 0, mid).wait_send()


def row_of(gains_ref, which):
    return jnp.concatenate([gains_ref[shard, which : which + 1, :] for shard in range(8)], axis=-1)


def swap_halves(rows):
    lane = lax.broadcasted_iota(jnp.int32, rows.shape, 1)
    return jnp.where(
        lax.rem(lane, HD) < HD // 2, pltpu.roll(rows, 96, 1), pltpu.roll(rows, 32, 1)
    )


class Scatter:
    def __init__(self, me, index, last, width, x_of, y_of, chips, refs):
        self.me, self.index, self.last, self.width = me, index, last, width
        self.x_of, self.y_of, self.chips = x_of, y_of, chips
        self.stage, self.core_in, self.diag_in, self.near_in = refs[:4]
        self.send, self.recv, self.credit = refs[4:]
        self.to_x, self.to_y, self.to_core = me.at(c=me.cx), me.at(c=me.cy), me.at(f=me.of)
        self.sent = []

    def copy(self, slot, src, dst, device):
        return remote(
            src, dst, self.send.at[self.index, slot], self.recv.at[self.index, slot], device
        )

    def lanes(self, ref):
        return ref.at[:, pl.ds(0, self.width)]

    def core_copy(self, role):
        return self.copy(
            role, self.stage(self.width, role), self.lanes(self.core_in.at[role]), self.to_core
        )

    def chunk(self, core, role):
        c = self.me.c
        high = lax.rem(c // 2 + role // 2, 2)
        low = lax.rem(lax.rem(c, 2) + lax.rem(role, 2), 2)
        return dotg(self.x_of(core * 4 + 2 * high + low), self.y_of(), 0, 0)

    def roles(self, body):
        def pair(step, carry):
            body(3 - step)
            body(1 - step)
            return carry

        lax.fori_loop(0, 2, pair, 0)

    def partner(self):
        def body(role):
            self.stage(self.width, role)[...] = self.chunk(self.me.of, role).astype(BF)
            if self.index > 0:
                pl.semaphore_wait(self.credit.at[role], 1)
            self.core_copy(role).start()

        self.roles(body)

    def own(self):
        def body(role):
            value = self.chunk(self.me.f, role)
            self.core_copy(role).wait_recv()
            chip = self.chips(role)
            chip[...] = (value + self.lanes(self.core_in.at[role])[...].astype(F32)).astype(BF)
            if not self.last:
                pl.semaphore_signal(
                    self.credit.at[role], inc=1, device_id=self.to_core, device_id_type=MESH
                )

        self.roles(body)
        for role in range(4):
            self.core_copy(role).wait_send()

    def near(self, role, half, slot):
        rows = pl.ds(half * 128, 128)
        side = role - 1
        device = self.to_x if role == 1 else self.to_y
        return self.copy(
            slot, self.chips(role).at[rows, :], self.near_in.at[side, rows, :], device
        )

    def diag(self, half):
        device = self.to_x if half == 0 else self.to_y
        return self.copy(
            4 + half,
            self.chips(3).at[pl.ds(half * 128, 128), :],
            self.lanes(self.diag_in.at[half]),
            device,
        )

    def push_diag(self):
        self.diag(0).start()
        self.diag(1).start()

    def push_near(self):
        self.near(1, 0, 6).start()
        self.near(2, 1, 7).start()

    def relay_a(self):
        first = pl.ds(0, 128)
        self.diag(0).wait_recv()
        rows = self.chips(2).at[first, :]
        rows[...] = (
            rows[...].astype(F32) + self.lanes(self.diag_in.at[0])[...].astype(F32)
        ).astype(BF)
        self.near(2, 0, 8).start()

    def relay_b(self):
        second = pl.ds(128, 128)
        self.diag(1).wait_recv()
        rows = self.chips(1).at[second, :]
        rows[...] = (
            rows[...].astype(F32) + self.lanes(self.diag_in.at[1])[...].astype(F32)
        ).astype(BF)
        self.near(1, 1, 9).start()

    def collect(self, buffer, sem):
        for role, half, slot in ((1, 0, 6), (2, 1, 7), (2, 0, 8), (1, 1, 9)):
            self.near(role, half, slot).wait_recv()
        for side in range(2):
            pltpu.make_async_copy(
                self.near_in.at[side], self.lanes(buffer.at[side]), sem.at[side]
            ).start()

    def collected(self, buffer, sem):
        for side in range(2):
            pltpu.make_async_copy(
                self.near_in.at[side], self.lanes(buffer.at[side]), sem.at[side]
            ).wait()

    def settle(self):
        for half in range(2):
            self.diag(half).wait_send()
        for role, half, slot in ((1, 0, 6), (2, 1, 7), (2, 0, 8), (1, 1, 9)):
            self.near(role, half, slot).wait_send()


def norm_back(gradient, rows_in, gain):
    inv = lax.rsqrt(jnp.mean(rows_in * rows_in, axis=-1, keepdims=True) + EPSILON)
    unit = rows_in * inv
    scaled = gradient * gain
    back = inv * (scaled - unit * jnp.mean(scaled * unit, axis=-1, keepdims=True))
    return back, jnp.sum(gradient * unit, axis=0, keepdims=True)


def layer_kernel(
    tok_h,
    gain_one_in,
    gain_two_in,
    w_query_in,
    w_key_in,
    w_value_in,
    out_h,
    gate_h,
    up_h,
    down_h,
    cot_h,
    pos_in,
    seg_in,
    freq,
    o_result,
    o_input,
    o_gain_one,
    o_gain_two,
    o_query,
    o_key,
    o_value,
    o_out,
    o_gate,
    o_up,
    o_down,
    near_down,
    near_gate,
    near_up,
    near_out,
    near_qkv,
    n_one_h,
    own_gains,
    own_marks,
    gains,
    marks,
    tok,
    w_gate,
    w_up,
    w_down,
    w_out,
    w_qkv,
    cot,
    n_two,
    hid,
    gate_g,
    up_g,
    core_in,
    diag_in,
    diag_low,
    chip_out,
    chip_qkv,
    sum_stage,
    turn_stage,
    part,
    outer_in,
    inner_in,
    outer_two,
    inner_two,
    mlow,
    total,
    own_out,
    mid,
    mid_g,
    q_rot,
    bias,
    lse,
    kv,
    att,
    rope,
    do_rows,
    keys,
    vals_t,
    vals,
    keys_t,
    key_acc,
    val_acc,
    kv_send_buf,
    kv_in,
    d_qkv,
    vec,
    vec_in,
    vec_out,
    vec_near,
    g_send,
    g_recv,
    g_local,
    small_send,
    small_recv,
    first_send,
    first_recv,
    load_sem,
    sum_send,
    sum_recv,
    all_send,
    all_recv,
    rs_send,
    rs_recv,
    credit,
    kv_send,
    kv_recv,
    vec_send,
    vec_recv,
    fin_sem,
    put_sem,
    own_sem,
):
    me = Place()
    group = group_devices(me)
    hidden = hid.shape[1]

    rows_of = [pl.ds(g * 256, 256) for g in range(2)]
    load_tok = pltpu.make_async_copy(tok_h, tok, load_sem.at[0])
    load_cot = pltpu.make_async_copy(cot_h, cot, load_sem.at[1])
    save_one = pltpu.make_async_copy(mlow, n_one_h, load_sem.at[2])
    load_one = pltpu.make_async_copy(n_one_h, mlow, load_sem.at[3])
    load_tok.start()
    load_cot.start()
    barrier = pltpu.get_barrier_semaphore()
    for device in group + column_devices(me):
        pl.semaphore_signal(barrier, inc=1, device_id=device, device_id_type=MESH)

    w_qkv[me.own, :, 0:512] = w_query_in[...]
    turned = jnp.concatenate([w_key_in[...], w_value_in[...]], axis=0).astype(F32)
    w_qkv[me.own, :, 512:640] = jnp.transpose(turned).astype(BF)
    own_gains[0:1, :] = gain_one_in[...].reshape(1, 256).astype(F32)
    own_gains[1:2, :] = gain_two_in[...].reshape(1, 256).astype(F32)
    own_gains[2:8, :] = jnp.zeros((6, 256), F32)
    own_marks[0:1, :] = pos_in[...]
    own_marks[1:2, :] = seg_in[...]
    own_marks[2:8, :] = jnp.zeros((6, 512), jnp.int32)
    pl.semaphore_wait(barrier, 10)

    qkv = Gather(me, 0, None, w_qkv, g_send, g_recv, g_local)
    out = Gather(me, 1, out_h, w_out, g_send, g_recv, g_local)
    gate = Gather(me, 2, gate_h, w_gate, g_send, g_recv, g_local)
    up = Gather(me, 3, up_h, w_up, g_send, g_recv, g_local)
    down = Gather(me, 4, down_h, w_down, g_send, g_recv, g_local)

    sources = [me.sx, me.sy, me.sd, me.of * 4 + me.c, me.of * 4 + me.cx, me.of * 4 + me.cy, me.of * 4 + me.cd]

    def small_copies(gain_slots, mark_slots):
        return [
            remote(own_gains, gains.at[spot], small_send.at[slot], small_recv.at[slot], group[slot])
            for slot, spot in enumerate(gain_slots)
        ] + [
            remote(
                own_marks, marks.at[spot], small_send.at[7 + slot], small_recv.at[7 + slot], group[slot]
            )
            for slot, spot in enumerate(mark_slots)
        ]

    small = small_copies([me.own] * 7, [me.c] * 3)

    def small_begin():
        for piece in small:
            piece.start()
        gains[me.own] = own_gains[...]
        marks[me.c] = own_marks[...]

    def small_finish():
        for piece in small_copies(sources, (me.cx, me.cy, me.cd)):
            piece.wait_recv()

    def first_norm():
        load_tok.wait()
        gain_one = row_of(gains, 0)

        def body(step, carry):
            values = tok[pl.ds(pl.multiple_of(step * 64, 64), 64), :].astype(F32)
            inv = lax.rsqrt(jnp.mean(values * values, axis=-1, keepdims=True) + EPSILON)
            mlow[step // 4, lax.rem(step, 4)] = (values * inv * gain_one).astype(BF)
            return carry

        lax.fori_loop(0, 8, body, 0)
        save_one.start()

    def make_rope():
        lane = lax.broadcasted_iota(jnp.int32, (128, 128), 1)
        low_half = lax.rem(lane, HD) < HD // 2
        for step in range(4):
            rows = slice(step * 128, (step + 1) * 128)
            places = own_marks[0:1, rows].astype(F32)
            angles = jnp.transpose(jnp.broadcast_to(places, (128, 128))) * freq[...]
            sine = jnp.sin(angles)
            rope[rows, :128] = jnp.cos(angles)
            rope[rows, 128:] = jnp.where(low_half, -sine, sine)

    def make_bias(g):
        own_rows = own_marks[:, g * 256 : (g + 1) * 256].astype(F32)
        for source in range(4):
            key_rows = marks[source, :, g * 256 : (g + 1) * 256].astype(F32)
            key_pos = jnp.transpose(jnp.broadcast_to(key_rows[0:1, :], (128, 256)))
            key_seg = jnp.transpose(jnp.broadcast_to(key_rows[1:2, :], (128, 256)))
            for side in range(2):
                lanes = slice(side * 128, (side + 1) * 128)
                seen = (key_seg == own_rows[1:2, lanes]) & (key_pos <= own_rows[0:1, lanes])
                bias[g, source * 256 : (source + 1) * 256, lanes] = jnp.where(
                    seen, 0.0, MASKED_SCORE
                ).astype(BF)

    lane_pair = lax.broadcasted_iota(jnp.int32, (256, 128), 1)

    def project_in(first, width):
        total_rows = None
        for shard in range(8):
            term = dotg(
                mlow[:, :, :, shard * 256 : (shard + 1) * 256].reshape(512, 256),
                w_qkv[shard, :, first : first + width],
                1,
                0,
            )
            total_rows = term if total_rows is None else total_rows + term
        return total_rows

    def first_copies(places):
        return [
            remote(kv.at[place], kv.at[place], first_send.at[slot], first_recv.at[slot], group[slot])
            for slot, place in enumerate(places)
        ]

    def project_kv():
        rows = project_in(512, 128)
        is_key = lax.broadcasted_iota(jnp.int32, (512, 128), 1) < HD
        cos_rows = jnp.where(is_key, rope[:, :128], 1.0)
        sin_rows = jnp.where(is_key, rope[:, 128:], 0.0)
        kv[me.c] = (rows * cos_rows + swap_halves(rows) * sin_rows).astype(BF)
        for piece in first_copies([me.c] * 3):
            piece.start()

    def project_q(half):
        rows_all = project_in(half * 256, 256)
        for inner in range(2):
            pair = half * 2 + inner
            rows = rows_all[:, inner * 128 : (inner + 1) * 128]
            rot = (rows * rope[:, :128] + swap_halves(rows) * rope[:, 128:]).astype(BF)
            rot = rot * jnp.bfloat16(HD ** (-0.5))
            q_rot[:, pair * 128 : (pair + 1) * 128] = rot

    def kv_arrive():
        for piece in first_copies((me.cx, me.cy, me.cd)):
            piece.wait_recv()
        for g in range(2):
            for source in range(4):
                pairs = kv[source, g * 256 : (g + 1) * 256, :].astype(F32)
                rows = slice(source * 256, (source + 1) * 256)
                keys[g, rows, :] = jnp.where(
                    lane_pair < HD, pairs, pltpu.roll(pairs, HD, 1)
                ).astype(BF)
                vals_t[g, :, rows] = jnp.transpose(pairs)[HD:, :].astype(BF)

    def one_head(pair_rows, odd):
        kept = lane_pair >= HD if odd else lane_pair < HD
        return jnp.where(kept, pair_rows, jnp.zeros_like(pair_rows))

    def attend(step):
        g = step // 4
        pair = step - g * 4
        halves = []
        own = pl.ds(pl.multiple_of(g * 256, 256), 256)
        lanes = pl.ds(pl.multiple_of(pair * 128, 128), 128)
        queries = q_rot[own, lanes]
        for odd in range(2):
            head = step * 2 + odd
            scores = dotg(keys[g], one_head(queries, odd), 1, 1) + bias[g].astype(F32)
            top = jnp.max(scores, axis=0, keepdims=True)
            weights = jnp.exp(scores - top)
            norm = jnp.sum(weights, axis=0, keepdims=True)
            mixed = dotg(vals_t[g], weights.astype(BF), 1, 0)
            halves.append(mixed / norm)
            lse[head] = top + jnp.log(norm)
        rows = jnp.transpose(jnp.concatenate(halves, axis=0))
        att[own, lanes] = rows.astype(BF)

    def project_out(g):
        def body(shard, carry):
            part[g, :, :, pl.ds(pl.multiple_of(shard * 256, 256), 256)] = (
                dotg(att[rows_of[g], :], w_out[shard], 1, 0).astype(BF).reshape(4, 64, 256)
            )
            return carry

        lax.fori_loop(0, 8, body, 0)

    def second_norm(g):
        sum_att[g].finish(total)
        own = pl.ds(pl.multiple_of(g * 256 + me.z * 64, 64), 64)
        mid_rows = tok[own, :].astype(F32) + total[...]
        mid[g] = mid_rows
        inv = lax.rsqrt(jnp.mean(mid_rows * mid_rows, axis=-1, keepdims=True) + EPSILON)
        n_two[g, me.z] = (mid_rows * inv * row_of(gains, 1)).astype(BF)
        spread_two[g].begin()

    def looped(body, count, hooks):
        def step(i, carry):
            for spot, actions in hooks:

                @pl.when(i == spot)
                def _():
                    for action, *values in actions:
                        action(*values)

            body(i)
            return carry

        lax.fori_loop(0, count, step, 0)

    tile_count = (hidden + 255) // 256

    def feed(step):
        g = step // tile_count
        n = step - g * tile_count
        rows = pl.ds(pl.multiple_of(g * 256, 256), 256)
        lanes = pl.ds(pl.multiple_of(jnp.minimum(n * 256, hidden - 256), 128), 256)
        normed = n_two[g].reshape(256, 2048)
        gate = dotg(normed, w_gate[:, :, lanes].reshape(2048, 256), 1, 0)
        up = dotg(normed, w_up[:, :, lanes].reshape(2048, 256), 1, 0)
        hidden_grad = None
        for shard in range(8):
            term = dotg(
                cot[rows, shard * 256 : (shard + 1) * 256], w_down[shard, lanes, :], 1, 1
            )
            hidden_grad = term if hidden_grad is None else hidden_grad + term
        sig = jax.nn.sigmoid(gate)
        silu = gate * sig
        hid[rows, lanes] = (silu * up).astype(BF)
        up_g[rows, lanes] = (hidden_grad * silu).astype(BF)
        gate_g[rows, lanes] = (
            hidden_grad * up * sig * (1.0 + gate * (1.0 - sig))
        ).astype(BF)

    def feed_back(g):
        sum_att[g].drain()

        def body(shard, carry):
            term = dotg(gate_g[rows_of[g], :], w_gate[shard], 1, 1) + dotg(
                up_g[rows_of[g], :], w_up[shard], 1, 1
            )
            part[g, :, :, pl.ds(pl.multiple_of(shard * 256, 256), 256)] = term.astype(BF).reshape(
                4, 64, 256
            )
            return carry

        lax.fori_loop(0, 8, body, 0)

    part_two = n_two

    def feed_out(g):
        def body(shard, carry):
            term = dotg(hid[rows_of[g], :], w_down[shard], 1, 0)
            part_two[g, :, :, pl.ds(pl.multiple_of(shard * 256, 256), 256)] = term.astype(
                BF
            ).reshape(4, 64, 256)
            return carry

        lax.fori_loop(0, 8, body, 0)

    def line_sum(slot, part_ref, outer, inner):
        return LineSum(me, part_ref, outer, inner, sum_send.at[slot], sum_recv.at[slot])

    sum_two = [line_sum(g, part.at[g], outer_in.at[g], inner_in.at[g]) for g in range(2)]
    sum_one = [line_sum(2 + g, part.at[g], outer_in.at[g], inner_in.at[g]) for g in range(2)]

    sum_out = [
        line_sum(4 + g, part_two.at[g], outer_two.at[g], inner_two.at[g]) for g in range(2)
    ]
    sum_att = [line_sum(6 + g, part.at[g], outer_in.at[g], inner_in.at[g]) for g in range(2)]
    spread_two = [LineGather(me, n_two.at[g], all_send.at[6 + g], all_recv.at[6 + g]) for g in range(2)]
    spread_mid = [LineGather(me, mlow.at[g], all_send.at[g], all_recv.at[g]) for g in range(2)]
    spread_in = [LineGather(me, o_input.at[g], all_send.at[2 + g], all_recv.at[2 + g]) for g in range(2)]
    spread_out = [LineGather(me, o_result.at[g], all_send.at[4 + g], all_recv.at[4 + g]) for g in range(2)]

    def middle_back(g):
        sum_two[g].finish(total)
        own = pl.ds(pl.multiple_of(g * 256 + me.z * 64, 64), 64)
        back, gain_grad = norm_back(total[...], mid[g], row_of(gains, 1))
        if g == 0:
            vec[1:2, :] = gain_grad
        else:
            vec[1:2, :] += gain_grad
        grad = cot[own, :].astype(F32) + back
        mid_g[g] = grad
        mlow[g, me.z] = grad.astype(BF)
        spread_mid[g].begin()

    def put_own(g, ref, slot):
        copy = pltpu.make_async_copy(own_out, ref.at[g, me.z], own_sem.at[slot])
        copy.start()
        copy.wait()

    def input_back(g):
        sum_one[g].finish(total)
        own = pl.ds(pl.multiple_of(g * 256 + me.z * 64, 64), 64)
        back, gain_grad = norm_back(total[...], tok[own, :].astype(F32), row_of(gains, 0))
        if g == 0:
            vec[0:1, :] = gain_grad
        else:
            vec[0:1, :] += gain_grad
        own_out[...] = (mid_g[g] + back).astype(BF)
        put_own(g, o_input, 0)
        spread_in[g].begin()

    def result_rows(g):
        sum_out[g].finish(total)
        own_out[...] = (mid[g] + total[...]).astype(BF)
        put_own(g, o_result, 1)
        spread_out[g].begin()

    wide = lambda ref: (lambda shard: ref[:, pl.ds(pl.multiple_of(shard * 256, 256), 256)])

    def blocks_of(ref):
        return lambda shard: ref[
            :, :, :, pl.ds(pl.multiple_of(shard * 256, 256), 256)
        ].reshape(512, 256)

    def stage(width, slot):
        if width > 640:
            return w_up.at[4 + slot]
        first = lax.rem(slot, 2) * 640
        if not isinstance(slot, int):
            first = pl.multiple_of(first, 128)
        return w_up.at[4 + slot // 2, :, pl.ds(first, width)]

    landing = w_up.at[pl.ds(6, 2)]

    def scatter(index, width, x_of, y_of, chips, near):
        landed = diag_in.at[index] if index < 3 else diag_low.at[index - 3]
        refs = (stage, core_in, landed, near, rs_send, rs_recv, credit)
        return Scatter(me, index, index == 4, width, x_of, y_of, chips, refs)

    rs_down = scatter(
        0, hidden, wide(cot), lambda: hid[...], lambda role: w_gate.at[4 + role], near_down
    )
    rs_gate = scatter(
        1, hidden, blocks_of(n_two), lambda: gate_g[...], lambda role: w_gate.at[role], near_gate
    )
    rs_up = scatter(
        2, hidden, blocks_of(n_two), lambda: up_g[...], lambda role: w_up.at[role], near_up
    )
    rs_out = scatter(3, 512, blocks_of(mlow), lambda: att[...], lambda role: chip_out.at[role], near_out)
    rs_qkv = scatter(
        4,
        640,
        blocks_of(mlow),
        lambda: d_qkv[...],
        lambda role: chip_qkv.at[role],
        near_qkv,
    )

    def finish_rows(job, outs):
        job.collected(landing, fin_sem)
        width = job.width
        pending = [None, None]
        for step in range(4):
            slot = step % 2
            rows = slice(step * 64, (step + 1) * 64)
            if pending[slot] is not None:
                for piece in pending[slot]:
                    piece.wait()
            sum_stage[slot, :, :width] = (
                job.chips(0)[rows, :].astype(F32)
                + landing[0, rows, :width].astype(F32)
                + landing[1, rows, :width].astype(F32)
            )
            pending[slot] = [
                pltpu.make_async_copy(
                    sum_stage.at[slot, :, pl.ds(first, size)],
                    ref.at[pl.ds(step * 64, 64), :],
                    put_sem.at[slot, number],
                )
                for number, (ref, first, size) in enumerate(outs)
            ]
            for piece in pending[slot]:
                piece.start()
        for slot in range(2):
            for piece in pending[slot]:
                piece.wait()

    def finish_qkv(job):
        finish_rows(job, [(o_query, 0, 512)])
        lanes = slice(512, 640)
        turn_stage[0] = jnp.transpose(
            job.chips(0)[:, lanes].astype(F32)
            + landing[0, :, lanes].astype(F32)
            + landing[1, :, lanes].astype(F32)
        )
        copies = [
            pltpu.make_async_copy(
                turn_stage.at[0, pl.ds(first, HD), :], ref, put_sem.at[0, number]
            )
            for number, (first, ref) in enumerate(((0, o_key), (HD, o_value)))
        ]
        for piece in copies:
            piece.start()
        for piece in copies:
            piece.wait()

    def finish_turned(job, ref):
        job.collected(landing, fin_sem)

        def put(step, slot):
            rows = pl.ds(pl.multiple_of(step * 128, 128), 128)
            return pltpu.make_async_copy(turn_stage.at[slot], ref.at[rows, :], put_sem.at[slot, 0])

        def body(step, carry):
            slot = lax.rem(step, 2)
            lanes = pl.ds(pl.multiple_of(step * 128, 128), 128)

            @pl.when(step >= 2)
            def _():
                put(step, slot).wait()

            turn_stage[slot] = jnp.transpose(
                job.chips(0)[:, lanes].astype(F32)
                + landing[0, :, lanes].astype(F32)
                + landing[1, :, lanes].astype(F32)
            )
            put(step, slot).start()
            return carry

        lax.fori_loop(0, job.width // 128, body, 0)
        for slot in range(2):
            put(slot, slot).wait()

    def out_back(g):
        grad = None
        for shard in range(8):
            lanes = slice(shard * 256, (shard + 1) * 256)
            term = dotg(mlow[g, :, :, lanes].reshape(256, 256), w_out[shard], 1, 1)
            grad = term if grad is None else grad + term
        do_rows[...] = grad.astype(BF)
        for source in range(4):
            pairs = kv[source, rows_of[g], :].astype(F32)
            turned = pltpu.roll(pairs, HD, 1)
            rows = slice(source * 256, (source + 1) * 256)
            vals[rows, :] = jnp.where(lane_pair < HD, turned, pairs).astype(BF)
            keys_t[:, rows] = jnp.transpose(pairs)[:HD, :].astype(BF)
        key_acc[...] = jnp.zeros_like(key_acc)
        val_acc[...] = jnp.zeros_like(val_acc)

    def attend_back(step):
        g = step // 4
        pair = step - g * 4
        own = pl.ds(pl.multiple_of(g * 256, 256), 256)
        halves = []
        lanes = pl.ds(pl.multiple_of(pair * 128, 128), 128)
        queries, grads = q_rot[own, lanes], do_rows[:, lanes]
        for odd in range(2):
            query, grad = one_head(queries, odd), one_head(grads, odd)
            scores = dotg(keys[g], query, 1, 1) + bias[g].astype(F32)
            probs = jnp.exp(scores - lse[step * 2 + odd])
            prob_grad = dotg(vals[...], grad, 1, 1)
            delta = jnp.sum(probs * prob_grad, axis=0, keepdims=True)
            score_grad = (probs * (prob_grad - delta)).astype(BF)
            val_acc[...] += dotg(probs.astype(BF), grad, 1, 0)
            key_acc[...] += dotg(score_grad, query, 1, 0)
            halves.append(dotg(keys_t[...], score_grad, 1, 0))
        rows = jnp.transpose(jnp.concatenate(halves, axis=0)) * (HD ** (-0.5))
        rows = rows * rope[own, :128] - swap_halves(rows) * rope[own, 128:]
        d_qkv[own, lanes] = rows.astype(BF)

    def kv_copies(g):
        return [
            remote(
                kv_send_buf.at[g, column],
                kv_in.at[g, slot],
                kv_send.at[g, slot],
                kv_recv.at[g, slot],
                group[slot],
            )
            for slot, column in enumerate((me.cx, me.cy, me.cd))
        ]

    def kv_begin(g):
        for block in range(4):
            rows = slice(block * 256, (block + 1) * 256)
            key_rows, val_rows = key_acc[rows, :], val_acc[rows, :]
            joined = jnp.where(
                lane_pair < HD,
                key_rows + pltpu.roll(key_rows, HD, 1),
                val_rows + pltpu.roll(val_rows, HD, 1),
            )
            kv_send_buf[g, block] = joined.astype(BF)
        for piece in kv_copies(g):
            piece.start()

    def kv_finish(g):
        rows = kv_send_buf[g, me.c].astype(F32)
        for slot, piece in enumerate(kv_copies(g)):
            piece.wait_recv()
            rows = rows + kv_in[g, slot].astype(F32)
        cos_rows = jnp.where(lane_pair < HD, rope[rows_of[g], :128], 1.0)
        sin_rows = jnp.where(lane_pair < HD, rope[rows_of[g], 128:], 0.0)
        rows = rows * cos_rows - swap_halves(rows) * sin_rows
        d_qkv[rows_of[g], 512:640] = rows.astype(BF)

    def project_back_rows(g):
        sum_two[g].drain()

        def body(shard, carry):
            term = dotg(d_qkv[rows_of[g], :], w_qkv[shard], 1, 1)
            part[g, :, :, pl.ds(pl.multiple_of(shard * 256, 256), 256)] = term.astype(BF).reshape(
                4, 64, 256
            )
            return carry

        lax.fori_loop(0, 8, body, 0)

    line = column_devices(me)

    def vec_line():
        return [
            remote(vec_out, vec_in.at[slot], vec_send.at[slot], vec_recv.at[slot], device)
            for slot, device in enumerate(line)
        ]

    targets = [me.sx, me.sy, me.sd, me.of * 4 + me.c, me.of * 4 + me.cx, me.of * 4 + me.cy, me.of * 4 + me.cd]

    def vec_group():
        return [
            remote(
                vec_in.at[3, target],
                vec_near.at[slot],
                vec_send.at[3 + slot],
                vec_recv.at[3 + slot],
                device,
            )
            for slot, (target, device) in enumerate(zip(targets, group))
        ]

    def vec_begin():
        for shard in range(8):
            for which in range(2):
                for half in range(2):
                    first = shard * 256 + half * 128
                    vec_out[shard, 2 * which + half : 2 * which + half + 1, :] = vec[
                        which : which + 1, first : first + 128
                    ]
            vec_out[shard, 4:8, :] = jnp.zeros((4, 128), F32)
        for piece in vec_line():
            piece.start()

    def vec_middle():
        for piece in vec_line():
            piece.wait_recv()
        vec_in[3] = vec_out[...] + vec_in[0] + vec_in[1] + vec_in[2]
        for piece in vec_group():
            piece.start()

    def vec_finish():
        rows = vec_in[3, me.own]
        for slot, piece in enumerate(vec_group()):
            piece.wait_recv()
            rows = rows + vec_near[slot]
        o_gain_one[...] = rows[0:2, :]
        o_gain_two[...] = rows[2:4, :]

    def settle_weights():
        for piece in (qkv, out, gate, up, down):
            piece.settle()

    def settle():
        for job in sum_one + sum_out:
            job.drain()
        for spread in spread_in + spread_out:
            spread.finish()
        for job in (rs_down, rs_gate, rs_up, rs_out, rs_qkv):
            job.settle()
        for g in range(2):
            for piece in kv_copies(g):
                piece.wait_send()
        for piece in vec_line() + vec_group() + small + first_copies([me.c] * 3):
            piece.wait_send()

    order = (
        (qkv.begin,),
        (small_begin,),
        (make_rope,),
        (qkv.forward_a,),
        (qkv.forward_b,),
        (small_finish,),
        (first_norm,),
        (out.begin,),
        (qkv.diagonal_a,),
        (qkv.diagonal_b,),
        (qkv.arrive,),
        (project_kv,),
        (project_q, 0),
        (out.forward_a,),
        (make_bias, 0),
        (out.forward_b,),
        (project_q, 1),
        (save_one.wait,),
        (up.begin,),
        (kv_arrive,),
        (make_bias, 1),
        (down.begin,),
        (
            looped,
            attend,
            8,
            (
                (2, ((out.diagonal_a,), (out.diagonal_b,),)),
                (4, ((out.arrive,),)),
                (6, ((project_out, 0), (sum_att[0].begin,), (sum_att[0].step_one,),)),
            ),
        ),
        (project_out, 1),
        (load_cot.wait,),
        (gate.begin,),
        (sum_att[1].begin,),
        (sum_att[0].step_two,),
        (sum_att[0].step_three,),
        (second_norm, 0),
        (down.forward_a,),
        (down.forward_b,),
        (up.forward_a,),
        (sum_att[1].step_one,),
        (sum_att[1].step_two,),
        (spread_two[0].step_two,),
        (sum_att[1].step_three,),
        (second_norm, 1),
        (up.forward_b,),
        (down.diagonal_a,),
        (down.diagonal_b,),
        (spread_two[0].step_one,),
        (down.arrive,),
        (up.diagonal_a,),
        (gate.forward_a,),
        (spread_two[1].step_one,),
        (gate.forward_b,),
        (spread_two[0].step_three,),
        (up.diagonal_b,),
        (up.arrive,),
        (gate.diagonal_a,),
        (spread_two[1].step_two,),
        (gate.diagonal_b,),
        (spread_two[0].finish,),
        (gate.arrive,),
        (settle_weights,),
        (
            looped,
            feed,
            2 * tile_count,
            (
                (3, ((spread_two[1].step_three,),)),
                (6, ((feed_back, 0), (sum_two[0].begin,), (spread_two[1].finish,),)),
            ),
        ),
        (feed_back, 1),
        (sum_two[0].step_one,),
        (sum_two[0].step_two,),
        (sum_two[1].begin,),
        (rs_down.partner,),
        (sum_two[0].step_three,),
        (rs_down.own,),
        (rs_gate.partner,),
        (sum_two[1].step_one,),
        (middle_back, 0),
        (rs_gate.own,),
        (rs_up.partner,),
        (sum_two[1].step_three,),
        (sum_two[1].step_two,),
        (rs_up.own,),
        (spread_mid[0].step_one,),
        (spread_mid[0].step_two,),
        (rs_up.push_near,),
        (middle_back, 1),
        (rs_down.push_near,),
        (feed_out, 1),
        (spread_mid[1].step_one,),
        (rs_gate.push_near,),
        (feed_out, 0),
        (spread_mid[0].step_three,),
        (sum_out[1].begin,),
        (sum_out[1].step_one,),
        (sum_out[0].begin,),
        (spread_mid[0].finish,),
        (out_back, 0),
        (rs_gate.push_diag,),
        (spread_mid[1].step_two,),
        (
            looped,
            attend_back,
            8,
            (
                (4, ((spread_mid[1].step_three,), (spread_mid[1].finish,), (kv_begin, 0), (sum_out[1].step_two,), (out_back, 1),)),
                (6, ((sum_out[1].step_three,), (rs_out.partner,), (sum_out[0].step_one,), (result_rows, 1), (rs_down.push_diag,),)),
            ),
        ),
        (kv_begin, 1),
        (rs_up.push_diag,),
        (kv_finish, 0),
        (project_back_rows, 0),
        (sum_out[0].step_three,),
        (sum_out[0].step_two,),
        (spread_out[1].step_two,),
        (sum_one[0].begin,),
        (rs_out.own,),
        (rs_out.push_diag,),
        (spread_out[1].step_one,),
        (kv_finish, 1),
        (project_back_rows, 1),
        (sum_one[1].begin,),
        (rs_gate.relay_a,),
        (result_rows, 0),
        (load_one.start,),
        (sum_one[0].step_one,),
        (spread_out[1].step_three,),
        (load_one.wait,),
        (rs_down.relay_a,),
        (sum_one[0].step_two,),
        (rs_qkv.partner,),
        (spread_out[0].step_two,),
        (sum_one[0].step_three,),
        (rs_out.relay_a,),
        (rs_up.relay_a,),
        (rs_up.relay_b,),
        (rs_down.relay_b,),
        (sum_one[1].step_one,),
        (rs_qkv.own,),
        (input_back, 0),
        (sum_one[1].step_two,),
        (sum_one[1].step_three,),
        (rs_qkv.push_diag,),
        (spread_in[0].step_two,),
        (spread_out[0].step_one,),
        (rs_gate.relay_b,),
        (input_back, 1),
        (rs_out.push_near,),
        (spread_in[0].step_one,),
        (rs_qkv.push_near,),
        (vec_begin,),
        (rs_down.collect, landing, fin_sem),
        (finish_turned, rs_down, o_down),
        (spread_out[0].step_three,),
        (rs_qkv.relay_a,),
        (spread_in[1].step_one,),
        (spread_in[1].step_two,),
        (rs_out.relay_b,),
        (rs_gate.collect, landing, fin_sem),
        (finish_rows, rs_gate, [(o_gate, 0, hidden)]),
        (rs_up.collect, landing, fin_sem),
        (finish_rows, rs_up, [(o_up, 0, hidden)]),
        (spread_in[0].step_three,),
        (rs_out.collect, landing, fin_sem),
        (finish_turned, rs_out, o_out),
        (rs_qkv.relay_b,),
        (spread_in[1].step_three,),
        (vec_middle,),
        (vec_finish,),
        (rs_qkv.collect, landing, fin_sem),
        (finish_qkv, rs_qkv),
        (settle,),
    )
    for action, *values in order:
        action(*values)


def run_layer(
    tokens, attn_gain, w_query, w_key, w_value, w_out, mlp_gain, w_gate, w_up, w_down, cotangent,
    positions, segments,
):
    shape = jax.ShapeDtypeStruct
    width = tokens.shape[1]
    hidden = w_gate.shape[1]
    vmem = pl.BlockSpec(memory_space=pltpu.VMEM)
    anywhere = pl.BlockSpec(memory_space=pl.ANY)
    dma = pltpu.SemaphoreType.DMA
    buffer = pltpu.VMEM
    half_size = HD // 2
    frequency = THETA_BASE ** (-np.arange(half_size, dtype=np.float32) / half_size)
    frequency = np.concatenate([frequency] * 4)[None, :].astype(np.float32)
    return pl.pallas_call(
        layer_kernel,
        name="decoder_layer",
        out_shape=(
            shape((2, 4, 64, width), BF),
            shape((2, 4, 64, width), BF),
            shape((2, 128), F32),
            shape((2, 128), F32),
            shape((256, 512), F32),
            shape((HD, 256), F32),
            shape((HD, 256), F32),
            shape((512, 256), F32),
            shape((256, hidden), F32),
            shape((256, hidden), F32),
            shape((hidden, 256), F32),
            shape((2, 256, hidden), BF),
            shape((2, 256, hidden), BF),
            shape((2, 256, hidden), BF),
            shape((2, 256, 512), BF),
            shape((2, 256, 640), BF),
            shape((2, 4, 64, width), BF),
        ),
        in_specs=[anywhere, vmem, vmem, vmem, vmem, vmem]
        + [anywhere] * 5
        + [vmem] * 3,
        out_specs=(anywhere,) * 2 + (vmem,) * 2 + (anywhere,) * 13,
        scratch_shapes=[
            buffer((8, 256), F32),
            buffer((8, 512), jnp.int32),
            buffer((8, 8, 256), F32),
            buffer((4, 8, 512), jnp.int32),
            buffer((512, width), BF),
            buffer((8, 256, hidden), BF),
            buffer((8, 256, hidden), BF),
            buffer((8, hidden, 256), BF),
            buffer((8, 512, 256), BF),
            buffer((8, 256, 640), BF),
            buffer((512, width), BF),
            buffer((2, 4, 64, width), BF),
            buffer((512, hidden), BF),
            buffer((512, hidden), BF),
            buffer((512, hidden), BF),
            buffer((4, 256, hidden), BF),
            buffer((3, 2, 128, hidden), BF),
            buffer((2, 2, 128, 640), BF),
            buffer((4, 256, 512), BF),
            buffer((4, 256, 640), BF),
            buffer((2, 64, hidden), F32),
            buffer((2, 128, 256), F32),
            buffer((2, 4, 64, width), BF),
            buffer((2, 3, 64, width), BF),
            buffer((2, 2, 64, width), BF),
            buffer((2, 3, 64, width), BF),
            buffer((2, 2, 64, width), BF),
            buffer((2, 4, 64, width), BF),
            buffer((64, width), F32),
            buffer((64, width), BF),
            buffer((2, 64, width), F32),
            buffer((2, 64, width), F32),
            buffer((512, 512), BF),
            buffer((2, 1024, 256), BF),
            buffer((16, 1, 256), F32),
            buffer((4, 512, 128), BF),
            buffer((512, 512), BF),
            buffer((512, 256), F32),
            buffer((256, 512), BF),
            buffer((2, 1024, 128), BF),
            buffer((2, HD, 1024), BF),
            buffer((1024, 128), BF),
            buffer((HD, 1024), BF),
            buffer((1024, 128), F32),
            buffer((1024, 128), F32),
            buffer((2, 4, 256, 128), BF),
            buffer((2, 3, 256, 128), BF),
            buffer((512, 640), BF),
            buffer((2, width), F32),
            buffer((4, 8, 8, 128), F32),
            buffer((8, 8, 128), F32),
            buffer((7, 8, 128), F32),
            dma((5, 9)),
            dma((5, 9)),
            dma((5,)),
            dma((10,)),
            dma((10,)),
            dma((3,)),
            dma((3,)),
            dma((4,)),
            dma((8, 3)),
            dma((8, 5)),
            dma((8, 5)),
            dma((8, 4)),
            dma((5, 10)),
            dma((5, 10)),
            pltpu.SemaphoreType.REGULAR((4,)),
            dma((2, 3)),
            dma((2, 3)),
            dma((10,)),
            dma((10,)),
            dma((2,)),
            dma((2, 2)),
            dma((2,)),
        ],
        compiler_params=pltpu.CompilerParams(
            collective_id=0, has_side_effects=True, vmem_limit_bytes=67043328
        ),
    )(
        tokens, attn_gain, mlp_gain, w_query, w_key.T, w_value.T, w_out, w_gate, w_up,
        w_down, cotangent, positions[None, :], segments[None, :], frequency,
    )


def hand_over_kernel(*refs):
    count = (len(refs) - 2) // 3
    sources, targets, buffers = refs[:count], refs[count : 2 * count], refs[2 * count : 3 * count]
    in_sem, out_sem = refs[3 * count :]
    fetch = [
        pltpu.make_async_copy(source, buffers[n], in_sem.at[n]) for n, source in enumerate(sources)
    ]
    store = [
        pltpu.make_async_copy(buffers[n], target, out_sem.at[n]) for n, target in enumerate(targets)
    ]
    for piece in fetch:
        piece.start()
    for n in range(count):
        fetch[n].wait()
        store[n].start()
    for piece in store:
        piece.wait()


def hand_over(values):
    anywhere = pl.BlockSpec(memory_space=pl.ANY)
    dma = pltpu.SemaphoreType.DMA
    return pl.pallas_call(
        hand_over_kernel,
        name="hand_over",
        out_shape=tuple(jax.ShapeDtypeStruct(value.shape, value.dtype) for value in values),
        in_specs=[anywhere] * len(values),
        out_specs=(anywhere,) * len(values),
        scratch_shapes=[pltpu.VMEM(value.shape, value.dtype) for value in values]
        + [dma((len(values),)), dma((len(values),))],
        compiler_params=pltpu.CompilerParams(vmem_limit_bytes=67043328),
    )(*values)


def fast_shards(tokens, *others):
    made = run_layer(tokens, *others)
    (
        query_g, out_g, gate_g, up_g, down_g, key_g, value_g, gain_one_g, gain_two_g, result, input_grad,
    ) = hand_over(made[4:5] + made[7:11] + made[5:7] + made[2:4] + made[0:2])
    return (
        result.reshape(tokens.shape),
        input_grad.reshape(tokens.shape),
        gain_one_g.reshape(-1),
        query_g,
        key_g.T,
        value_g.T,
        out_g,
        gain_two_g.reshape(-1),
        gate_g,
        up_g,
        down_g,
    )


def solution(mesh):
    in_specs = (
        P(("fsdp", "ctx"), None),
        P(("fsdp", "ctx")),
        P(("fsdp", "ctx"), "tp"),
        P(("fsdp", "ctx"), "tp"),
        P(("fsdp", "ctx"), "tp"),
        P("tp", ("fsdp", "ctx")),
        P(("fsdp", "ctx")),
        P(("fsdp", "ctx"), "tp"),
        P(("fsdp", "ctx"), "tp"),
        P("tp", ("fsdp", "ctx")),
        P(("fsdp", "ctx"), None),
        P(("fsdp", "ctx")),
        P(("fsdp", "ctx")),
    )
    out_specs = (
        P(("fsdp", "ctx"), None),
        P(("fsdp", "ctx"), None),
        P(("fsdp", "ctx")),
        P(("fsdp", "ctx"), "tp"),
        P(("fsdp", "ctx"), "tp"),
        P(("fsdp", "ctx"), "tp"),
        P("tp", ("fsdp", "ctx")),
        P(("fsdp", "ctx")),
        P(("fsdp", "ctx"), "tp"),
        P(("fsdp", "ctx"), "tp"),
        P("tp", ("fsdp", "ctx")),
    )
    small = (mesh.shape["fsdp"], mesh.shape["ctx"], mesh.shape["tp"]) == (2, 4, 4)
    return jax.shard_map(fast_shards if small else shards, mesh=mesh, in_specs=in_specs, out_specs=out_specs, check_vma=False)
```

```python
import jax
import jax.numpy as jnp
import numpy as np
from jax import lax
from jax.experimental import pallas as pl
from jax.experimental.pallas import tpu as pltpu
from jax.sharding import PartitionSpec as P

H = 32
KVH = 4
HD = 64


EPSILON = 1e-05
THETA_BASE = 10000.0
MASKED_SCORE = -1e30


def shifted(value, axis, steps):
    count = lax.axis_size(axis)
    pairs = [(source, (source + steps) % count) for source in range(count)]
    return lax.ppermute(value, axis, pairs)


def rope_tables(token_pos, half_size):
    frequency = THETA_BASE ** (-jnp.arange(half_size, dtype=jnp.float32) / half_size)
    angles = token_pos.astype(jnp.float32)[:, None] * frequency[None, :]
    return (jnp.cos(angles), jnp.sin(angles))


def rotate(head_rows, cosine, sine):
    half_size = head_rows.shape[-1] // 2
    first_half = head_rows[..., :half_size]
    second_half = head_rows[..., half_size:]
    cos_rows = cosine[:, None, :]
    sin_rows = sine[:, None, :]
    return jnp.concatenate(
        [
            first_half * cos_rows - second_half * sin_rows,
            second_half * cos_rows + first_half * sin_rows,
        ],
        axis=-1,
    )


def rotate_back(head_rows, cosine, sine):
    half_size = head_rows.shape[-1] // 2
    first_half = head_rows[..., :half_size]
    second_half = head_rows[..., half_size:]
    cos_rows = cosine[:, None, :]
    sin_rows = sine[:, None, :]
    return jnp.concatenate(
        [
            first_half * cos_rows + second_half * sin_rows,
            second_half * cos_rows - first_half * sin_rows,
        ],
        axis=-1,
    )


def project(left_side, right_side):
    return jnp.dot(left_side, right_side, preferred_element_type=jnp.float32)


def project_back(left_side, right_side):
    return lax.dot_general(
        left_side, right_side, (((1,), (1,)), ((), ())), preferred_element_type=jnp.float32
    )


def weight_grad(left_side, right_side):
    return lax.dot_general(
        left_side, right_side, (((0,), (0,)), ((), ())), preferred_element_type=jnp.float32
    )


def rms_norm(rows_in, gain_vec):
    inv_rms = lax.rsqrt(jnp.mean(rows_in * rows_in, axis=-1, keepdims=True) + EPSILON)
    unit_rows = rows_in * inv_rms
    return (unit_rows * gain_vec, unit_rows, inv_rms)


def rms_norm_back(gradient, gain_vec, unit_rows, inv_rms):
    gain_grad = jnp.sum(gradient * unit_rows, axis=0)
    scaled_grad = gradient * gain_vec
    return (
        inv_rms
        * (scaled_grad - unit_rows * jnp.mean(scaled_grad * unit_rows, axis=-1, keepdims=True)),
        gain_grad,
    )


def pair_mask(query_pos, query_seg, key_pos, key_seg):
    return (query_seg[:, None] == key_seg[None, :]) & (key_pos[None, :] <= query_pos[:, None])


def split_block(kv_block, kv_heads):
    key_rows = kv_block[:, : kv_heads * HD].reshape(-1, kv_heads, HD)
    value_rows = kv_block[:, kv_heads * HD :].reshape(-1, kv_heads, HD)
    return (key_rows, value_rows)


def attend_block(state_in, queries, kv_block, visible):
    row_top, row_total, output_sum = state_in
    key_rows, value_rows = split_block(kv_block, queries.shape[1])
    scores = jnp.einsum(
        "qkgd,pkd->kgqp", queries, key_rows, preferred_element_type=jnp.float32
    ) * HD ** (-0.5)
    scores = jnp.where(visible, scores, MASKED_SCORE)
    new_top = jnp.maximum(row_top, jnp.max(scores, axis=-1))
    weights = jnp.where(visible, jnp.exp(scores - new_top[..., None]), 0.0)
    decay_factor = jnp.exp(row_top - new_top)
    row_total = row_total * decay_factor + jnp.sum(weights, axis=-1)
    mixed_heads = jnp.einsum(
        "kgqp,pkd->qkgd",
        weights.astype(jnp.bfloat16),
        value_rows,
        preferred_element_type=jnp.float32,
    )
    output_sum = output_sum * jnp.transpose(decay_factor, (2, 0, 1))[..., None] + mixed_heads
    return (new_top, row_total, output_sum)


def block_grads(queries, out_grad, kv_block, visible, log_total, delta_rows):
    key_rows, value_rows = split_block(kv_block, queries.shape[1])
    scale_factor = HD ** (-0.5)
    scores = (
        jnp.einsum("qkgd,pkd->kgqp", queries, key_rows, preferred_element_type=jnp.float32)
        * scale_factor
    )
    probs_full = jnp.where(
        visible, jnp.exp(jnp.where(visible, scores, MASKED_SCORE) - log_total[..., None]), 0.0
    )
    value_grad = jnp.einsum(
        "kgqp,qkgd->pkd",
        probs_full.astype(jnp.bfloat16),
        out_grad,
        preferred_element_type=jnp.float32,
    )
    prob_grad = jnp.einsum(
        "qkgd,pkd->kgqp", out_grad, value_rows, preferred_element_type=jnp.float32
    )
    score_grad = (probs_full * (prob_grad - delta_rows[..., None])).astype(jnp.bfloat16)
    query_grad = (
        jnp.einsum("kgqp,pkd->qkgd", score_grad, key_rows, preferred_element_type=jnp.float32)
        * scale_factor
    )
    key_grad = (
        jnp.einsum("kgqp,qkgd->pkd", score_grad, queries, preferred_element_type=jnp.float32)
        * scale_factor
    )
    block_rows = kv_block.shape[0]
    return (
        query_grad,
        jnp.concatenate(
            [key_grad.reshape(block_rows, -1), value_grad.reshape(block_rows, -1)], axis=-1
        ),
    )


def shards(
    tokens,
    attn_gain,
    w_query,
    w_key,
    w_value,
    w_out,
    mlp_gain,
    w_gate,
    w_up,
    w_down,
    cotangent,
    positions,
    segments,
):
    token_rows = tokens.shape[0]
    gain_one, query_w, key_w, value_w, out_w = (
        lax.all_gather(attn_gain, ("fsdp", "ctx"), axis=0, tiled=True),
        lax.all_gather(w_query, ("fsdp", "ctx"), axis=0, tiled=True),
        lax.all_gather(w_key, ("fsdp", "ctx"), axis=0, tiled=True),
        lax.all_gather(w_value, ("fsdp", "ctx"), axis=0, tiled=True),
        lax.all_gather(w_out, ("fsdp", "ctx"), axis=1, tiled=True),
    )
    gain_two, gate_w, up_w, down_w = (
        lax.all_gather(mlp_gain, ("fsdp", "ctx"), axis=0, tiled=True),
        lax.all_gather(w_gate, ("fsdp", "ctx"), axis=0, tiled=True),
        lax.all_gather(w_up, ("fsdp", "ctx"), axis=0, tiled=True),
        lax.all_gather(w_down, ("fsdp", "ctx"), axis=1, tiled=True),
    )
    head_count = query_w.shape[1] // HD
    kv_heads = key_w.shape[1] // HD
    groups = H // KVH
    cosine, sine = rope_tables(positions, HD // 2)
    token_float = tokens.astype(jnp.float32)
    gain_one_float = gain_one.astype(jnp.float32)
    normed_one, unit_one, inv_one = rms_norm(token_float, gain_one_float)
    normed_low = normed_one.astype(jnp.bfloat16)
    query_lin = project(normed_low, query_w)
    key_lin = project(normed_low, key_w)
    value_low = project(normed_low, value_w).astype(jnp.bfloat16)
    query_rot = rotate(query_lin.reshape(token_rows, head_count, HD), cosine, sine).astype(
        jnp.bfloat16
    )
    key_rot = rotate(key_lin.reshape(token_rows, kv_heads, HD), cosine, sine).astype(jnp.bfloat16)
    queries = query_rot.reshape(token_rows, kv_heads, groups, HD)
    kv_local = jnp.concatenate([key_rot.reshape(token_rows, kv_heads * HD), value_low], axis=-1)
    key_positions, key_segments = (
        lax.all_gather(positions, "ctx", axis=0, tiled=True),
        lax.all_gather(segments, "ctx", axis=0, tiled=True),
    )
    my_index = lax.axis_index("ctx")
    cycle_size = lax.axis_size("ctx")

    def block_marks(source):
        start_row = source * token_rows
        return pair_mask(
            positions,
            segments,
            lax.dynamic_slice_in_dim(key_positions, start_row, token_rows),
            lax.dynamic_slice_in_dim(key_segments, start_row, token_rows),
        )

    start_state = (
        jnp.full((kv_heads, groups, token_rows), MASKED_SCORE, jnp.float32),
        jnp.zeros((kv_heads, groups, token_rows), jnp.float32),
        jnp.zeros((token_rows, kv_heads, groups, HD), jnp.float32),
    )

    def forward_block(state_in, kv_block, source):
        visible = block_marks(source)
        return attend_block(state_in, queries, kv_block, visible)

    def cycle_step(state_in, step_index):
        attn_state, kv_block = state_in
        attn_state = forward_block(attn_state, kv_block, (my_index - step_index) % cycle_size)
        passed = shifted(kv_block, "ctx", 1)
        return ((attn_state, passed), kv_block)

    (attn_state, last_block), kept_blocks = lax.scan(
        cycle_step, (start_state, kv_local), jnp.arange(cycle_size - 1)
    )
    attn_state = forward_block(attn_state, last_block, (my_index + 1) % cycle_size)
    kv_blocks = jnp.concatenate([kept_blocks, last_block[None]], axis=0)
    sources = (my_index - jnp.arange(cycle_size)) % cycle_size
    row_top, row_total, output_sum = attn_state
    attended = output_sum / jnp.transpose(row_total, (2, 0, 1))[..., None]
    log_total = row_top + jnp.log(row_total)
    attended_low = attended.reshape(token_rows, head_count * HD).astype(jnp.bfloat16)
    middle = token_float + lax.psum(project(attended_low, out_w).astype(jnp.bfloat16), "tp").astype(
        jnp.float32
    )
    gain_two_float = gain_two.astype(jnp.float32)
    normed_two, unit_two, inv_two = rms_norm(middle, gain_two_float)
    normed_two_low = normed_two.astype(jnp.bfloat16)
    gate_lin = project(normed_two_low, gate_w)
    up_lin = project(normed_two_low, up_w)
    hidden_low = (jax.nn.silu(gate_lin) * up_lin).astype(jnp.bfloat16)
    result = middle + lax.psum(project(hidden_low, down_w).astype(jnp.bfloat16), "tp").astype(
        jnp.float32
    )
    output = result.astype(jnp.bfloat16)
    hidden_grad = project_back(cotangent, down_w)
    down_w_grad = weight_grad(hidden_low, cotangent)
    sigmoid_gate = jax.nn.sigmoid(gate_lin)
    gate_grad_low = (
        hidden_grad * up_lin * sigmoid_gate * (1.0 + gate_lin * (1.0 - sigmoid_gate))
    ).astype(jnp.bfloat16)
    up_grad_low = (hidden_grad * gate_lin * sigmoid_gate).astype(jnp.bfloat16)
    normed_two_grad = lax.psum(
        (project_back(gate_grad_low, gate_w) + project_back(up_grad_low, up_w)).astype(
            jnp.bfloat16
        ),
        "tp",
    ).astype(jnp.float32)
    gate_w_grad = weight_grad(normed_two_low, gate_grad_low)
    up_w_grad = weight_grad(normed_two_low, up_grad_low)
    norm_back_two, gain_two_grad = rms_norm_back(normed_two_grad, gain_two_float, unit_two, inv_two)
    middle_grad = cotangent.astype(jnp.float32) + norm_back_two
    middle_low = middle_grad.astype(jnp.bfloat16)
    attended_grad_low = project_back(middle_low, out_w).astype(jnp.bfloat16)
    out_w_grad = weight_grad(attended_low, middle_low)
    out_grad = attended_grad_low.reshape(token_rows, kv_heads, groups, HD)
    delta_rows = jnp.transpose(jnp.sum(out_grad.astype(jnp.float32) * attended, axis=-1), (1, 2, 0))

    def backward_block(kv_block, source):
        visible = block_marks(source)
        return block_grads(queries, out_grad, kv_block, visible, log_total, delta_rows)

    query_start = jnp.zeros((token_rows, kv_heads, groups, HD), jnp.float32)

    def back_step(state_in, pieces):
        query_acc, kv_acc = state_in
        query_term, kv_term = backward_block(pieces[0], pieces[1])
        passed = shifted((kv_acc + kv_term).astype(jnp.bfloat16), "ctx", 1).astype(jnp.float32)
        return ((query_acc + query_term, passed), None)

    (query_grad, kv_grad), unused = lax.scan(
        back_step, (query_start, jnp.zeros(kv_local.shape, jnp.float32)), (kv_blocks, sources)
    )
    query_grad_low = (
        rotate_back(query_grad.reshape(token_rows, head_count, HD), cosine, sine)
        .reshape(token_rows, head_count * HD)
        .astype(jnp.bfloat16)
    )
    key_grad_low = (
        rotate_back(kv_grad[:, : kv_heads * HD].reshape(token_rows, kv_heads, HD), cosine, sine)
        .reshape(token_rows, kv_heads * HD)
        .astype(jnp.bfloat16)
    )
    value_grad_low = kv_grad[:, kv_heads * HD :].astype(jnp.bfloat16)
    normed_one_grad = lax.psum(
        (
            project_back(query_grad_low, query_w)
            + project_back(key_grad_low, key_w)
            + project_back(value_grad_low, value_w)
        ).astype(jnp.bfloat16),
        "tp",
    ).astype(jnp.float32)
    query_w_grad = weight_grad(normed_low, query_grad_low)
    key_w_grad = weight_grad(normed_low, key_grad_low)
    value_w_grad = weight_grad(normed_low, value_grad_low)
    norm_back_one, gain_one_grad = rms_norm_back(normed_one_grad, gain_one_float, unit_one, inv_one)
    input_grad = (middle_grad + norm_back_one).astype(jnp.bfloat16)
    summed = (
        lax.psum_scatter(
            gain_one_grad.astype(jnp.bfloat16), ("fsdp", "ctx"), scatter_dimension=0, tiled=True
        ).astype(jnp.float32),
        lax.psum_scatter(
            query_w_grad.astype(jnp.bfloat16), ("fsdp", "ctx"), scatter_dimension=0, tiled=True
        ).astype(jnp.float32),
        lax.psum_scatter(
            key_w_grad.astype(jnp.bfloat16), ("fsdp", "ctx"), scatter_dimension=0, tiled=True
        ).astype(jnp.float32),
        lax.psum_scatter(
            value_w_grad.astype(jnp.bfloat16), ("fsdp", "ctx"), scatter_dimension=0, tiled=True
        ).astype(jnp.float32),
        lax.psum_scatter(
            out_w_grad.astype(jnp.bfloat16), ("fsdp", "ctx"), scatter_dimension=1, tiled=True
        ).astype(jnp.float32),
        lax.psum_scatter(
            gain_two_grad.astype(jnp.bfloat16), ("fsdp", "ctx"), scatter_dimension=0, tiled=True
        ).astype(jnp.float32),
        lax.psum_scatter(
            gate_w_grad.astype(jnp.bfloat16), ("fsdp", "ctx"), scatter_dimension=0, tiled=True
        ).astype(jnp.float32),
        lax.psum_scatter(
            up_w_grad.astype(jnp.bfloat16), ("fsdp", "ctx"), scatter_dimension=0, tiled=True
        ).astype(jnp.float32),
        lax.psum_scatter(
            down_w_grad.astype(jnp.bfloat16), ("fsdp", "ctx"), scatter_dimension=1, tiled=True
        ).astype(jnp.float32),
    )
    return (output, input_grad) + tuple(summed)


MESH = pl.DeviceIdType.MESH
BF = jnp.bfloat16
F32 = jnp.float32


def dotg(left_side, right_side, left_dim, right_dim):
    return lax.dot_general(
        left_side,
        right_side,
        (((left_dim,), (right_dim,)), ((), ())),
        preferred_element_type=F32,
    )


def remote(src, dst, send_sem, recv_sem, device):
    return pltpu.make_async_remote_copy(
        src_ref=src,
        dst_ref=dst,
        send_sem=send_sem,
        recv_sem=recv_sem,
        device_id=device,
        device_id_type=MESH,
    )


class Place:
    def __init__(self):
        self.f = lax.axis_index("fsdp")
        self.c = lax.axis_index("ctx")
        self.z = lax.axis_index("tp")
        self.cx = self.c + 1 - 2 * lax.rem(self.c, 2)
        self.cy = lax.rem(self.c + 2, 4)
        self.cd = 3 - self.c
        self.of = 1 - self.f
        self.own = self.f * 4 + self.c
        self.sx = self.f * 4 + self.cx
        self.sy = self.f * 4 + self.cy
        self.sd = self.f * 4 + self.cd

    def at(self, f=None, c=None, z=None):
        return (
            self.f if f is None else f,
            self.c if c is None else c,
            self.z if z is None else z,
        )


def group_devices(me):
    return [
        me.at(c=me.cx),
        me.at(c=me.cy),
        me.at(c=me.cd),
        me.at(f=me.of),
        me.at(f=me.of, c=me.cx),
        me.at(f=me.of, c=me.cy),
        me.at(f=me.of, c=me.cd),
    ]


def column_devices(me):
    return [me.at(z=lax.rem(me.z + step, 4)) for step in (1, 2, 3)]


class Gather:
    def __init__(self, me, index, own, full, send, recv, local_sem):
        self.me, self.full, self.placed = me, full, own is None
        own = full.at[me.own] if own is None else own
        rows = full.shape[1]
        self.half_a = pl.ds(0, rows // 2)
        self.half_b = pl.ds(rows // 2, rows // 2)

        def copy(slot, src, dst, device):
            return remote(src, dst, send.at[index, slot], recv.at[index, slot], device)

        slot_own, slot_x, slot_y = full.at[me.own], full.at[me.sx], full.at[me.sy]
        to_x, to_y, to_core = me.at(c=me.cx), me.at(c=me.cy), me.at(f=me.of)
        diag_a = full.at[me.sd, self.half_a]
        diag_b = full.at[me.sd, self.half_b]
        self.own_x = copy(0, own, slot_own, to_x)
        self.own_y = copy(1, own, slot_own, to_y)
        self.own_core = copy(2, own, slot_own, to_core)
        self.pass_x = copy(3, full.at[me.sy, self.half_a], full.at[me.sy, self.half_a], to_x)
        self.pass_y = copy(4, full.at[me.sx, self.half_b], full.at[me.sx, self.half_b], to_y)
        self.core_x = copy(5, slot_x, slot_x, to_core)
        self.core_y = copy(6, slot_y, slot_y, to_core)
        self.core_a = copy(7, diag_a, diag_a, to_core)
        self.core_b = copy(8, diag_b, diag_b, to_core)
        other = me.of * 4
        into = lambda slot, ref, device: copy(slot, ref, ref, device)
        self.in_x = into(0, slot_x, to_x)
        self.in_y = into(1, slot_y, to_y)
        self.in_a = into(3, diag_a, to_x)
        self.in_b = into(4, diag_b, to_y)
        self.in_core = [
            into(2, full.at[other + me.c], to_core),
            into(5, full.at[other + me.cx], to_core),
            into(6, full.at[other + me.cy], to_core),
            into(7, full.at[other + me.cd, self.half_a], to_core),
            into(8, full.at[other + me.cd, self.half_b], to_core),
        ]
        self.keep = None if self.placed else pltpu.make_async_copy(own, slot_own, local_sem.at[index])

    def begin(self):
        self.own_x.start()
        self.own_y.start()
        self.own_core.start()
        if not self.placed:
            self.keep.start()

    def forward_a(self):
        self.in_y.wait_recv()
        self.pass_x.start()
        self.core_y.start()

    def forward_b(self):
        self.in_x.wait_recv()
        self.pass_y.start()
        self.core_x.start()

    def diagonal_a(self):
        self.in_a.wait_recv()
        self.core_a.start()

    def diagonal_b(self):
        self.in_b.wait_recv()
        self.core_b.start()

    def arrive(self):
        if not self.placed:
            self.keep.wait()
        for piece in self.in_core:
            piece.wait_recv()

    def settle(self):
        for piece in (
            self.own_x,
            self.own_y,
            self.own_core,
            self.pass_x,
            self.pass_y,
            self.core_x,
            self.core_y,
            self.core_a,
            self.core_b,
        ):
            piece.wait_send()


class LineSum:
    def __init__(self, me, part, outer_in, inner_in, send, recv):
        self.me, self.part = me, part
        self.outer_in, self.inner_in = outer_in, inner_in
        self.send, self.recv = send, recv
        z = me.z
        self.is_mid = (z == 1) | (z == 2)
        self.is_end = (z == 0) | (z == 3)
        self.mid_of_end = 1 + z // 3
        self.outer_of_mid = 3 * (z - 1)

    def end_copies(self):
        me, part = self.me, self.part
        mid = self.mid_of_end
        to_mid = me.at(z=mid)
        owners = (3 - me.z, 3 - mid, mid)
        return [
            remote(
                part.at[owner],
                self.outer_in.at[slot],
                self.send.at[slot],
                self.recv.at[slot],
                to_mid,
            )
            for slot, owner in enumerate(owners)
        ]

    def mid_copies(self):
        me, part = self.me, self.part
        far_mid, outer = 3 - me.z, self.outer_of_mid
        far = 3 - outer
        to_mid, to_outer = me.at(z=far_mid), me.at(z=outer)
        return [
            remote(part.at[far], self.inner_in.at[0], self.send.at[0], self.recv.at[3], to_mid),
            remote(part.at[far_mid], self.inner_in.at[1], self.send.at[1], self.recv.at[4], to_mid),
            remote(part.at[outer], self.inner_in.at[0], self.send.at[2], self.recv.at[3], to_outer),
        ]

    def wait_in(self, slot, buffer):
        remote(buffer, buffer, self.send.at[0], self.recv.at[slot], self.me.at(z=3 - self.me.z)).wait_recv()

    def add(self, owner, buffer):
        self.part[owner] = (self.part[owner].astype(F32) + buffer[...].astype(F32)).astype(BF)

    def begin(self):
        @pl.when(self.is_end)
        def _():
            for piece in self.end_copies():
                piece.start()

    def step_one(self):
        @pl.when(self.is_mid)
        def _():
            far = 3 - self.outer_of_mid
            self.wait_in(0, self.outer_in.at[0])
            self.add(far, self.outer_in.at[0])
            self.mid_copies()[0].start()

    def step_two(self):
        @pl.when(self.is_mid)
        def _():
            copies = self.mid_copies()
            self.wait_in(1, self.outer_in.at[1])
            self.add(3 - self.me.z, self.outer_in.at[1])
            copies[1].start()

    def step_three(self):
        @pl.when(self.is_mid)
        def _():
            self.wait_in(3, self.inner_in.at[0])
            self.add(self.outer_of_mid, self.inner_in.at[0])
            self.mid_copies()[2].start()

    def finish(self, total):
        me = self.me

        @pl.when(self.is_mid)
        def _():
            self.wait_in(2, self.outer_in.at[2])
            self.wait_in(4, self.inner_in.at[1])
            total[...] = (
                self.part[me.z].astype(F32)
                + self.outer_in[2].astype(F32)
                + self.inner_in[1].astype(F32)
            )

        @pl.when(self.is_end)
        def _():
            self.wait_in(3, self.inner_in.at[0])
            total[...] = self.part[me.z].astype(F32) + self.inner_in[0].astype(F32)
            for piece in self.end_copies():
                piece.wait_send()

    def drain(self):
        @pl.when(self.is_mid)
        def _():
            for piece in self.mid_copies():
                piece.wait_send()


class LineGather:
    def __init__(self, me, blocks, send, recv):
        self.me, self.blocks, self.send, self.recv = me, blocks, send, recv
        z = me.z
        self.is_mid = (z == 1) | (z == 2)
        self.is_end = (z == 0) | (z == 3)
        self.mid_of_end = 1 + z // 3
        self.outer_of_mid = 3 * (z - 1)

    def copy(self, owner, slot, z):
        ref = self.blocks.at[owner]
        return remote(ref, ref, self.send.at[slot], self.recv.at[owner], self.me.at(z=z))

    def wait_in(self, owner):
        ref = self.blocks.at[owner]
        remote(ref, ref, self.send.at[0], self.recv.at[owner], self.me.at(z=3 - self.me.z)).wait_recv()

    def begin(self):
        me = self.me

        @pl.when(self.is_end)
        def _():
            self.copy(me.z, 0, self.mid_of_end).start()

        @pl.when(self.is_mid)
        def _():
            self.copy(me.z, 0, self.outer_of_mid).start()
            self.copy(me.z, 1, 3 - me.z).start()

    def step_one(self):
        me = self.me

        @pl.when(self.is_mid)
        def _():
            self.wait_in(self.outer_of_mid)
            self.copy(self.outer_of_mid, 2, 3 - me.z).start()

    def step_two(self):
        me = self.me

        @pl.when(self.is_mid)
        def _():
            self.wait_in(3 - me.z)
            self.copy(3 - me.z, 3, self.outer_of_mid).start()

    def step_three(self):
        @pl.when(self.is_mid)
        def _():
            far = 3 - self.outer_of_mid
            self.wait_in(far)
            self.copy(far, 4, self.outer_of_mid).start()

    def finish(self):
        me = self.me

        @pl.when(self.is_mid)
        def _():
            self.copy(me.z, 0, self.outer_of_mid).wait_send()
            self.copy(me.z, 1, 3 - me.z).wait_send()
            self.copy(self.outer_of_mid, 2, 3 - me.z).wait_send()
            self.copy(3 - me.z, 3, self.outer_of_mid).wait_send()
            self.copy(3 - self.outer_of_mid, 4, self.outer_of_mid).wait_send()

        @pl.when(self.is_end)
        def _():
            mid = self.mid_of_end
            self.wait_in(mid)
            self.wait_in(3 - mid)
            self.wait_in(3 - me.z)
            self.copy(me.z, 0, mid).wait_send()


def row_of(gains_ref, which):
    return jnp.concatenate([gains_ref[shard, which : which + 1, :] for shard in range(8)], axis=-1)


def swap_halves(rows):
    lane = lax.broadcasted_iota(jnp.int32, rows.shape, 1)
    return jnp.where(
        lax.rem(lane, HD) < HD // 2, pltpu.roll(rows, 96, 1), pltpu.roll(rows, 32, 1)
    )


class Scatter:
    def __init__(self, me, index, last, width, x_of, y_of, chips, refs):
        self.me, self.index, self.last, self.width = me, index, last, width
        self.x_of, self.y_of, self.chips = x_of, y_of, chips
        self.stage, self.core_in, self.diag_in, self.near_in = refs[:4]
        self.send, self.recv, self.credit = refs[4:]
        self.to_x, self.to_y, self.to_core = me.at(c=me.cx), me.at(c=me.cy), me.at(f=me.of)
        self.sent = []

    def copy(self, slot, src, dst, device):
        return remote(
            src, dst, self.send.at[self.index, slot], self.recv.at[self.index, slot], device
        )

    def lanes(self, ref):
        return ref.at[:, pl.ds(0, self.width)]

    def core_copy(self, role):
        return self.copy(
            role, self.stage(self.width, role), self.lanes(self.core_in.at[role]), self.to_core
        )

    def chunk(self, core, role):
        c = self.me.c
        high = lax.rem(c // 2 + role // 2, 2)
        low = lax.rem(lax.rem(c, 2) + lax.rem(role, 2), 2)
        return dotg(self.x_of(core * 4 + 2 * high + low), self.y_of(), 0, 0)

    def roles(self, body):
        def pair(step, carry):
            body(3 - step)
            body(1 - step)
            return carry

        lax.fori_loop(0, 2, pair, 0)

    def partner(self):
        def body(role):
            self.stage(self.width, role)[...] = self.chunk(self.me.of, role).astype(BF)
            if self.index > 0:
                pl.semaphore_wait(self.credit.at[role], 1)
            self.core_copy(role).start()

        self.roles(body)

    def own(self):
        def body(role):
            value = self.chunk(self.me.f, role)
            self.core_copy(role).wait_recv()
            chip = self.chips(role)
            chip[...] = (value + self.lanes(self.core_in.at[role])[...].astype(F32)).astype(BF)
            if not self.last:
                pl.semaphore_signal(
                    self.credit.at[role], inc=1, device_id=self.to_core, device_id_type=MESH
                )

        self.roles(body)
        for role in range(4):
            self.core_copy(role).wait_send()

    def near(self, role, half, slot):
        rows = pl.ds(half * 128, 128)
        side = role - 1
        device = self.to_x if role == 1 else self.to_y
        return self.copy(
            slot, self.chips(role).at[rows, :], self.near_in.at[side, rows, :], device
        )

    def diag(self, half):
        device = self.to_x if half == 0 else self.to_y
        return self.copy(
            4 + half,
            self.chips(3).at[pl.ds(half * 128, 128), :],
            self.lanes(self.diag_in.at[half]),
            device,
        )

    def push_diag(self):
        self.diag(0).start()
        self.diag(1).start()

    def push_near(self):
        self.near(1, 0, 6).start()
        self.near(2, 1, 7).start()

    def relay_a(self):
        first = pl.ds(0, 128)
        self.diag(0).wait_recv()
        rows = self.chips(2).at[first, :]
        rows[...] = (
            rows[...].astype(F32) + self.lanes(self.diag_in.at[0])[...].astype(F32)
        ).astype(BF)
        self.near(2, 0, 8).start()

    def relay_b(self):
        second = pl.ds(128, 128)
        self.diag(1).wait_recv()
        rows = self.chips(1).at[second, :]
        rows[...] = (
            rows[...].astype(F32) + self.lanes(self.diag_in.at[1])[...].astype(F32)
        ).astype(BF)
        self.near(1, 1, 9).start()

    def collect(self, buffer, sem):
        for role, half, slot in ((1, 0, 6), (2, 1, 7), (2, 0, 8), (1, 1, 9)):
            self.near(role, half, slot).wait_recv()
        for side in range(2):
            pltpu.make_async_copy(
                self.near_in.at[side], self.lanes(buffer.at[side]), sem.at[side]
            ).start()

    def collected(self, buffer, sem):
        for side in range(2):
            pltpu.make_async_copy(
                self.near_in.at[side], self.lanes(buffer.at[side]), sem.at[side]
            ).wait()

    def settle(self):
        for half in range(2):
            self.diag(half).wait_send()
        for role, half, slot in ((1, 0, 6), (2, 1, 7), (2, 0, 8), (1, 1, 9)):
            self.near(role, half, slot).wait_send()


def norm_back(gradient, rows_in, gain):
    inv = lax.rsqrt(jnp.mean(rows_in * rows_in, axis=-1, keepdims=True) + EPSILON)
    unit = rows_in * inv
    scaled = gradient * gain
    back = inv * (scaled - unit * jnp.mean(scaled * unit, axis=-1, keepdims=True))
    return back, jnp.sum(gradient * unit, axis=0, keepdims=True)


def layer_kernel(
    tok_h,
    gain_one_in,
    gain_two_in,
    w_query_in,
    w_key_in,
    w_value_in,
    out_h,
    gate_h,
    up_h,
    down_h,
    cot_h,
    pos_in,
    seg_in,
    freq,
    o_result,
    o_input,
    o_gain_one,
    o_gain_two,
    o_query,
    o_key,
    o_value,
    o_out,
    o_gate,
    o_up,
    o_down,
    near_down,
    near_gate,
    near_up,
    near_out,
    near_qkv,
    n_one_h,
    own_gains,
    own_marks,
    gains,
    marks,
    tok,
    w_gate,
    w_up,
    w_down,
    w_out,
    w_qkv,
    cot,
    n_two,
    hid,
    gate_g,
    up_g,
    core_in,
    diag_in,
    diag_low,
    chip_out,
    chip_qkv,
    sum_stage,
    turn_stage,
    part,
    outer_in,
    inner_in,
    outer_two,
    inner_two,
    mlow,
    total,
    own_out,
    mid,
    mid_g,
    q_rot,
    bias,
    lse,
    kv,
    att,
    rope,
    do_rows,
    keys,
    vals_t,
    vals,
    keys_t,
    key_acc,
    val_acc,
    kv_send_buf,
    kv_in,
    d_qkv,
    vec,
    vec_in,
    vec_out,
    vec_near,
    g_send,
    g_recv,
    g_local,
    small_send,
    small_recv,
    first_send,
    first_recv,
    load_sem,
    sum_send,
    sum_recv,
    all_send,
    all_recv,
    rs_send,
    rs_recv,
    credit,
    kv_send,
    kv_recv,
    vec_send,
    vec_recv,
    fin_sem,
    put_sem,
    own_sem,
):
    me = Place()
    group = group_devices(me)
    hidden = hid.shape[1]

    rows_of = [pl.ds(g * 256, 256) for g in range(2)]
    load_tok = pltpu.make_async_copy(tok_h, tok, load_sem.at[0])
    load_cot = pltpu.make_async_copy(cot_h, cot, load_sem.at[1])
    save_one = pltpu.make_async_copy(mlow, n_one_h, load_sem.at[2])
    load_one = pltpu.make_async_copy(n_one_h, mlow, load_sem.at[3])
    load_tok.start()
    load_cot.start()
    barrier = pltpu.get_barrier_semaphore()
    for device in group + column_devices(me):
        pl.semaphore_signal(barrier, inc=1, device_id=device, device_id_type=MESH)

    w_qkv[me.own, :, 0:512] = w_query_in[...]
    turned = jnp.concatenate([w_key_in[...], w_value_in[...]], axis=0).astype(F32)
    w_qkv[me.own, :, 512:640] = jnp.transpose(turned).astype(BF)
    own_gains[0:1, :] = gain_one_in[...].reshape(1, 256).astype(F32)
    own_gains[1:2, :] = gain_two_in[...].reshape(1, 256).astype(F32)
    own_gains[2:8, :] = jnp.zeros((6, 256), F32)
    own_marks[0:1, :] = pos_in[...]
    own_marks[1:2, :] = seg_in[...]
    own_marks[2:8, :] = jnp.zeros((6, 512), jnp.int32)
    pl.semaphore_wait(barrier, 10)

    qkv = Gather(me, 0, None, w_qkv, g_send, g_recv, g_local)
    out = Gather(me, 1, out_h, w_out, g_send, g_recv, g_local)
    gate = Gather(me, 2, gate_h, w_gate, g_send, g_recv, g_local)
    up = Gather(me, 3, up_h, w_up, g_send, g_recv, g_local)
    down = Gather(me, 4, down_h, w_down, g_send, g_recv, g_local)

    sources = [me.sx, me.sy, me.sd, me.of * 4 + me.c, me.of * 4 + me.cx, me.of * 4 + me.cy, me.of * 4 + me.cd]

    def small_copies(gain_slots, mark_slots):
        return [
            remote(own_gains, gains.at[spot], small_send.at[slot], small_recv.at[slot], group[slot])
            for slot, spot in enumerate(gain_slots)
        ] + [
            remote(
                own_marks, marks.at[spot], small_send.at[7 + slot], small_recv.at[7 + slot], group[slot]
            )
            for slot, spot in enumerate(mark_slots)
        ]

    small = small_copies([me.own] * 7, [me.c] * 3)

    def small_begin():
        for piece in small:
            piece.start()
        gains[me.own] = own_gains[...]
        marks[me.c] = own_marks[...]

    def small_finish():
        for piece in small_copies(sources, (me.cx, me.cy, me.cd)):
            piece.wait_recv()

    def first_norm():
        load_tok.wait()
        gain_one = row_of(gains, 0)

        def body(step, carry):
            values = tok[pl.ds(pl.multiple_of(step * 64, 64), 64), :].astype(F32)
            inv = lax.rsqrt(jnp.mean(values * values, axis=-1, keepdims=True) + EPSILON)
            mlow[step // 4, lax.rem(step, 4)] = (values * inv * gain_one).astype(BF)
            return carry

        lax.fori_loop(0, 8, body, 0)
        save_one.start()

    def make_rope():
        lane = lax.broadcasted_iota(jnp.int32, (128, 128), 1)
        low_half = lax.rem(lane, HD) < HD // 2
        for step in range(4):
            rows = slice(step * 128, (step + 1) * 128)
            places = own_marks[0:1, rows].astype(F32)
            angles = jnp.transpose(jnp.broadcast_to(places, (128, 128))) * freq[...]
            sine = jnp.sin(angles)
            rope[rows, :128] = jnp.cos(angles)
            rope[rows, 128:] = jnp.where(low_half, -sine, sine)

    def make_bias(g):
        own_rows = own_marks[:, g * 256 : (g + 1) * 256].astype(F32)
        for source in range(4):
            key_rows = marks[source, :, g * 256 : (g + 1) * 256].astype(F32)
            key_pos = jnp.transpose(jnp.broadcast_to(key_rows[0:1, :], (128, 256)))
            key_seg = jnp.transpose(jnp.broadcast_to(key_rows[1:2, :], (128, 256)))
            for side in range(2):
                lanes = slice(side * 128, (side + 1) * 128)
                seen = (key_seg == own_rows[1:2, lanes]) & (key_pos <= own_rows[0:1, lanes])
                bias[g, source * 256 : (source + 1) * 256, lanes] = jnp.where(
                    seen, 0.0, MASKED_SCORE
                ).astype(BF)

    lane_pair = lax.broadcasted_iota(jnp.int32, (256, 128), 1)

    def project_in(first, width):
        total_rows = None
        for shard in range(8):
            term = dotg(
                mlow[:, :, :, shard * 256 : (shard + 1) * 256].reshape(512, 256),
                w_qkv[shard, :, first : first + width],
                1,
                0,
            )
            total_rows = term if total_rows is None else total_rows + term
        return total_rows

    def first_copies(places):
        return [
            remote(kv.at[place], kv.at[place], first_send.at[slot], first_recv.at[slot], group[slot])
            for slot, place in enumerate(places)
        ]

    def project_kv():
        rows = project_in(512, 128)
        is_key = lax.broadcasted_iota(jnp.int32, (512, 128), 1) < HD
        cos_rows = jnp.where(is_key, rope[:, :128], 1.0)
        sin_rows = jnp.where(is_key, rope[:, 128:], 0.0)
        kv[me.c] = (rows * cos_rows + swap_halves(rows) * sin_rows).astype(BF)
        for piece in first_copies([me.c] * 3):
            piece.start()

    def project_q(half):
        rows_all = project_in(half * 256, 256)
        for inner in range(2):
            pair = half * 2 + inner
            rows = rows_all[:, inner * 128 : (inner + 1) * 128]
            rot = (rows * rope[:, :128] + swap_halves(rows) * rope[:, 128:]).astype(BF)
            rot = rot * jnp.bfloat16(HD ** (-0.5))
            q_rot[:, pair * 128 : (pair + 1) * 128] = rot

    def kv_arrive():
        for piece in first_copies((me.cx, me.cy, me.cd)):
            piece.wait_recv()
        for g in range(2):
            for source in range(4):
                pairs = kv[source, g * 256 : (g + 1) * 256, :].astype(F32)
                rows = slice(source * 256, (source + 1) * 256)
                keys[g, rows, :] = jnp.where(
                    lane_pair < HD, pairs, pltpu.roll(pairs, HD, 1)
                ).astype(BF)
                vals_t[g, :, rows] = jnp.transpose(pairs)[HD:, :].astype(BF)

    def one_head(pair_rows, odd):
        kept = lane_pair >= HD if odd else lane_pair < HD
        return jnp.where(kept, pair_rows, jnp.zeros_like(pair_rows))

    def attend(step):
        g = step // 4
        pair = step - g * 4
        halves = []
        own = pl.ds(pl.multiple_of(g * 256, 256), 256)
        lanes = pl.ds(pl.multiple_of(pair * 128, 128), 128)
        queries = q_rot[own, lanes]
        for odd in range(2):
            head = step * 2 + odd
            scores = dotg(keys[g], one_head(queries, odd), 1, 1) + bias[g].astype(F32)
            top = jnp.max(scores, axis=0, keepdims=True)
            weights = jnp.exp(scores - top)
            norm = jnp.sum(weights, axis=0, keepdims=True)
            mixed = dotg(vals_t[g], weights.astype(BF), 1, 0)
            halves.append(mixed / norm)
            lse[head] = top + jnp.log(norm)
        rows = jnp.transpose(jnp.concatenate(halves, axis=0))
        att[own, lanes] = rows.astype(BF)

    def project_out(g):
        def body(shard, carry):
            part[g, :, :, pl.ds(pl.multiple_of(shard * 256, 256), 256)] = (
                dotg(att[rows_of[g], :], w_out[shard], 1, 0).astype(BF).reshape(4, 64, 256)
            )
            return carry

        lax.fori_loop(0, 8, body, 0)

    def second_norm(g):
        sum_att[g].finish(total)
        own = pl.ds(pl.multiple_of(g * 256 + me.z * 64, 64), 64)
        mid_rows = tok[own, :].astype(F32) + total[...]
        mid[g] = mid_rows
        inv = lax.rsqrt(jnp.mean(mid_rows * mid_rows, axis=-1, keepdims=True) + EPSILON)
        n_two[g, me.z] = (mid_rows * inv * row_of(gains, 1)).astype(BF)
        spread_two[g].begin()

    def looped(body, count, hooks):
        def step(i, carry):
            for spot, actions in hooks:

                @pl.when(i == spot)
                def _():
                    for action, *values in actions:
                        action(*values)

            body(i)
            return carry

        lax.fori_loop(0, count, step, 0)

    tile_count = (hidden + 255) // 256

    def feed(step):
        g = step // tile_count
        n = step - g * tile_count
        rows = pl.ds(pl.multiple_of(g * 256, 256), 256)
        lanes = pl.ds(pl.multiple_of(jnp.minimum(n * 256, hidden - 256), 128), 256)
        normed = n_two[g].reshape(256, 2048)
        gate = dotg(normed, w_gate[:, :, lanes].reshape(2048, 256), 1, 0)
        up = dotg(normed, w_up[:, :, lanes].reshape(2048, 256), 1, 0)
        hidden_grad = None
        for shard in range(8):
            term = dotg(
                cot[rows, shard * 256 : (shard + 1) * 256], w_down[shard, lanes, :], 1, 1
            )
            hidden_grad = term if hidden_grad is None else hidden_grad + term
        sig = jax.nn.sigmoid(gate)
        silu = gate * sig
        hid[rows, lanes] = (silu * up).astype(BF)
        up_g[rows, lanes] = (hidden_grad * silu).astype(BF)
        gate_g[rows, lanes] = (
            hidden_grad * up * sig * (1.0 + gate * (1.0 - sig))
        ).astype(BF)

    def feed_back(g):
        sum_att[g].drain()

        def body(shard, carry):
            term = dotg(gate_g[rows_of[g], :], w_gate[shard], 1, 1) + dotg(
                up_g[rows_of[g], :], w_up[shard], 1, 1
            )
            part[g, :, :, pl.ds(pl.multiple_of(shard * 256, 256), 256)] = term.astype(BF).reshape(
                4, 64, 256
            )
            return carry

        lax.fori_loop(0, 8, body, 0)

    part_two = n_two

    def feed_out(g):
        def body(shard, carry):
            term = dotg(hid[rows_of[g], :], w_down[shard], 1, 0)
            part_two[g, :, :, pl.ds(pl.multiple_of(shard * 256, 256), 256)] = term.astype(
                BF
            ).reshape(4, 64, 256)
            return carry

        lax.fori_loop(0, 8, body, 0)

    def line_sum(slot, part_ref, outer, inner):
        return LineSum(me, part_ref, outer, inner, sum_send.at[slot], sum_recv.at[slot])

    sum_two = [line_sum(g, part.at[g], outer_in.at[g], inner_in.at[g]) for g in range(2)]
    sum_one = [line_sum(2 + g, part.at[g], outer_in.at[g], inner_in.at[g]) for g in range(2)]

    sum_out = [
        line_sum(4 + g, part_two.at[g], outer_two.at[g], inner_two.at[g]) for g in range(2)
    ]
    sum_att = [line_sum(6 + g, part.at[g], outer_in.at[g], inner_in.at[g]) for g in range(2)]
    spread_two = [LineGather(me, n_two.at[g], all_send.at[6 + g], all_recv.at[6 + g]) for g in range(2)]
    spread_mid = [LineGather(me, mlow.at[g], all_send.at[g], all_recv.at[g]) for g in range(2)]
    spread_in = [LineGather(me, o_input.at[g], all_send.at[2 + g], all_recv.at[2 + g]) for g in range(2)]
    spread_out = [LineGather(me, o_result.at[g], all_send.at[4 + g], all_recv.at[4 + g]) for g in range(2)]

    def middle_back(g):
        sum_two[g].finish(total)
        own = pl.ds(pl.multiple_of(g * 256 + me.z * 64, 64), 64)
        back, gain_grad = norm_back(total[...], mid[g], row_of(gains, 1))
        if g == 0:
            vec[1:2, :] = gain_grad
        else:
            vec[1:2, :] += gain_grad
        grad = cot[own, :].astype(F32) + back
        mid_g[g] = grad
        mlow[g, me.z] = grad.astype(BF)
        spread_mid[g].begin()

    def put_own(g, ref, slot):
        copy = pltpu.make_async_copy(own_out, ref.at[g, me.z], own_sem.at[slot])
        copy.start()
        copy.wait()

    def input_back(g):
        sum_one[g].finish(total)
        own = pl.ds(pl.multiple_of(g * 256 + me.z * 64, 64), 64)
        back, gain_grad = norm_back(total[...], tok[own, :].astype(F32), row_of(gains, 0))
        if g == 0:
            vec[0:1, :] = gain_grad
        else:
            vec[0:1, :] += gain_grad
        own_out[...] = (mid_g[g] + back).astype(BF)
        put_own(g, o_input, 0)
        spread_in[g].begin()

    def result_rows(g):
        sum_out[g].finish(total)
        own_out[...] = (mid[g] + total[...]).astype(BF)
        put_own(g, o_result, 1)
        spread_out[g].begin()

    wide = lambda ref: (lambda shard: ref[:, pl.ds(pl.multiple_of(shard * 256, 256), 256)])

    def blocks_of(ref):
        return lambda shard: ref[
            :, :, :, pl.ds(pl.multiple_of(shard * 256, 256), 256)
        ].reshape(512, 256)

    def stage(width, slot):
        if width > 640:
            return w_up.at[4 + slot]
        first = lax.rem(slot, 2) * 640
        if not isinstance(slot, int):
            first = pl.multiple_of(first, 128)
        return w_up.at[4 + slot // 2, :, pl.ds(first, width)]

    landing = w_up.at[pl.ds(6, 2)]

    def scatter(index, width, x_of, y_of, chips, near):
        landed = diag_in.at[index] if index < 3 else diag_low.at[index - 3]
        refs = (stage, core_in, landed, near, rs_send, rs_recv, credit)
        return Scatter(me, index, index == 4, width, x_of, y_of, chips, refs)

    rs_down = scatter(
        0, hidden, wide(cot), lambda: hid[...], lambda role: w_gate.at[4 + role], near_down
    )
    rs_gate = scatter(
        1, hidden, blocks_of(n_two), lambda: gate_g[...], lambda role: w_gate.at[role], near_gate
    )
    rs_up = scatter(
        2, hidden, blocks_of(n_two), lambda: up_g[...], lambda role: w_up.at[role], near_up
    )
    rs_out = scatter(3, 512, blocks_of(mlow), lambda: att[...], lambda role: chip_out.at[role], near_out)
    rs_qkv = scatter(
        4,
        640,
        blocks_of(mlow),
        lambda: d_qkv[...],
        lambda role: chip_qkv.at[role],
        near_qkv,
    )

    def finish_rows(job, outs):
        job.collected(landing, fin_sem)
        width = job.width
        pending = [None, None]
        for step in range(4):
            slot = step % 2
            rows = slice(step * 64, (step + 1) * 64)
            if pending[slot] is not None:
                for piece in pending[slot]:
                    piece.wait()
            sum_stage[slot, :, :width] = (
                job.chips(0)[rows, :].astype(F32)
                + landing[0, rows, :width].astype(F32)
                + landing[1, rows, :width].astype(F32)
            )
            pending[slot] = [
                pltpu.make_async_copy(
                    sum_stage.at[slot, :, pl.ds(first, size)],
                    ref.at[pl.ds(step * 64, 64), :],
                    put_sem.at[slot, number],
                )
                for number, (ref, first, size) in enumerate(outs)
            ]
            for piece in pending[slot]:
                piece.start()
        for slot in range(2):
            for piece in pending[slot]:
                piece.wait()

    def finish_qkv(job):
        finish_rows(job, [(o_query, 0, 512)])
        lanes = slice(512, 640)
        turn_stage[0] = jnp.transpose(
            job.chips(0)[:, lanes].astype(F32)
            + landing[0, :, lanes].astype(F32)
            + landing[1, :, lanes].astype(F32)
        )
        copies = [
            pltpu.make_async_copy(
                turn_stage.at[0, pl.ds(first, HD), :], ref, put_sem.at[0, number]
            )
            for number, (first, ref) in enumerate(((0, o_key), (HD, o_value)))
        ]
        for piece in copies:
            piece.start()
        for piece in copies:
            piece.wait()

    def finish_turned(job, ref):
        job.collected(landing, fin_sem)

        def put(step, slot):
            rows = pl.ds(pl.multiple_of(step * 128, 128), 128)
            return pltpu.make_async_copy(turn_stage.at[slot], ref.at[rows, :], put_sem.at[slot, 0])

        def body(step, carry):
            slot = lax.rem(step, 2)
            lanes = pl.ds(pl.multiple_of(step * 128, 128), 128)

            @pl.when(step >= 2)
            def _():
                put(step, slot).wait()

            turn_stage[slot] = jnp.transpose(
                job.chips(0)[:, lanes].astype(F32)
                + landing[0, :, lanes].astype(F32)
                + landing[1, :, lanes].astype(F32)
            )
            put(step, slot).start()
            return carry

        lax.fori_loop(0, job.width // 128, body, 0)
        for slot in range(2):
            put(slot, slot).wait()

    def out_back(g):
        grad = None
        for shard in range(8):
            lanes = slice(shard * 256, (shard + 1) * 256)
            term = dotg(mlow[g, :, :, lanes].reshape(256, 256), w_out[shard], 1, 1)
            grad = term if grad is None else grad + term
        do_rows[...] = grad.astype(BF)
        for source in range(4):
            pairs = kv[source, rows_of[g], :].astype(F32)
            turned = pltpu.roll(pairs, HD, 1)
            rows = slice(source * 256, (source + 1) * 256)
            vals[rows, :] = jnp.where(lane_pair < HD, turned, pairs).astype(BF)
            keys_t[:, rows] = jnp.transpose(pairs)[:HD, :].astype(BF)
        key_acc[...] = jnp.zeros_like(key_acc)
        val_acc[...] = jnp.zeros_like(val_acc)

    def attend_back(step):
        g = step // 4
        pair = step - g * 4
        own = pl.ds(pl.multiple_of(g * 256, 256), 256)
        halves = []
        lanes = pl.ds(pl.multiple_of(pair * 128, 128), 128)
        queries, grads = q_rot[own, lanes], do_rows[:, lanes]
        for odd in range(2):
            query, grad = one_head(queries, odd), one_head(grads, odd)
            scores = dotg(keys[g], query, 1, 1) + bias[g].astype(F32)
            probs = jnp.exp(scores - lse[step * 2 + odd])
            prob_grad = dotg(vals[...], grad, 1, 1)
            delta = jnp.sum(probs * prob_grad, axis=0, keepdims=True)
            score_grad = (probs * (prob_grad - delta)).astype(BF)
            val_acc[...] += dotg(probs.astype(BF), grad, 1, 0)
            key_acc[...] += dotg(score_grad, query, 1, 0)
            halves.append(dotg(keys_t[...], score_grad, 1, 0))
        rows = jnp.transpose(jnp.concatenate(halves, axis=0)) * (HD ** (-0.5))
        rows = rows * rope[own, :128] - swap_halves(rows) * rope[own, 128:]
        d_qkv[own, lanes] = rows.astype(BF)

    def kv_copies(g):
        return [
            remote(
                kv_send_buf.at[g, column],
                kv_in.at[g, slot],
                kv_send.at[g, slot],
                kv_recv.at[g, slot],
                group[slot],
            )
            for slot, column in enumerate((me.cx, me.cy, me.cd))
        ]

    def kv_begin(g):
        for block in range(4):
            rows = slice(block * 256, (block + 1) * 256)
            key_rows, val_rows = key_acc[rows, :], val_acc[rows, :]
            joined = jnp.where(
                lane_pair < HD,
                key_rows + pltpu.roll(key_rows, HD, 1),
                val_rows + pltpu.roll(val_rows, HD, 1),
            )
            kv_send_buf[g, block] = joined.astype(BF)
        for piece in kv_copies(g):
            piece.start()

    def kv_finish(g):
        rows = kv_send_buf[g, me.c].astype(F32)
        for slot, piece in enumerate(kv_copies(g)):
            piece.wait_recv()
            rows = rows + kv_in[g, slot].astype(F32)
        cos_rows = jnp.where(lane_pair < HD, rope[rows_of[g], :128], 1.0)
        sin_rows = jnp.where(lane_pair < HD, rope[rows_of[g], 128:], 0.0)
        rows = rows * cos_rows - swap_halves(rows) * sin_rows
        d_qkv[rows_of[g], 512:640] = rows.astype(BF)

    def project_back_rows(g):
        sum_two[g].drain()

        def body(shard, carry):
            term = dotg(d_qkv[rows_of[g], :], w_qkv[shard], 1, 1)
            part[g, :, :, pl.ds(pl.multiple_of(shard * 256, 256), 256)] = term.astype(BF).reshape(
                4, 64, 256
            )
            return carry

        lax.fori_loop(0, 8, body, 0)

    line = column_devices(me)

    def vec_line():
        return [
            remote(vec_out, vec_in.at[slot], vec_send.at[slot], vec_recv.at[slot], device)
            for slot, device in enumerate(line)
        ]

    targets = [me.sx, me.sy, me.sd, me.of * 4 + me.c, me.of * 4 + me.cx, me.of * 4 + me.cy, me.of * 4 + me.cd]

    def vec_group():
        return [
            remote(
                vec_in.at[3, target],
                vec_near.at[slot],
                vec_send.at[3 + slot],
                vec_recv.at[3 + slot],
                device,
            )
            for slot, (target, device) in enumerate(zip(targets, group))
        ]

    def vec_begin():
        for shard in range(8):
            for which in range(2):
                for half in range(2):
                    first = shard * 256 + half * 128
                    vec_out[shard, 2 * which + half : 2 * which + half + 1, :] = vec[
                        which : which + 1, first : first + 128
                    ]
            vec_out[shard, 4:8, :] = jnp.zeros((4, 128), F32)
        for piece in vec_line():
            piece.start()

    def vec_middle():
        for piece in vec_line():
            piece.wait_recv()
        vec_in[3] = vec_out[...] + vec_in[0] + vec_in[1] + vec_in[2]
        for piece in vec_group():
            piece.start()

    def vec_finish():
        rows = vec_in[3, me.own]
        for slot, piece in enumerate(vec_group()):
            piece.wait_recv()
            rows = rows + vec_near[slot]
        o_gain_one[...] = rows[0:2, :]
        o_gain_two[...] = rows[2:4, :]

    def settle_weights():
        for piece in (qkv, out, gate, up, down):
            piece.settle()

    def settle():
        for job in sum_one + sum_out:
            job.drain()
        for spread in spread_in + spread_out:
            spread.finish()
        for job in (rs_down, rs_gate, rs_up, rs_out, rs_qkv):
            job.settle()
        for g in range(2):
            for piece in kv_copies(g):
                piece.wait_send()
        for piece in vec_line() + vec_group() + small + first_copies([me.c] * 3):
            piece.wait_send()

    order = (
        (qkv.begin,),
        (small_begin,),
        (make_rope,),
        (qkv.forward_a,),
        (qkv.forward_b,),
        (small_finish,),
        (first_norm,),
        (out.begin,),
        (qkv.diagonal_a,),
        (qkv.diagonal_b,),
        (qkv.arrive,),
        (project_kv,),
        (project_q, 0),
        (out.forward_a,),
        (make_bias, 0),
        (out.forward_b,),
        (project_q, 1),
        (save_one.wait,),
        (up.begin,),
        (kv_arrive,),
        (make_bias, 1),
        (down.begin,),
        (
            looped,
            attend,
            8,
            (
                (2, ((out.diagonal_a,), (out.diagonal_b,),)),
                (4, ((out.arrive,),)),
                (6, ((project_out, 0), (sum_att[0].begin,), (sum_att[0].step_one,),)),
            ),
        ),
        (project_out, 1),
        (load_cot.wait,),
        (gate.begin,),
        (sum_att[1].begin,),
        (sum_att[0].step_two,),
        (sum_att[0].step_three,),
        (second_norm, 0),
        (down.forward_a,),
        (down.forward_b,),
        (up.forward_a,),
        (sum_att[1].step_one,),
        (sum_att[1].step_two,),
        (spread_two[0].step_two,),
        (sum_att[1].step_three,),
        (second_norm, 1),
        (up.forward_b,),
        (down.diagonal_a,),
        (down.diagonal_b,),
        (spread_two[0].step_one,),
        (down.arrive,),
        (up.diagonal_a,),
        (gate.forward_a,),
        (spread_two[1].step_one,),
        (gate.forward_b,),
        (spread_two[0].step_three,),
        (up.diagonal_b,),
        (up.arrive,),
        (gate.diagonal_a,),
        (spread_two[1].step_two,),
        (gate.diagonal_b,),
        (spread_two[0].finish,),
        (gate.arrive,),
        (settle_weights,),
        (
            looped,
            feed,
            2 * tile_count,
            (
                (3, ((spread_two[1].step_three,),)),
                (6, ((feed_back, 0), (sum_two[0].begin,), (spread_two[1].finish,),)),
            ),
        ),
        (feed_back, 1),
        (sum_two[0].step_one,),
        (sum_two[0].step_two,),
        (sum_two[1].begin,),
        (rs_down.partner,),
        (sum_two[0].step_three,),
        (rs_down.own,),
        (rs_gate.partner,),
        (sum_two[1].step_one,),
        (middle_back, 0),
        (rs_gate.own,),
        (rs_up.partner,),
        (sum_two[1].step_three,),
        (sum_two[1].step_two,),
        (rs_up.own,),
        (spread_mid[0].step_one,),
        (spread_mid[0].step_two,),
        (rs_up.push_near,),
        (middle_back, 1),
        (rs_down.push_near,),
        (feed_out, 1),
        (spread_mid[1].step_one,),
        (rs_gate.push_near,),
        (feed_out, 0),
        (spread_mid[0].step_three,),
        (sum_out[1].begin,),
        (sum_out[1].step_one,),
        (sum_out[0].begin,),
        (spread_mid[0].finish,),
        (out_back, 0),
        (rs_gate.push_diag,),
        (spread_mid[1].step_two,),
        (
            looped,
            attend_back,
            8,
            (
                (4, ((spread_mid[1].step_three,), (spread_mid[1].finish,), (kv_begin, 0), (sum_out[1].step_two,), (out_back, 1),)),
                (6, ((sum_out[1].step_three,), (rs_out.partner,), (sum_out[0].step_one,), (result_rows, 1), (rs_down.push_diag,),)),
            ),
        ),
        (kv_begin, 1),
        (rs_up.push_diag,),
        (kv_finish, 0),
        (project_back_rows, 0),
        (sum_out[0].step_three,),
        (sum_out[0].step_two,),
        (spread_out[1].step_two,),
        (sum_one[0].begin,),
        (rs_out.own,),
        (rs_out.push_diag,),
        (spread_out[1].step_one,),
        (kv_finish, 1),
        (project_back_rows, 1),
        (sum_one[1].begin,),
        (rs_gate.relay_a,),
        (result_rows, 0),
        (load_one.start,),
        (sum_one[0].step_one,),
        (spread_out[1].step_three,),
        (load_one.wait,),
        (rs_down.relay_a,),
        (sum_one[0].step_two,),
        (rs_qkv.partner,),
        (spread_out[0].step_two,),
        (sum_one[0].step_three,),
        (rs_out.relay_a,),
        (rs_up.relay_a,),
        (rs_up.relay_b,),
        (rs_down.relay_b,),
        (sum_one[1].step_one,),
        (rs_qkv.own,),
        (input_back, 0),
        (sum_one[1].step_two,),
        (sum_one[1].step_three,),
        (rs_qkv.push_diag,),
        (spread_in[0].step_two,),
        (spread_out[0].step_one,),
        (rs_gate.relay_b,),
        (input_back, 1),
        (rs_out.push_near,),
        (spread_in[0].step_one,),
        (rs_qkv.push_near,),
        (vec_begin,),
        (rs_down.collect, landing, fin_sem),
        (finish_turned, rs_down, o_down),
        (spread_out[0].step_three,),
        (rs_qkv.relay_a,),
        (spread_in[1].step_one,),
        (spread_in[1].step_two,),
        (rs_out.relay_b,),
        (rs_gate.collect, landing, fin_sem),
        (finish_rows, rs_gate, [(o_gate, 0, hidden)]),
        (rs_up.collect, landing, fin_sem),
        (finish_rows, rs_up, [(o_up, 0, hidden)]),
        (spread_in[0].step_three,),
        (rs_out.collect, landing, fin_sem),
        (finish_turned, rs_out, o_out),
        (rs_qkv.relay_b,),
        (spread_in[1].step_three,),
        (vec_middle,),
        (vec_finish,),
        (rs_qkv.collect, landing, fin_sem),
        (finish_qkv, rs_qkv),
        (settle,),
    )
    for action, *values in order:
        action(*values)


def run_layer(
    tokens, attn_gain, w_query, w_key, w_value, w_out, mlp_gain, w_gate, w_up, w_down, cotangent,
    positions, segments,
):
    shape = jax.ShapeDtypeStruct
    width = tokens.shape[1]
    hidden = w_gate.shape[1]
    vmem = pl.BlockSpec(memory_space=pltpu.VMEM)
    anywhere = pl.BlockSpec(memory_space=pl.ANY)
    dma = pltpu.SemaphoreType.DMA
    buffer = pltpu.VMEM
    half_size = HD // 2
    frequency = THETA_BASE ** (-np.arange(half_size, dtype=np.float32) / half_size)
    frequency = np.concatenate([frequency] * 4)[None, :].astype(np.float32)
    return pl.pallas_call(
        layer_kernel,
        name="decoder_layer",
        out_shape=(
            shape((2, 4, 64, width), BF),
            shape((2, 4, 64, width), BF),
            shape((2, 128), F32),
            shape((2, 128), F32),
            shape((256, 512), F32),
            shape((HD, 256), F32),
            shape((HD, 256), F32),
            shape((512, 256), F32),
            shape((256, hidden), F32),
            shape((256, hidden), F32),
            shape((hidden, 256), F32),
            shape((2, 256, hidden), BF),
            shape((2, 256, hidden), BF),
            shape((2, 256, hidden), BF),
            shape((2, 256, 512), BF),
            shape((2, 256, 640), BF),
            shape((2, 4, 64, width), BF),
        ),
        in_specs=[anywhere, vmem, vmem, vmem, vmem, vmem]
        + [anywhere] * 5
        + [vmem] * 3,
        out_specs=(anywhere,) * 2 + (vmem,) * 2 + (anywhere,) * 13,
        scratch_shapes=[
            buffer((8, 256), F32),
            buffer((8, 512), jnp.int32),
            buffer((8, 8, 256), F32),
            buffer((4, 8, 512), jnp.int32),
            buffer((512, width), BF),
            buffer((8, 256, hidden), BF),
            buffer((8, 256, hidden), BF),
            buffer((8, hidden, 256), BF),
            buffer((8, 512, 256), BF),
            buffer((8, 256, 640), BF),
            buffer((512, width), BF),
            buffer((2, 4, 64, width), BF),
            buffer((512, hidden), BF),
            buffer((512, hidden), BF),
            buffer((512, hidden), BF),
            buffer((4, 256, hidden), BF),
            buffer((3, 2, 128, hidden), BF),
            buffer((2, 2, 128, 640), BF),
            buffer((4, 256, 512), BF),
            buffer((4, 256, 640), BF),
            buffer((2, 64, hidden), F32),
            buffer((2, 128, 256), F32),
            buffer((2, 4, 64, width), BF),
            buffer((2, 3, 64, width), BF),
            buffer((2, 2, 64, width), BF),
            buffer((2, 3, 64, width), BF),
            buffer((2, 2, 64, width), BF),
            buffer((2, 4, 64, width), BF),
            buffer((64, width), F32),
            buffer((64, width), BF),
            buffer((2, 64, width), F32),
            buffer((2, 64, width), F32),
            buffer((512, 512), BF),
            buffer((2, 1024, 256), BF),
            buffer((16, 1, 256), F32),
            buffer((4, 512, 128), BF),
            buffer((512, 512), BF),
            buffer((512, 256), F32),
            buffer((256, 512), BF),
            buffer((2, 1024, 128), BF),
            buffer((2, HD, 1024), BF),
            buffer((1024, 128), BF),
            buffer((HD, 1024), BF),
            buffer((1024, 128), F32),
            buffer((1024, 128), F32),
            buffer((2, 4, 256, 128), BF),
            buffer((2, 3, 256, 128), BF),
            buffer((512, 640), BF),
            buffer((2, width), F32),
            buffer((4, 8, 8, 128), F32),
            buffer((8, 8, 128), F32),
            buffer((7, 8, 128), F32),
            dma((5, 9)),
            dma((5, 9)),
            dma((5,)),
            dma((10,)),
            dma((10,)),
            dma((3,)),
            dma((3,)),
            dma((4,)),
            dma((8, 3)),
            dma((8, 5)),
            dma((8, 5)),
            dma((8, 4)),
            dma((5, 10)),
            dma((5, 10)),
            pltpu.SemaphoreType.REGULAR((4,)),
            dma((2, 3)),
            dma((2, 3)),
            dma((10,)),
            dma((10,)),
            dma((2,)),
            dma((2, 2)),
            dma((2,)),
        ],
        compiler_params=pltpu.CompilerParams(
            collective_id=0, has_side_effects=True, vmem_limit_bytes=67043328
        ),
    )(
        tokens, attn_gain, mlp_gain, w_query, w_key.T, w_value.T, w_out, w_gate, w_up,
        w_down, cotangent, positions[None, :], segments[None, :], frequency,
    )


def hand_over_kernel(*refs):
    count = (len(refs) - 2) // 3
    sources, targets, buffers = refs[:count], refs[count : 2 * count], refs[2 * count : 3 * count]
    in_sem, out_sem = refs[3 * count :]
    fetch, store = [], []
    for n in range(count):
        rows = sources[n].shape[0]
        cut = rows // 2 if rows >= 256 or len(sources[n].shape) == 4 else rows
        for part, first in enumerate(range(0, rows, cut)):
            piece = pl.ds(first, cut)
            held = buffers[n].at[piece]
            fetch.append(pltpu.make_async_copy(sources[n].at[piece], held, in_sem.at[n, part]))
            store.append(pltpu.make_async_copy(held, targets[n].at[piece], out_sem.at[n, part]))
    for piece in fetch:
        piece.start()
    for arrival, leave in zip(fetch, store):
        arrival.wait()
        leave.start()
    for piece in store:
        piece.wait()


def hand_over(values):
    anywhere = pl.BlockSpec(memory_space=pl.ANY)
    dma = pltpu.SemaphoreType.DMA
    return pl.pallas_call(
        hand_over_kernel,
        name="hand_over",
        out_shape=tuple(jax.ShapeDtypeStruct(value.shape, value.dtype) for value in values),
        in_specs=[anywhere] * len(values),
        out_specs=(anywhere,) * len(values),
        scratch_shapes=[pltpu.VMEM(value.shape, value.dtype) for value in values]
        + [dma((len(values), 2)), dma((len(values), 2))],
        compiler_params=pltpu.CompilerParams(vmem_limit_bytes=67043328),
    )(*values)


def fast_shards(tokens, *others):
    made = run_layer(tokens, *others)
    (
        query_g, out_g, gate_g, up_g, down_g, key_g, value_g, gain_one_g, gain_two_g, result, input_grad,
    ) = hand_over(made[4:5] + made[7:11] + made[5:7] + made[2:4] + made[0:2])
    return (
        result.reshape(tokens.shape),
        input_grad.reshape(tokens.shape),
        gain_one_g.reshape(-1),
        query_g,
        key_g.T,
        value_g.T,
        out_g,
        gain_two_g.reshape(-1),
        gate_g,
        up_g,
        down_g,
    )


def solution(mesh):
    in_specs = (
        P(("fsdp", "ctx"), None),
        P(("fsdp", "ctx")),
        P(("fsdp", "ctx"), "tp"),
        P(("fsdp", "ctx"), "tp"),
        P(("fsdp", "ctx"), "tp"),
        P("tp", ("fsdp", "ctx")),
        P(("fsdp", "ctx")),
        P(("fsdp", "ctx"), "tp"),
        P(("fsdp", "ctx"), "tp"),
        P("tp", ("fsdp", "ctx")),
        P(("fsdp", "ctx"), None),
        P(("fsdp", "ctx")),
        P(("fsdp", "ctx")),
    )
    out_specs = (
        P(("fsdp", "ctx"), None),
        P(("fsdp", "ctx"), None),
        P(("fsdp", "ctx")),
        P(("fsdp", "ctx"), "tp"),
        P(("fsdp", "ctx"), "tp"),
        P(("fsdp", "ctx"), "tp"),
        P("tp", ("fsdp", "ctx")),
        P(("fsdp", "ctx")),
        P(("fsdp", "ctx"), "tp"),
        P(("fsdp", "ctx"), "tp"),
        P("tp", ("fsdp", "ctx")),
    )
    small = (mesh.shape["fsdp"], mesh.shape["ctx"], mesh.shape["tp"]) == (2, 4, 4)
    return jax.shard_map(fast_shards if small else shards, mesh=mesh, in_specs=in_specs, out_specs=out_specs, check_vma=False)
```
